32 devices in a mesh: dp: 4 (over y, x), seq: 2 (over core), head: 4 (over z).
Axes of the slice: x: 2, y: 2, z: 4, core: 2. Of those that a mesh axis runs over, the one named last changes fastest.
Arguments:
- inputs: bfloat16 [8, 1024, 1024], P('dp', ('seq', 'head')), may hold values from -6 to 6
- cotangent: bfloat16 [8, 1024, 1024], P('dp', ('seq', 'head')), may hold values from -6 to 6
- routes: int32 [2, 8, 1024, 2, 4, 2], P(None, 'dp', ('seq', 'head')), may hold values from 0 to 4, all different within a row
- lengths: int32 [8], P('dp'), may hold values from 1 to 1024, as said below
- matrix: float32 [2, 1024, 13568], P(None, ('dp', 'seq', 'head'))
- matrix_first: float32 [2, 1024, 13568], P(None, ('dp', 'seq', 'head'))
- matrix_second: float32 [2, 1024, 13568], P(None, ('dp', 'seq', 'head'))
- small: float32 [2, 1024, 44], P(None, ('dp', 'seq', 'head'))
- small_first: float32 [2, 1024, 44], P(None, ('dp', 'seq', 'head'))
- small_second: float32 [2, 1024, 44], P(None, ('dp', 'seq', 'head'))
Outputs:
- output: bfloat16 [8, 1024, 1024], P('dp', ('seq', 'head'))
- input_grad: bfloat16 [8, 1024, 1024], P('dp', ('seq', 'head'))
- matrix_grad: float32 [2, 1024, 13568], P(None, ('dp', 'seq', 'head'))
- matrix_new: float32 [2, 1024, 13568], P(None, ('dp', 'seq', 'head'))
- matrix_copy: bfloat16 [2, 1024, 13568], P(None, ('dp', 'seq', 'head'))
- matrix_first_new: float32 [2, 1024, 13568], P(None, ('dp', 'seq', 'head'))
- matrix_second_new: float32 [2, 1024, 13568], P(None, ('dp', 'seq', 'head'))
- small_grad: float32 [2, 1024, 44], P(None, ('dp', 'seq', 'head'))
- small_new: float32 [2, 1024, 44], P(None, ('dp', 'seq', 'head'))
- small_copy: bfloat16 [2, 1024, 44], P(None, ('dp', 'seq', 'head'))
- small_first_new: float32 [2, 1024, 44], P(None, ('dp', 'seq', 'head'))
- small_second_new: float32 [2, 1024, 44], P(None, ('dp', 'seq', 'head'))
- loads: float32 [2, 2, 4, 5], replicated
The draws below stay inside these ranges and needn't reach their ends.
Inputs may be any that keep to these rules, and one draw needn't show every extreme that they name: `lengths`: in each aligned group of 2 entries (the sequences of one index of dp), one equals 1024. `routes`: each row names 2 different experts.
All inputs are finite; a program needn't handle non-finite values.
Results may differ from the reference program's by a relative error of at most 0.02.
Values may be sent and summed in bfloat16 or wider, within the bound.
A program may use at most 320 MiB of HBM per device.

```python
import math
import jax
import jax.numpy as jnp
from jax import lax

D = 1024
HEADS = 4
HEAD_DIM = 112
EXPERTS = 5
FF = 4096
TOP = 2
LAYERS = 2
STEP = 10
SEQS = 2
SEG = 512
CTX = 1024
BATCH = 8
COLS = 13568
SMALL = 44


def unit_noise(key, shape):
    return jax.random.normal(key, shape, jnp.float32)


def column_scales():
    query_end = 2 * HEADS * HEAD_DIM
    value_end = query_end + HEADS * EXPERTS * HEAD_DIM
    output_end = value_end + HEADS * EXPERTS * HEAD_DIM
    up_end = output_end + FF
    column = jnp.arange(COLS)
    tokens = float(BATCH * CTX)
    spread = jnp.where(column < value_end, D ** (-0.5), jnp.where(column < output_end, 0.7 * math.sqrt(SEG) / HEAD_DIM, jnp.where(column < up_end, D ** (-0.5), FF ** (-0.5))))
    grad = jnp.where(column < query_end, 0.44 * math.sqrt(D * tokens / HEAD_DIM), jnp.where(column < value_end, 0.2 * math.sqrt(D * tokens / HEAD_DIM), jnp.where(column < output_end, 0.29 * math.sqrt(tokens / SEG), jnp.where(column < up_end, 0.26 * math.sqrt(tokens), 0.5 * math.sqrt(tokens)))))
    return (spread.astype(jnp.float32), grad.astype(jnp.float32))


def small_scales():
    column = jnp.arange(SMALL)
    router_cols = 2 * HEADS * EXPERTS
    tokens = float(BATCH * CTX)
    spread = jnp.where(column < router_cols, 0.7 * D ** (-0.5), 0.1).astype(jnp.float32)
    grad = jnp.where(column < router_cols, 0.087 * math.sqrt(D * tokens), math.sqrt(tokens)).astype(jnp.float32)
    center = jnp.where((column == router_cols) | (column == router_cols + 2), 1.0, 0.0).astype(jnp.float32)
    return (spread, grad, center)


def second_factor(key, shape):
    return jnp.exp(jax.random.uniform(key, shape, jnp.float32, 0.0, math.log(4.0)))


def draw_matrix(key, part):
    spread, grad = column_scales()
    return spread * unit_noise(jax.random.fold_in(key, 11), (LAYERS, D, COLS))


def draw_matrix_first(key, part):
    spread, grad = column_scales()
    return grad * (0.1 / 0.9) * unit_noise(jax.random.fold_in(key, 12), (LAYERS, D, COLS))


def draw_matrix_second(key, part):
    spread, grad = column_scales()
    return grad * grad * (0.05 / 0.95) * second_factor(jax.random.fold_in(key, 13), (LAYERS, D, COLS))


def draw_small(key, part):
    spread, grad, center = small_scales()
    return center + spread * unit_noise(jax.random.fold_in(key, 21), (LAYERS, D, SMALL))


def draw_small_first(key, part):
    spread, grad, center = small_scales()
    return grad * (0.1 / 0.9) * unit_noise(jax.random.fold_in(key, 22), (LAYERS, D, SMALL))


def draw_small_second(key, part):
    spread, grad, center = small_scales()
    return grad * grad * (0.05 / 0.95) * second_factor(jax.random.fold_in(key, 23), (LAYERS, D, SMALL))


def draw_lengths(key, part):
    groups = BATCH // SEQS
    first_key = jax.random.fold_in(key, 31)
    second_key = jax.random.fold_in(key, 32)
    drawn = jax.random.randint(first_key, (groups, SEQS), 1, CTX + 1)
    full = jax.random.randint(second_key, (groups, 1), 0, SEQS)
    drawn = jnp.where(jnp.arange(SEQS, dtype=jnp.int32)[None, :] == full, CTX, drawn)
    return drawn.reshape(BATCH).astype(jnp.int32)


def block_levels(key, shape, cuts, smallest, high):
    def one(position, blocks):
        heights = jax.random.uniform(jax.random.fold_in(jax.random.fold_in(key, 6), position), (blocks,), jnp.float32, smallest / len(cuts), high / len(cuts))
        return jnp.repeat(jnp.exp(heights), shape[position] // blocks).reshape((-1,) + (1,) * (len(shape) - position - 1))

    loudness = one(*cuts[0])
    for cut in cuts[1:]:
        loudness = loudness * one(*cut)
    return loudness


def choose_distinct(rng, rows, count, top, lift):
    sequence = jax.random.permutation(jax.random.fold_in(rng, 1), count)
    favour = sequence
    for power in range(3):
        favour = favour * favour // count
    favour = favour * lift // count
    chance = jax.random.randint(jax.random.fold_in(rng, 2), (rows, count), 0, 4096) + favour
    fixed_rows = jax.random.permutation(jax.random.fold_in(rng, 3), rows)[jnp.arange(count) % rows]
    chance = jnp.where(jnp.arange(rows)[:, None] == fixed_rows[None, :], 1 << 14, chance)
    score = chance * count + jnp.arange(count)
    return lax.top_k(score.astype(jnp.int32), top)[1].astype(jnp.int32)


def scatter_about(stream_key, shape, width, limit, shards=(), kind=jnp.bfloat16):
    values = width * jax.random.normal(stream_key, shape, jnp.float32)
    if shards:
        values = values * block_levels(stream_key, shape, shards, -0.22, 0.18)
    return jnp.clip(values, -limit, limit).astype(kind)


def setup_inputs(seed: int = 0) -> dict:
    arg_keys = jax.random.split(jax.random.key(seed), 11)
    inputs = scatter_about(arg_keys[0], (BATCH, CTX, D), 1.0, 6.0, ((0, 4), (1, 8)))
    cotangent = scatter_about(arg_keys[1], (BATCH, CTX, D), 1.0, 6.0, ((0, 4), (1, 8)))
    routes = choose_distinct(arg_keys[2], LAYERS * BATCH * CTX * 2 * HEADS, EXPERTS, TOP, 3276).reshape((LAYERS, BATCH, CTX, 2, HEADS, TOP))
    lengths = draw_lengths(jax.random.fold_in(arg_keys[10], 71), 0)
    matrix = draw_matrix(jax.random.fold_in(arg_keys[10], 71), 0)
    matrix_first = draw_matrix_first(jax.random.fold_in(arg_keys[10], 71), 0)
    matrix_second = draw_matrix_second(jax.random.fold_in(arg_keys[10], 71), 0)
    small = draw_small(jax.random.fold_in(arg_keys[10], 71), 0)
    small_first = draw_small_first(jax.random.fold_in(arg_keys[10], 71), 0)
    small_second = draw_small_second(jax.random.fold_in(arg_keys[10], 71), 0)
    return {"inputs": inputs, "cotangent": cotangent, "routes": routes, "lengths": lengths, "matrix": matrix, "matrix_first": matrix_first, "matrix_second": matrix_second, "small": small, "small_first": small_first, "small_second": small_second}


NORM_EPS = 1e-05
BETA_ONE = 0.9
BETA_TWO = 0.95
ADAM_EPS = 1e-08
WEIGHT_DECAY = 0.1
NORM_RATE = 0.5
MASKED = -1e+30
HIGHEST = lax.Precision.HIGHEST

@jax.custom_vjp
def low(v):
    return lax.optimization_barrier(v.astype(jnp.bfloat16)).astype(jnp.float32)

@jax.custom_vjp
def low_back(v):
    return v

def low_keep(v):
    return (low(v), None)

def low_pass(kept, grad):
    return (grad,)

def back_keep(v):
    return (v, None)

def back_low(kept, grad):
    return (low(grad),)
low.defvjp(low_keep, low_pass)
low_back.defvjp(back_keep, back_low)

def both_ways(value):
    return low(low_back(value))

def column_bounds():
    query_end = 2 * HEADS * HEAD_DIM
    value_end = query_end + HEADS * EXPERTS * HEAD_DIM
    output_end = value_end + HEADS * EXPERTS * HEAD_DIM
    return (query_end, value_end, output_end, output_end + FF)

def column_rates(segment):
    query_end, value_end, output_end, up_end = column_bounds()
    column = jnp.arange(up_end + FF)
    inner = D ** (-0.5)
    outer = 0.7 * math.sqrt(segment) / HEAD_DIM
    rates = jnp.where(column < value_end, inner, jnp.where(column < output_end, outer, jnp.where(column < up_end, inner, FF ** (-0.5))))
    return rates.astype(jnp.float32)

def small_rates():
    column = jnp.arange(2 * HEADS * EXPERTS + 4)
    return jnp.where(column < 2 * HEADS * EXPERTS, 0.7 * D ** (-0.5), NORM_RATE).astype(jnp.float32)

def adam_update(weight, grad, first, second, rates, decay):
    first_new = BETA_ONE * first + (1.0 - BETA_ONE) * grad
    second_new = BETA_TWO * second + (1.0 - BETA_TWO) * grad * grad
    first_hat = first_new / (1.0 - BETA_ONE ** STEP)
    second_hat = second_new / (1.0 - BETA_TWO ** STEP)
    new = weight - rates * (first_hat / (jnp.sqrt(second_hat) + ADAM_EPS) + decay * weight)
    return (new, first_new, second_new)

def rotary_tables(positions):
    half = HEAD_DIM // 2
    inverse = jnp.exp(-math.log(10000.0) * jnp.arange(half, dtype=jnp.float32) / half)
    angle = positions.astype(jnp.float32)[:, None] * inverse[None, :]
    return (jnp.cos(angle), jnp.sin(angle))

def rotate_pairs(tensor, cosines, sines):
    half = tensor.shape[-1] // 2
    first, second = (tensor[..., :half], tensor[..., half:])
    return jnp.concatenate([first * cosines - second * sines, second * cosines + first * sines], axis=-1)

def layer_norm(values, gain, bias):
    mean = lax.optimization_barrier(jnp.mean(values, axis=-1, keepdims=True))
    centered = values - mean
    variance = lax.optimization_barrier(jnp.mean(centered * centered, axis=-1, keepdims=True))
    return centered * lax.rsqrt(variance + NORM_EPS) * gain + bias

def attention(query, key, value, lengths):
    blocks = CTX // SEG
    shape = (BATCH, blocks, SEG, HEADS, HEAD_DIM)
    query_blocks = query.reshape(shape)
    key_blocks = key.reshape(shape)
    value_blocks = value.reshape(shape)
    empty = jnp.zeros((BATCH, 1, SEG, HEADS, HEAD_DIM), jnp.float32)
    key_memory = low_back(jnp.concatenate([empty, key_blocks[:, :-1]], axis=1))
    value_memory = low_back(jnp.concatenate([empty, value_blocks[:, :-1]], axis=1))
    flat = (BATCH * blocks, SEG, HEADS, HEAD_DIM)
    block_lengths = jnp.repeat(lengths, blocks)
    block_starts = jnp.tile(jnp.arange(blocks, dtype=jnp.int32) * SEG, BATCH)
    scale = HEAD_DIM ** (-0.5)

    def one_block(pieces):
        queries, keys_own, values_own, keys_mem, values_mem, length, start = pieces
        keys = jnp.concatenate([keys_mem, keys_own], axis=0)
        values = jnp.concatenate([values_mem, values_own], axis=0)
        query_pos = start + jnp.arange(SEG, dtype=jnp.int32)
        key_pos = start - SEG + jnp.arange(2 * SEG, dtype=jnp.int32)
        allowed = (key_pos[None, :] <= query_pos[:, None]) & (key_pos[None, :] >= 0) & ((key_pos[None, :] < length) | (key_pos[None, :] == query_pos[:, None]))
        raw = low_back(jnp.einsum('qhc,khc->hqk', queries, keys, precision=HIGHEST))
        scores = jnp.where(allowed[None], raw * scale, MASKED)
        top = lax.optimization_barrier(jnp.max(scores, axis=-1, keepdims=True))
        weights = jnp.exp(scores - top)
        probs = low(weights / lax.optimization_barrier(jnp.sum(weights, axis=-1, keepdims=True)))
        return jnp.einsum('hqk,khc->qhc', probs, values, precision=HIGHEST)
    result = lax.map(jax.checkpoint(one_block), (query_blocks.reshape(flat), key_blocks.reshape(flat), value_blocks.reshape(flat), key_memory.reshape(flat), value_memory.reshape(flat), block_lengths, block_starts))
    return result.reshape(BATCH, CTX, HEADS, HEAD_DIM)

def block(hidden, weights, smalls, chosen_here, lengths, cosines, sines):
    query_end, value_end, output_end, up_end = column_bounds()
    router_cols = 2 * HEADS * EXPERTS
    first_in = low(layer_norm(hidden, smalls[:, router_cols], smalls[:, router_cols + 1]))
    logits = low_back(jnp.dot(first_in, smalls[:, :router_cols], precision=HIGHEST))
    gate_prob = jax.nn.sigmoid(logits).reshape(BATCH, CTX, 2, HEADS, EXPERTS)
    gates = gate_prob * chosen_here
    query_key = low_back(jnp.dot(first_in, weights[:, :query_end], precision=HIGHEST)).reshape(BATCH, CTX, 2, HEADS, HEAD_DIM)
    query = both_ways(rotate_pairs(query_key[:, :, 0], cosines, sines))
    key = both_ways(rotate_pairs(query_key[:, :, 1], cosines, sines))
    projected = low_back(jnp.dot(first_in, weights[:, query_end:value_end], precision=HIGHEST)).reshape(BATCH, CTX, HEADS, EXPERTS, HEAD_DIM)
    value = both_ways(lax.optimization_barrier(jnp.sum(gates[:, :, 0, :, :, None] * projected, axis=3)))
    attended = both_ways(attention(query, key, value, lengths))
    mixed = low(gates[:, :, 1, :, :, None] * attended[:, :, :, None, :]).reshape(BATCH, CTX, HEADS * EXPERTS * HEAD_DIM)
    residual = hidden + low_back(jnp.dot(mixed, weights[:, value_end:output_end].T, precision=HIGHEST))
    second_in = low(layer_norm(residual, smalls[:, router_cols + 2], smalls[:, router_cols + 3]))
    up = low_back(jnp.dot(second_in, weights[:, output_end:up_end], precision=HIGHEST))
    act = low(jax.nn.gelu(up, approximate=True))
    return residual + low_back(jnp.dot(act, weights[:, up_end:].T, precision=HIGHEST))

def reference(inputs, cotangent, routes, lengths, matrix, matrix_first, matrix_second, small, small_first, small_second):
    positions = jnp.arange(CTX, dtype=jnp.int32)
    valid = (positions[None, :] < lengths[:, None]).astype(jnp.float32)
    cosines, sines = rotary_tables(positions)
    cosines = cosines[:, None, :]
    sines = sines[:, None, :]
    chosen = lax.optimization_barrier(jnp.sum((routes[..., None] == jnp.arange(EXPERTS, dtype=jnp.int32)).astype(jnp.float32), axis=-2))
    loads = lax.optimization_barrier(jnp.sum(chosen * valid[None, :, :, None, None, None], axis=(1, 2)))
    start_hidden = inputs.astype(jnp.float32)
    matrix_low = matrix.astype(jnp.bfloat16).astype(jnp.float32)
    small_low = small.astype(jnp.bfloat16).astype(jnp.float32)

    def network(hidden, matrices, smalls):
        for layer in range(LAYERS):
            hidden = block(hidden, matrices[layer], smalls[layer], chosen[layer], lengths, cosines, sines)
        return hidden
    output, pull = jax.vjp(network, start_hidden, matrix_low, small_low)
    grad_input, matrix_grad, small_grad = pull(cotangent.astype(jnp.float32) * valid[:, :, None])
    matrix_new, matrix_first_new, matrix_second_new = adam_update(matrix, matrix_grad, matrix_first, matrix_second, column_rates(SEG), WEIGHT_DECAY)
    small_new, small_first_new, small_second_new = adam_update(small, small_grad, small_first, small_second, small_rates(), 0.0)
    return (output.astype(jnp.bfloat16), grad_input.astype(jnp.bfloat16), matrix_grad, matrix_new, matrix_new.astype(jnp.bfloat16), matrix_first_new, matrix_second_new, small_grad, small_new, small_new.astype(jnp.bfloat16), small_first_new, small_second_new, loads)
```

```python
import math

import jax
import jax.numpy as jnp
from jax import lax
from jax.sharding import PartitionSpec as P

D = 1024
HEADS = 4
HEAD_DIM = 112
EXPERTS = 5
FF = 4096
LAYERS = 2
STEP = 10


NORM_EPS = 1e-05
BETA_ONE = 0.9
BETA_TWO = 0.95
ADAM_EPS = 1e-08
WEIGHT_DECAY = 0.1
NORM_RATE = 0.5
MASKED = -1e30


def passed_along(value, axis, by):
    devices = lax.axis_size(axis)
    pairs = [(i, i + by) for i in range(devices) if 0 <= i + by < devices]
    return lax.ppermute(value, axis, pairs)


def column_bounds():
    query_end = 2 * HEADS * HEAD_DIM
    value_end = query_end + HEADS * EXPERTS * HEAD_DIM
    output_end = value_end + HEADS * EXPERTS * HEAD_DIM
    return (query_end, value_end, output_end, output_end + FF)


def column_rates(segment):
    query_end, value_end, output_end, up_end = column_bounds()
    column = jnp.arange(up_end + FF)
    inner = D ** (-0.5)
    outer = 0.7 * math.sqrt(segment) / HEAD_DIM
    rates = jnp.where(
        column < value_end,
        inner,
        jnp.where(column < output_end, outer, jnp.where(column < up_end, inner, FF ** (-0.5))),
    )
    return rates.astype(jnp.float32)


def small_rates():
    column = jnp.arange(2 * HEADS * EXPERTS + 4)
    return jnp.where(column < 2 * HEADS * EXPERTS, 0.7 * D ** (-0.5), NORM_RATE).astype(jnp.float32)


def adam_update(weight, grad, first, second, rates, decay):
    first_new = BETA_ONE * first + (1.0 - BETA_ONE) * grad
    second_new = BETA_TWO * second + (1.0 - BETA_TWO) * grad * grad
    first_hat = first_new / (1.0 - BETA_ONE**STEP)
    second_hat = second_new / (1.0 - BETA_TWO**STEP)
    new = weight - rates * (first_hat / (jnp.sqrt(second_hat) + ADAM_EPS) + decay * weight)
    return (new, first_new, second_new)


def rotary_tables(positions):
    half = HEAD_DIM // 2
    inverse = jnp.exp(-math.log(10000.0) * jnp.arange(half, dtype=jnp.float32) / half)
    angle = positions.astype(jnp.float32)[:, None] * inverse[None, :]
    return (jnp.cos(angle), jnp.sin(angle))


def rotate_pairs(tensor, cosines, sines):
    half = tensor.shape[-1] // 2
    first, second = (tensor[..., :half], tensor[..., half:])
    return jnp.concatenate(
        [first * cosines - second * sines, second * cosines + first * sines], axis=-1
    )


def rotate_back(tensor, cosines, sines):
    half = tensor.shape[-1] // 2
    first, second = (tensor[..., :half], tensor[..., half:])
    return jnp.concatenate(
        [first * cosines + second * sines, second * cosines - first * sines], axis=-1
    )


def layer_stats(values):
    mean = jnp.mean(values, axis=-1, keepdims=True)
    centered = values - mean
    variance = jnp.mean(centered * centered, axis=-1, keepdims=True)
    inverse = lax.rsqrt(variance + NORM_EPS)
    return (centered * inverse, inverse)


def norm_back(grad_normed, normed, inverse, gain):
    scaled = grad_normed * gain
    return inverse * (
        scaled
        - jnp.mean(scaled, axis=-1, keepdims=True)
        - normed * jnp.mean(scaled * normed, axis=-1, keepdims=True)
    )


def contract_last(left, right):
    return lax.dot_general(
        left, right, (((1,), (1,)), ((), ())), preferred_element_type=jnp.float32
    )


def contract_first(left, right):
    return lax.dot_general(
        left, right, (((0,), (0,)), ((), ())), preferred_element_type=jnp.float32
    )


def reduction_order(tensor):
    dp, seq, head = (lax.axis_size("dp"), lax.axis_size("seq"), lax.axis_size("head"))
    count, width = tensor.shape
    split = tensor.reshape(count, dp, seq, width // (dp * seq))
    return split.transpose(0, 2, 1, 3).reshape(count, width)


def reduce_rows(grad):
    parts = lax.psum_scatter(grad, "seq", scatter_dimension=0, tiled=True)
    parts = lax.psum_scatter(parts, "dp", scatter_dimension=0, tiled=True)
    return lax.psum_scatter(parts, "head", scatter_dimension=0, tiled=True)


def weight_grad(left, right):
    return contract_first(reduction_order(left), right).astype(jnp.bfloat16)


def to_heads(tensor, pieces):
    seq_count, sub_rows = tensor.shape[:2]
    heads = HEADS
    sent = tensor.transpose(3, 2, 0, 1, 4)
    got = lax.all_to_all(sent, "head", split_axis=0, concat_axis=0, tiled=True)
    return got.transpose(1, 2, 0, 3, 4).reshape(pieces, seq_count, heads * sub_rows, HEAD_DIM)


def to_tokens(tensor, sub_rows):
    pieces, seq_count, segment, head_dim = tensor.shape
    sent = tensor.reshape(pieces, seq_count, segment // sub_rows, sub_rows, head_dim)
    sent = sent.transpose(2, 0, 1, 3, 4)
    got = lax.all_to_all(sent, "head", split_axis=0, concat_axis=0, tiled=True)
    return got.transpose(2, 3, 1, 0, 4)


def block_scores(query_block, keys, query_pos, key_pos, lengths):
    raw = jnp.einsum("sqc,skc->sqk", query_block, keys, preferred_element_type=jnp.float32)
    later = key_pos[None, None, :] <= query_pos[None, :, None]
    inside = key_pos[None, None, :] >= 0
    used = (key_pos[None, None, :] < lengths[:, None, None]) | (
        key_pos[None, None, :] == query_pos[None, :, None]
    )
    allowed = later & inside & used
    return jnp.where(allowed, raw * HEAD_DIM ** (-0.5), MASKED)


def attend_forward(query_heads, keys, values, seq_start, lengths, segment):
    rows = min(512, segment)
    key_pos = seq_start - segment + jnp.arange(2 * segment, dtype=jnp.int32)
    outputs, tops, totals = ([], [], [])
    query_pos = seq_start + 0 + jnp.arange(rows, dtype=jnp.int32)
    scores = block_scores(query_heads, keys, query_pos, key_pos, lengths)
    top = jnp.max(scores, axis=-1, keepdims=True)
    weights = jnp.exp(scores - top)
    total = jnp.sum(weights, axis=-1, keepdims=True)
    probs = (weights / total).astype(jnp.bfloat16)
    outputs.append(jnp.einsum("sqk,skc->sqc", probs, values, preferred_element_type=jnp.float32))
    tops.append(top)
    totals.append(total)
    return (outputs[0], tops, totals)


def attend_backward(
    query_heads, keys, values, grad_heads, tops, totals, seq_start, lengths, segment
):
    rows = min(512, segment)
    key_pos = seq_start - segment + jnp.arange(2 * segment, dtype=jnp.int32)
    grad_keys = jnp.zeros(keys.shape, jnp.float32)
    grad_values = jnp.zeros(values.shape, jnp.float32)
    grad_queries = []
    for index, start in enumerate(range(0, segment, rows)):
        query_pos = seq_start + start + jnp.arange(rows, dtype=jnp.int32)
        scores = block_scores(query_heads, keys, query_pos, key_pos, lengths)
        probs = jnp.exp(scores - tops[index]) / totals[index]
        grad_probs = jnp.einsum(
            "sqc,skc->sqk", grad_heads, values, preferred_element_type=jnp.float32
        )
        delta = jnp.sum(probs * grad_probs, axis=-1, keepdims=True)
        grad_raw = (probs * (grad_probs - delta) * HEAD_DIM ** (-0.5)).astype(jnp.bfloat16)
        grad_queries.append(
            jnp.einsum("sqk,skc->sqc", grad_raw, keys, preferred_element_type=jnp.float32)
        )
        grad_keys = jnp.einsum(
            "sqk,sqc->skc", grad_raw, query_heads, preferred_element_type=jnp.float32
        )
        grad_values = jnp.einsum(
            "sqk,sqc->skc",
            probs.astype(jnp.bfloat16),
            grad_heads,
            preferred_element_type=jnp.float32,
        )
    return (grad_queries[0], grad_keys, grad_values)


def gelu_tanh(values):
    return jax.nn.gelu(values, approximate=True)


def local(
    inputs,
    cotangent,
    routes,
    lengths,
    matrix,
    matrix_first,
    matrix_second,
    small,
    small_first,
    small_second,
):
    head_count = lax.axis_size("head")
    seq_count, sub_rows, width = inputs.shape
    segment = sub_rows * head_count
    tokens = seq_count * sub_rows
    router_cols = 2 * HEADS * EXPERTS
    group = HEADS * EXPERTS
    query_end, value_end, output_end, up_end = column_bounds()
    seq_start = lax.axis_index("seq") * segment
    positions = (
        seq_start + lax.axis_index("head") * sub_rows + jnp.arange(sub_rows, dtype=jnp.int32)
    )
    valid = (positions[None, :] < lengths[:, None]).astype(jnp.float32)
    cosines, sines = rotary_tables(positions)
    cosines = cosines[:, None, None, :]
    sines = sines[:, None, None, :]
    chosen = jnp.sum(
        (routes[..., None] == jnp.arange(EXPERTS, dtype=jnp.int32)).astype(jnp.float32), axis=-2
    )
    load_part = jnp.sum(chosen * valid[None, :, :, None, None, None], axis=(1, 2))
    matrix_low = matrix.astype(jnp.bfloat16)
    small_size = small.size
    carried = jnp.concatenate([small.reshape(-1), load_part.reshape(-1)])
    carried = jnp.pad(carried, (0, (-carried.size) % 1024))[None]
    carried = lax.all_gather(carried, ("dp", "seq", "head"), axis=0, tiled=True)
    loads = jnp.sum(carried[:, small_size : small_size + load_part.size], axis=0).reshape(load_part.shape)
    small_all = (
        carried[:, :small_size]
        .reshape(carried.shape[0], LAYERS, small.shape[1], small.shape[2])
        .transpose(1, 0, 2, 3)
        .reshape(LAYERS, width, small.shape[2])
        .astype(jnp.bfloat16)
    )
    hidden = inputs.astype(jnp.float32).reshape(tokens, width)
    kept = []
    gathered = [
        lax.all_gather(part, ("dp", "seq", "head"), axis=0, tiled=True)
        for layer in range(LAYERS)
        for part in (matrix_low[layer, :, :output_end], matrix_low[layer, :, output_end:])
    ]
    for layer in range(LAYERS):
        attn_w, ffn_w = (gathered[2 * layer], gathered[2 * layer + 1])
        small_w = small_all[layer]
        gains = small_w[:, router_cols:].astype(jnp.float32)
        normed_one, inverse_one = layer_stats(hidden)
        first_in = (normed_one * gains[:, 0] + gains[:, 1]).astype(jnp.bfloat16)
        gate_prob = jax.nn.sigmoid(
            jnp.dot(first_in, small_w[:, :router_cols], preferred_element_type=jnp.float32)
        ).reshape(tokens, 2, HEADS, EXPERTS)
        chosen_here = chosen[layer].reshape(tokens, 2, HEADS, EXPERTS)
        gates = gate_prob * chosen_here
        query_key = jnp.dot(
            first_in, attn_w[:, :query_end], preferred_element_type=jnp.float32
        ).reshape(seq_count, sub_rows, 2, HEADS, HEAD_DIM)
        rotated = rotate_pairs(query_key, cosines, sines).astype(jnp.bfloat16)
        projected = jnp.dot(
            first_in, attn_w[:, query_end:value_end], preferred_element_type=jnp.float32
        ).reshape(tokens, HEADS, EXPERTS, HEAD_DIM)
        value_rows = jnp.sum(gates[:, 0, :, :, None] * projected, axis=2).astype(jnp.bfloat16)
        heads_in = to_heads(
            jnp.concatenate(
                [rotated, value_rows.reshape(seq_count, sub_rows, 1, HEADS, HEAD_DIM)], axis=2
            ),
            3,
        )
        memory = passed_along(heads_in[1:], "seq", 1)
        query_heads = heads_in[0]
        keys = jnp.concatenate([memory[0], heads_in[1]], axis=1)
        values = jnp.concatenate([memory[1], heads_in[2]], axis=1)
        attended, tops, totals = attend_forward(
            query_heads, keys, values, seq_start, lengths, segment
        )
        attended_rows = to_tokens(attended.astype(jnp.bfloat16)[None], sub_rows).reshape(
            tokens, HEADS, HEAD_DIM
        )
        mixed = (
            (gates[:, 1, :, :, None] * attended_rows[:, :, None, :].astype(jnp.float32))
            .astype(jnp.bfloat16)
            .reshape(tokens, group * HEAD_DIM)
        )
        residual = hidden + contract_last(mixed, attn_w[:, value_end:])
        normed_two, inverse_two = layer_stats(residual)
        second_in = (normed_two * gains[:, 2] + gains[:, 3]).astype(jnp.bfloat16)
        up = jnp.dot(second_in, ffn_w[:, :FF], preferred_element_type=jnp.float32)
        act = gelu_tanh(up).astype(jnp.bfloat16)
        hidden = residual + contract_last(act, ffn_w[:, FF:])
        kept.append(
            (
                normed_one,
                inverse_one,
                first_in,
                gate_prob,
                chosen_here,
                gates,
                projected,
                query_heads,
                keys,
                values,
                tops,
                totals,
                attended_rows,
                mixed,
                normed_two,
                inverse_two,
                second_in,
                up,
                act,
            )
        )
    output = hidden.reshape(seq_count, sub_rows, width).astype(jnp.bfloat16)
    grad_hidden = (cotangent.astype(jnp.float32) * valid[:, :, None]).reshape(tokens, width)
    matrix_rows = [None] * LAYERS
    small_rows = [None] * LAYERS
    for layer in reversed(range(LAYERS)):
        (
            normed_one,
            inverse_one,
            first_in,
            gate_prob,
            chosen_here,
            gates,
            projected,
            query_heads,
            keys,
            values,
            tops,
            totals,
            attended_rows,
            mixed,
            normed_two,
            inverse_two,
            second_in,
            up,
            act,
        ) = kept[layer]
        attn_w, ffn_w = (gathered[2 * layer], gathered[2 * layer + 1])
        small_w = small_all[layer]
        gains = small_w[:, router_cols:].astype(jnp.float32)
        grad_low = grad_hidden.astype(jnp.bfloat16)
        grad_act = jnp.dot(grad_low, ffn_w[:, FF:], preferred_element_type=jnp.float32)
        gelu_value, gelu_pull = jax.vjp(gelu_tanh, up)
        grad_up = gelu_pull(grad_act)[0].astype(jnp.bfloat16)
        up_share = reduce_rows(weight_grad(second_in, grad_up))
        down_share = reduce_rows(weight_grad(grad_low, act))
        grad_second = contract_last(grad_up, ffn_w[:, :FF])
        gain_two_grad = jnp.sum(grad_second * normed_two, axis=0)
        bias_two_grad = jnp.sum(grad_second, axis=0)
        grad_residual = grad_hidden + norm_back(grad_second, normed_two, inverse_two, gains[:, 2])
        residual_low = grad_residual.astype(jnp.bfloat16)
        grad_mixed = jnp.dot(
            residual_low, attn_w[:, value_end:], preferred_element_type=jnp.float32
        ).reshape(tokens, HEADS, EXPERTS, HEAD_DIM)
        out_share = reduce_rows(weight_grad(residual_low, mixed))
        grad_gate_out = jnp.sum(
            grad_mixed * attended_rows[:, :, None, :].astype(jnp.float32), axis=-1
        )
        grad_att_rows = jnp.sum(grad_mixed * gates[:, 1, :, :, None], axis=2).astype(jnp.bfloat16)
        grad_heads_in = to_heads(
            grad_att_rows.reshape(seq_count, sub_rows, 1, HEADS, HEAD_DIM), 1
        )[0]
        grad_query, grad_keys, grad_values = attend_backward(
            query_heads, keys, values, grad_heads_in, tops, totals, seq_start, lengths, segment
        )
        grad_kv = jnp.stack([grad_keys, grad_values], axis=0)
        kv_back = passed_along(grad_kv[:, :, :segment].astype(jnp.bfloat16), "seq", -1)
        grad_kv_own = (grad_kv[:, :, segment:] + kv_back.astype(jnp.float32)).astype(jnp.bfloat16)
        grads_tok = to_tokens(
            jnp.concatenate([grad_query.astype(jnp.bfloat16)[None], grad_kv_own], axis=0), sub_rows
        )
        grads_tok = grads_tok.astype(jnp.float32)
        grad_qk = (
            rotate_back(grads_tok[:, :, :2], cosines, sines)
            .astype(jnp.bfloat16)
            .reshape(tokens, query_end)
        )
        grad_value_rows = grads_tok[:, :, 2].reshape(tokens, HEADS, HEAD_DIM)
        grad_proj = (
            (gates[:, 0, :, :, None] * grad_value_rows[:, :, None, :])
            .astype(jnp.bfloat16)
            .reshape(tokens, group * HEAD_DIM)
        )
        grad_gate_value = jnp.sum(projected * grad_value_rows[:, :, None, :], axis=-1)
        grad_gates = jnp.stack([grad_gate_value, grad_gate_out], axis=1) * chosen_here
        grad_logit = (
            (grad_gates * gate_prob * (1.0 - gate_prob)).astype(jnp.bfloat16).reshape(tokens, -1)
        )
        grad_in = jnp.concatenate([grad_qk, grad_proj], axis=1)
        grad_first = contract_last(grad_in, attn_w[:, :value_end]) + contract_last(
            grad_logit, small_w[:, :router_cols]
        )
        gain_one_grad = jnp.sum(grad_first * normed_one, axis=0)
        bias_one_grad = jnp.sum(grad_first, axis=0)
        grad_hidden = grad_residual + norm_back(grad_first, normed_one, inverse_one, gains[:, 0])
        norm_grads = jnp.stack(
            [gain_one_grad, bias_one_grad, gain_two_grad, bias_two_grad], axis=1
        )
        side = (-(value_end + router_cols + 4)) % 128
        in_share = reduce_rows(
            jnp.concatenate(
                [
                    weight_grad(first_in, grad_in),
                    weight_grad(first_in, grad_logit),
                    reduction_order(norm_grads.T).T.astype(jnp.bfloat16),
                    jnp.zeros((width, side), jnp.bfloat16),
                ],
                axis=1,
            )
        )
        matrix_rows[layer] = jnp.concatenate(
            [in_share[:, :value_end], out_share, up_share, down_share], axis=1
        ).astype(jnp.float32)
        small_rows[layer] = in_share[:, value_end : value_end + router_cols + 4].astype(jnp.float32)
    input_grad = grad_hidden.reshape(seq_count, sub_rows, width).astype(jnp.bfloat16)
    matrix_grad = jnp.stack(matrix_rows, axis=0)
    small_grad = jnp.stack(small_rows, axis=0)
    matrix_new, matrix_first_new, matrix_second_new = adam_update(
        matrix, matrix_grad, matrix_first, matrix_second, column_rates(segment), WEIGHT_DECAY
    )
    small_new, small_first_new, small_second_new = adam_update(
        small, small_grad, small_first, small_second, small_rates(), 0.0
    )
    return (
        output,
        input_grad,
        matrix_grad,
        matrix_new,
        matrix_new.astype(jnp.bfloat16),
        matrix_first_new,
        matrix_second_new,
        small_grad,
        small_new,
        small_new.astype(jnp.bfloat16),
        small_first_new,
        small_second_new,
        loads,
    )


def solution(mesh):
    in_specs = (
        P("dp", ("seq", "head"), None),
        P("dp", ("seq", "head"), None),
        P(None, "dp", ("seq", "head"), None, None, None),
        P("dp"),
        P(None, ("dp", "seq", "head"), None),
        P(None, ("dp", "seq", "head"), None),
        P(None, ("dp", "seq", "head"), None),
        P(None, ("dp", "seq", "head"), None),
        P(None, ("dp", "seq", "head"), None),
        P(None, ("dp", "seq", "head"), None),
    )
    out_specs = (
        P("dp", ("seq", "head"), None),
        P("dp", ("seq", "head"), None),
        P(None, ("dp", "seq", "head"), None),
        P(None, ("dp", "seq", "head"), None),
        P(None, ("dp", "seq", "head"), None),
        P(None, ("dp", "seq", "head"), None),
        P(None, ("dp", "seq", "head"), None),
        P(None, ("dp", "seq", "head"), None),
        P(None, ("dp", "seq", "head"), None),
        P(None, ("dp", "seq", "head"), None),
        P(None, ("dp", "seq", "head"), None),
        P(None, ("dp", "seq", "head"), None),
        P(),
    )
    return jax.shard_map(local, mesh=mesh, in_specs=in_specs, out_specs=out_specs, check_vma=False)
```

```python
import math

import jax
import jax.numpy as jnp
from jax import lax
from jax.experimental import pallas as pl
from jax.experimental.pallas import tpu as pltpu
from jax.sharding import PartitionSpec as P

D = 1024
HEADS = 4
HEAD_DIM = 112
EXPERTS = 5
FF = 4096
LAYERS = 2
STEP = 10


NORM_EPS = 1e-05
BETA_ONE = 0.9
BETA_TWO = 0.95
ADAM_EPS = 1e-08
WEIGHT_DECAY = 0.1
NORM_RATE = 0.5
MASKED = -1e30
CHUNK = 512


def passed_along(value, axis, by):
    devices = lax.axis_size(axis)
    pairs = [(i, i + by) for i in range(devices) if 0 <= i + by < devices]
    return lax.ppermute(value, axis, pairs)


def column_bounds():
    query_end = 2 * HEADS * HEAD_DIM
    value_end = query_end + HEADS * EXPERTS * HEAD_DIM
    output_end = value_end + HEADS * EXPERTS * HEAD_DIM
    return (query_end, value_end, output_end, output_end + FF)


def column_rates(segment):
    query_end, value_end, output_end, up_end = column_bounds()
    column = jnp.arange(up_end + FF)
    inner = D ** (-0.5)
    outer = 0.7 * math.sqrt(segment) / HEAD_DIM
    rates = jnp.where(
        column < value_end,
        inner,
        jnp.where(column < output_end, outer, jnp.where(column < up_end, inner, FF ** (-0.5))),
    )
    return rates.astype(jnp.float32)


def small_rates():
    column = jnp.arange(2 * HEADS * EXPERTS + 4)
    return jnp.where(column < 2 * HEADS * EXPERTS, 0.7 * D ** (-0.5), NORM_RATE).astype(jnp.float32)


def adam_update(weight, grad, first, second, rates, decay):
    first_new = BETA_ONE * first + (1.0 - BETA_ONE) * grad
    second_new = BETA_TWO * second + (1.0 - BETA_TWO) * grad * grad
    first_hat = first_new / (1.0 - BETA_ONE**STEP)
    second_hat = second_new / (1.0 - BETA_TWO**STEP)
    new = weight - rates * (first_hat / (jnp.sqrt(second_hat) + ADAM_EPS) + decay * weight)
    return (new, first_new, second_new)


def rotary_tables(positions):
    half = HEAD_DIM // 2
    inverse = jnp.exp(-math.log(10000.0) * jnp.arange(half, dtype=jnp.float32) / half)
    angle = positions.astype(jnp.float32)[:, None] * inverse[None, :]
    return (jnp.cos(angle), jnp.sin(angle))


def rotate_pairs(tensor, cosines, sines):
    half = tensor.shape[-1] // 2
    first, second = (tensor[..., :half], tensor[..., half:])
    return jnp.concatenate(
        [first * cosines - second * sines, second * cosines + first * sines], axis=-1
    )


def rotate_back(tensor, cosines, sines):
    half = tensor.shape[-1] // 2
    first, second = (tensor[..., :half], tensor[..., half:])
    return jnp.concatenate(
        [first * cosines + second * sines, second * cosines - first * sines], axis=-1
    )


def layer_stats(values):
    mean = jnp.mean(values, axis=-1, keepdims=True)
    centered = values - mean
    variance = jnp.mean(centered * centered, axis=-1, keepdims=True)
    inverse = lax.rsqrt(variance + NORM_EPS)
    return (centered * inverse, inverse)


def norm_back(grad_normed, normed, inverse, gain):
    scaled = grad_normed * gain
    return inverse * (
        scaled
        - jnp.mean(scaled, axis=-1, keepdims=True)
        - normed * jnp.mean(scaled * normed, axis=-1, keepdims=True)
    )


def contract_last(left, right):
    return lax.dot_general(
        left, right, (((1,), (1,)), ((), ())), preferred_element_type=jnp.float32
    )


def contract_first(left, right):
    return lax.dot_general(
        left, right, (((0,), (0,)), ((), ())), preferred_element_type=jnp.float32
    )


AXES = ("dp", "seq", "head")


def halving_plan(sizes, width):
    dims = [
        (axis, bit) for axis in AXES for bit in reversed(range(sizes[axis].bit_length() - 1))
    ]
    dp_dims, seq_dims, head_dims = (
        [index for index, (axis, bit) in enumerate(dims) if axis == name] for name in AXES
    )
    orders = (
        seq_dims[::-1] + dp_dims[::-1] + head_dims[::-1],
        seq_dims[::-1] + dp_dims + head_dims[::-1],
    )
    stages = []
    for stage in range(len(dims)):
        together = set(orders[0][:stage]) == set(orders[1][:stage]) and (
            orders[0][stage] == orders[1][stage]
        )
        columns = [(0, 0, width)] if together else [(0, 0, width // 2), (1, width // 2, width // 2)]
        parts = []
        for which, start, count in columns:
            left = [d for d in range(len(dims)) if d not in orders[which][:stage]]
            parts.append((start, count, orders[which][stage], left))
        stages.append(parts)
    lags = [2 if dims[parts[0][2]][0] == "dp" else 2 for parts in stages]
    return dims, stages, lags


def reduce_weight_grads(pairs, extras, width):
    sizes = {axis: lax.axis_size(axis) for axis in AXES}
    dims, stages, lags = halving_plan(sizes, width)
    depth = len(dims)
    tokens, model = pairs[0][0].shape
    rows = model >> depth
    firsts = [0]
    for left, right in pairs:
        firsts.append(firsts[-1] + right.shape[1] // width)
    chunks = firsts[-1]
    per_layer = len(pairs) // len(extras)
    spots = [
        (firsts[per_layer * index] + near // width, near % width)
        for index, (_, near) in enumerate(extras)
    ]
    starts = [sum(lags[:stage]) for stage in range(depth + 1)]
    count_pairs, count_extras = (len(pairs), len(extras))

    def kernel(*refs):
        lefts = refs[:count_pairs]
        rights = refs[count_pairs : 2 * count_pairs]
        added = refs[2 * count_pairs : 2 * count_pairs + count_extras]
        rest = refs[2 * count_pairs + count_extras :]
        out_ref, left_buf, turned, right_buf, load_sem = rest[:5]
        pool = iter(rest[5:])
        buffers = [[tuple(next(pool) for _ in range(4)) for _ in parts] for parts in stages]
        step = pl.program_id(0)
        place = {axis: lax.axis_index(axis) for axis in AXES}
        bits = [lax.rem(place[axis] // (1 << bit), 2) for axis, bit in dims]
        partners = [
            {axis: place[axis] + (1 << bit) * (1 - 2 * bits[index])}
            for index, (axis, bit) in enumerate(dims)
        ]

        def exchange(stage, part, slot):
            start, count, dim, left = stages[stage][part]
            own, got, send_sem, recv_sem = buffers[stage][part]
            lead = (slot,) + (slice(None),) * left.index(dim)
            return pltpu.make_async_remote_copy(
                src_ref=own.at[lead + (1 - bits[dim],)],
                dst_ref=got.at[slot],
                send_sem=send_sem.at[slot],
                recv_sem=recv_sem.at[slot],
                device_id=partners[dim],
                device_id_type=pl.DeviceIdType.MESH,
            )

        def load_left(index):
            return pltpu.make_async_copy(lefts[index], left_buf, load_sem.at[2])

        def load_right(index, chunk):
            slot = lax.rem(chunk, 2)
            columns = pl.ds(pl.multiple_of((chunk - firsts[index]) * width, width), width)
            return pltpu.make_async_copy(
                rights[index].at[:, columns], right_buf.at[slot], load_sem.at[slot]
            )

        def prefetch(chunk):
            for index in range(count_pairs):

                @pl.when((chunk >= firsts[index]) & (chunk < firsts[index + 1]))
                def _(index=index):
                    load_right(index, chunk).start()

                @pl.when(chunk == firsts[index])
                def _(index=index):
                    load_left(index).start()

        @pl.when(step == 0)
        def _():
            prefetch(step)
            barrier = pltpu.get_barrier_semaphore()
            for partner in partners:
                pl.semaphore_signal(
                    barrier, inc=1, device_id=partner, device_id_type=pl.DeviceIdType.MESH
                )
            pl.semaphore_wait(barrier, depth)

        @pl.when(step + 1 < chunks)
        def _():
            prefetch(step + 1)

        for stage in range(depth, -1, -1):
            chunk = step - starts[stage]

            @pl.when((chunk >= 0) & (chunk < chunks))
            def _(stage=stage, chunk=chunk):
                if stage == 0:
                    for first in firsts[:-1]:

                        @pl.when(chunk == first)
                        def _():
                            load_left(0).wait()
                            turned[...] = left_buf[...].T

                    load_right(0, lax.rem(chunk, 2)).wait()
                    product = jnp.dot(
                        turned[...],
                        right_buf[lax.rem(chunk, 2)],
                        preferred_element_type=jnp.float32,
                    )
                    slot = lax.rem(chunk, 2 * lags[0])
                    for part, (start, count, dim, left) in enumerate(stages[0]):
                        piece = product[:, start : start + count].astype(jnp.bfloat16)
                        buffers[0][part][0][slot] = piece.reshape((2,) * depth + (rows, count))
                    for index in range(count_extras):

                        @pl.when(chunk == spots[index][0])
                        def _(index=index):
                            at = (slot, Ellipsis, slice(spots[index][1], spots[index][1] + 128))
                            own = buffers[0][0][0]
                            total = own[at].astype(jnp.float32) + added[index][...].astype(
                                jnp.float32
                            )
                            own[at] = total.astype(jnp.bfloat16)

                else:
                    back = lax.rem(chunk, 2 * lags[stage - 1])
                    for part, (start, count, dim, left) in enumerate(stages[stage - 1]):
                        exchange(stage - 1, part, back).wait()
                        own, got = buffers[stage - 1][part][:2]
                        lead = (back,) + (slice(None),) * left.index(dim)
                        total = own[lead + (bits[dim],)].astype(jnp.float32) + got[back].astype(
                            jnp.float32
                        )
                        if stage == depth:
                            out_ref[:, start : start + count] = total
                            continue
                        slot = lax.rem(chunk, 2 * lags[stage])
                        low = total.astype(jnp.bfloat16)
                        for other, (begin, length, _, kept) in enumerate(stages[stage]):
                            lo, hi = max(start, begin), min(start + count, begin + length)
                            if lo < hi:
                                at = (slot,) + (slice(None),) * (len(kept) + 1)
                                buffers[stage][other][0][at + (slice(lo - begin, hi - begin),)] = (
                                    low[..., lo - start : hi - start]
                                )
                if stage < depth:
                    for part in range(len(stages[stage])):
                        exchange(stage, part, lax.rem(chunk, 2 * lags[stage])).start()

    scratch = [
        pltpu.VMEM((tokens, model), jnp.bfloat16),
        pltpu.VMEM((model, tokens), jnp.bfloat16),
        pltpu.VMEM((2, tokens, width), jnp.bfloat16),
        pltpu.SemaphoreType.DMA((3,)),
    ]
    for stage, parts in enumerate(stages):
        slots = 2 * lags[stage]
        for start, count, dim, left in parts:
            scratch += [
                pltpu.VMEM((slots,) + (2,) * len(left) + (rows, count), jnp.bfloat16),
                pltpu.VMEM((slots,) + (2,) * (len(left) - 1) + (rows, count), jnp.bfloat16),
                pltpu.SemaphoreType.DMA((slots,)),
                pltpu.SemaphoreType.DMA((slots,)),
            ]
    in_place = pl.BlockSpec(memory_space=pl.ANY)
    whole = [value.reshape((2,) * depth + (rows, 128)) for value, _ in extras]
    return pl.pallas_call(
        kernel,
        grid=(chunks + starts[depth],),
        in_specs=[in_place] * (2 * count_pairs)
        + [pl.BlockSpec(value.shape, lambda step: (0,) * (depth + 2)) for value in whole],
        out_specs=pl.BlockSpec(
            (rows, width), lambda step: (0, jnp.clip(step - starts[depth], 0, chunks - 1))
        ),
        out_shape=jax.ShapeDtypeStruct((rows, chunks * width), jnp.float32),
        scratch_shapes=scratch,
        compiler_params=pltpu.CompilerParams(
            collective_id=1,
            has_side_effects=True,
            vmem_limit_bytes=48 << 20,
            dimension_semantics=("arbitrary",),
        ),
    )(*[left for left, _ in pairs], *[right for _, right in pairs], *whole)


def padded(pieces):
    have = sum(piece.shape[1] for piece in pieces)
    fill = jnp.zeros((pieces[0].shape[0], (-have) % CHUNK), pieces[0].dtype)
    return jnp.concatenate(list(pieces) + [fill], axis=1)


def to_heads(tensor, pieces):
    seq_count, sub_rows = tensor.shape[:2]
    heads = HEADS
    sent = tensor.transpose(3, 2, 0, 1, 4)
    got = lax.all_to_all(sent, "head", split_axis=0, concat_axis=0, tiled=True)
    return got.transpose(1, 2, 0, 3, 4).reshape(pieces, seq_count, heads * sub_rows, HEAD_DIM)


def to_tokens(tensor, sub_rows):
    pieces, seq_count, segment, head_dim = tensor.shape
    sent = tensor.reshape(pieces, seq_count, segment // sub_rows, sub_rows, head_dim)
    sent = sent.transpose(2, 0, 1, 3, 4)
    got = lax.all_to_all(sent, "head", split_axis=0, concat_axis=0, tiled=True)
    return got.transpose(2, 3, 1, 0, 4)


def block_scores(query_block, keys, query_pos, key_pos, lengths):
    raw = jnp.einsum("sqc,skc->sqk", query_block, keys, preferred_element_type=jnp.float32)
    later = key_pos[None, None, :] <= query_pos[None, :, None]
    inside = key_pos[None, None, :] >= 0
    used = (key_pos[None, None, :] < lengths[:, None, None]) | (
        key_pos[None, None, :] == query_pos[None, :, None]
    )
    allowed = later & inside & used
    return jnp.where(allowed, raw * HEAD_DIM ** (-0.5), MASKED)


def attend_forward(query_heads, keys, values, seq_start, lengths, segment):
    rows = min(512, segment)
    key_pos = seq_start - segment + jnp.arange(2 * segment, dtype=jnp.int32)
    outputs, tops, totals = ([], [], [])
    query_pos = seq_start + 0 + jnp.arange(rows, dtype=jnp.int32)
    scores = block_scores(query_heads, keys, query_pos, key_pos, lengths)
    top = jnp.max(scores, axis=-1, keepdims=True)
    weights = jnp.exp(scores - top)
    total = jnp.sum(weights, axis=-1, keepdims=True)
    probs = (weights / total).astype(jnp.bfloat16)
    outputs.append(jnp.einsum("sqk,skc->sqc", probs, values, preferred_element_type=jnp.float32))
    tops.append(top)
    totals.append(total)
    return (outputs[0], tops, totals)


def attend_backward(
    query_heads, keys, values, grad_heads, tops, totals, seq_start, lengths, segment
):
    rows = min(512, segment)
    key_pos = seq_start - segment + jnp.arange(2 * segment, dtype=jnp.int32)
    grad_keys = jnp.zeros(keys.shape, jnp.float32)
    grad_values = jnp.zeros(values.shape, jnp.float32)
    grad_queries = []
    for index, start in enumerate(range(0, segment, rows)):
        query_pos = seq_start + start + jnp.arange(rows, dtype=jnp.int32)
        scores = block_scores(query_heads, keys, query_pos, key_pos, lengths)
        probs = jnp.exp(scores - tops[index]) / totals[index]
        grad_probs = jnp.einsum(
            "sqc,skc->sqk", grad_heads, values, preferred_element_type=jnp.float32
        )
        delta = jnp.sum(probs * grad_probs, axis=-1, keepdims=True)
        grad_raw = (probs * (grad_probs - delta) * HEAD_DIM ** (-0.5)).astype(jnp.bfloat16)
        grad_queries.append(
            jnp.einsum("sqk,skc->sqc", grad_raw, keys, preferred_element_type=jnp.float32)
        )
        grad_keys = jnp.einsum(
            "sqk,sqc->skc", grad_raw, query_heads, preferred_element_type=jnp.float32
        )
        grad_values = jnp.einsum(
            "sqk,sqc->skc",
            probs.astype(jnp.bfloat16),
            grad_heads,
            preferred_element_type=jnp.float32,
        )
    return (grad_queries[0], grad_keys, grad_values)


def gelu_tanh(values):
    return jax.nn.gelu(values, approximate=True)


def local(
    inputs,
    cotangent,
    routes,
    lengths,
    matrix,
    matrix_first,
    matrix_second,
    small,
    small_first,
    small_second,
):
    head_count = lax.axis_size("head")
    seq_count, sub_rows, width = inputs.shape
    segment = sub_rows * head_count
    tokens = seq_count * sub_rows
    router_cols = 2 * HEADS * EXPERTS
    group = HEADS * EXPERTS
    query_end, value_end, output_end, up_end = column_bounds()
    seq_start = lax.axis_index("seq") * segment
    positions = (
        seq_start + lax.axis_index("head") * sub_rows + jnp.arange(sub_rows, dtype=jnp.int32)
    )
    valid = (positions[None, :] < lengths[:, None]).astype(jnp.float32)
    cosines, sines = rotary_tables(positions)
    cosines = cosines[:, None, None, :]
    sines = sines[:, None, None, :]
    chosen = jnp.sum(
        (routes[..., None] == jnp.arange(EXPERTS, dtype=jnp.int32)).astype(jnp.float32), axis=-2
    )
    load_part = jnp.sum(chosen * valid[None, :, :, None, None, None], axis=(1, 2))
    matrix_low = matrix.astype(jnp.bfloat16)
    small_size = small.size
    carried = jnp.concatenate([small.reshape(-1), load_part.reshape(-1)])
    carried = jnp.pad(carried, (0, (-carried.size) % 1024))[None]
    carried = lax.all_gather(carried, ("dp", "seq", "head"), axis=0, tiled=True)
    loads = jnp.sum(carried[:, small_size : small_size + load_part.size], axis=0).reshape(load_part.shape)
    small_all = (
        carried[:, :small_size]
        .reshape(carried.shape[0], LAYERS, small.shape[1], small.shape[2])
        .transpose(1, 0, 2, 3)
        .reshape(LAYERS, width, small.shape[2])
        .astype(jnp.bfloat16)
    )
    hidden = inputs.astype(jnp.float32).reshape(tokens, width)
    kept = []
    gathered = [
        lax.all_gather(part, ("dp", "seq", "head"), axis=0, tiled=True)
        for layer in range(LAYERS)
        for part in (matrix_low[layer, :, :output_end], matrix_low[layer, :, output_end:])
    ]
    for layer in range(LAYERS):
        attn_w, ffn_w = (gathered[2 * layer], gathered[2 * layer + 1])
        small_w = small_all[layer]
        gains = small_w[:, router_cols:].astype(jnp.float32)
        normed_one, inverse_one = layer_stats(hidden)
        first_in = (normed_one * gains[:, 0] + gains[:, 1]).astype(jnp.bfloat16)
        gate_prob = jax.nn.sigmoid(
            jnp.dot(first_in, small_w[:, :router_cols], preferred_element_type=jnp.float32)
        ).reshape(tokens, 2, HEADS, EXPERTS)
        chosen_here = chosen[layer].reshape(tokens, 2, HEADS, EXPERTS)
        gates = gate_prob * chosen_here
        query_key = jnp.dot(
            first_in, attn_w[:, :query_end], preferred_element_type=jnp.float32
        ).reshape(seq_count, sub_rows, 2, HEADS, HEAD_DIM)
        rotated = rotate_pairs(query_key, cosines, sines).astype(jnp.bfloat16)
        projected = jnp.dot(
            first_in, attn_w[:, query_end:value_end], preferred_element_type=jnp.float32
        ).reshape(tokens, HEADS, EXPERTS, HEAD_DIM)
        value_rows = jnp.sum(gates[:, 0, :, :, None] * projected, axis=2).astype(jnp.bfloat16)
        heads_in = to_heads(
            jnp.concatenate(
                [rotated, value_rows.reshape(seq_count, sub_rows, 1, HEADS, HEAD_DIM)], axis=2
            ),
            3,
        )
        memory = passed_along(heads_in[1:], "seq", 1)
        query_heads = heads_in[0]
        keys = jnp.concatenate([memory[0], heads_in[1]], axis=1)
        values = jnp.concatenate([memory[1], heads_in[2]], axis=1)
        attended, tops, totals = attend_forward(
            query_heads, keys, values, seq_start, lengths, segment
        )
        attended_rows = to_tokens(attended.astype(jnp.bfloat16)[None], sub_rows).reshape(
            tokens, HEADS, HEAD_DIM
        )
        mixed = (
            (gates[:, 1, :, :, None] * attended_rows[:, :, None, :].astype(jnp.float32))
            .astype(jnp.bfloat16)
            .reshape(tokens, group * HEAD_DIM)
        )
        residual = hidden + contract_last(mixed, attn_w[:, value_end:])
        normed_two, inverse_two = layer_stats(residual)
        second_in = (normed_two * gains[:, 2] + gains[:, 3]).astype(jnp.bfloat16)
        up = jnp.dot(second_in, ffn_w[:, :FF], preferred_element_type=jnp.float32)
        act = gelu_tanh(up).astype(jnp.bfloat16)
        hidden = residual + contract_last(act, ffn_w[:, FF:])
        kept.append(
            (
                normed_one,
                inverse_one,
                first_in,
                gate_prob,
                chosen_here,
                gates,
                projected,
                query_heads,
                keys,
                values,
                tops,
                totals,
                attended_rows,
                mixed,
                normed_two,
                inverse_two,
                second_in,
                up,
                act,
            )
        )
    output = hidden.reshape(seq_count, sub_rows, width).astype(jnp.bfloat16)
    grad_hidden = (cotangent.astype(jnp.float32) * valid[:, :, None]).reshape(tokens, width)
    pairs, extras = ([], [])
    for layer in reversed(range(LAYERS)):
        (
            normed_one,
            inverse_one,
            first_in,
            gate_prob,
            chosen_here,
            gates,
            projected,
            query_heads,
            keys,
            values,
            tops,
            totals,
            attended_rows,
            mixed,
            normed_two,
            inverse_two,
            second_in,
            up,
            act,
        ) = kept[layer]
        attn_w, ffn_w = (gathered[2 * layer], gathered[2 * layer + 1])
        small_w = small_all[layer]
        gains = small_w[:, router_cols:].astype(jnp.float32)
        grad_low = grad_hidden.astype(jnp.bfloat16)
        grad_act = jnp.dot(grad_low, ffn_w[:, FF:], preferred_element_type=jnp.float32)
        gelu_value, gelu_pull = jax.vjp(gelu_tanh, up)
        grad_up = gelu_pull(grad_act)[0].astype(jnp.bfloat16)
        grad_second = contract_last(grad_up, ffn_w[:, :FF])
        gain_two_grad = jnp.sum(grad_second * normed_two, axis=0)
        bias_two_grad = jnp.sum(grad_second, axis=0)
        grad_residual = grad_hidden + norm_back(grad_second, normed_two, inverse_two, gains[:, 2])
        residual_low = grad_residual.astype(jnp.bfloat16)
        grad_mixed = jnp.dot(
            residual_low, attn_w[:, value_end:], preferred_element_type=jnp.float32
        ).reshape(tokens, HEADS, EXPERTS, HEAD_DIM)
        grad_gate_out = jnp.sum(
            grad_mixed * attended_rows[:, :, None, :].astype(jnp.float32), axis=-1
        )
        grad_att_rows = jnp.sum(grad_mixed * gates[:, 1, :, :, None], axis=2).astype(jnp.bfloat16)
        grad_heads_in = to_heads(
            grad_att_rows.reshape(seq_count, sub_rows, 1, HEADS, HEAD_DIM), 1
        )[0]
        grad_query, grad_keys, grad_values = attend_backward(
            query_heads, keys, values, grad_heads_in, tops, totals, seq_start, lengths, segment
        )
        grad_kv = jnp.stack([grad_keys, grad_values], axis=0)
        kv_back = passed_along(grad_kv[:, :, :segment].astype(jnp.bfloat16), "seq", -1)
        grad_kv_own = (grad_kv[:, :, segment:] + kv_back.astype(jnp.float32)).astype(jnp.bfloat16)
        grads_tok = to_tokens(
            jnp.concatenate([grad_query.astype(jnp.bfloat16)[None], grad_kv_own], axis=0), sub_rows
        )
        grads_tok = grads_tok.astype(jnp.float32)
        grad_qk = (
            rotate_back(grads_tok[:, :, :2], cosines, sines)
            .astype(jnp.bfloat16)
            .reshape(tokens, query_end)
        )
        grad_value_rows = grads_tok[:, :, 2].reshape(tokens, HEADS, HEAD_DIM)
        grad_proj = (
            (gates[:, 0, :, :, None] * grad_value_rows[:, :, None, :])
            .astype(jnp.bfloat16)
            .reshape(tokens, group * HEAD_DIM)
        )
        grad_gate_value = jnp.sum(projected * grad_value_rows[:, :, None, :], axis=-1)
        grad_gates = jnp.stack([grad_gate_value, grad_gate_out], axis=1) * chosen_here
        grad_logit = (
            (grad_gates * gate_prob * (1.0 - gate_prob)).astype(jnp.bfloat16).reshape(tokens, -1)
        )
        grad_in = jnp.concatenate([grad_qk, grad_proj], axis=1)
        grad_first = contract_last(grad_in, attn_w[:, :value_end]) + contract_last(
            grad_logit, small_w[:, :router_cols]
        )
        gain_one_grad = jnp.sum(grad_first * normed_one, axis=0)
        bias_one_grad = jnp.sum(grad_first, axis=0)
        grad_hidden = grad_residual + norm_back(grad_first, normed_one, inverse_one, gains[:, 0])
        norm_grads = jnp.stack(
            [gain_one_grad, bias_one_grad, gain_two_grad, bias_two_grad], axis=1
        ).astype(jnp.bfloat16)
        at = value_end + router_cols
        near = at // 128 * 128
        norm_grads = jnp.pad(norm_grads, ((0, 0), (at - near, 128 - 4 - (at - near))))
        pairs += [
            (first_in, padded([grad_in, grad_logit, jnp.zeros((tokens, 4), jnp.bfloat16)])),
            (residual_low, padded([mixed])),
            (second_in, grad_up),
            (grad_low, act),
        ]
        extras.append((norm_grads, near))
    reduced = reduce_weight_grads(pairs, extras, CHUNK)
    matrix_rows = [None] * LAYERS
    small_rows = [None] * LAYERS
    start = 0
    for slot, layer in enumerate(reversed(range(LAYERS))):
        widths = [right.shape[1] for _, right in pairs[4 * slot : 4 * slot + 4]]
        begins = [start + sum(widths[:group_index]) for group_index in range(4)]
        start += sum(widths)
        shares = [
            reduced[:, begin : begin + used]
            for begin, used in zip(
                begins, (value_end, output_end - value_end, FF, FF)
            )
        ]
        matrix_rows[layer] = jnp.concatenate(shares, axis=1)
        small_rows[layer] = reduced[
            :, begins[0] + value_end : begins[0] + value_end + router_cols + 4
        ]
    input_grad = grad_hidden.reshape(seq_count, sub_rows, width).astype(jnp.bfloat16)
    matrix_grad = jnp.stack(matrix_rows, axis=0)
    small_grad = jnp.stack(small_rows, axis=0)
    matrix_new, matrix_first_new, matrix_second_new = adam_update(
        matrix, matrix_grad, matrix_first, matrix_second, column_rates(segment), WEIGHT_DECAY
    )
    small_new, small_first_new, small_second_new = adam_update(
        small, small_grad, small_first, small_second, small_rates(), 0.0
    )
    return (
        output,
        input_grad,
        matrix_grad,
        matrix_new,
        matrix_new.astype(jnp.bfloat16),
        matrix_first_new,
        matrix_second_new,
        small_grad,
        small_new,
        small_new.astype(jnp.bfloat16),
        small_first_new,
        small_second_new,
        loads,
    )


def solution(mesh):
    in_specs = (
        P("dp", ("seq", "head"), None),
        P("dp", ("seq", "head"), None),
        P(None, "dp", ("seq", "head"), None, None, None),
        P("dp"),
        P(None, ("dp", "seq", "head"), None),
        P(None, ("dp", "seq", "head"), None),
        P(None, ("dp", "seq", "head"), None),
        P(None, ("dp", "seq", "head"), None),
        P(None, ("dp", "seq", "head"), None),
        P(None, ("dp", "seq", "head"), None),
    )
    out_specs = (
        P("dp", ("seq", "head"), None),
        P("dp", ("seq", "head"), None),
        P(None, ("dp", "seq", "head"), None),
        P(None, ("dp", "seq", "head"), None),
        P(None, ("dp", "seq", "head"), None),
        P(None, ("dp", "seq", "head"), None),
        P(None, ("dp", "seq", "head"), None),
        P(None, ("dp", "seq", "head"), None),
        P(None, ("dp", "seq", "head"), None),
        P(None, ("dp", "seq", "head"), None),
        P(None, ("dp", "seq", "head"), None),
        P(None, ("dp", "seq", "head"), None),
        P(),
    )
    return jax.shard_map(local, mesh=mesh, in_specs=in_specs, out_specs=out_specs, check_vma=False)
```

```python
import math

import jax
import jax.numpy as jnp
from jax import lax
from jax.experimental import pallas as pl
from jax.experimental.pallas import tpu as pltpu
from jax.sharding import PartitionSpec as P

D = 1024
HEADS = 4
HEAD_DIM = 112
EXPERTS = 5
FF = 4096
LAYERS = 2
STEP = 10


NORM_EPS = 1e-05
BETA_ONE = 0.9
BETA_TWO = 0.95
ADAM_EPS = 1e-08
WEIGHT_DECAY = 0.1
NORM_RATE = 0.5
MASKED = -1e30
CHUNK = 512


def passed_along(value, axis, by):
    devices = lax.axis_size(axis)
    pairs = [(i, i + by) for i in range(devices) if 0 <= i + by < devices]
    return lax.ppermute(value, axis, pairs)


def column_bounds():
    query_end = 2 * HEADS * HEAD_DIM
    value_end = query_end + HEADS * EXPERTS * HEAD_DIM
    output_end = value_end + HEADS * EXPERTS * HEAD_DIM
    return (query_end, value_end, output_end, output_end + FF)


def column_rates(segment):
    query_end, value_end, output_end, up_end = column_bounds()
    column = jnp.arange(up_end + FF)
    inner = D ** (-0.5)
    outer = 0.7 * math.sqrt(segment) / HEAD_DIM
    rates = jnp.where(
        column < value_end,
        inner,
        jnp.where(column < output_end, outer, jnp.where(column < up_end, inner, FF ** (-0.5))),
    )
    return rates.astype(jnp.float32)


def small_rates():
    column = jnp.arange(2 * HEADS * EXPERTS + 4)
    return jnp.where(column < 2 * HEADS * EXPERTS, 0.7 * D ** (-0.5), NORM_RATE).astype(jnp.float32)


def adam_update(weight, grad, first, second, rates, decay):
    first_new = BETA_ONE * first + (1.0 - BETA_ONE) * grad
    second_new = BETA_TWO * second + (1.0 - BETA_TWO) * grad * grad
    first_hat = first_new / (1.0 - BETA_ONE**STEP)
    second_hat = second_new / (1.0 - BETA_TWO**STEP)
    new = weight - rates * (first_hat / (jnp.sqrt(second_hat) + ADAM_EPS) + decay * weight)
    return (new, first_new, second_new)


def rotary_tables(positions):
    half = HEAD_DIM // 2
    inverse = jnp.exp(-math.log(10000.0) * jnp.arange(half, dtype=jnp.float32) / half)
    angle = positions.astype(jnp.float32)[:, None] * inverse[None, :]
    return (jnp.cos(angle), jnp.sin(angle))


def rotate_pairs(tensor, cosines, sines):
    half = tensor.shape[-1] // 2
    first, second = (tensor[..., :half], tensor[..., half:])
    return jnp.concatenate(
        [first * cosines - second * sines, second * cosines + first * sines], axis=-1
    )


def rotate_back(tensor, cosines, sines):
    half = tensor.shape[-1] // 2
    first, second = (tensor[..., :half], tensor[..., half:])
    return jnp.concatenate(
        [first * cosines + second * sines, second * cosines - first * sines], axis=-1
    )


def layer_stats(values):
    mean = jnp.mean(values, axis=-1, keepdims=True)
    centered = values - mean
    variance = jnp.mean(centered * centered, axis=-1, keepdims=True)
    inverse = lax.rsqrt(variance + NORM_EPS)
    return (centered * inverse, inverse)


def norm_back(grad_normed, normed, inverse, gain):
    scaled = grad_normed * gain
    return inverse * (
        scaled
        - jnp.mean(scaled, axis=-1, keepdims=True)
        - normed * jnp.mean(scaled * normed, axis=-1, keepdims=True)
    )


def contract_last(left, right):
    return lax.dot_general(
        left, right, (((1,), (1,)), ((), ())), preferred_element_type=jnp.float32
    )


def contract_first(left, right):
    return lax.dot_general(
        left, right, (((0,), (0,)), ((), ())), preferred_element_type=jnp.float32
    )


AXES = ("dp", "seq", "head")


def mesh_bits():
    dims = [
        (axis, bit)
        for axis in AXES
        for bit in reversed(range(lax.axis_size(axis).bit_length() - 1))
    ]
    groups = [[index for index, (axis, _) in enumerate(dims) if axis == name] for name in AXES]
    return (dims, *groups)


def my_bits(dims):
    place = {axis: lax.axis_index(axis) for axis in AXES}
    bits = [lax.rem(place[axis] // (1 << bit), 2) for axis, bit in dims]
    partners = [
        {axis: place[axis] + (1 << bit) * (1 - 2 * bits[index])}
        for index, (axis, bit) in enumerate(dims)
    ]
    return (bits, partners)


def greet(partners):
    barrier = pltpu.get_barrier_semaphore()
    for partner in partners:
        pl.semaphore_signal(
            barrier, inc=1, device_id=partner, device_id_type=pl.DeviceIdType.MESH
        )
    pl.semaphore_wait(barrier, len(partners))


def gather_rows(shares, pieces, name):
    dims, dp_dims, seq_dims, head_dims = mesh_bits()
    orders = (
        head_dims + dp_dims[::-1] + seq_dims,
        head_dims + dp_dims + seq_dims,
        dp_dims + head_dims + seq_dims,
    )
    depth = len(dims)
    total = len(shares)
    lag, slots = (2, 4)
    steps = max(piece[3] for piece in pieces) + lag * depth

    def kernel(*refs):
        ins, outs = (refs[:total], refs[total : 2 * total])
        send_sem, recv_sem, local_sem = refs[2 * total :]
        bits, partners = my_bits(dims)
        own = [
            pltpu.make_async_copy(ins[index], outs[index].at[tuple(bits)], local_sem.at[index])
            for index in range(total)
        ]
        for copy in own:
            copy.start()
        greet(partners)
        for copy in own:
            copy.wait()

        def exchange(number, stage, chunk):
            array, start, width, _, which = pieces[number]
            done = orders[which][:stage]
            at = tuple(slice(None) if dim in done else bits[dim] for dim in range(depth))
            columns = pl.ds(pl.multiple_of(start + chunk * width, 128), width)
            view = outs[array].at[at + (slice(None), columns)]
            slot = lax.rem(chunk, slots)
            return pltpu.make_async_remote_copy(
                src_ref=view,
                dst_ref=view,
                send_sem=send_sem.at[number, stage, slot],
                recv_sem=recv_sem.at[number, stage, slot],
                device_id=partners[orders[which][stage]],
                device_id_type=pl.DeviceIdType.MESH,
            )

        def body(step, carry):
            for stage in range(depth, -1, -1):
                chunk = step - lag * stage
                for number, piece in enumerate(pieces):

                    @pl.when((chunk >= 0) & (chunk < piece[3]))
                    def _(stage=stage, chunk=chunk, number=number):
                        if stage > 0:
                            exchange(number, stage - 1, chunk).wait()
                        if stage < depth:
                            exchange(number, stage, chunk).start()

            return carry

        lax.fori_loop(0, steps, body, 0)

    in_place = pl.BlockSpec(memory_space=pl.ANY)
    semaphores = pltpu.SemaphoreType.DMA((len(pieces), depth, slots))
    gathered = pl.pallas_call(
        kernel,
        in_specs=[in_place] * total,
        out_specs=[in_place] * total,
        out_shape=[
            jax.ShapeDtypeStruct((2,) * depth + share.shape, share.dtype) for share in shares
        ],
        scratch_shapes=[semaphores, semaphores, pltpu.SemaphoreType.DMA((total,))],
        compiler_params=pltpu.CompilerParams(collective_id=name, has_side_effects=True),
    )(*shares)
    return [value.reshape(-1, value.shape[-1]) for value in gathered]


def halving_plan(width):
    dims, dp_dims, seq_dims, head_dims = mesh_bits()
    first = seq_dims[::-1]
    orders = (
        (0, width // 2, first + dp_dims[::-1] + head_dims[::-1]),
        (width // 2, width // 4, first + dp_dims + head_dims[::-1]),
        (3 * width // 4, width // 4, first + head_dims[::-1] + dp_dims[::-1]),
    )
    stages = []
    for stage in range(len(dims)):
        parts = []
        for start, count, order in orders:
            left = [dim for dim in range(len(dims)) if dim not in order[:stage]]
            if parts and parts[-1][2:] == (order[stage], left):
                parts[-1] = (parts[-1][0], parts[-1][1] + count, order[stage], left)
            else:
                parts.append((start, count, order[stage], left))
        stages.append(parts)
    lags = [1 if stage < len(seq_dims) else 2 for stage in range(len(dims))]
    return dims, stages, lags


def reduce_weight_grads(pairs, extras, width):
    dims, stages, lags = halving_plan(width)
    depth = len(dims)
    tokens, model = pairs[0][0].shape
    rows = model >> depth
    firsts = [0]
    for left, right in pairs:
        firsts.append(firsts[-1] + right.shape[1] // width)
    chunks = firsts[-1]
    per_layer = len(pairs) // len(extras)
    spots = [
        (firsts[per_layer * index] + near // width, near % width)
        for index, (_, near) in enumerate(extras)
    ]
    starts = [sum(lags[:stage]) for stage in range(depth + 1)]
    count_pairs, count_extras = (len(pairs), len(extras))

    def kernel(*refs):
        lefts = refs[:count_pairs]
        rights = refs[count_pairs : 2 * count_pairs]
        added = refs[2 * count_pairs : 2 * count_pairs + count_extras]
        rest = refs[2 * count_pairs + count_extras :]
        out_ref, left_buf, turned, right_buf, load_sem = rest[:5]
        pool = iter(rest[5:])
        buffers = [[tuple(next(pool) for _ in range(4)) for _ in parts] for parts in stages]
        step = pl.program_id(0)
        bits, partners = my_bits(dims)

        def exchange(stage, part, slot):
            start, count, dim, left = stages[stage][part]
            own, got, send_sem, recv_sem = buffers[stage][part]
            lead = (slot,) + (slice(None),) * left.index(dim)
            return pltpu.make_async_remote_copy(
                src_ref=own.at[lead + (1 - bits[dim],)],
                dst_ref=got.at[slot],
                send_sem=send_sem.at[slot],
                recv_sem=recv_sem.at[slot],
                device_id=partners[dim],
                device_id_type=pl.DeviceIdType.MESH,
            )

        def load_left(index):
            return pltpu.make_async_copy(lefts[index], left_buf, load_sem.at[2])

        def load_right(index, chunk):
            slot = lax.rem(chunk, 2)
            columns = pl.ds(pl.multiple_of((chunk - firsts[index]) * width, width), width)
            return pltpu.make_async_copy(
                rights[index].at[:, columns], right_buf.at[slot], load_sem.at[slot]
            )

        def prefetch(chunk):
            for index in range(count_pairs):

                @pl.when((chunk >= firsts[index]) & (chunk < firsts[index + 1]))
                def _(index=index):
                    load_right(index, chunk).start()

                @pl.when(chunk == firsts[index])
                def _(index=index):
                    load_left(index).start()

        @pl.when(step == 0)
        def _():
            prefetch(step)
            greet(partners)

        @pl.when(step + 1 < chunks)
        def _():
            prefetch(step + 1)

        for stage in range(depth, -1, -1):
            chunk = step - starts[stage]

            @pl.when((chunk >= 0) & (chunk < chunks))
            def _(stage=stage, chunk=chunk):
                if stage == 0:
                    for first in firsts[:-1]:

                        @pl.when(chunk == first)
                        def _():
                            load_left(0).wait()
                            turned[...] = left_buf[...].T

                    load_right(0, lax.rem(chunk, 2)).wait()
                    product = jnp.dot(
                        turned[...],
                        right_buf[lax.rem(chunk, 2)],
                        preferred_element_type=jnp.float32,
                    )
                    slot = lax.rem(chunk, 2 * lags[0])
                    for part, (start, count, dim, left) in enumerate(stages[0]):
                        piece = product[:, start : start + count].astype(jnp.bfloat16)
                        buffers[0][part][0][slot] = piece.reshape((2,) * depth + (rows, count))
                    for index in range(count_extras):

                        @pl.when(chunk == spots[index][0])
                        def _(index=index):
                            at = (slot, Ellipsis, slice(spots[index][1], spots[index][1] + 128))
                            own = buffers[0][0][0]
                            total = own[at].astype(jnp.float32) + added[index][...].astype(
                                jnp.float32
                            )
                            own[at] = total.astype(jnp.bfloat16)

                else:
                    back = lax.rem(chunk, 2 * lags[stage - 1])
                    for part, (start, count, dim, left) in enumerate(stages[stage - 1]):
                        exchange(stage - 1, part, back).wait()
                        own, got = buffers[stage - 1][part][:2]
                        lead = (back,) + (slice(None),) * left.index(dim)
                        total = own[lead + (bits[dim],)].astype(jnp.float32) + got[back].astype(
                            jnp.float32
                        )
                        if stage == depth:
                            out_ref[:, start : start + count] = total
                            continue
                        slot = lax.rem(chunk, 2 * lags[stage])
                        low = total.astype(jnp.bfloat16)
                        for other, (begin, length, _, kept) in enumerate(stages[stage]):
                            lo, hi = max(start, begin), min(start + count, begin + length)
                            if lo < hi:
                                at = (slot,) + (slice(None),) * (len(kept) + 1)
                                buffers[stage][other][0][at + (slice(lo - begin, hi - begin),)] = (
                                    low[..., lo - start : hi - start]
                                )
                if stage < depth:
                    for part in range(len(stages[stage])):
                        exchange(stage, part, lax.rem(chunk, 2 * lags[stage])).start()

    scratch = [
        pltpu.VMEM((tokens, model), jnp.bfloat16),
        pltpu.VMEM((model, tokens), jnp.bfloat16),
        pltpu.VMEM((2, tokens, width), jnp.bfloat16),
        pltpu.SemaphoreType.DMA((3,)),
    ]
    for stage, parts in enumerate(stages):
        slots = 2 * lags[stage]
        for start, count, dim, left in parts:
            scratch += [
                pltpu.VMEM((slots,) + (2,) * len(left) + (rows, count), jnp.bfloat16),
                pltpu.VMEM((slots,) + (2,) * (len(left) - 1) + (rows, count), jnp.bfloat16),
                pltpu.SemaphoreType.DMA((slots,)),
                pltpu.SemaphoreType.DMA((slots,)),
            ]
    in_place = pl.BlockSpec(memory_space=pl.ANY)
    whole = [value.reshape((2,) * depth + (rows, 128)) for value, _ in extras]
    return pl.pallas_call(
        kernel,
        grid=(chunks + starts[depth],),
        in_specs=[in_place] * (2 * count_pairs)
        + [pl.BlockSpec(value.shape, lambda step: (0,) * (depth + 2)) for value in whole],
        out_specs=pl.BlockSpec(
            (rows, width), lambda step: (0, jnp.clip(step - starts[depth], 0, chunks - 1))
        ),
        out_shape=jax.ShapeDtypeStruct((rows, chunks * width), jnp.float32),
        scratch_shapes=scratch,
        compiler_params=pltpu.CompilerParams(
            collective_id=1,
            has_side_effects=True,
            vmem_limit_bytes=48 << 20,
            dimension_semantics=("arbitrary",),
        ),
    )(*[left for left, _ in pairs], *[right for _, right in pairs], *whole)


def lane_whole(count):
    return count + (-count) % 128


def chunk_whole(count):
    return count + (-count) % CHUNK


def padded(pieces, width):
    have = sum(piece.shape[1] for piece in pieces)
    fill = jnp.zeros((pieces[0].shape[0], width - have), pieces[0].dtype)
    return jnp.concatenate(list(pieces) + [fill], axis=1)


def columns_plan(array, width):
    unit = 256 if width % 256 == 0 else 128
    units = width // unit
    near = (3 * units + 4) // 8
    plan, start = ([], 0)
    for which, count in ((0, near), (1, near), (2, units - 2 * near)):
        plan.append((array, start, unit, count, which))
        start += count * unit
    return plan


def to_heads(tensor, pieces):
    seq_count, sub_rows = tensor.shape[:2]
    heads = HEADS
    sent = tensor.transpose(3, 2, 0, 1, 4)
    got = lax.all_to_all(sent, "head", split_axis=0, concat_axis=0, tiled=True)
    return got.transpose(1, 2, 0, 3, 4).reshape(pieces, seq_count, heads * sub_rows, HEAD_DIM)


def to_tokens(tensor, sub_rows):
    pieces, seq_count, segment, head_dim = tensor.shape
    sent = tensor.reshape(pieces, seq_count, segment // sub_rows, sub_rows, head_dim)
    sent = sent.transpose(2, 0, 1, 3, 4)
    got = lax.all_to_all(sent, "head", split_axis=0, concat_axis=0, tiled=True)
    return got.transpose(2, 3, 1, 0, 4)


def block_scores(query_block, keys, query_pos, key_pos, lengths):
    raw = jnp.einsum("sqc,skc->sqk", query_block, keys, preferred_element_type=jnp.float32)
    later = key_pos[None, None, :] <= query_pos[None, :, None]
    inside = key_pos[None, None, :] >= 0
    used = (key_pos[None, None, :] < lengths[:, None, None]) | (
        key_pos[None, None, :] == query_pos[None, :, None]
    )
    allowed = later & inside & used
    return jnp.where(allowed, raw * HEAD_DIM ** (-0.5), MASKED)


def attend_forward(query_heads, keys, values, seq_start, lengths, segment):
    rows = min(512, segment)
    key_pos = seq_start - segment + jnp.arange(2 * segment, dtype=jnp.int32)
    outputs, tops, totals = ([], [], [])
    query_pos = seq_start + 0 + jnp.arange(rows, dtype=jnp.int32)
    scores = block_scores(query_heads, keys, query_pos, key_pos, lengths)
    top = jnp.max(scores, axis=-1, keepdims=True)
    weights = jnp.exp(scores - top)
    total = jnp.sum(weights, axis=-1, keepdims=True)
    probs = (weights / total).astype(jnp.bfloat16)
    outputs.append(jnp.einsum("sqk,skc->sqc", probs, values, preferred_element_type=jnp.float32))
    tops.append(top)
    totals.append(total)
    return (outputs[0], tops, totals)


def attend_backward(
    query_heads, keys, values, grad_heads, tops, totals, seq_start, lengths, segment
):
    rows = min(512, segment)
    key_pos = seq_start - segment + jnp.arange(2 * segment, dtype=jnp.int32)
    grad_keys = jnp.zeros(keys.shape, jnp.float32)
    grad_values = jnp.zeros(values.shape, jnp.float32)
    grad_queries = []
    for index, start in enumerate(range(0, segment, rows)):
        query_pos = seq_start + start + jnp.arange(rows, dtype=jnp.int32)
        scores = block_scores(query_heads, keys, query_pos, key_pos, lengths)
        probs = jnp.exp(scores - tops[index]) / totals[index]
        grad_probs = jnp.einsum(
            "sqc,skc->sqk", grad_heads, values, preferred_element_type=jnp.float32
        )
        delta = jnp.sum(probs * grad_probs, axis=-1, keepdims=True)
        grad_raw = (probs * (grad_probs - delta) * HEAD_DIM ** (-0.5)).astype(jnp.bfloat16)
        grad_queries.append(
            jnp.einsum("sqk,skc->sqc", grad_raw, keys, preferred_element_type=jnp.float32)
        )
        grad_keys = jnp.einsum(
            "sqk,sqc->skc", grad_raw, query_heads, preferred_element_type=jnp.float32
        )
        grad_values = jnp.einsum(
            "sqk,sqc->skc",
            probs.astype(jnp.bfloat16),
            grad_heads,
            preferred_element_type=jnp.float32,
        )
    return (grad_queries[0], grad_keys, grad_values)


def gelu_tanh(values):
    return jax.nn.gelu(values, approximate=True)


def local(
    inputs,
    cotangent,
    routes,
    lengths,
    matrix,
    matrix_first,
    matrix_second,
    small,
    small_first,
    small_second,
):
    head_count = lax.axis_size("head")
    seq_count, sub_rows, width = inputs.shape
    segment = sub_rows * head_count
    tokens = seq_count * sub_rows
    router_cols = 2 * HEADS * EXPERTS
    group = HEADS * EXPERTS
    query_end, value_end, output_end, up_end = column_bounds()
    seq_start = lax.axis_index("seq") * segment
    positions = (
        seq_start + lax.axis_index("head") * sub_rows + jnp.arange(sub_rows, dtype=jnp.int32)
    )
    valid = (positions[None, :] < lengths[:, None]).astype(jnp.float32)
    cosines, sines = rotary_tables(positions)
    cosines = cosines[:, None, None, :]
    sines = sines[:, None, None, :]
    chosen = jnp.sum(
        (routes[..., None] == jnp.arange(EXPERTS, dtype=jnp.int32)).astype(jnp.float32), axis=-2
    )
    load_part = jnp.sum(chosen * valid[None, :, :, None, None, None], axis=(1, 2))
    in_width = lane_whole(value_end + router_cols + 4)
    out_width = lane_whole(output_end - value_end)
    matrix_low = matrix.astype(jnp.bfloat16)
    small_low = small.astype(jnp.bfloat16)
    in_low = [
        padded([matrix_low[layer, :, :value_end], small_low[layer]], in_width)
        for layer in range(LAYERS)
    ]
    out_low = [
        padded([matrix_low[layer, :, value_end:output_end]], out_width) for layer in range(LAYERS)
    ]
    counts = jnp.pad(load_part.reshape(-1), (0, (-load_part.size) % 1024)).reshape(8, -1)
    in_first, out_first, counts = gather_rows(
        [in_low[0], out_low[0], counts],
        columns_plan(0, in_width) + columns_plan(1, out_width) + [(2, 0, counts.shape[1], 1, 0)],
        2,
    )
    loads = (
        jnp.sum(counts.reshape(-1, load_part.size + (-load_part.size) % 1024), axis=0)[
            : load_part.size
        ]
        .reshape(load_part.shape)
    )
    everyone = ("dp", "seq", "head")
    in_ws, out_ws = ([in_first], [out_first])
    ffn_ws = [lax.all_gather(matrix_low[0, :, output_end:], everyone, axis=0, tiled=True)]
    for layer in range(1, LAYERS):
        both = lax.all_gather(
            jnp.concatenate([in_low[layer], out_low[layer]], axis=1), everyone, axis=0, tiled=True
        )
        in_ws.append(both[:, :in_width])
        out_ws.append(both[:, in_width:])
        ffn_ws.append(
            lax.all_gather(matrix_low[layer, :, output_end:], everyone, axis=0, tiled=True)
        )
    hidden = inputs.astype(jnp.float32).reshape(tokens, width)
    kept = []
    for layer in range(LAYERS):
        in_w, out_w, ffn_w = (in_ws[layer], out_ws[layer], ffn_ws[layer])
        gains = in_w[:, value_end + router_cols : value_end + router_cols + 4].astype(jnp.float32)
        normed_one, inverse_one = layer_stats(hidden)
        first_in = (normed_one * gains[:, 0] + gains[:, 1]).astype(jnp.bfloat16)
        entered = lax.optimization_barrier(
            jnp.dot(first_in, in_w, preferred_element_type=jnp.float32)
        )
        gate_prob = jax.nn.sigmoid(entered[:, value_end : value_end + router_cols]).reshape(
            tokens, 2, HEADS, EXPERTS
        )
        chosen_here = chosen[layer].reshape(tokens, 2, HEADS, EXPERTS)
        gates = gate_prob * chosen_here
        query_key = entered[:, :query_end].reshape(seq_count, sub_rows, 2, HEADS, HEAD_DIM)
        rotated = rotate_pairs(query_key, cosines, sines).astype(jnp.bfloat16)
        projected = entered[:, query_end:value_end].reshape(tokens, HEADS, EXPERTS, HEAD_DIM)
        value_rows = jnp.sum(gates[:, 0, :, :, None] * projected, axis=2).astype(jnp.bfloat16)
        heads_in = to_heads(
            jnp.concatenate(
                [rotated, value_rows.reshape(seq_count, sub_rows, 1, HEADS, HEAD_DIM)], axis=2
            ),
            3,
        )
        memory = passed_along(heads_in[1:], "seq", 1)
        query_heads = heads_in[0]
        keys = jnp.concatenate([memory[0], heads_in[1]], axis=1)
        values = jnp.concatenate([memory[1], heads_in[2]], axis=1)
        attended, tops, totals = attend_forward(
            query_heads, keys, values, seq_start, lengths, segment
        )
        attended_rows = to_tokens(attended.astype(jnp.bfloat16)[None], sub_rows).reshape(
            tokens, HEADS, HEAD_DIM
        )
        mixed = padded(
            [
                (gates[:, 1, :, :, None] * attended_rows[:, :, None, :].astype(jnp.float32))
                .astype(jnp.bfloat16)
                .reshape(tokens, group * HEAD_DIM)
            ],
            out_width,
        )
        residual = hidden + contract_last(mixed, out_w)
        normed_two, inverse_two = layer_stats(residual)
        second_in = (normed_two * gains[:, 2] + gains[:, 3]).astype(jnp.bfloat16)
        up = jnp.dot(second_in, ffn_w[:, :FF], preferred_element_type=jnp.float32)
        act = gelu_tanh(up).astype(jnp.bfloat16)
        hidden = residual + contract_last(act, ffn_w[:, FF:])
        kept.append(
            (
                normed_one,
                inverse_one,
                first_in,
                gate_prob,
                chosen_here,
                gates,
                projected,
                query_heads,
                keys,
                values,
                tops,
                totals,
                attended_rows,
                mixed,
                normed_two,
                inverse_two,
                second_in,
                up,
                act,
            )
        )
    output = hidden.reshape(seq_count, sub_rows, width).astype(jnp.bfloat16)
    grad_hidden = (cotangent.astype(jnp.float32) * valid[:, :, None]).reshape(tokens, width)
    pairs, extras = ([], [])
    for layer in reversed(range(LAYERS)):
        (
            normed_one,
            inverse_one,
            first_in,
            gate_prob,
            chosen_here,
            gates,
            projected,
            query_heads,
            keys,
            values,
            tops,
            totals,
            attended_rows,
            mixed,
            normed_two,
            inverse_two,
            second_in,
            up,
            act,
        ) = kept[layer]
        in_w, out_w, ffn_w = (in_ws[layer], out_ws[layer], ffn_ws[layer])
        gains = in_w[:, value_end + router_cols : value_end + router_cols + 4].astype(jnp.float32)
        grad_low = grad_hidden.astype(jnp.bfloat16)
        grad_act = jnp.dot(grad_low, ffn_w[:, FF:], preferred_element_type=jnp.float32)
        gelu_value, gelu_pull = jax.vjp(gelu_tanh, up)
        grad_up = gelu_pull(grad_act)[0].astype(jnp.bfloat16)
        grad_second = contract_last(grad_up, ffn_w[:, :FF])
        gain_two_grad = jnp.sum(grad_second * normed_two, axis=0)
        bias_two_grad = jnp.sum(grad_second, axis=0)
        grad_residual = grad_hidden + norm_back(grad_second, normed_two, inverse_two, gains[:, 2])
        residual_low = grad_residual.astype(jnp.bfloat16)
        grad_mixed = lax.optimization_barrier(
            jnp.dot(residual_low, out_w, preferred_element_type=jnp.float32)
        )[:, : group * HEAD_DIM].reshape(tokens, HEADS, EXPERTS, HEAD_DIM)
        grad_gate_out = jnp.sum(
            grad_mixed * attended_rows[:, :, None, :].astype(jnp.float32), axis=-1
        )
        grad_att_rows = jnp.sum(grad_mixed * gates[:, 1, :, :, None], axis=2).astype(jnp.bfloat16)
        grad_heads_in = to_heads(
            grad_att_rows.reshape(seq_count, sub_rows, 1, HEADS, HEAD_DIM), 1
        )[0]
        grad_query, grad_keys, grad_values = attend_backward(
            query_heads, keys, values, grad_heads_in, tops, totals, seq_start, lengths, segment
        )
        grad_kv = jnp.stack([grad_keys, grad_values], axis=0)
        kv_back = passed_along(grad_kv[:, :, :segment].astype(jnp.bfloat16), "seq", -1)
        grad_kv_own = (grad_kv[:, :, segment:] + kv_back.astype(jnp.float32)).astype(jnp.bfloat16)
        grads_tok = to_tokens(
            jnp.concatenate([grad_query.astype(jnp.bfloat16)[None], grad_kv_own], axis=0), sub_rows
        )
        grads_tok = grads_tok.astype(jnp.float32)
        grad_qk = (
            rotate_back(grads_tok[:, :, :2], cosines, sines)
            .astype(jnp.bfloat16)
            .reshape(tokens, query_end)
        )
        grad_value_rows = grads_tok[:, :, 2].reshape(tokens, HEADS, HEAD_DIM)
        grad_proj = (
            (gates[:, 0, :, :, None] * grad_value_rows[:, :, None, :])
            .astype(jnp.bfloat16)
            .reshape(tokens, group * HEAD_DIM)
        )
        grad_gate_value = jnp.sum(projected * grad_value_rows[:, :, None, :], axis=-1)
        grad_gates = jnp.stack([grad_gate_value, grad_gate_out], axis=1) * chosen_here
        grad_logit = (
            (grad_gates * gate_prob * (1.0 - gate_prob)).astype(jnp.bfloat16).reshape(tokens, -1)
        )
        grad_in = padded([grad_qk, grad_proj, grad_logit], in_width)
        grad_first = contract_last(grad_in, in_w)
        gain_one_grad = jnp.sum(grad_first * normed_one, axis=0)
        bias_one_grad = jnp.sum(grad_first, axis=0)
        grad_hidden = grad_residual + norm_back(grad_first, normed_one, inverse_one, gains[:, 0])
        norm_grads = jnp.stack(
            [gain_one_grad, bias_one_grad, gain_two_grad, bias_two_grad], axis=1
        ).astype(jnp.bfloat16)
        at = value_end + router_cols
        near = at // 128 * 128
        norm_grads = jnp.pad(norm_grads, ((0, 0), (at - near, 128 - 4 - (at - near))))
        pairs += [
            (first_in, padded([grad_in], chunk_whole(in_width))),
            (residual_low, padded([mixed], chunk_whole(out_width))),
            (second_in, grad_up),
            (grad_low, act),
        ]
        extras.append((norm_grads, near))
    reduced = reduce_weight_grads(pairs, extras, CHUNK)
    matrix_rows = [None] * LAYERS
    small_rows = [None] * LAYERS
    start = 0
    for slot, layer in enumerate(reversed(range(LAYERS))):
        widths = [right.shape[1] for _, right in pairs[4 * slot : 4 * slot + 4]]
        begins = [start + sum(widths[:group_index]) for group_index in range(4)]
        start += sum(widths)
        shares = [
            reduced[:, begin : begin + used]
            for begin, used in zip(
                begins, (value_end, output_end - value_end, FF, FF)
            )
        ]
        matrix_rows[layer] = jnp.concatenate(shares, axis=1)
        small_rows[layer] = reduced[
            :, begins[0] + value_end : begins[0] + value_end + router_cols + 4
        ]
    input_grad = grad_hidden.reshape(seq_count, sub_rows, width).astype(jnp.bfloat16)
    matrix_grad = jnp.stack(matrix_rows, axis=0)
    small_grad = jnp.stack(small_rows, axis=0)
    matrix_new, matrix_first_new, matrix_second_new = adam_update(
        matrix, matrix_grad, matrix_first, matrix_second, column_rates(segment), WEIGHT_DECAY
    )
    small_new, small_first_new, small_second_new = adam_update(
        small, small_grad, small_first, small_second, small_rates(), 0.0
    )
    return (
        output,
        input_grad,
        matrix_grad,
        matrix_new,
        matrix_new.astype(jnp.bfloat16),
        matrix_first_new,
        matrix_second_new,
        small_grad,
        small_new,
        small_new.astype(jnp.bfloat16),
        small_first_new,
        small_second_new,
        loads,
    )


def solution(mesh):
    in_specs = (
        P("dp", ("seq", "head"), None),
        P("dp", ("seq", "head"), None),
        P(None, "dp", ("seq", "head"), None, None, None),
        P("dp"),
        P(None, ("dp", "seq", "head"), None),
        P(None, ("dp", "seq", "head"), None),
        P(None, ("dp", "seq", "head"), None),
        P(None, ("dp", "seq", "head"), None),
        P(None, ("dp", "seq", "head"), None),
        P(None, ("dp", "seq", "head"), None),
    )
    out_specs = (
        P("dp", ("seq", "head"), None),
        P("dp", ("seq", "head"), None),
        P(None, ("dp", "seq", "head"), None),
        P(None, ("dp", "seq", "head"), None),
        P(None, ("dp", "seq", "head"), None),
        P(None, ("dp", "seq", "head"), None),
        P(None, ("dp", "seq", "head"), None),
        P(None, ("dp", "seq", "head"), None),
        P(None, ("dp", "seq", "head"), None),
        P(None, ("dp", "seq", "head"), None),
        P(None, ("dp", "seq", "head"), None),
        P(None, ("dp", "seq", "head"), None),
        P(),
    )
    return jax.shard_map(local, mesh=mesh, in_specs=in_specs, out_specs=out_specs, check_vma=False)
```

```python
import math

import jax
import jax.numpy as jnp
from jax import lax
from jax.experimental import pallas as pl
from jax.experimental.pallas import tpu as pltpu
from jax.sharding import PartitionSpec as P

D = 1024
HEADS = 4
HEAD_DIM = 112
EXPERTS = 5
FF = 4096
LAYERS = 2
STEP = 10


NORM_EPS = 1e-05
BETA_ONE = 0.9
BETA_TWO = 0.95
ADAM_EPS = 1e-08
WEIGHT_DECAY = 0.1
NORM_RATE = 0.5
MASKED = -1e30
CHUNK = 512


def column_bounds():
    query_end = 2 * HEADS * HEAD_DIM
    value_end = query_end + HEADS * EXPERTS * HEAD_DIM
    output_end = value_end + HEADS * EXPERTS * HEAD_DIM
    return (query_end, value_end, output_end, output_end + FF)


def column_rates(segment):
    query_end, value_end, output_end, up_end = column_bounds()
    column = jnp.arange(up_end + FF)
    inner = D ** (-0.5)
    outer = 0.7 * math.sqrt(segment) / HEAD_DIM
    rates = jnp.where(
        column < value_end,
        inner,
        jnp.where(column < output_end, outer, jnp.where(column < up_end, inner, FF ** (-0.5))),
    )
    return rates.astype(jnp.float32)


def small_rates():
    column = jnp.arange(2 * HEADS * EXPERTS + 4)
    return jnp.where(column < 2 * HEADS * EXPERTS, 0.7 * D ** (-0.5), NORM_RATE).astype(jnp.float32)


def adam_update(weight, grad, first, second, rates, decay):
    first_new = BETA_ONE * first + (1.0 - BETA_ONE) * grad
    second_new = BETA_TWO * second + (1.0 - BETA_TWO) * grad * grad
    first_hat = first_new / (1.0 - BETA_ONE**STEP)
    second_hat = second_new / (1.0 - BETA_TWO**STEP)
    new = weight - rates * (first_hat / (jnp.sqrt(second_hat) + ADAM_EPS) + decay * weight)
    return (new, first_new, second_new)


def rotary_tables(positions):
    half = HEAD_DIM // 2
    inverse = jnp.exp(-math.log(10000.0) * jnp.arange(half, dtype=jnp.float32) / half)
    angle = positions.astype(jnp.float32)[:, None] * inverse[None, :]
    return (jnp.cos(angle), jnp.sin(angle))


def layer_stats(values):
    mean = jnp.mean(values, axis=-1, keepdims=True)
    centered = values - mean
    variance = jnp.mean(centered * centered, axis=-1, keepdims=True)
    inverse = lax.rsqrt(variance + NORM_EPS)
    return (centered * inverse, inverse)


def norm_back(grad_normed, normed, inverse, gain):
    scaled = grad_normed * gain
    return inverse * (
        scaled
        - jnp.mean(scaled, axis=-1, keepdims=True)
        - normed * jnp.mean(scaled * normed, axis=-1, keepdims=True)
    )


def contract_last(left, right):
    return lax.dot_general(
        left, right, (((1,), (1,)), ((), ())), preferred_element_type=jnp.float32
    )


def contract_first(left, right):
    return lax.dot_general(
        left, right, (((0,), (0,)), ((), ())), preferred_element_type=jnp.float32
    )


AXES = ("dp", "seq", "head")


def mesh_bits():
    dims = [
        (axis, bit)
        for axis in AXES
        for bit in reversed(range(lax.axis_size(axis).bit_length() - 1))
    ]
    groups = [[index for index, (axis, _) in enumerate(dims) if axis == name] for name in AXES]
    return (dims, *groups)


def my_bits(dims):
    place = {axis: lax.axis_index(axis) for axis in AXES}
    bits = [lax.rem(place[axis] // (1 << bit), 2) for axis, bit in dims]
    partners = [
        {axis: place[axis] + (1 << bit) * (1 - 2 * bits[index])}
        for index, (axis, bit) in enumerate(dims)
    ]
    return (bits, partners)


def greet(partners):
    barrier = pltpu.get_barrier_semaphore()
    for partner in partners:
        pl.semaphore_signal(
            barrier, inc=1, device_id=partner, device_id_type=pl.DeviceIdType.MESH
        )
    pl.semaphore_wait(barrier, len(partners))


def gather_rows(shares, pieces, name):
    dims, dp_dims, seq_dims, head_dims = mesh_bits()
    orders = (
        head_dims + dp_dims[::-1] + seq_dims,
        head_dims + dp_dims + seq_dims,
        dp_dims + head_dims + seq_dims,
    )
    depth = len(dims)
    total = len(shares)
    lag, slots = (2, 4)
    steps = max(piece[3] for piece in pieces) + lag * depth

    def kernel(*refs):
        ins, outs = (refs[:total], refs[total : 2 * total])
        send_sem, recv_sem, local_sem = refs[2 * total :]
        bits, partners = my_bits(dims)
        own = [
            pltpu.make_async_copy(ins[index], outs[index].at[tuple(bits)], local_sem.at[index])
            for index in range(total)
        ]
        for copy in own:
            copy.start()
        greet(partners)
        for copy in own:
            copy.wait()

        def exchange(number, stage, chunk):
            array, start, width, _, which = pieces[number]
            done = orders[which][:stage]
            at = tuple(slice(None) if dim in done else bits[dim] for dim in range(depth))
            columns = pl.ds(pl.multiple_of(start + chunk * width, 128), width)
            view = outs[array].at[at + (slice(None), columns)]
            slot = lax.rem(chunk, slots)
            return pltpu.make_async_remote_copy(
                src_ref=view,
                dst_ref=view,
                send_sem=send_sem.at[number, stage, slot],
                recv_sem=recv_sem.at[number, stage, slot],
                device_id=partners[orders[which][stage]],
                device_id_type=pl.DeviceIdType.MESH,
            )

        def body(step, carry):
            for stage in range(depth, -1, -1):
                chunk = step - lag * stage
                for number, piece in enumerate(pieces):

                    @pl.when((chunk >= 0) & (chunk < piece[3]))
                    def _(stage=stage, chunk=chunk, number=number):
                        if stage > 0:
                            exchange(number, stage - 1, chunk).wait()
                        if stage < depth:
                            exchange(number, stage, chunk).start()

            return carry

        lax.fori_loop(0, steps, body, 0)

    in_place = pl.BlockSpec(memory_space=pl.ANY)
    semaphores = pltpu.SemaphoreType.DMA((len(pieces), depth, slots))
    gathered = pl.pallas_call(
        kernel,
        in_specs=[in_place] * total,
        out_specs=[in_place] * total,
        out_shape=[
            jax.ShapeDtypeStruct((2,) * depth + share.shape, share.dtype) for share in shares
        ],
        scratch_shapes=[semaphores, semaphores, pltpu.SemaphoreType.DMA((total,))],
        compiler_params=pltpu.CompilerParams(collective_id=name, has_side_effects=True),
    )(*shares)
    return [value.reshape(-1, value.shape[-1]) for value in gathered]


def halving_plan(width):
    dims, dp_dims, seq_dims, head_dims = mesh_bits()
    first = seq_dims[::-1]
    orders = (
        (0, width // 2, first + dp_dims[::-1] + head_dims[::-1]),
        (width // 2, width // 4, first + dp_dims + head_dims[::-1]),
        (3 * width // 4, width // 4, first + head_dims[::-1] + dp_dims[::-1]),
    )
    stages = []
    for stage in range(len(dims)):
        parts = []
        for start, count, order in orders:
            left = [dim for dim in range(len(dims)) if dim not in order[:stage]]
            if parts and parts[-1][2:] == (order[stage], left):
                parts[-1] = (parts[-1][0], parts[-1][1] + count, order[stage], left)
            else:
                parts.append((start, count, order[stage], left))
        stages.append(parts)
    lags = [1 if stage < len(seq_dims) else 2 for stage in range(len(dims))]
    return dims, stages, lags


def reduce_weight_grads(pairs, extras, width):
    dims, stages, lags = halving_plan(width)
    depth = len(dims)
    tokens, model = pairs[0][0].shape
    rows = model >> depth
    firsts = [0]
    for left, right in pairs:
        firsts.append(firsts[-1] + right.shape[1] // width)
    chunks = firsts[-1]
    per_layer = len(pairs) // len(extras)
    spots = [
        (firsts[per_layer * index] + near // width, near % width)
        for index, (_, near) in enumerate(extras)
    ]
    starts = [sum(lags[:stage]) for stage in range(depth + 1)]
    count_pairs, count_extras = (len(pairs), len(extras))

    def kernel(*refs):
        lefts = refs[:count_pairs]
        rights = refs[count_pairs : 2 * count_pairs]
        added = refs[2 * count_pairs : 2 * count_pairs + count_extras]
        rest = refs[2 * count_pairs + count_extras :]
        out_ref, left_buf, turned, right_buf, load_sem = rest[:5]
        pool = iter(rest[5:])
        buffers = [[tuple(next(pool) for _ in range(4)) for _ in parts] for parts in stages]
        step = pl.program_id(0)
        bits, partners = my_bits(dims)

        def exchange(stage, part, slot):
            start, count, dim, left = stages[stage][part]
            own, got, send_sem, recv_sem = buffers[stage][part]
            lead = (slot,) + (slice(None),) * left.index(dim)
            return pltpu.make_async_remote_copy(
                src_ref=own.at[lead + (1 - bits[dim],)],
                dst_ref=got.at[slot],
                send_sem=send_sem.at[slot],
                recv_sem=recv_sem.at[slot],
                device_id=partners[dim],
                device_id_type=pl.DeviceIdType.MESH,
            )

        def load_left(index):
            return pltpu.make_async_copy(lefts[index], left_buf, load_sem.at[2])

        def load_right(index, chunk):
            slot = lax.rem(chunk, 2)
            columns = pl.ds(pl.multiple_of((chunk - firsts[index]) * width, width), width)
            return pltpu.make_async_copy(
                rights[index].at[:, columns], right_buf.at[slot], load_sem.at[slot]
            )

        def prefetch(chunk):
            for index in range(count_pairs):

                @pl.when((chunk >= firsts[index]) & (chunk < firsts[index + 1]))
                def _(index=index):
                    load_right(index, chunk).start()

                @pl.when(chunk == firsts[index])
                def _(index=index):
                    load_left(index).start()

        @pl.when(step == 0)
        def _():
            prefetch(step)
            greet(partners)

        @pl.when(step + 1 < chunks)
        def _():
            prefetch(step + 1)

        for stage in range(depth, -1, -1):
            chunk = step - starts[stage]

            @pl.when((chunk >= 0) & (chunk < chunks))
            def _(stage=stage, chunk=chunk):
                if stage == 0:
                    for first in firsts[:-1]:

                        @pl.when(chunk == first)
                        def _():
                            load_left(0).wait()
                            turned[...] = left_buf[...].T

                    load_right(0, lax.rem(chunk, 2)).wait()
                    product = jnp.dot(
                        turned[...],
                        right_buf[lax.rem(chunk, 2)],
                        preferred_element_type=jnp.float32,
                    )
                    slot = lax.rem(chunk, 2 * lags[0])
                    for part, (start, count, dim, left) in enumerate(stages[0]):
                        piece = product[:, start : start + count].astype(jnp.bfloat16)
                        buffers[0][part][0][slot] = piece.reshape((2,) * depth + (rows, count))
                    for index in range(count_extras):

                        @pl.when(chunk == spots[index][0])
                        def _(index=index):
                            at = (slot, Ellipsis, slice(spots[index][1], spots[index][1] + 128))
                            own = buffers[0][0][0]
                            total = own[at].astype(jnp.float32) + added[index][...].astype(
                                jnp.float32
                            )
                            own[at] = total.astype(jnp.bfloat16)

                else:
                    back = lax.rem(chunk, 2 * lags[stage - 1])
                    for part, (start, count, dim, left) in enumerate(stages[stage - 1]):
                        exchange(stage - 1, part, back).wait()
                        own, got = buffers[stage - 1][part][:2]
                        lead = (back,) + (slice(None),) * left.index(dim)
                        total = own[lead + (bits[dim],)].astype(jnp.float32) + got[back].astype(
                            jnp.float32
                        )
                        if stage == depth:
                            out_ref[:, start : start + count] = total
                            continue
                        slot = lax.rem(chunk, 2 * lags[stage])
                        low = total.astype(jnp.bfloat16)
                        for other, (begin, length, _, kept) in enumerate(stages[stage]):
                            lo, hi = max(start, begin), min(start + count, begin + length)
                            if lo < hi:
                                at = (slot,) + (slice(None),) * (len(kept) + 1)
                                buffers[stage][other][0][at + (slice(lo - begin, hi - begin),)] = (
                                    low[..., lo - start : hi - start]
                                )
                if stage < depth:
                    for part in range(len(stages[stage])):
                        exchange(stage, part, lax.rem(chunk, 2 * lags[stage])).start()

    scratch = [
        pltpu.VMEM((tokens, model), jnp.bfloat16),
        pltpu.VMEM((model, tokens), jnp.bfloat16),
        pltpu.VMEM((2, tokens, width), jnp.bfloat16),
        pltpu.SemaphoreType.DMA((3,)),
    ]
    for stage, parts in enumerate(stages):
        slots = 2 * lags[stage]
        for start, count, dim, left in parts:
            scratch += [
                pltpu.VMEM((slots,) + (2,) * len(left) + (rows, count), jnp.bfloat16),
                pltpu.VMEM((slots,) + (2,) * (len(left) - 1) + (rows, count), jnp.bfloat16),
                pltpu.SemaphoreType.DMA((slots,)),
                pltpu.SemaphoreType.DMA((slots,)),
            ]
    in_place = pl.BlockSpec(memory_space=pl.ANY)
    whole = [value.reshape((2,) * depth + (rows, 128)) for value, _ in extras]
    return pl.pallas_call(
        kernel,
        grid=(chunks + starts[depth],),
        in_specs=[in_place] * (2 * count_pairs)
        + [pl.BlockSpec(value.shape, lambda step: (0,) * (depth + 2)) for value in whole],
        out_specs=pl.BlockSpec(
            (rows, width), lambda step: (0, jnp.clip(step - starts[depth], 0, chunks - 1))
        ),
        out_shape=jax.ShapeDtypeStruct((rows, chunks * width), jnp.float32),
        scratch_shapes=scratch,
        compiler_params=pltpu.CompilerParams(
            collective_id=1,
            has_side_effects=True,
            vmem_limit_bytes=48 << 20,
            dimension_semantics=("arbitrary",),
        ),
    )(*[left for left, _ in pairs], *[right for _, right in pairs], *whole)


def lane_whole(count):
    return count + (-count) % 128


def chunk_whole(count):
    return count + (-count) % CHUNK


def padded(pieces, width):
    have = sum(piece.shape[1] for piece in pieces)
    fill = jnp.zeros((pieces[0].shape[0], width - have), pieces[0].dtype)
    return jnp.concatenate(list(pieces) + [fill], axis=1)


def columns_plan(array, width):
    unit = 256 if width % 256 == 0 else 128
    units = width // unit
    near = (3 * units + 4) // 8
    plan, start = ([], 0)
    for which, count in ((0, near), (1, near), (2, units - 2 * near)):
        plan.append((array, start, unit, count, which))
        start += count * unit
    return plan


LANES = 128
QUERY_TILE = 256


def swap_halves(tensor):
    half = HEAD_DIM // 2
    return jnp.concatenate([tensor[:, half:], tensor[:, :half]], axis=1)


def lane_filled(tensor):
    fill = jnp.zeros((tensor.shape[0], LANES - tensor.shape[1]), tensor.dtype)
    return jnp.concatenate([tensor, fill], axis=1)


def weights_block(keys_mem, keys_own, query, start, first, segment, length):
    contract = (((1,), (1,)), ((), ()))
    raw = jnp.concatenate(
        [
            lax.dot_general(keys, query, contract, preferred_element_type=jnp.float32)
            for keys in (keys_mem, keys_own)
        ],
        axis=0,
    )
    key_pos = start - segment + lax.broadcasted_iota(jnp.int32, raw.shape, 0)
    query_pos = start + first + lax.broadcasted_iota(jnp.int32, raw.shape, 1)
    used = (key_pos < length) & (key_pos < query_pos) & (key_pos >= 0)
    allowed = used | (key_pos == query_pos)
    scores = jnp.where(allowed, raw * HEAD_DIM ** (-0.5), MASKED)
    weights = jnp.exp(scores - jnp.max(scores, axis=0, keepdims=True))
    return weights * (1.0 / jnp.sum(weights, axis=0, keepdims=True))


def contract_rows(left, right):
    return lax.dot_general(
        left, right, (((0,), (0,)), ((), ())), preferred_element_type=jnp.float32
    )


def across(axis, offset):
    size = lax.axis_size(axis)
    return {axis: lax.rem(lax.axis_index(axis) + offset + size, size)}


def sent_to(source, target, send_sem, recv_sem, device):
    return pltpu.make_async_remote_copy(
        src_ref=source,
        dst_ref=target,
        send_sem=send_sem,
        recv_sem=recv_sem,
        device_id=device,
        device_id_type=pl.DeviceIdType.MESH,
    )


def meet(memory_step):
    barrier = pltpu.get_barrier_semaphore()
    heads = lax.axis_size("head")
    writers = [across("head", step) for step in range(1, heads)]
    writers.append(across("seq", -memory_step))
    for device in writers:
        pl.semaphore_signal(barrier, inc=1, device_id=device, device_id_type=pl.DeviceIdType.MESH)
    pl.semaphore_wait(barrier, len(writers))


def gate_values(entered_ref, chosen_ref, rows):
    at = column_bounds()[1]
    logits = entered_ref[rows, at : at + 2 * HEADS * EXPERTS]
    prob = 1.0 / (1.0 + jnp.exp(-logits))
    return (prob, prob * chosen_ref[rows, :])


def column(tensor, index):
    return tensor[:, index : index + 1]


def attention_forward(entered, chosen, turn_cos, turn_sin, lengths, mixed_width, name):
    seq_count = lengths.shape[0]
    tokens = entered.shape[0]
    sub = tokens // seq_count
    heads = lax.axis_size("head")
    segment = heads * sub
    query_end = column_bounds()[0]
    sides = range(1, heads)

    def kernel(*refs):
        length_ref, entered_ref, chosen_ref, cos_ref, sin_ref = refs[:5]
        mixed_ref, attended_ref, query_ref, key_ref, value_ref = refs[5:10]
        out_buf, heads_buf, mem_buf, done_buf, back_buf = refs[10:15]
        out_sem, in_sem, mem_sem, done_sem, back_sem = refs[15:]
        me = lax.axis_index("head")
        start = lax.axis_index("seq") * segment
        turn, wind = (cos_ref[...], sin_ref[...])

        def outward(b, side):
            there = across("head", side)
            return sent_to(
                out_buf.at[b, there["head"]],
                heads_buf.at[b, :, me],
                out_sem.at[b, side - 1],
                in_sem.at[b, side - 1],
                there,
            )

        def onward(b):
            return sent_to(
                heads_buf.at[b, 1:3],
                mem_buf.at[b],
                mem_sem.at[0, b],
                mem_sem.at[1, b],
                across("seq", 1),
            )

        def homeward(b, side):
            there = across("head", side)
            return sent_to(
                done_buf.at[b, there["head"]],
                back_buf.at[b, me],
                done_sem.at[b, side - 1],
                back_sem.at[b, side - 1],
                there,
            )

        meet(1)
        gates_of = []
        for b in range(seq_count):
            rows = slice(b * sub, (b + 1) * sub)
            gates = gate_values(entered_ref, chosen_ref, rows)[1]
            gates_of.append(gates)
            for head in range(HEADS):
                for kind in range(2):
                    at = (kind * HEADS + head) * HEAD_DIM
                    vector = entered_ref[rows, at : at + HEAD_DIM]
                    turned = vector * turn + swap_halves(vector) * wind
                    out_buf[b, head, kind] = lane_filled(turned).astype(jnp.bfloat16)
                value = jnp.zeros((sub, HEAD_DIM), jnp.float32)
                for expert in range(EXPERTS):
                    index = head * EXPERTS + expert
                    at = query_end + index * HEAD_DIM
                    value += column(gates, index) * entered_ref[rows, at : at + HEAD_DIM]
                out_buf[b, head, 2] = lane_filled(value).astype(jnp.bfloat16)
            for side in sides:
                outward(b, side).start()
            for kind in range(3):
                heads_buf[b, kind, me] = out_buf[b, me, kind]
        for b in range(seq_count):
            for side in sides:
                outward(b, side).wait_recv()
            onward(b).start()
        for b in range(seq_count):
            onward(b).wait_recv()
            keys_own = heads_buf[b, 1].reshape(segment, LANES)
            values = jnp.concatenate(
                [mem_buf[b, 1].reshape(segment, LANES), heads_buf[b, 2].reshape(segment, LANES)],
                axis=0,
            )
            for first in range(0, segment, QUERY_TILE):
                tile = slice(first // sub, (first + QUERY_TILE) // sub)
                query = heads_buf[b, 0, tile].reshape(QUERY_TILE, LANES)
                probs = weights_block(
                    mem_buf[b, 0].reshape(segment, LANES),
                    keys_own,
                    query,
                    start,
                    first,
                    segment,
                    length_ref[b],
                ).astype(jnp.bfloat16)
                attended = contract_rows(values, probs).T.astype(jnp.bfloat16)
                done_buf[b, tile] = attended.reshape(QUERY_TILE // sub, sub, LANES)
            for side in sides:
                homeward(b, side).start()
            back_buf[b, me] = done_buf[b, me]
        for b in range(seq_count):
            query_ref[b] = heads_buf[b, 0]
            key_ref[b, 0] = mem_buf[b, 0]
            key_ref[b, 1] = heads_buf[b, 1]
            value_ref[b, 0] = mem_buf[b, 1]
            value_ref[b, 1] = heads_buf[b, 2]
        used = HEADS * EXPERTS * HEAD_DIM
        mixed_ref[:, used:] = jnp.zeros((tokens, mixed_width - used), jnp.bfloat16)
        for b in range(seq_count):
            rows = slice(b * sub, (b + 1) * sub)
            for side in sides:
                homeward(b, side).wait_recv()
            for head in range(HEADS):
                attended = back_buf[b, head]
                attended_ref[rows, head * LANES : (head + 1) * LANES] = attended
                wide = attended.astype(jnp.float32)[:, :HEAD_DIM]
                for expert in range(EXPERTS):
                    index = head * EXPERTS + expert
                    gate = column(gates_of[b], HEADS * EXPERTS + index)
                    mixed_ref[rows, index * HEAD_DIM : (index + 1) * HEAD_DIM] = (
                        gate * wide
                    ).astype(jnp.bfloat16)
        for b in range(seq_count):
            onward(b).wait_send()
            for side in sides:
                outward(b, side).wait_send()
                homeward(b, side).wait_send()

    def shape(*dims):
        return jax.ShapeDtypeStruct(dims, jnp.bfloat16)

    vmem = pl.BlockSpec(memory_space=pltpu.VMEM)
    paired = pltpu.SemaphoreType.DMA((seq_count, heads - 1))
    return pl.pallas_call(
        kernel,
        in_specs=[pl.BlockSpec(memory_space=pltpu.SMEM)] + [vmem] * 4,
        out_specs=[vmem] * 5,
        out_shape=[
            shape(tokens, mixed_width),
            shape(tokens, HEADS * LANES),
            shape(seq_count, heads, sub, LANES),
            shape(seq_count, 2, heads, sub, LANES),
            shape(seq_count, 2, heads, sub, LANES),
        ],
        scratch_shapes=[
            pltpu.VMEM((seq_count, heads, 3, sub, LANES), jnp.bfloat16),
            pltpu.VMEM((seq_count, 3, heads, sub, LANES), jnp.bfloat16),
            pltpu.VMEM((seq_count, 2, heads, sub, LANES), jnp.bfloat16),
            pltpu.VMEM((seq_count, heads, sub, LANES), jnp.bfloat16),
            pltpu.VMEM((seq_count, heads, sub, LANES), jnp.bfloat16),
            paired,
            paired,
            pltpu.SemaphoreType.DMA((2, seq_count)),
            paired,
            paired,
        ],
        compiler_params=pltpu.CompilerParams(
            collective_id=name, has_side_effects=True, vmem_limit_bytes=40 << 20
        ),
    )(lengths, entered, chosen, turn_cos, turn_sin)


def attention_backward(
    grad_mixed, attended, entered, chosen, turn_cos, turn_sin, lengths, saved, grad_width, name
):
    query, keys, values = saved
    seq_count = lengths.shape[0]
    tokens = entered.shape[0]
    sub = tokens // seq_count
    heads = lax.axis_size("head")
    segment = heads * sub
    query_end, value_end = column_bounds()[:2]
    router_cols = 2 * HEADS * EXPERTS
    sides = range(1, heads)

    def kernel(*refs):
        length_ref, grad_ref, attended_ref, entered_ref, chosen_ref, cos_ref, sin_ref = refs[:7]
        query_ref, key_ref, value_ref, result_ref = refs[7:11]
        out_buf, heads_buf, mem_out, mem_in, own_buf, done_buf, back_buf = refs[11:18]
        out_sem, in_sem, mem_sem, done_sem, back_sem = refs[18:]
        me = lax.axis_index("head")
        start = lax.axis_index("seq") * segment
        turn, wind = (cos_ref[...], sin_ref[...])

        def outward(b, side):
            there = across("head", side)
            return sent_to(
                out_buf.at[b, there["head"]],
                heads_buf.at[b, me],
                out_sem.at[b, side - 1],
                in_sem.at[b, side - 1],
                there,
            )

        def onward(b):
            return sent_to(
                mem_out.at[b], mem_in.at[b], mem_sem.at[0, b], mem_sem.at[1, b], across("seq", -1)
            )

        def homeward(b, side):
            there = across("head", side)
            return sent_to(
                done_buf.at[b, there["head"]],
                back_buf.at[b, me],
                done_sem.at[b, side - 1],
                back_sem.at[b, side - 1],
                there,
            )

        meet(-1)
        lane = lax.broadcasted_iota(jnp.int32, (sub, router_cols), 1)
        gate_grads, probs_of, gates_of = ([], [], [])
        for b in range(seq_count):
            rows = slice(b * sub, (b + 1) * sub)
            prob, gates = gate_values(entered_ref, chosen_ref, rows)
            probs_of.append(prob)
            gates_of.append(gates)
            gate_grad = jnp.zeros((sub, router_cols), jnp.float32)
            for head in range(HEADS):
                seen = attended_ref[rows, head * LANES : head * LANES + HEAD_DIM].astype(
                    jnp.float32
                )
                total = jnp.zeros((sub, HEAD_DIM), jnp.float32)
                for expert in range(EXPERTS):
                    index = head * EXPERTS + expert
                    part = grad_ref[rows, index * HEAD_DIM : (index + 1) * HEAD_DIM]
                    total += column(gates, HEADS * EXPERTS + index) * part
                    gate_grad = jnp.where(
                        lane == HEADS * EXPERTS + index,
                        jnp.sum(part * seen, axis=1, keepdims=True),
                        gate_grad,
                    )
                out_buf[b, head] = lane_filled(total).astype(jnp.bfloat16)
            gate_grads.append(gate_grad)
            for side in sides:
                outward(b, side).start()
            heads_buf[b, me] = out_buf[b, me]
        for b in range(seq_count):
            for side in sides:
                outward(b, side).wait_recv()
            keys_mem = key_ref[b, 0].reshape(segment, LANES)
            keys_own = key_ref[b, 1].reshape(segment, LANES)
            keys_all = jnp.concatenate([keys_mem, keys_own], axis=0)
            values_all = jnp.concatenate(
                [value_ref[b, 0].reshape(segment, LANES), value_ref[b, 1].reshape(segment, LANES)],
                axis=0,
            )
            grad_keys = jnp.zeros((2 * segment, LANES), jnp.float32)
            grad_values = jnp.zeros((2 * segment, LANES), jnp.float32)
            for first in range(0, segment, QUERY_TILE):
                tile = slice(first // sub, (first + QUERY_TILE) // sub)
                here = query_ref[b, tile].reshape(QUERY_TILE, LANES)
                arrived = heads_buf[b, tile].reshape(QUERY_TILE, LANES)
                probs = weights_block(
                    keys_mem, keys_own, here, start, first, segment, length_ref[b]
                )
                grad_probs = contract_last(values_all, arrived)
                delta = jnp.sum(probs * grad_probs, axis=0, keepdims=True)
                grad_raw = (probs * (grad_probs - delta) * HEAD_DIM ** (-0.5)).astype(
                    jnp.bfloat16
                )
                grad_values += jnp.dot(
                    probs.astype(jnp.bfloat16), arrived, preferred_element_type=jnp.float32
                )
                grad_keys += jnp.dot(grad_raw, here, preferred_element_type=jnp.float32)
                grad_query = contract_rows(keys_all, grad_raw).T.astype(jnp.bfloat16)
                done_buf[b, tile, 0] = grad_query.reshape(QUERY_TILE // sub, sub, LANES)
            for kind, grads in enumerate((grad_keys, grad_values)):
                mem_out[b, kind] = grads[:segment].astype(jnp.bfloat16)
                own_buf[b, kind] = grads[segment:]
            onward(b).start()
        for b in range(seq_count):
            onward(b).wait_recv()
            for kind in range(2):
                total = own_buf[b, kind] + mem_in[b, kind].astype(jnp.float32)
                done_buf[b, :, kind + 1] = total.astype(jnp.bfloat16).reshape(heads, sub, LANES)
            for side in sides:
                homeward(b, side).start()
            back_buf[b, me] = done_buf[b, me]
        used = value_end + router_cols
        result_ref[:, used:] = jnp.zeros((tokens, grad_width - used), jnp.bfloat16)
        for b in range(seq_count):
            rows = slice(b * sub, (b + 1) * sub)
            for side in sides:
                homeward(b, side).wait_recv()
            gate_grad = gate_grads[b]
            for head in range(HEADS):
                for kind in range(2):
                    vector = back_buf[b, head, kind].astype(jnp.float32)[:, :HEAD_DIM]
                    turned = vector * turn - swap_halves(vector) * wind
                    at = (kind * HEADS + head) * HEAD_DIM
                    result_ref[rows, at : at + HEAD_DIM] = turned.astype(jnp.bfloat16)
                grad_value = back_buf[b, head, 2].astype(jnp.float32)[:, :HEAD_DIM]
                for expert in range(EXPERTS):
                    index = head * EXPERTS + expert
                    at = query_end + index * HEAD_DIM
                    gate_grad = jnp.where(
                        lane == index,
                        jnp.sum(
                            entered_ref[rows, at : at + HEAD_DIM] * grad_value,
                            axis=1,
                            keepdims=True,
                        ),
                        gate_grad,
                    )
                    result_ref[rows, at : at + HEAD_DIM] = (
                        column(gates_of[b], index) * grad_value
                    ).astype(jnp.bfloat16)
            prob = probs_of[b]
            result_ref[rows, value_end:used] = (
                gate_grad * chosen_ref[rows, :] * prob * (1.0 - prob)
            ).astype(jnp.bfloat16)
        for b in range(seq_count):
            onward(b).wait_send()
            for side in sides:
                outward(b, side).wait_send()
                homeward(b, side).wait_send()

    vmem = pl.BlockSpec(memory_space=pltpu.VMEM)
    paired = pltpu.SemaphoreType.DMA((seq_count, heads - 1))
    return pl.pallas_call(
        kernel,
        in_specs=[pl.BlockSpec(memory_space=pltpu.SMEM)] + [vmem] * 9,
        out_specs=vmem,
        out_shape=jax.ShapeDtypeStruct((tokens, grad_width), jnp.bfloat16),
        scratch_shapes=[
            pltpu.VMEM((seq_count, heads, sub, LANES), jnp.bfloat16),
            pltpu.VMEM((seq_count, heads, sub, LANES), jnp.bfloat16),
            pltpu.VMEM((seq_count, 2, segment, LANES), jnp.bfloat16),
            pltpu.VMEM((seq_count, 2, segment, LANES), jnp.bfloat16),
            pltpu.VMEM((seq_count, 2, segment, LANES), jnp.float32),
            pltpu.VMEM((seq_count, heads, 3, sub, LANES), jnp.bfloat16),
            pltpu.VMEM((seq_count, heads, 3, sub, LANES), jnp.bfloat16),
            paired,
            paired,
            pltpu.SemaphoreType.DMA((2, seq_count)),
            paired,
            paired,
        ],
        compiler_params=pltpu.CompilerParams(
            collective_id=name, has_side_effects=True, vmem_limit_bytes=48 << 20
        ),
    )(lengths, grad_mixed, attended, entered, chosen, turn_cos, turn_sin, query, keys, values)


def gelu_tanh(values):
    return jax.nn.gelu(values, approximate=True)


def local(
    inputs,
    cotangent,
    routes,
    lengths,
    matrix,
    matrix_first,
    matrix_second,
    small,
    small_first,
    small_second,
):
    head_count = lax.axis_size("head")
    seq_count, sub_rows, width = inputs.shape
    segment = sub_rows * head_count
    tokens = seq_count * sub_rows
    router_cols = 2 * HEADS * EXPERTS
    group = HEADS * EXPERTS
    query_end, value_end, output_end, up_end = column_bounds()
    seq_start = lax.axis_index("seq") * segment
    positions = (
        seq_start + lax.axis_index("head") * sub_rows + jnp.arange(sub_rows, dtype=jnp.int32)
    )
    valid = (positions[None, :] < lengths[:, None]).astype(jnp.float32)
    cosines, sines = rotary_tables(positions)
    turn_cos = jnp.concatenate([cosines, cosines], axis=1)
    turn_sin = jnp.concatenate([-sines, sines], axis=1)
    chosen = jnp.sum(
        (routes[..., None] == jnp.arange(EXPERTS, dtype=jnp.int32)).astype(jnp.float32), axis=-2
    )
    load_part = jnp.sum(chosen * valid[None, :, :, None, None, None], axis=(1, 2))
    in_width = lane_whole(value_end + router_cols + 4)
    out_width = lane_whole(output_end - value_end)
    matrix_low = matrix.astype(jnp.bfloat16)
    small_low = small.astype(jnp.bfloat16)
    in_low = [
        padded([matrix_low[layer, :, :value_end], small_low[layer]], in_width)
        for layer in range(LAYERS)
    ]
    out_low = [
        padded([matrix_low[layer, :, value_end:output_end]], out_width) for layer in range(LAYERS)
    ]
    counts = jnp.pad(load_part.reshape(-1), (0, (-load_part.size) % 1024)).reshape(8, -1)
    in_first, out_first, counts = gather_rows(
        [in_low[0], out_low[0], counts],
        columns_plan(0, in_width) + columns_plan(1, out_width) + [(2, 0, counts.shape[1], 1, 0)],
        2,
    )
    loads = (
        jnp.sum(counts.reshape(-1, load_part.size + (-load_part.size) % 1024), axis=0)[
            : load_part.size
        ]
        .reshape(load_part.shape)
    )
    everyone = ("dp", "seq", "head")
    in_ws, out_ws = ([in_first], [out_first])
    ffn_ws = [lax.all_gather(matrix_low[0, :, output_end:], everyone, axis=0, tiled=True)]
    for layer in range(1, LAYERS):
        attn_low = jnp.concatenate([in_low[layer], out_low[layer]], axis=1)
        ffn_ws[-1], attn_low = lax.optimization_barrier((ffn_ws[-1], attn_low))
        both = lax.all_gather(attn_low, everyone, axis=0, tiled=True)
        both, ffn_low = lax.optimization_barrier((both, matrix_low[layer, :, output_end:]))
        in_ws.append(both[:, :in_width])
        out_ws.append(both[:, in_width:])
        ffn_ws.append(lax.all_gather(ffn_low, everyone, axis=0, tiled=True))
    hidden = inputs.astype(jnp.float32).reshape(tokens, width)
    kept = []
    for layer in range(LAYERS):
        in_w, out_w, ffn_w = (in_ws[layer], out_ws[layer], ffn_ws[layer])
        gains = in_w[:, value_end + router_cols : value_end + router_cols + 4].astype(jnp.float32)
        normed_one, inverse_one = layer_stats(hidden)
        first_in = (normed_one * gains[:, 0] + gains[:, 1]).astype(jnp.bfloat16)
        entered = jnp.dot(first_in, in_w, preferred_element_type=jnp.float32)
        chosen_here = chosen[layer].reshape(tokens, router_cols)
        mixed, attended, *saved = attention_forward(
            entered,
            chosen_here,
            turn_cos,
            turn_sin,
            lengths,
            chunk_whole(out_width),
            3 + layer,
        )
        residual = hidden + contract_last(mixed[:, :out_width], out_w)
        normed_two, inverse_two = layer_stats(residual)
        second_in = (normed_two * gains[:, 2] + gains[:, 3]).astype(jnp.bfloat16)
        up = jnp.dot(second_in, ffn_w[:, :FF], preferred_element_type=jnp.float32)
        act = gelu_tanh(up).astype(jnp.bfloat16)
        hidden = residual + contract_last(act, ffn_w[:, FF:])
        kept.append(
            (
                normed_one,
                inverse_one,
                first_in,
                entered,
                chosen_here,
                mixed,
                attended,
                saved,
                normed_two,
                inverse_two,
                second_in,
                up,
                act,
            )
        )
    output = hidden.reshape(seq_count, sub_rows, width).astype(jnp.bfloat16)
    grad_hidden = (cotangent.astype(jnp.float32) * valid[:, :, None]).reshape(tokens, width)
    pairs, extras = ([], [])
    for layer in reversed(range(LAYERS)):
        (
            normed_one,
            inverse_one,
            first_in,
            entered,
            chosen_here,
            mixed,
            attended,
            saved,
            normed_two,
            inverse_two,
            second_in,
            up,
            act,
        ) = kept[layer]
        in_w, out_w, ffn_w = (in_ws[layer], out_ws[layer], ffn_ws[layer])
        gains = in_w[:, value_end + router_cols : value_end + router_cols + 4].astype(jnp.float32)
        grad_low = grad_hidden.astype(jnp.bfloat16)
        grad_act = jnp.dot(grad_low, ffn_w[:, FF:], preferred_element_type=jnp.float32)
        gelu_value, gelu_pull = jax.vjp(gelu_tanh, up)
        grad_up = gelu_pull(grad_act)[0].astype(jnp.bfloat16)
        grad_second = contract_last(grad_up, ffn_w[:, :FF])
        gain_two_grad = jnp.sum(grad_second * normed_two, axis=0)
        bias_two_grad = jnp.sum(grad_second, axis=0)
        grad_residual = grad_hidden + norm_back(grad_second, normed_two, inverse_two, gains[:, 2])
        residual_low = grad_residual.astype(jnp.bfloat16)
        grad_in = attention_backward(
            jnp.dot(residual_low, out_w, preferred_element_type=jnp.float32),
            attended,
            entered,
            chosen_here,
            turn_cos,
            turn_sin,
            lengths,
            saved,
            chunk_whole(in_width),
            3 + LAYERS + layer,
        )
        grad_first = contract_last(grad_in[:, :in_width], in_w)
        gain_one_grad = jnp.sum(grad_first * normed_one, axis=0)
        bias_one_grad = jnp.sum(grad_first, axis=0)
        grad_hidden = grad_residual + norm_back(grad_first, normed_one, inverse_one, gains[:, 0])
        norm_grads = jnp.stack(
            [gain_one_grad, bias_one_grad, gain_two_grad, bias_two_grad], axis=1
        ).astype(jnp.bfloat16)
        at = value_end + router_cols
        near = at // 128 * 128
        norm_grads = jnp.pad(norm_grads, ((0, 0), (at - near, 128 - 4 - (at - near))))
        pairs += [
            (first_in, grad_in),
            (residual_low, mixed),
            (second_in, grad_up),
            (grad_low, act),
        ]
        extras.append((norm_grads, near))
    reduced = reduce_weight_grads(pairs, extras, CHUNK)
    matrix_rows = [None] * LAYERS
    small_rows = [None] * LAYERS
    start = 0
    for slot, layer in enumerate(reversed(range(LAYERS))):
        widths = [right.shape[1] for _, right in pairs[4 * slot : 4 * slot + 4]]
        begins = [start + sum(widths[:group_index]) for group_index in range(4)]
        start += sum(widths)
        shares = [
            reduced[:, begin : begin + used]
            for begin, used in zip(
                begins, (value_end, output_end - value_end, FF, FF)
            )
        ]
        matrix_rows[layer] = jnp.concatenate(shares, axis=1)
        small_rows[layer] = reduced[
            :, begins[0] + value_end : begins[0] + value_end + router_cols + 4
        ]
    input_grad = grad_hidden.reshape(seq_count, sub_rows, width).astype(jnp.bfloat16)
    matrix_grad = jnp.stack(matrix_rows, axis=0)
    small_grad = jnp.stack(small_rows, axis=0)
    matrix_new, matrix_first_new, matrix_second_new = adam_update(
        matrix, matrix_grad, matrix_first, matrix_second, column_rates(segment), WEIGHT_DECAY
    )
    small_new, small_first_new, small_second_new = adam_update(
        small, small_grad, small_first, small_second, small_rates(), 0.0
    )
    return (
        output,
        input_grad,
        matrix_grad,
        matrix_new,
        matrix_new.astype(jnp.bfloat16),
        matrix_first_new,
        matrix_second_new,
        small_grad,
        small_new,
        small_new.astype(jnp.bfloat16),
        small_first_new,
        small_second_new,
        loads,
    )


def solution(mesh):
    in_specs = (
        P("dp", ("seq", "head"), None),
        P("dp", ("seq", "head"), None),
        P(None, "dp", ("seq", "head"), None, None, None),
        P("dp"),
        P(None, ("dp", "seq", "head"), None),
        P(None, ("dp", "seq", "head"), None),
        P(None, ("dp", "seq", "head"), None),
        P(None, ("dp", "seq", "head"), None),
        P(None, ("dp", "seq", "head"), None),
        P(None, ("dp", "seq", "head"), None),
    )
    out_specs = (
        P("dp", ("seq", "head"), None),
        P("dp", ("seq", "head"), None),
        P(None, ("dp", "seq", "head"), None),
        P(None, ("dp", "seq", "head"), None),
        P(None, ("dp", "seq", "head"), None),
        P(None, ("dp", "seq", "head"), None),
        P(None, ("dp", "seq", "head"), None),
        P(None, ("dp", "seq", "head"), None),
        P(None, ("dp", "seq", "head"), None),
        P(None, ("dp", "seq", "head"), None),
        P(None, ("dp", "seq", "head"), None),
        P(None, ("dp", "seq", "head"), None),
        P(),
    )
    return jax.shard_map(local, mesh=mesh, in_specs=in_specs, out_specs=out_specs, check_vma=False)
```

```python
import math

import jax
import jax.numpy as jnp
from jax import lax
from jax.experimental import pallas as pl
from jax.experimental.pallas import tpu as pltpu
from jax.sharding import PartitionSpec as P

D = 1024
HEADS = 4
HEAD_DIM = 112
EXPERTS = 5
FF = 4096
LAYERS = 2
STEP = 10


NORM_EPS = 1e-05
BETA_ONE = 0.9
BETA_TWO = 0.95
ADAM_EPS = 1e-08
WEIGHT_DECAY = 0.1
NORM_RATE = 0.5
MASKED = -1e30
CHUNK = 512


def column_bounds():
    query_end = 2 * HEADS * HEAD_DIM
    value_end = query_end + HEADS * EXPERTS * HEAD_DIM
    output_end = value_end + HEADS * EXPERTS * HEAD_DIM
    return (query_end, value_end, output_end, output_end + FF)


def column_rates(segment):
    query_end, value_end, output_end, up_end = column_bounds()
    column = jnp.arange(up_end + FF)
    inner = D ** (-0.5)
    outer = 0.7 * math.sqrt(segment) / HEAD_DIM
    rates = jnp.where(
        column < value_end,
        inner,
        jnp.where(column < output_end, outer, jnp.where(column < up_end, inner, FF ** (-0.5))),
    )
    return rates.astype(jnp.float32)


def small_rates():
    column = jnp.arange(2 * HEADS * EXPERTS + 4)
    return jnp.where(column < 2 * HEADS * EXPERTS, 0.7 * D ** (-0.5), NORM_RATE).astype(jnp.float32)


def adam_update(weight, grad, first, second, rates, decay):
    first_new = BETA_ONE * first + (1.0 - BETA_ONE) * grad
    second_new = BETA_TWO * second + (1.0 - BETA_TWO) * grad * grad
    first_hat = first_new / (1.0 - BETA_ONE**STEP)
    second_hat = second_new / (1.0 - BETA_TWO**STEP)
    new = weight - rates * (first_hat / (jnp.sqrt(second_hat) + ADAM_EPS) + decay * weight)
    return (new, first_new, second_new)


def rotary_tables(positions):
    half = HEAD_DIM // 2
    inverse = jnp.exp(-math.log(10000.0) * jnp.arange(half, dtype=jnp.float32) / half)
    angle = positions.astype(jnp.float32)[:, None] * inverse[None, :]
    return (jnp.cos(angle), jnp.sin(angle))


def layer_stats(values):
    mean = jnp.mean(values, axis=-1, keepdims=True)
    centered = values - mean
    variance = jnp.mean(centered * centered, axis=-1, keepdims=True)
    inverse = lax.rsqrt(variance + NORM_EPS)
    return (centered * inverse, inverse)


def norm_back(grad_normed, normed, inverse, gain):
    scaled = grad_normed * gain
    return inverse * (
        scaled
        - jnp.mean(scaled, axis=-1, keepdims=True)
        - normed * jnp.mean(scaled * normed, axis=-1, keepdims=True)
    )


def contract_last(left, right):
    return lax.dot_general(
        left, right, (((1,), (1,)), ((), ())), preferred_element_type=jnp.float32
    )


def contract_first(left, right):
    return lax.dot_general(
        left, right, (((0,), (0,)), ((), ())), preferred_element_type=jnp.float32
    )


AXES = ("dp", "seq", "head")


def mesh_bits():
    dims = [
        (axis, bit)
        for axis in AXES
        for bit in reversed(range(lax.axis_size(axis).bit_length() - 1))
    ]
    groups = [[index for index, (axis, _) in enumerate(dims) if axis == name] for name in AXES]
    return (dims, *groups)


def my_bits(dims):
    place = {axis: lax.axis_index(axis) for axis in AXES}
    bits = [lax.rem(place[axis] // (1 << bit), 2) for axis, bit in dims]
    partners = [
        {axis: place[axis] + (1 << bit) * (1 - 2 * bits[index])}
        for index, (axis, bit) in enumerate(dims)
    ]
    return (bits, partners)


def greet(partners):
    barrier = pltpu.get_barrier_semaphore()
    for partner in partners:
        pl.semaphore_signal(
            barrier, inc=1, device_id=partner, device_id_type=pl.DeviceIdType.MESH
        )
    pl.semaphore_wait(barrier, len(partners))


def gather_rows(share, counts, unit, name):
    dims, dp_dims, seq_dims, head_dims = mesh_bits()
    orders = (
        head_dims + dp_dims[::-1] + seq_dims,
        head_dims + dp_dims + seq_dims,
        dp_dims + head_dims + seq_dims,
    )
    depth = len(dims)
    rows, width = share.shape
    units = width // unit
    near = (3 * units + 4) // 8
    pieces, start = ([], 0)
    for which, count in ((0, near), (1, near), (2, units - 2 * near)):
        pieces.append((start, count, which))
        start += count * unit
    lag, slots = (2, 4)
    ring = (depth + 1) * lag + 6
    steps = max(count for _, count, _ in pieces) + lag * depth

    def kernel(*refs):
        share_ref, counts_ref, out_ref, counts_out = refs[:4]
        send_sem, recv_sem, load_sem, store_sem, small_send, small_recv, small_load = refs[4:11]
        buffers = refs[11:]
        bits, partners = my_bits(dims)

        def at_stage(which, stage):
            done = orders[which][:stage]
            return tuple(slice(None) if dim in done else bits[dim] for dim in range(depth))

        def columns(number, chunk):
            return pl.ds(pl.multiple_of(pieces[number][0] + chunk * unit, 128), unit)

        def exchange(number, stage, chunk):
            which = pieces[number][2]
            view = buffers[number].at[(lax.rem(chunk, ring),) + at_stage(which, stage)]
            slot = lax.rem(chunk, slots)
            return sent_to(
                view,
                view,
                send_sem.at[number, stage, slot],
                recv_sem.at[number, stage, slot],
                partners[orders[which][stage]],
            )

        def load(number, chunk):
            return pltpu.make_async_copy(
                share_ref.at[:, columns(number, chunk)],
                buffers[number].at[(lax.rem(chunk, ring),) + tuple(bits)],
                load_sem.at[number, lax.rem(chunk, slots)],
            )

        def store(number, chunk):
            return pltpu.make_async_copy(
                buffers[number].at[lax.rem(chunk, ring)],
                out_ref.at[(slice(None),) * (depth + 1) + (columns(number, chunk),)],
                store_sem.at[number, lax.rem(chunk, slots)],
            )

        def small(stage):
            view = counts_out.at[at_stage(0, stage)]
            return sent_to(
                view, view, small_send.at[stage], small_recv.at[stage], partners[orders[0][stage]]
            )

        own_counts = pltpu.make_async_copy(counts_ref, counts_out.at[tuple(bits)], small_load)
        own_counts.start()
        for number in range(len(pieces)):
            for chunk in range(2):
                load(number, jnp.int32(chunk)).start()
        greet(partners)
        own_counts.wait()

        def body(step, carry):
            for stage in range(depth, -1, -1):
                chunk = step - lag * stage
                for number, piece in enumerate(pieces):

                    @pl.when((chunk >= 0) & (chunk < piece[1]))
                    def _(stage=stage, chunk=chunk, number=number, piece=piece):
                        if stage > 0:
                            exchange(number, stage - 1, chunk).wait()
                        else:
                            load(number, chunk).wait()

                            @pl.when(chunk + 2 < piece[1])
                            def _():
                                load(number, chunk + 2).start()

                        if stage < depth:
                            exchange(number, stage, chunk).start()
                        else:

                            @pl.when(chunk >= slots)
                            def _():
                                store(number, chunk - slots).wait()

                            store(number, chunk).start()

                @pl.when(chunk == 0)
                def _(stage=stage):
                    if stage > 0:
                        small(stage - 1).wait()
                    if stage < depth:
                        small(stage).start()

            return carry

        lax.fori_loop(0, steps, body, 0)
        for number, piece in enumerate(pieces):
            for back in range(min(slots, piece[1])):
                store(number, jnp.int32(piece[1] - 1 - back)).wait()

    in_place = pl.BlockSpec(memory_space=pl.ANY)
    semaphores = pltpu.SemaphoreType.DMA((len(pieces), depth, slots))
    local = pltpu.SemaphoreType.DMA((len(pieces), slots))
    gathered, all_counts = pl.pallas_call(
        kernel,
        in_specs=[in_place] * 2,
        out_specs=[in_place] * 2,
        out_shape=[
            jax.ShapeDtypeStruct((2,) * depth + value.shape, value.dtype)
            for value in (share, counts)
        ],
        scratch_shapes=[
            semaphores,
            semaphores,
            local,
            local,
            pltpu.SemaphoreType.DMA((depth,)),
            pltpu.SemaphoreType.DMA((depth,)),
            pltpu.SemaphoreType.DMA,
        ]
        + [pltpu.VMEM((ring,) + (2,) * depth + (rows, unit), share.dtype) for _ in pieces],
        compiler_params=pltpu.CompilerParams(
            collective_id=name, has_side_effects=True, vmem_limit_bytes=48 << 20
        ),
    )(share, counts)
    return (gathered.reshape(-1, width), all_counts.reshape(-1, counts.shape[1]))


def halving_plan(width):
    dims, dp_dims, seq_dims, head_dims = mesh_bits()
    first = seq_dims[::-1]
    orders = (
        (0, width // 2, first + dp_dims[::-1] + head_dims[::-1]),
        (width // 2, width // 4, first + dp_dims + head_dims[::-1]),
        (3 * width // 4, width // 4, first + head_dims[::-1] + dp_dims[::-1]),
    )
    stages = []
    for stage in range(len(dims)):
        parts = []
        for start, count, order in orders:
            left = [dim for dim in range(len(dims)) if dim not in order[:stage]]
            if parts and parts[-1][2:] == (order[stage], left):
                parts[-1] = (parts[-1][0], parts[-1][1] + count, order[stage], left)
            else:
                parts.append((start, count, order[stage], left))
        stages.append(parts)
    lags = [1 if stage < len(seq_dims) else 2 for stage in range(len(dims))]
    return dims, stages, lags


def reduce_weight_grads(pairs, extras, width):
    dims, stages, lags = halving_plan(width)
    depth = len(dims)
    tokens, model = pairs[0][0].shape
    rows = model >> depth
    firsts = [0]
    for left, right in pairs:
        firsts.append(firsts[-1] + right.shape[1] // width)
    chunks = firsts[-1]
    per_layer = len(pairs) // len(extras)
    spots = [
        (firsts[per_layer * index] + near // width, near % width)
        for index, (_, near) in enumerate(extras)
    ]
    starts = [sum(lags[:stage]) for stage in range(depth + 1)]
    count_pairs, count_extras = (len(pairs), len(extras))

    def kernel(*refs):
        lefts = refs[:count_pairs]
        rights = refs[count_pairs : 2 * count_pairs]
        added = refs[2 * count_pairs : 2 * count_pairs + count_extras]
        rest = refs[2 * count_pairs + count_extras :]
        out_ref, left_buf, turned, right_buf, load_sem = rest[:5]
        pool = iter(rest[5:])
        buffers = [[tuple(next(pool) for _ in range(4)) for _ in parts] for parts in stages]
        step = pl.program_id(0)
        bits, partners = my_bits(dims)

        def exchange(stage, part, slot):
            start, count, dim, left = stages[stage][part]
            own, got, send_sem, recv_sem = buffers[stage][part]
            lead = (slot,) + (slice(None),) * left.index(dim)
            return pltpu.make_async_remote_copy(
                src_ref=own.at[lead + (1 - bits[dim],)],
                dst_ref=got.at[slot],
                send_sem=send_sem.at[slot],
                recv_sem=recv_sem.at[slot],
                device_id=partners[dim],
                device_id_type=pl.DeviceIdType.MESH,
            )

        def load_left(index):
            return pltpu.make_async_copy(lefts[index], left_buf, load_sem.at[2])

        def load_right(index, chunk):
            slot = lax.rem(chunk, 2)
            columns = pl.ds(pl.multiple_of((chunk - firsts[index]) * width, width), width)
            return pltpu.make_async_copy(
                rights[index].at[:, columns], right_buf.at[slot], load_sem.at[slot]
            )

        def prefetch(chunk):
            for index in range(count_pairs):

                @pl.when((chunk >= firsts[index]) & (chunk < firsts[index + 1]))
                def _(index=index):
                    load_right(index, chunk).start()

                @pl.when(chunk == firsts[index])
                def _(index=index):
                    load_left(index).start()

        @pl.when(step == 0)
        def _():
            prefetch(step)
            greet(partners)

        @pl.when(step + 1 < chunks)
        def _():
            prefetch(step + 1)

        for stage in range(depth, -1, -1):
            chunk = step - starts[stage]

            @pl.when((chunk >= 0) & (chunk < chunks))
            def _(stage=stage, chunk=chunk):
                if stage == 0:
                    for first in firsts[:-1]:

                        @pl.when(chunk == first)
                        def _():
                            load_left(0).wait()
                            turned[...] = left_buf[...].T

                    load_right(0, lax.rem(chunk, 2)).wait()
                    product = jnp.dot(
                        turned[...],
                        right_buf[lax.rem(chunk, 2)],
                        preferred_element_type=jnp.float32,
                    )
                    slot = lax.rem(chunk, 2 * lags[0])
                    for part, (start, count, dim, left) in enumerate(stages[0]):
                        piece = product[:, start : start + count].astype(jnp.bfloat16)
                        buffers[0][part][0][slot] = piece.reshape((2,) * depth + (rows, count))
                    for index in range(count_extras):

                        @pl.when(chunk == spots[index][0])
                        def _(index=index):
                            at = (slot, Ellipsis, slice(spots[index][1], spots[index][1] + 128))
                            own = buffers[0][0][0]
                            total = own[at].astype(jnp.float32) + added[index][...].astype(
                                jnp.float32
                            )
                            own[at] = total.astype(jnp.bfloat16)

                else:
                    back = lax.rem(chunk, 2 * lags[stage - 1])
                    for part, (start, count, dim, left) in enumerate(stages[stage - 1]):
                        exchange(stage - 1, part, back).wait()
                        own, got = buffers[stage - 1][part][:2]
                        lead = (back,) + (slice(None),) * left.index(dim)
                        total = own[lead + (bits[dim],)].astype(jnp.float32) + got[back].astype(
                            jnp.float32
                        )
                        if stage == depth:
                            out_ref[:, start : start + count] = total
                            continue
                        slot = lax.rem(chunk, 2 * lags[stage])
                        low = total.astype(jnp.bfloat16)
                        for other, (begin, length, _, kept) in enumerate(stages[stage]):
                            lo, hi = max(start, begin), min(start + count, begin + length)
                            if lo < hi:
                                at = (slot,) + (slice(None),) * (len(kept) + 1)
                                buffers[stage][other][0][at + (slice(lo - begin, hi - begin),)] = (
                                    low[..., lo - start : hi - start]
                                )
                if stage < depth:
                    for part in range(len(stages[stage])):
                        exchange(stage, part, lax.rem(chunk, 2 * lags[stage])).start()

    scratch = [
        pltpu.VMEM((tokens, model), jnp.bfloat16),
        pltpu.VMEM((model, tokens), jnp.bfloat16),
        pltpu.VMEM((2, tokens, width), jnp.bfloat16),
        pltpu.SemaphoreType.DMA((3,)),
    ]
    for stage, parts in enumerate(stages):
        slots = 2 * lags[stage]
        for start, count, dim, left in parts:
            scratch += [
                pltpu.VMEM((slots,) + (2,) * len(left) + (rows, count), jnp.bfloat16),
                pltpu.VMEM((slots,) + (2,) * (len(left) - 1) + (rows, count), jnp.bfloat16),
                pltpu.SemaphoreType.DMA((slots,)),
                pltpu.SemaphoreType.DMA((slots,)),
            ]
    in_place = pl.BlockSpec(memory_space=pl.ANY)
    whole = [value.reshape((2,) * depth + (rows, 128)) for value, _ in extras]
    return pl.pallas_call(
        kernel,
        grid=(chunks + starts[depth],),
        in_specs=[in_place] * (2 * count_pairs)
        + [pl.BlockSpec(value.shape, lambda step: (0,) * (depth + 2)) for value in whole],
        out_specs=pl.BlockSpec(
            (rows, width), lambda step: (0, jnp.clip(step - starts[depth], 0, chunks - 1))
        ),
        out_shape=jax.ShapeDtypeStruct((rows, chunks * width), jnp.float32),
        scratch_shapes=scratch,
        compiler_params=pltpu.CompilerParams(
            collective_id=1,
            has_side_effects=True,
            vmem_limit_bytes=48 << 20,
            dimension_semantics=("arbitrary",),
        ),
    )(*[left for left, _ in pairs], *[right for _, right in pairs], *whole)


def lane_whole(count):
    return count + (-count) % 128


def chunk_whole(count):
    return count + (-count) % CHUNK


def padded(pieces, width):
    have = sum(piece.shape[1] for piece in pieces)
    fill = jnp.zeros((pieces[0].shape[0], width - have), pieces[0].dtype)
    return jnp.concatenate(list(pieces) + [fill], axis=1)


LANES = 128
QUERY_TILE = 256


def swap_halves(tensor):
    half = HEAD_DIM // 2
    return jnp.concatenate([tensor[:, half:], tensor[:, :half]], axis=1)


def lane_filled(tensor):
    fill = jnp.zeros((tensor.shape[0], LANES - tensor.shape[1]), tensor.dtype)
    return jnp.concatenate([tensor, fill], axis=1)


def weights_block(keys_mem, keys_own, query, start, first, segment, length):
    contract = (((1,), (1,)), ((), ()))
    raw = jnp.concatenate(
        [
            lax.dot_general(keys, query, contract, preferred_element_type=jnp.float32)
            for keys in (keys_mem, keys_own)
        ],
        axis=0,
    )
    key_pos = start - segment + lax.broadcasted_iota(jnp.int32, raw.shape, 0)
    query_pos = start + first + lax.broadcasted_iota(jnp.int32, raw.shape, 1)
    used = (key_pos < length) & (key_pos < query_pos) & (key_pos >= 0)
    allowed = used | (key_pos == query_pos)
    scores = jnp.where(allowed, raw * HEAD_DIM ** (-0.5), MASKED)
    weights = jnp.exp(scores - jnp.max(scores, axis=0, keepdims=True))
    return weights * (1.0 / jnp.sum(weights, axis=0, keepdims=True))


def contract_rows(left, right):
    return lax.dot_general(
        left, right, (((0,), (0,)), ((), ())), preferred_element_type=jnp.float32
    )


def across(axis, offset):
    size = lax.axis_size(axis)
    return {axis: lax.rem(lax.axis_index(axis) + offset + size, size)}


def sent_to(source, target, send_sem, recv_sem, device):
    return pltpu.make_async_remote_copy(
        src_ref=source,
        dst_ref=target,
        send_sem=send_sem,
        recv_sem=recv_sem,
        device_id=device,
        device_id_type=pl.DeviceIdType.MESH,
    )


def meet(memory_step):
    barrier = pltpu.get_barrier_semaphore()
    heads = lax.axis_size("head")
    writers = [across("head", step) for step in range(1, heads)]
    writers.append(across("seq", -memory_step))
    for device in writers:
        pl.semaphore_signal(barrier, inc=1, device_id=device, device_id_type=pl.DeviceIdType.MESH)
    pl.semaphore_wait(barrier, len(writers))


def gate_values(entered_ref, chosen_ref, rows):
    at = column_bounds()[1]
    logits = entered_ref[rows, at : at + 2 * HEADS * EXPERTS]
    prob = 1.0 / (1.0 + jnp.exp(-logits))
    return (prob, prob * chosen_ref[rows, :])


def column(tensor, index):
    return tensor[:, index : index + 1]


def attention_forward(entered, chosen, turn_cos, turn_sin, lengths, mixed_width, name):
    seq_count = lengths.shape[0]
    tokens = entered.shape[0]
    sub = tokens // seq_count
    heads = lax.axis_size("head")
    segment = heads * sub
    query_end = column_bounds()[0]
    sides = range(1, heads)

    def kernel(*refs):
        length_ref, entered_ref, chosen_ref, cos_ref, sin_ref = refs[:5]
        mixed_ref, attended_ref, query_ref, key_ref, value_ref = refs[5:10]
        out_buf, heads_buf, mem_buf, done_buf, back_buf = refs[10:15]
        out_sem, in_sem, mem_sem, done_sem, back_sem = refs[15:]
        me = lax.axis_index("head")
        start = lax.axis_index("seq") * segment
        turn, wind = (cos_ref[...], sin_ref[...])

        def outward(b, side):
            there = across("head", side)
            return sent_to(
                out_buf.at[b, there["head"]],
                heads_buf.at[b, :, me],
                out_sem.at[b, side - 1],
                in_sem.at[b, side - 1],
                there,
            )

        def onward(b):
            return sent_to(
                heads_buf.at[b, 1:3],
                mem_buf.at[b],
                mem_sem.at[0, b],
                mem_sem.at[1, b],
                across("seq", 1),
            )

        def homeward(b, side):
            there = across("head", side)
            return sent_to(
                done_buf.at[b, there["head"]],
                back_buf.at[b, me],
                done_sem.at[b, side - 1],
                back_sem.at[b, side - 1],
                there,
            )

        meet(1)
        gates_of = []
        for b in range(seq_count):
            rows = slice(b * sub, (b + 1) * sub)
            gates = gate_values(entered_ref, chosen_ref, rows)[1]
            gates_of.append(gates)
            for head in range(HEADS):
                for kind in range(2):
                    at = (kind * HEADS + head) * HEAD_DIM
                    vector = entered_ref[rows, at : at + HEAD_DIM]
                    turned = vector * turn + swap_halves(vector) * wind
                    out_buf[b, head, kind] = lane_filled(turned).astype(jnp.bfloat16)
                value = jnp.zeros((sub, HEAD_DIM), jnp.float32)
                for expert in range(EXPERTS):
                    index = head * EXPERTS + expert
                    at = query_end + index * HEAD_DIM
                    value += column(gates, index) * entered_ref[rows, at : at + HEAD_DIM]
                out_buf[b, head, 2] = lane_filled(value).astype(jnp.bfloat16)
            for side in sides:
                outward(b, side).start()
            for kind in range(3):
                heads_buf[b, kind, me] = out_buf[b, me, kind]
        for b in range(seq_count):
            for side in sides:
                outward(b, side).wait_recv()
            onward(b).start()
        for b in range(seq_count):
            onward(b).wait_recv()
            keys_own = heads_buf[b, 1].reshape(segment, LANES)
            values = jnp.concatenate(
                [mem_buf[b, 1].reshape(segment, LANES), heads_buf[b, 2].reshape(segment, LANES)],
                axis=0,
            )
            for first in range(0, segment, QUERY_TILE):
                tile = slice(first // sub, (first + QUERY_TILE) // sub)
                query = heads_buf[b, 0, tile].reshape(QUERY_TILE, LANES)
                probs = weights_block(
                    mem_buf[b, 0].reshape(segment, LANES),
                    keys_own,
                    query,
                    start,
                    first,
                    segment,
                    length_ref[b],
                ).astype(jnp.bfloat16)
                attended = contract_rows(values, probs).T.astype(jnp.bfloat16)
                done_buf[b, tile] = attended.reshape(QUERY_TILE // sub, sub, LANES)
            for side in sides:
                homeward(b, side).start()
            back_buf[b, me] = done_buf[b, me]
        for b in range(seq_count):
            query_ref[b] = heads_buf[b, 0]
            key_ref[b, 0] = mem_buf[b, 0]
            key_ref[b, 1] = heads_buf[b, 1]
            value_ref[b, 0] = mem_buf[b, 1]
            value_ref[b, 1] = heads_buf[b, 2]
        used = HEADS * EXPERTS * HEAD_DIM
        mixed_ref[:, used:] = jnp.zeros((tokens, mixed_width - used), jnp.bfloat16)
        for b in range(seq_count):
            rows = slice(b * sub, (b + 1) * sub)
            for side in sides:
                homeward(b, side).wait_recv()
            for head in range(HEADS):
                attended = back_buf[b, head]
                attended_ref[rows, head * LANES : (head + 1) * LANES] = attended
                wide = attended.astype(jnp.float32)[:, :HEAD_DIM]
                for expert in range(EXPERTS):
                    index = head * EXPERTS + expert
                    gate = column(gates_of[b], HEADS * EXPERTS + index)
                    mixed_ref[rows, index * HEAD_DIM : (index + 1) * HEAD_DIM] = (
                        gate * wide
                    ).astype(jnp.bfloat16)
        for b in range(seq_count):
            onward(b).wait_send()
            for side in sides:
                outward(b, side).wait_send()
                homeward(b, side).wait_send()

    def shape(*dims):
        return jax.ShapeDtypeStruct(dims, jnp.bfloat16)

    vmem = pl.BlockSpec(memory_space=pltpu.VMEM)
    paired = pltpu.SemaphoreType.DMA((seq_count, heads - 1))
    return pl.pallas_call(
        kernel,
        in_specs=[pl.BlockSpec(memory_space=pltpu.SMEM)] + [vmem] * 4,
        out_specs=[vmem] * 5,
        out_shape=[
            shape(tokens, mixed_width),
            shape(tokens, HEADS * LANES),
            shape(seq_count, heads, sub, LANES),
            shape(seq_count, 2, heads, sub, LANES),
            shape(seq_count, 2, heads, sub, LANES),
        ],
        scratch_shapes=[
            pltpu.VMEM((seq_count, heads, 3, sub, LANES), jnp.bfloat16),
            pltpu.VMEM((seq_count, 3, heads, sub, LANES), jnp.bfloat16),
            pltpu.VMEM((seq_count, 2, heads, sub, LANES), jnp.bfloat16),
            pltpu.VMEM((seq_count, heads, sub, LANES), jnp.bfloat16),
            pltpu.VMEM((seq_count, heads, sub, LANES), jnp.bfloat16),
            paired,
            paired,
            pltpu.SemaphoreType.DMA((2, seq_count)),
            paired,
            paired,
        ],
        compiler_params=pltpu.CompilerParams(
            collective_id=name, has_side_effects=True, vmem_limit_bytes=40 << 20
        ),
    )(lengths, entered, chosen, turn_cos, turn_sin)


def attention_backward(
    grad_mixed, attended, entered, chosen, turn_cos, turn_sin, lengths, saved, grad_width, name
):
    query, keys, values = saved
    seq_count = lengths.shape[0]
    tokens = entered.shape[0]
    sub = tokens // seq_count
    heads = lax.axis_size("head")
    segment = heads * sub
    query_end, value_end = column_bounds()[:2]
    router_cols = 2 * HEADS * EXPERTS
    sides = range(1, heads)

    def kernel(*refs):
        length_ref, grad_ref, attended_ref, entered_ref, chosen_ref, cos_ref, sin_ref = refs[:7]
        query_ref, key_ref, value_ref, result_ref = refs[7:11]
        out_buf, heads_buf, mem_out, mem_in, own_buf, done_buf, back_buf = refs[11:18]
        out_sem, in_sem, mem_sem, done_sem, back_sem = refs[18:]
        me = lax.axis_index("head")
        start = lax.axis_index("seq") * segment
        turn, wind = (cos_ref[...], sin_ref[...])

        def outward(b, side):
            there = across("head", side)
            return sent_to(
                out_buf.at[b, there["head"]],
                heads_buf.at[b, me],
                out_sem.at[b, side - 1],
                in_sem.at[b, side - 1],
                there,
            )

        def onward(b):
            return sent_to(
                mem_out.at[b], mem_in.at[b], mem_sem.at[0, b], mem_sem.at[1, b], across("seq", -1)
            )

        def homeward(b, side):
            there = across("head", side)
            return sent_to(
                done_buf.at[b, there["head"]],
                back_buf.at[b, me],
                done_sem.at[b, side - 1],
                back_sem.at[b, side - 1],
                there,
            )

        meet(-1)
        lane = lax.broadcasted_iota(jnp.int32, (sub, router_cols), 1)
        gate_grads, probs_of, gates_of = ([], [], [])
        for b in range(seq_count):
            rows = slice(b * sub, (b + 1) * sub)
            prob, gates = gate_values(entered_ref, chosen_ref, rows)
            probs_of.append(prob)
            gates_of.append(gates)
            gate_grad = jnp.zeros((sub, router_cols), jnp.float32)
            for head in range(HEADS):
                seen = attended_ref[rows, head * LANES : head * LANES + HEAD_DIM].astype(
                    jnp.float32
                )
                total = jnp.zeros((sub, HEAD_DIM), jnp.float32)
                for expert in range(EXPERTS):
                    index = head * EXPERTS + expert
                    part = grad_ref[rows, index * HEAD_DIM : (index + 1) * HEAD_DIM]
                    total += column(gates, HEADS * EXPERTS + index) * part
                    gate_grad = jnp.where(
                        lane == HEADS * EXPERTS + index,
                        jnp.sum(part * seen, axis=1, keepdims=True),
                        gate_grad,
                    )
                out_buf[b, head] = lane_filled(total).astype(jnp.bfloat16)
            gate_grads.append(gate_grad)
            for side in sides:
                outward(b, side).start()
            heads_buf[b, me] = out_buf[b, me]
        for b in range(seq_count):
            for side in sides:
                outward(b, side).wait_recv()
            keys_mem = key_ref[b, 0].reshape(segment, LANES)
            keys_own = key_ref[b, 1].reshape(segment, LANES)
            keys_all = jnp.concatenate([keys_mem, keys_own], axis=0)
            values_all = jnp.concatenate(
                [value_ref[b, 0].reshape(segment, LANES), value_ref[b, 1].reshape(segment, LANES)],
                axis=0,
            )
            grad_keys = jnp.zeros((2 * segment, LANES), jnp.float32)
            grad_values = jnp.zeros((2 * segment, LANES), jnp.float32)
            for first in range(0, segment, QUERY_TILE):
                tile = slice(first // sub, (first + QUERY_TILE) // sub)
                here = query_ref[b, tile].reshape(QUERY_TILE, LANES)
                arrived = heads_buf[b, tile].reshape(QUERY_TILE, LANES)
                probs = weights_block(
                    keys_mem, keys_own, here, start, first, segment, length_ref[b]
                )
                grad_probs = contract_last(values_all, arrived)
                delta = jnp.sum(probs * grad_probs, axis=0, keepdims=True)
                grad_raw = (probs * (grad_probs - delta) * HEAD_DIM ** (-0.5)).astype(
                    jnp.bfloat16
                )
                grad_values += jnp.dot(
                    probs.astype(jnp.bfloat16), arrived, preferred_element_type=jnp.float32
                )
                grad_keys += jnp.dot(grad_raw, here, preferred_element_type=jnp.float32)
                grad_query = contract_rows(keys_all, grad_raw).T.astype(jnp.bfloat16)
                done_buf[b, tile, 0] = grad_query.reshape(QUERY_TILE // sub, sub, LANES)
            for kind, grads in enumerate((grad_keys, grad_values)):
                mem_out[b, kind] = grads[:segment].astype(jnp.bfloat16)
                own_buf[b, kind] = grads[segment:]
            onward(b).start()
        for b in range(seq_count):
            onward(b).wait_recv()
            for kind in range(2):
                total = own_buf[b, kind] + mem_in[b, kind].astype(jnp.float32)
                done_buf[b, :, kind + 1] = total.astype(jnp.bfloat16).reshape(heads, sub, LANES)
            for side in sides:
                homeward(b, side).start()
            back_buf[b, me] = done_buf[b, me]
        used = value_end + router_cols
        result_ref[:, used:] = jnp.zeros((tokens, grad_width - used), jnp.bfloat16)
        for b in range(seq_count):
            rows = slice(b * sub, (b + 1) * sub)
            for side in sides:
                homeward(b, side).wait_recv()
            gate_grad = gate_grads[b]
            for head in range(HEADS):
                for kind in range(2):
                    vector = back_buf[b, head, kind].astype(jnp.float32)[:, :HEAD_DIM]
                    turned = vector * turn - swap_halves(vector) * wind
                    at = (kind * HEADS + head) * HEAD_DIM
                    result_ref[rows, at : at + HEAD_DIM] = turned.astype(jnp.bfloat16)
                grad_value = back_buf[b, head, 2].astype(jnp.float32)[:, :HEAD_DIM]
                for expert in range(EXPERTS):
                    index = head * EXPERTS + expert
                    at = query_end + index * HEAD_DIM
                    gate_grad = jnp.where(
                        lane == index,
                        jnp.sum(
                            entered_ref[rows, at : at + HEAD_DIM] * grad_value,
                            axis=1,
                            keepdims=True,
                        ),
                        gate_grad,
                    )
                    result_ref[rows, at : at + HEAD_DIM] = (
                        column(gates_of[b], index) * grad_value
                    ).astype(jnp.bfloat16)
            prob = probs_of[b]
            result_ref[rows, value_end:used] = (
                gate_grad * chosen_ref[rows, :] * prob * (1.0 - prob)
            ).astype(jnp.bfloat16)
        for b in range(seq_count):
            onward(b).wait_send()
            for side in sides:
                outward(b, side).wait_send()
                homeward(b, side).wait_send()

    vmem = pl.BlockSpec(memory_space=pltpu.VMEM)
    paired = pltpu.SemaphoreType.DMA((seq_count, heads - 1))
    return pl.pallas_call(
        kernel,
        in_specs=[pl.BlockSpec(memory_space=pltpu.SMEM)] + [vmem] * 9,
        out_specs=vmem,
        out_shape=jax.ShapeDtypeStruct((tokens, grad_width), jnp.bfloat16),
        scratch_shapes=[
            pltpu.VMEM((seq_count, heads, sub, LANES), jnp.bfloat16),
            pltpu.VMEM((seq_count, heads, sub, LANES), jnp.bfloat16),
            pltpu.VMEM((seq_count, 2, segment, LANES), jnp.bfloat16),
            pltpu.VMEM((seq_count, 2, segment, LANES), jnp.bfloat16),
            pltpu.VMEM((seq_count, 2, segment, LANES), jnp.float32),
            pltpu.VMEM((seq_count, heads, 3, sub, LANES), jnp.bfloat16),
            pltpu.VMEM((seq_count, heads, 3, sub, LANES), jnp.bfloat16),
            paired,
            paired,
            pltpu.SemaphoreType.DMA((2, seq_count)),
            paired,
            paired,
        ],
        compiler_params=pltpu.CompilerParams(
            collective_id=name, has_side_effects=True, vmem_limit_bytes=48 << 20
        ),
    )(lengths, grad_mixed, attended, entered, chosen, turn_cos, turn_sin, query, keys, values)


def gelu_tanh(values):
    return jax.nn.gelu(values, approximate=True)


def local(
    inputs,
    cotangent,
    routes,
    lengths,
    matrix,
    matrix_first,
    matrix_second,
    small,
    small_first,
    small_second,
):
    head_count = lax.axis_size("head")
    seq_count, sub_rows, width = inputs.shape
    segment = sub_rows * head_count
    tokens = seq_count * sub_rows
    router_cols = 2 * HEADS * EXPERTS
    group = HEADS * EXPERTS
    query_end, value_end, output_end, up_end = column_bounds()
    seq_start = lax.axis_index("seq") * segment
    positions = (
        seq_start + lax.axis_index("head") * sub_rows + jnp.arange(sub_rows, dtype=jnp.int32)
    )
    valid = (positions[None, :] < lengths[:, None]).astype(jnp.float32)
    cosines, sines = rotary_tables(positions)
    turn_cos = jnp.concatenate([cosines, cosines], axis=1)
    turn_sin = jnp.concatenate([-sines, sines], axis=1)
    chosen = jnp.sum(
        (routes[..., None] == jnp.arange(EXPERTS, dtype=jnp.int32)).astype(jnp.float32), axis=-2
    )
    load_part = jnp.sum(chosen * valid[None, :, :, None, None, None], axis=(1, 2))
    in_width = lane_whole(value_end + router_cols + 4)
    out_width = lane_whole(output_end - value_end)
    matrix_low = matrix.astype(jnp.bfloat16)
    small_low = small.astype(jnp.bfloat16)
    in_low = [
        padded([matrix_low[layer, :, :value_end], small_low[layer]], in_width)
        for layer in range(LAYERS)
    ]
    out_low = [
        padded([matrix_low[layer, :, value_end:output_end]], out_width) for layer in range(LAYERS)
    ]
    ffn_low = [matrix_low[layer, :, output_end:] for layer in range(LAYERS)]
    size = load_part.size
    counts = jnp.pad(load_part.reshape(-1), (0, (-size) % 1024)).reshape(8, -1)
    early = []
    for layer in range(LAYERS):
        early += [in_low[layer], out_low[layer]] + ([ffn_low[layer]] if layer + 1 < LAYERS else [])
    gathered, counts = gather_rows(jnp.concatenate(early, axis=1), counts, 128, 2)
    counts, late = lax.optimization_barrier((counts, ffn_low[-1]))
    loads = jnp.sum(counts.reshape(-1, size + (-size) % 1024), axis=0)[:size].reshape(
        load_part.shape
    )
    late = lax.all_gather(late, ("dp", "seq", "head"), axis=0, tiled=True)
    pieces, start = ([], 0)
    for value in early:
        pieces.append(gathered[:, start : start + value.shape[1]])
        start += value.shape[1]
    pieces.append(late)
    in_ws, out_ws, ffn_ws = (pieces[0::3], pieces[1::3], pieces[2::3])
    hidden = inputs.astype(jnp.float32).reshape(tokens, width)
    kept = []
    for layer in range(LAYERS):
        in_w, out_w, ffn_w = (in_ws[layer], out_ws[layer], ffn_ws[layer])
        gains = in_w[:, value_end + router_cols : value_end + router_cols + 4].astype(jnp.float32)
        normed_one, inverse_one = layer_stats(hidden)
        first_in = (normed_one * gains[:, 0] + gains[:, 1]).astype(jnp.bfloat16)
        entered = jnp.dot(first_in, in_w, preferred_element_type=jnp.float32)
        chosen_here = chosen[layer].reshape(tokens, router_cols)
        mixed, attended, *saved = attention_forward(
            entered,
            chosen_here,
            turn_cos,
            turn_sin,
            lengths,
            chunk_whole(out_width),
            3 + layer,
        )
        residual = hidden + contract_last(mixed[:, :out_width], out_w)
        normed_two, inverse_two = layer_stats(residual)
        second_in = (normed_two * gains[:, 2] + gains[:, 3]).astype(jnp.bfloat16)
        up = jnp.dot(second_in, ffn_w[:, :FF], preferred_element_type=jnp.float32)
        act = gelu_tanh(up).astype(jnp.bfloat16)
        hidden = residual + contract_last(act, ffn_w[:, FF:])
        kept.append(
            (
                normed_one,
                inverse_one,
                first_in,
                entered,
                chosen_here,
                mixed,
                attended,
                saved,
                normed_two,
                inverse_two,
                second_in,
                up,
                act,
            )
        )
    output = hidden.reshape(seq_count, sub_rows, width).astype(jnp.bfloat16)
    grad_hidden = (cotangent.astype(jnp.float32) * valid[:, :, None]).reshape(tokens, width)
    pairs, extras = ([], [])
    for layer in reversed(range(LAYERS)):
        (
            normed_one,
            inverse_one,
            first_in,
            entered,
            chosen_here,
            mixed,
            attended,
            saved,
            normed_two,
            inverse_two,
            second_in,
            up,
            act,
        ) = kept[layer]
        in_w, out_w, ffn_w = (in_ws[layer], out_ws[layer], ffn_ws[layer])
        gains = in_w[:, value_end + router_cols : value_end + router_cols + 4].astype(jnp.float32)
        grad_low = grad_hidden.astype(jnp.bfloat16)
        grad_act = jnp.dot(grad_low, ffn_w[:, FF:], preferred_element_type=jnp.float32)
        gelu_value, gelu_pull = jax.vjp(gelu_tanh, up)
        grad_up = gelu_pull(grad_act)[0].astype(jnp.bfloat16)
        grad_second = contract_last(grad_up, ffn_w[:, :FF])
        gain_two_grad = jnp.sum(grad_second * normed_two, axis=0)
        bias_two_grad = jnp.sum(grad_second, axis=0)
        grad_residual = grad_hidden + norm_back(grad_second, normed_two, inverse_two, gains[:, 2])
        residual_low = grad_residual.astype(jnp.bfloat16)
        grad_in = attention_backward(
            jnp.dot(residual_low, out_w, preferred_element_type=jnp.float32),
            attended,
            entered,
            chosen_here,
            turn_cos,
            turn_sin,
            lengths,
            saved,
            chunk_whole(in_width),
            3 + LAYERS + layer,
        )
        grad_first = contract_last(grad_in[:, :in_width], in_w)
        gain_one_grad = jnp.sum(grad_first * normed_one, axis=0)
        bias_one_grad = jnp.sum(grad_first, axis=0)
        grad_hidden = grad_residual + norm_back(grad_first, normed_one, inverse_one, gains[:, 0])
        norm_grads = jnp.stack(
            [gain_one_grad, bias_one_grad, gain_two_grad, bias_two_grad], axis=1
        ).astype(jnp.bfloat16)
        at = value_end + router_cols
        near = at // 128 * 128
        norm_grads = jnp.pad(norm_grads, ((0, 0), (at - near, 128 - 4 - (at - near))))
        pairs += [
            (first_in, grad_in),
            (residual_low, mixed),
            (second_in, grad_up),
            (grad_low, act),
        ]
        extras.append((norm_grads, near))
    reduced = reduce_weight_grads(pairs, extras, CHUNK)
    matrix_rows = [None] * LAYERS
    small_rows = [None] * LAYERS
    start = 0
    for slot, layer in enumerate(reversed(range(LAYERS))):
        widths = [right.shape[1] for _, right in pairs[4 * slot : 4 * slot + 4]]
        begins = [start + sum(widths[:group_index]) for group_index in range(4)]
        start += sum(widths)
        shares = [
            reduced[:, begin : begin + used]
            for begin, used in zip(
                begins, (value_end, output_end - value_end, FF, FF)
            )
        ]
        matrix_rows[layer] = jnp.concatenate(shares, axis=1)
        small_rows[layer] = reduced[
            :, begins[0] + value_end : begins[0] + value_end + router_cols + 4
        ]
    input_grad = grad_hidden.reshape(seq_count, sub_rows, width).astype(jnp.bfloat16)
    matrix_grad = jnp.stack(matrix_rows, axis=0)
    small_grad = jnp.stack(small_rows, axis=0)
    matrix_new, matrix_first_new, matrix_second_new = adam_update(
        matrix, matrix_grad, matrix_first, matrix_second, column_rates(segment), WEIGHT_DECAY
    )
    small_new, small_first_new, small_second_new = adam_update(
        small, small_grad, small_first, small_second, small_rates(), 0.0
    )
    return (
        output,
        input_grad,
        matrix_grad,
        matrix_new,
        matrix_new.astype(jnp.bfloat16),
        matrix_first_new,
        matrix_second_new,
        small_grad,
        small_new,
        small_new.astype(jnp.bfloat16),
        small_first_new,
        small_second_new,
        loads,
    )


def solution(mesh):
    in_specs = (
        P("dp", ("seq", "head"), None),
        P("dp", ("seq", "head"), None),
        P(None, "dp", ("seq", "head"), None, None, None),
        P("dp"),
        P(None, ("dp", "seq", "head"), None),
        P(None, ("dp", "seq", "head"), None),
        P(None, ("dp", "seq", "head"), None),
        P(None, ("dp", "seq", "head"), None),
        P(None, ("dp", "seq", "head"), None),
        P(None, ("dp", "seq", "head"), None),
    )
    out_specs = (
        P("dp", ("seq", "head"), None),
        P("dp", ("seq", "head"), None),
        P(None, ("dp", "seq", "head"), None),
        P(None, ("dp", "seq", "head"), None),
        P(None, ("dp", "seq", "head"), None),
        P(None, ("dp", "seq", "head"), None),
        P(None, ("dp", "seq", "head"), None),
        P(None, ("dp", "seq", "head"), None),
        P(None, ("dp", "seq", "head"), None),
        P(None, ("dp", "seq", "head"), None),
        P(None, ("dp", "seq", "head"), None),
        P(None, ("dp", "seq", "head"), None),
        P(),
    )
    return jax.shard_map(local, mesh=mesh, in_specs=in_specs, out_specs=out_specs, check_vma=False)
```

```python
import math

import jax
import jax.numpy as jnp
from jax import lax
from jax.experimental import pallas as pl
from jax.experimental.pallas import tpu as pltpu
from jax.sharding import PartitionSpec as P

D = 1024
HEADS = 4
HEAD_DIM = 112
EXPERTS = 5
FF = 4096
LAYERS = 2
STEP = 10


NORM_EPS = 1e-05
BETA_ONE = 0.9
BETA_TWO = 0.95
ADAM_EPS = 1e-08
WEIGHT_DECAY = 0.1
NORM_RATE = 0.5
MASKED = -1e30
CHUNK = 512
NATIVE = ((LAYERS - 1, "up"), (LAYERS - 1, "down"))


def column_bounds():
    query_end = 2 * HEADS * HEAD_DIM
    value_end = query_end + HEADS * EXPERTS * HEAD_DIM
    output_end = value_end + HEADS * EXPERTS * HEAD_DIM
    return (query_end, value_end, output_end, output_end + FF)


def column_rates(segment):
    query_end, value_end, output_end, up_end = column_bounds()
    column = jnp.arange(up_end + FF)
    inner = D ** (-0.5)
    outer = 0.7 * math.sqrt(segment) / HEAD_DIM
    rates = jnp.where(
        column < value_end,
        inner,
        jnp.where(column < output_end, outer, jnp.where(column < up_end, inner, FF ** (-0.5))),
    )
    return rates.astype(jnp.float32)


def small_rates():
    column = jnp.arange(2 * HEADS * EXPERTS + 4)
    return jnp.where(column < 2 * HEADS * EXPERTS, 0.7 * D ** (-0.5), NORM_RATE).astype(jnp.float32)


def adam_update(weight, grad, first, second, rates, decay):
    first_new = BETA_ONE * first + (1.0 - BETA_ONE) * grad
    second_new = BETA_TWO * second + (1.0 - BETA_TWO) * grad * grad
    first_hat = first_new / (1.0 - BETA_ONE**STEP)
    second_hat = second_new / (1.0 - BETA_TWO**STEP)
    new = weight - rates * (first_hat / (jnp.sqrt(second_hat) + ADAM_EPS) + decay * weight)
    return (new, first_new, second_new)


def rotary_tables(positions):
    half = HEAD_DIM // 2
    inverse = jnp.exp(-math.log(10000.0) * jnp.arange(half, dtype=jnp.float32) / half)
    angle = positions.astype(jnp.float32)[:, None] * inverse[None, :]
    return (jnp.cos(angle), jnp.sin(angle))


def layer_stats(values):
    mean = jnp.mean(values, axis=-1, keepdims=True)
    centered = values - mean
    variance = jnp.mean(centered * centered, axis=-1, keepdims=True)
    inverse = lax.rsqrt(variance + NORM_EPS)
    return (centered * inverse, inverse)


def norm_back(grad_normed, normed, inverse, gain):
    scaled = grad_normed * gain
    return inverse * (
        scaled
        - jnp.mean(scaled, axis=-1, keepdims=True)
        - normed * jnp.mean(scaled * normed, axis=-1, keepdims=True)
    )


def contract_last(left, right):
    return lax.dot_general(
        left, right, (((1,), (1,)), ((), ())), preferred_element_type=jnp.float32
    )


def contract_first(left, right):
    return lax.dot_general(
        left, right, (((0,), (0,)), ((), ())), preferred_element_type=jnp.float32
    )


AXES = ("dp", "seq", "head")


def mesh_bits():
    dims = [
        (axis, bit)
        for axis in AXES
        for bit in reversed(range(lax.axis_size(axis).bit_length() - 1))
    ]
    groups = [[index for index, (axis, _) in enumerate(dims) if axis == name] for name in AXES]
    return (dims, *groups)


def my_bits(dims):
    place = {axis: lax.axis_index(axis) for axis in AXES}
    bits = [lax.rem(place[axis] // (1 << bit), 2) for axis, bit in dims]
    partners = [
        {axis: place[axis] + (1 << bit) * (1 - 2 * bits[index])}
        for index, (axis, bit) in enumerate(dims)
    ]
    return (bits, partners)


def greet(partners):
    barrier = pltpu.get_barrier_semaphore()
    for partner in partners:
        pl.semaphore_signal(
            barrier, inc=1, device_id=partner, device_id_type=pl.DeviceIdType.MESH
        )
    pl.semaphore_wait(barrier, len(partners))


def gather_rows(share, counts, unit, name):
    dims, dp_dims, seq_dims, head_dims = mesh_bits()
    orders = (
        head_dims + dp_dims[::-1] + seq_dims,
        head_dims + dp_dims + seq_dims,
        dp_dims + head_dims + seq_dims,
    )
    depth = len(dims)
    rows, width = share.shape
    units = width // unit
    near = (3 * units + 4) // 8
    pieces, start = ([], 0)
    for which, count in ((0, near), (1, near), (2, units - 2 * near)):
        pieces.append((start, count, which))
        start += count * unit
    lag, slots = (2, 4)
    ring = (depth + 1) * lag + 6
    steps = max(count for _, count, _ in pieces) + lag * depth

    def kernel(*refs):
        share_ref, counts_ref, out_ref, counts_out = refs[:4]
        send_sem, recv_sem, load_sem, store_sem, small_send, small_recv, small_load = refs[4:11]
        buffers = refs[11:]
        bits, partners = my_bits(dims)

        def at_stage(which, stage):
            done = orders[which][:stage]
            return tuple(slice(None) if dim in done else bits[dim] for dim in range(depth))

        def columns(number, chunk):
            return pl.ds(pl.multiple_of(pieces[number][0] + chunk * unit, 128), unit)

        def exchange(number, stage, chunk):
            which = pieces[number][2]
            view = buffers[number].at[(lax.rem(chunk, ring),) + at_stage(which, stage)]
            slot = lax.rem(chunk, slots)
            return sent_to(
                view,
                view,
                send_sem.at[number, stage, slot],
                recv_sem.at[number, stage, slot],
                partners[orders[which][stage]],
            )

        def load(number, chunk):
            return pltpu.make_async_copy(
                share_ref.at[:, columns(number, chunk)],
                buffers[number].at[(lax.rem(chunk, ring),) + tuple(bits)],
                load_sem.at[number, lax.rem(chunk, slots)],
            )

        def store(number, chunk):
            return pltpu.make_async_copy(
                buffers[number].at[lax.rem(chunk, ring)],
                out_ref.at[(slice(None),) * (depth + 1) + (columns(number, chunk),)],
                store_sem.at[number, lax.rem(chunk, slots)],
            )

        def small(stage):
            view = counts_out.at[at_stage(0, stage)]
            return sent_to(
                view, view, small_send.at[stage], small_recv.at[stage], partners[orders[0][stage]]
            )

        own_counts = pltpu.make_async_copy(counts_ref, counts_out.at[tuple(bits)], small_load)
        own_counts.start()
        for number in range(len(pieces)):
            for chunk in range(2):
                load(number, jnp.int32(chunk)).start()
        greet(partners)
        own_counts.wait()

        def body(step, carry):
            for stage in range(depth, -1, -1):
                chunk = step - lag * stage
                for number, piece in enumerate(pieces):

                    @pl.when((chunk >= 0) & (chunk < piece[1]))
                    def _(stage=stage, chunk=chunk, number=number, piece=piece):
                        if stage > 0:
                            exchange(number, stage - 1, chunk).wait()
                        else:
                            load(number, chunk).wait()

                            @pl.when(chunk + 2 < piece[1])
                            def _():
                                load(number, chunk + 2).start()

                        if stage < depth:
                            exchange(number, stage, chunk).start()
                        else:

                            @pl.when(chunk >= slots)
                            def _():
                                store(number, chunk - slots).wait()

                            store(number, chunk).start()

                @pl.when(chunk == 0)
                def _(stage=stage):
                    if stage > 0:
                        small(stage - 1).wait()
                    if stage < depth:
                        small(stage).start()

            return carry

        lax.fori_loop(0, steps, body, 0)
        for number, piece in enumerate(pieces):
            for back in range(min(slots, piece[1])):
                store(number, jnp.int32(piece[1] - 1 - back)).wait()

    in_place = pl.BlockSpec(memory_space=pl.ANY)
    semaphores = pltpu.SemaphoreType.DMA((len(pieces), depth, slots))
    local = pltpu.SemaphoreType.DMA((len(pieces), slots))
    gathered, all_counts = pl.pallas_call(
        kernel,
        in_specs=[in_place] * 2,
        out_specs=[in_place] * 2,
        out_shape=[
            jax.ShapeDtypeStruct((2,) * depth + value.shape, value.dtype)
            for value in (share, counts)
        ],
        scratch_shapes=[
            semaphores,
            semaphores,
            local,
            local,
            pltpu.SemaphoreType.DMA((depth,)),
            pltpu.SemaphoreType.DMA((depth,)),
            pltpu.SemaphoreType.DMA,
        ]
        + [pltpu.VMEM((ring,) + (2,) * depth + (rows, unit), share.dtype) for _ in pieces],
        compiler_params=pltpu.CompilerParams(
            collective_id=name, has_side_effects=True, vmem_limit_bytes=48 << 20
        ),
    )(share, counts)
    return (gathered.reshape(-1, width), all_counts.reshape(-1, counts.shape[1]))


def halving_plan(width):
    dims, dp_dims, seq_dims, head_dims = mesh_bits()
    first = seq_dims[::-1]
    orders = (
        (0, width // 2, first + dp_dims[::-1] + head_dims[::-1]),
        (width // 2, width // 4, first + dp_dims + head_dims[::-1]),
        (3 * width // 4, width // 4, first + head_dims[::-1] + dp_dims[::-1]),
    )
    stages = []
    for stage in range(len(dims)):
        parts = []
        for start, count, order in orders:
            left = [dim for dim in range(len(dims)) if dim not in order[:stage]]
            if parts and parts[-1][2:] == (order[stage], left):
                parts[-1] = (parts[-1][0], parts[-1][1] + count, order[stage], left)
            else:
                parts.append((start, count, order[stage], left))
        stages.append(parts)
    lags = [1 if stage < len(seq_dims) else 2 for stage in range(len(dims))]
    return dims, stages, lags


def reduce_weight_grads(pairs, extras, width):
    dims, stages, lags = halving_plan(width)
    depth = len(dims)
    tokens, model = pairs[0][0].shape
    rows = model >> depth
    firsts = [0]
    for left, right in pairs:
        firsts.append(firsts[-1] + right.shape[1] // width)
    chunks = firsts[-1]
    spots = [(firsts[pair] + near // width, near % width) for _, pair, near in extras]
    starts = [sum(lags[:stage]) for stage in range(depth + 1)]
    count_pairs, count_extras = (len(pairs), len(extras))

    def kernel(*refs):
        lefts = refs[:count_pairs]
        rights = refs[count_pairs : 2 * count_pairs]
        added = refs[2 * count_pairs : 2 * count_pairs + count_extras]
        rest = refs[2 * count_pairs + count_extras :]
        out_ref, left_buf, turned, right_buf, load_sem = rest[:5]
        pool = iter(rest[5:])
        buffers = [[tuple(next(pool) for _ in range(4)) for _ in parts] for parts in stages]
        step = pl.program_id(0)
        bits, partners = my_bits(dims)

        def exchange(stage, part, slot):
            start, count, dim, left = stages[stage][part]
            own, got, send_sem, recv_sem = buffers[stage][part]
            lead = (slot,) + (slice(None),) * left.index(dim)
            return pltpu.make_async_remote_copy(
                src_ref=own.at[lead + (1 - bits[dim],)],
                dst_ref=got.at[slot],
                send_sem=send_sem.at[slot],
                recv_sem=recv_sem.at[slot],
                device_id=partners[dim],
                device_id_type=pl.DeviceIdType.MESH,
            )

        def load_left(index):
            return pltpu.make_async_copy(lefts[index], left_buf, load_sem.at[2])

        def load_right(index, chunk):
            slot = lax.rem(chunk, 2)
            columns = pl.ds(pl.multiple_of((chunk - firsts[index]) * width, width), width)
            return pltpu.make_async_copy(
                rights[index].at[:, columns], right_buf.at[slot], load_sem.at[slot]
            )

        def prefetch(chunk):
            for index in range(count_pairs):

                @pl.when((chunk >= firsts[index]) & (chunk < firsts[index + 1]))
                def _(index=index):
                    load_right(index, chunk).start()

                @pl.when(chunk == firsts[index])
                def _(index=index):
                    load_left(index).start()

        @pl.when(step == 0)
        def _():
            prefetch(step)
            greet(partners)

        @pl.when(step + 1 < chunks)
        def _():
            prefetch(step + 1)

        for stage in range(depth, -1, -1):
            chunk = step - starts[stage]

            @pl.when((chunk >= 0) & (chunk < chunks))
            def _(stage=stage, chunk=chunk):
                if stage == 0:
                    for first in firsts[:-1]:

                        @pl.when(chunk == first)
                        def _():
                            load_left(0).wait()
                            turned[...] = left_buf[...].T

                    load_right(0, lax.rem(chunk, 2)).wait()
                    product = jnp.dot(
                        turned[...],
                        right_buf[lax.rem(chunk, 2)],
                        preferred_element_type=jnp.float32,
                    )
                    slot = lax.rem(chunk, 2 * lags[0])
                    for part, (start, count, dim, left) in enumerate(stages[0]):
                        piece = product[:, start : start + count].astype(jnp.bfloat16)
                        buffers[0][part][0][slot] = piece.reshape((2,) * depth + (rows, count))
                    for index in range(count_extras):

                        @pl.when(chunk == spots[index][0])
                        def _(index=index):
                            at = (slot, Ellipsis, slice(spots[index][1], spots[index][1] + 128))
                            own = buffers[0][0][0]
                            total = own[at].astype(jnp.float32) + added[index][...].astype(
                                jnp.float32
                            )
                            own[at] = total.astype(jnp.bfloat16)

                else:
                    back = lax.rem(chunk, 2 * lags[stage - 1])
                    for part, (start, count, dim, left) in enumerate(stages[stage - 1]):
                        exchange(stage - 1, part, back).wait()
                        own, got = buffers[stage - 1][part][:2]
                        lead = (back,) + (slice(None),) * left.index(dim)
                        total = own[lead + (bits[dim],)].astype(jnp.float32) + got[back].astype(
                            jnp.float32
                        )
                        if stage == depth:
                            out_ref[:, start : start + count] = total
                            continue
                        slot = lax.rem(chunk, 2 * lags[stage])
                        low = total.astype(jnp.bfloat16)
                        for other, (begin, length, _, kept) in enumerate(stages[stage]):
                            lo, hi = max(start, begin), min(start + count, begin + length)
                            if lo < hi:
                                at = (slot,) + (slice(None),) * (len(kept) + 1)
                                buffers[stage][other][0][at + (slice(lo - begin, hi - begin),)] = (
                                    low[..., lo - start : hi - start]
                                )
                if stage < depth:
                    for part in range(len(stages[stage])):
                        exchange(stage, part, lax.rem(chunk, 2 * lags[stage])).start()

    scratch = [
        pltpu.VMEM((tokens, model), jnp.bfloat16),
        pltpu.VMEM((model, tokens), jnp.bfloat16),
        pltpu.VMEM((2, tokens, width), jnp.bfloat16),
        pltpu.SemaphoreType.DMA((3,)),
    ]
    for stage, parts in enumerate(stages):
        slots = 2 * lags[stage]
        for start, count, dim, left in parts:
            scratch += [
                pltpu.VMEM((slots,) + (2,) * len(left) + (rows, count), jnp.bfloat16),
                pltpu.VMEM((slots,) + (2,) * (len(left) - 1) + (rows, count), jnp.bfloat16),
                pltpu.SemaphoreType.DMA((slots,)),
                pltpu.SemaphoreType.DMA((slots,)),
            ]
    in_place = pl.BlockSpec(memory_space=pl.ANY)
    whole = [value.reshape((2,) * depth + (rows, 128)) for value, _, _ in extras]
    return pl.pallas_call(
        kernel,
        grid=(chunks + starts[depth],),
        in_specs=[in_place] * (2 * count_pairs)
        + [pl.BlockSpec(value.shape, lambda step: (0,) * (depth + 2)) for value in whole],
        out_specs=pl.BlockSpec(
            (rows, width), lambda step: (0, jnp.clip(step - starts[depth], 0, chunks - 1))
        ),
        out_shape=jax.ShapeDtypeStruct((rows, chunks * width), jnp.float32),
        scratch_shapes=scratch,
        compiler_params=pltpu.CompilerParams(
            collective_id=1,
            has_side_effects=True,
            vmem_limit_bytes=48 << 20,
            dimension_semantics=("arbitrary",),
        ),
    )(*[left for left, _ in pairs], *[right for _, right in pairs], *whole)


def reduction_order(tensor):
    dp, seq = (lax.axis_size("dp"), lax.axis_size("seq"))
    count, width = tensor.shape
    split = tensor.reshape(count, dp, seq, width // (dp * seq))
    return split.transpose(0, 2, 1, 3).reshape(count, width)


def reduced_natively(left, right):
    share = contract_first(reduction_order(left), right).astype(jnp.bfloat16)
    for axis in ("seq", "dp"):
        share = lax.psum_scatter(share, axis, scatter_dimension=0, tiled=True)
    return share


def lane_whole(count):
    return count + (-count) % 128


def chunk_whole(count):
    return count + (-count) % CHUNK


def padded(pieces, width):
    have = sum(piece.shape[1] for piece in pieces)
    fill = jnp.zeros((pieces[0].shape[0], width - have), pieces[0].dtype)
    return jnp.concatenate(list(pieces) + [fill], axis=1)


LANES = 128
QUERY_TILE = 256


def swap_halves(tensor):
    half = HEAD_DIM // 2
    return jnp.concatenate([tensor[:, half:], tensor[:, :half]], axis=1)


def lane_filled(tensor):
    fill = jnp.zeros((tensor.shape[0], LANES - tensor.shape[1]), tensor.dtype)
    return jnp.concatenate([tensor, fill], axis=1)


def weights_block(keys_mem, keys_own, query, start, first, segment, length):
    contract = (((1,), (1,)), ((), ()))
    raw = jnp.concatenate(
        [
            lax.dot_general(keys, query, contract, preferred_element_type=jnp.float32)
            for keys in (keys_mem, keys_own)
        ],
        axis=0,
    )
    key_pos = start - segment + lax.broadcasted_iota(jnp.int32, raw.shape, 0)
    query_pos = start + first + lax.broadcasted_iota(jnp.int32, raw.shape, 1)
    used = (key_pos < length) & (key_pos < query_pos) & (key_pos >= 0)
    allowed = used | (key_pos == query_pos)
    scores = jnp.where(allowed, raw * HEAD_DIM ** (-0.5), MASKED)
    weights = jnp.exp(scores - jnp.max(scores, axis=0, keepdims=True))
    return weights * (1.0 / jnp.sum(weights, axis=0, keepdims=True))


def contract_rows(left, right):
    return lax.dot_general(
        left, right, (((0,), (0,)), ((), ())), preferred_element_type=jnp.float32
    )


def across(axis, offset):
    size = lax.axis_size(axis)
    return {axis: lax.rem(lax.axis_index(axis) + offset + size, size)}


def sent_to(source, target, send_sem, recv_sem, device):
    return pltpu.make_async_remote_copy(
        src_ref=source,
        dst_ref=target,
        send_sem=send_sem,
        recv_sem=recv_sem,
        device_id=device,
        device_id_type=pl.DeviceIdType.MESH,
    )


def meet(memory_step):
    barrier = pltpu.get_barrier_semaphore()
    heads = lax.axis_size("head")
    writers = [across("head", step) for step in range(1, heads)]
    writers.append(across("seq", -memory_step))
    for device in writers:
        pl.semaphore_signal(barrier, inc=1, device_id=device, device_id_type=pl.DeviceIdType.MESH)
    pl.semaphore_wait(barrier, len(writers))


def gate_values(entered_ref, chosen_ref, rows):
    at = column_bounds()[1]
    logits = entered_ref[rows, at : at + 2 * HEADS * EXPERTS]
    prob = 1.0 / (1.0 + jnp.exp(-logits))
    return (prob, prob * chosen_ref[rows, :])


def column(tensor, index):
    return tensor[:, index : index + 1]


def attention_forward(entered, chosen, turn_cos, turn_sin, lengths, mixed_width, name):
    seq_count = lengths.shape[0]
    tokens = entered.shape[0]
    sub = tokens // seq_count
    heads = lax.axis_size("head")
    segment = heads * sub
    query_end = column_bounds()[0]
    sides = range(1, heads)

    def kernel(*refs):
        length_ref, entered_ref, chosen_ref, cos_ref, sin_ref = refs[:5]
        mixed_ref, attended_ref, query_ref, key_ref, value_ref = refs[5:10]
        out_buf, heads_buf, mem_buf, done_buf, back_buf = refs[10:15]
        out_sem, in_sem, mem_sem, done_sem, back_sem = refs[15:]
        me = lax.axis_index("head")
        start = lax.axis_index("seq") * segment
        turn, wind = (cos_ref[...], sin_ref[...])

        def outward(b, side):
            there = across("head", side)
            return sent_to(
                out_buf.at[b, there["head"]],
                heads_buf.at[b, :, me],
                out_sem.at[b, side - 1],
                in_sem.at[b, side - 1],
                there,
            )

        def onward(b):
            return sent_to(
                heads_buf.at[b, 1:3],
                mem_buf.at[b],
                mem_sem.at[0, b],
                mem_sem.at[1, b],
                across("seq", 1),
            )

        def homeward(b, side):
            there = across("head", side)
            return sent_to(
                done_buf.at[b, there["head"]],
                back_buf.at[b, me],
                done_sem.at[b, side - 1],
                back_sem.at[b, side - 1],
                there,
            )

        meet(1)
        gates_of = []
        for b in range(seq_count):
            rows = slice(b * sub, (b + 1) * sub)
            gates = gate_values(entered_ref, chosen_ref, rows)[1]
            gates_of.append(gates)
            for head in range(HEADS):
                for kind in range(2):
                    at = (kind * HEADS + head) * HEAD_DIM
                    vector = entered_ref[rows, at : at + HEAD_DIM]
                    turned = vector * turn + swap_halves(vector) * wind
                    out_buf[b, head, kind] = lane_filled(turned).astype(jnp.bfloat16)
                value = jnp.zeros((sub, HEAD_DIM), jnp.float32)
                for expert in range(EXPERTS):
                    index = head * EXPERTS + expert
                    at = query_end + index * HEAD_DIM
                    value += column(gates, index) * entered_ref[rows, at : at + HEAD_DIM]
                out_buf[b, head, 2] = lane_filled(value).astype(jnp.bfloat16)
            for side in sides:
                outward(b, side).start()
            for kind in range(3):
                heads_buf[b, kind, me] = out_buf[b, me, kind]
        for b in range(seq_count):
            for side in sides:
                outward(b, side).wait_recv()
            onward(b).start()
        for b in range(seq_count):
            onward(b).wait_recv()
            keys_own = heads_buf[b, 1].reshape(segment, LANES)
            values = jnp.concatenate(
                [mem_buf[b, 1].reshape(segment, LANES), heads_buf[b, 2].reshape(segment, LANES)],
                axis=0,
            )
            for first in range(0, segment, QUERY_TILE):
                tile = slice(first // sub, (first + QUERY_TILE) // sub)
                query = heads_buf[b, 0, tile].reshape(QUERY_TILE, LANES)
                probs = weights_block(
                    mem_buf[b, 0].reshape(segment, LANES),
                    keys_own,
                    query,
                    start,
                    first,
                    segment,
                    length_ref[b],
                ).astype(jnp.bfloat16)
                attended = contract_rows(values, probs).T.astype(jnp.bfloat16)
                done_buf[b, tile] = attended.reshape(QUERY_TILE // sub, sub, LANES)
            for side in sides:
                homeward(b, side).start()
            back_buf[b, me] = done_buf[b, me]
        for b in range(seq_count):
            query_ref[b] = heads_buf[b, 0]
            key_ref[b, 0] = mem_buf[b, 0]
            key_ref[b, 1] = heads_buf[b, 1]
            value_ref[b, 0] = mem_buf[b, 1]
            value_ref[b, 1] = heads_buf[b, 2]
        used = HEADS * EXPERTS * HEAD_DIM
        mixed_ref[:, used:] = jnp.zeros((tokens, mixed_width - used), jnp.bfloat16)
        for b in range(seq_count):
            rows = slice(b * sub, (b + 1) * sub)
            for side in sides:
                homeward(b, side).wait_recv()
            for head in range(HEADS):
                attended = back_buf[b, head]
                attended_ref[rows, head * LANES : (head + 1) * LANES] = attended
                wide = attended.astype(jnp.float32)[:, :HEAD_DIM]
                for expert in range(EXPERTS):
                    index = head * EXPERTS + expert
                    gate = column(gates_of[b], HEADS * EXPERTS + index)
                    mixed_ref[rows, index * HEAD_DIM : (index + 1) * HEAD_DIM] = (
                        gate * wide
                    ).astype(jnp.bfloat16)
        for b in range(seq_count):
            onward(b).wait_send()
            for side in sides:
                outward(b, side).wait_send()
                homeward(b, side).wait_send()

    def shape(*dims):
        return jax.ShapeDtypeStruct(dims, jnp.bfloat16)

    vmem = pl.BlockSpec(memory_space=pltpu.VMEM)
    paired = pltpu.SemaphoreType.DMA((seq_count, heads - 1))
    return pl.pallas_call(
        kernel,
        in_specs=[pl.BlockSpec(memory_space=pltpu.SMEM)] + [vmem] * 4,
        out_specs=[vmem] * 5,
        out_shape=[
            shape(tokens, mixed_width),
            shape(tokens, HEADS * LANES),
            shape(seq_count, heads, sub, LANES),
            shape(seq_count, 2, heads, sub, LANES),
            shape(seq_count, 2, heads, sub, LANES),
        ],
        scratch_shapes=[
            pltpu.VMEM((seq_count, heads, 3, sub, LANES), jnp.bfloat16),
            pltpu.VMEM((seq_count, 3, heads, sub, LANES), jnp.bfloat16),
            pltpu.VMEM((seq_count, 2, heads, sub, LANES), jnp.bfloat16),
            pltpu.VMEM((seq_count, heads, sub, LANES), jnp.bfloat16),
            pltpu.VMEM((seq_count, heads, sub, LANES), jnp.bfloat16),
            paired,
            paired,
            pltpu.SemaphoreType.DMA((2, seq_count)),
            paired,
            paired,
        ],
        compiler_params=pltpu.CompilerParams(
            collective_id=name, has_side_effects=True, vmem_limit_bytes=40 << 20
        ),
    )(lengths, entered, chosen, turn_cos, turn_sin)


def attention_backward(
    grad_mixed, attended, entered, chosen, turn_cos, turn_sin, lengths, saved, grad_width, name
):
    query, keys, values = saved
    seq_count = lengths.shape[0]
    tokens = entered.shape[0]
    sub = tokens // seq_count
    heads = lax.axis_size("head")
    segment = heads * sub
    query_end, value_end = column_bounds()[:2]
    router_cols = 2 * HEADS * EXPERTS
    sides = range(1, heads)

    def kernel(*refs):
        length_ref, grad_ref, attended_ref, entered_ref, chosen_ref, cos_ref, sin_ref = refs[:7]
        query_ref, key_ref, value_ref, result_ref = refs[7:11]
        out_buf, heads_buf, mem_out, mem_in, own_buf, done_buf, back_buf = refs[11:18]
        out_sem, in_sem, mem_sem, query_sem, done_sem, back_sem = refs[18:]
        me = lax.axis_index("head")
        start = lax.axis_index("seq") * segment
        turn, wind = (cos_ref[...], sin_ref[...])

        def outward(b, side):
            there = across("head", side)
            return sent_to(
                out_buf.at[b, there["head"]],
                heads_buf.at[b, me],
                out_sem.at[b, side - 1],
                in_sem.at[b, side - 1],
                there,
            )

        def onward(b):
            return sent_to(
                mem_out.at[b], mem_in.at[b], mem_sem.at[0, b], mem_sem.at[1, b], across("seq", -1)
            )

        def queries_home(b, side):
            there = across("head", side)
            return sent_to(
                done_buf.at[b, there["head"], 0],
                back_buf.at[b, me, 0],
                query_sem.at[0, b, side - 1],
                query_sem.at[1, b, side - 1],
                there,
            )

        def homeward(b, side):
            there = across("head", side)
            return sent_to(
                done_buf.at[b, there["head"], 1:3],
                back_buf.at[b, me, 1:3],
                done_sem.at[b, side - 1],
                back_sem.at[b, side - 1],
                there,
            )

        def join_memory(b):
            onward(b).wait_recv()
            for kind in range(2):
                total = own_buf[b, kind] + mem_in[b, kind].astype(jnp.float32)
                done_buf[b, :, kind + 1] = total.astype(jnp.bfloat16).reshape(heads, sub, LANES)
            for side in sides:
                homeward(b, side).start()
            back_buf[b, me] = done_buf[b, me]

        meet(-1)
        lane = lax.broadcasted_iota(jnp.int32, (sub, router_cols), 1)
        gate_grads, probs_of, gates_of = ([], [], [])
        for b in range(seq_count):
            rows = slice(b * sub, (b + 1) * sub)
            prob, gates = gate_values(entered_ref, chosen_ref, rows)
            probs_of.append(prob)
            gates_of.append(gates)
            gate_grad = jnp.zeros((sub, router_cols), jnp.float32)
            for head in range(HEADS):
                seen = attended_ref[rows, head * LANES : head * LANES + HEAD_DIM].astype(
                    jnp.float32
                )
                total = jnp.zeros((sub, HEAD_DIM), jnp.float32)
                for expert in range(EXPERTS):
                    index = head * EXPERTS + expert
                    part = grad_ref[rows, index * HEAD_DIM : (index + 1) * HEAD_DIM]
                    total += column(gates, HEADS * EXPERTS + index) * part
                    gate_grad = jnp.where(
                        lane == HEADS * EXPERTS + index,
                        jnp.sum(part * seen, axis=1, keepdims=True),
                        gate_grad,
                    )
                out_buf[b, head] = lane_filled(total).astype(jnp.bfloat16)
            gate_grads.append(gate_grad)
            for side in sides:
                outward(b, side).start()
            heads_buf[b, me] = out_buf[b, me]
        for b in range(seq_count):
            for side in sides:
                outward(b, side).wait_recv()
            keys_mem = key_ref[b, 0].reshape(segment, LANES)
            keys_own = key_ref[b, 1].reshape(segment, LANES)
            keys_all = jnp.concatenate([keys_mem, keys_own], axis=0)
            values_all = jnp.concatenate(
                [value_ref[b, 0].reshape(segment, LANES), value_ref[b, 1].reshape(segment, LANES)],
                axis=0,
            )
            grad_keys = jnp.zeros((2 * segment, LANES), jnp.float32)
            grad_values = jnp.zeros((2 * segment, LANES), jnp.float32)
            for first in range(0, segment, QUERY_TILE):
                tile = slice(first // sub, (first + QUERY_TILE) // sub)
                here = query_ref[b, tile].reshape(QUERY_TILE, LANES)
                arrived = heads_buf[b, tile].reshape(QUERY_TILE, LANES)
                probs = weights_block(
                    keys_mem, keys_own, here, start, first, segment, length_ref[b]
                )
                grad_probs = contract_last(values_all, arrived)
                delta = jnp.sum(probs * grad_probs, axis=0, keepdims=True)
                grad_raw = (probs * (grad_probs - delta) * HEAD_DIM ** (-0.5)).astype(
                    jnp.bfloat16
                )
                grad_values += jnp.dot(
                    probs.astype(jnp.bfloat16), arrived, preferred_element_type=jnp.float32
                )
                grad_keys += jnp.dot(grad_raw, here, preferred_element_type=jnp.float32)
                grad_query = contract_rows(keys_all, grad_raw).T.astype(jnp.bfloat16)
                done_buf[b, tile, 0] = grad_query.reshape(QUERY_TILE // sub, sub, LANES)
                if b > 0 and first == 0:
                    join_memory(b - 1)
            for kind, grads in enumerate((grad_keys, grad_values)):
                mem_out[b, kind] = grads[:segment].astype(jnp.bfloat16)
                own_buf[b, kind] = grads[segment:]
            onward(b).start()
            for side in sides:
                queries_home(b, side).start()
        join_memory(seq_count - 1)
        used = value_end + router_cols
        result_ref[:, used:] = jnp.zeros((tokens, grad_width - used), jnp.bfloat16)
        for b in range(seq_count):
            rows = slice(b * sub, (b + 1) * sub)
            for side in sides:
                queries_home(b, side).wait_recv()
                homeward(b, side).wait_recv()
            gate_grad = gate_grads[b]
            for head in range(HEADS):
                for kind in range(2):
                    vector = back_buf[b, head, kind].astype(jnp.float32)[:, :HEAD_DIM]
                    turned = vector * turn - swap_halves(vector) * wind
                    at = (kind * HEADS + head) * HEAD_DIM
                    result_ref[rows, at : at + HEAD_DIM] = turned.astype(jnp.bfloat16)
                grad_value = back_buf[b, head, 2].astype(jnp.float32)[:, :HEAD_DIM]
                for expert in range(EXPERTS):
                    index = head * EXPERTS + expert
                    at = query_end + index * HEAD_DIM
                    gate_grad = jnp.where(
                        lane == index,
                        jnp.sum(
                            entered_ref[rows, at : at + HEAD_DIM] * grad_value,
                            axis=1,
                            keepdims=True,
                        ),
                        gate_grad,
                    )
                    result_ref[rows, at : at + HEAD_DIM] = (
                        column(gates_of[b], index) * grad_value
                    ).astype(jnp.bfloat16)
            prob = probs_of[b]
            result_ref[rows, value_end:used] = (
                gate_grad * chosen_ref[rows, :] * prob * (1.0 - prob)
            ).astype(jnp.bfloat16)
        for b in range(seq_count):
            onward(b).wait_send()
            for side in sides:
                outward(b, side).wait_send()
                queries_home(b, side).wait_send()
                homeward(b, side).wait_send()

    vmem = pl.BlockSpec(memory_space=pltpu.VMEM)
    paired = pltpu.SemaphoreType.DMA((seq_count, heads - 1))
    return pl.pallas_call(
        kernel,
        in_specs=[pl.BlockSpec(memory_space=pltpu.SMEM)] + [vmem] * 9,
        out_specs=vmem,
        out_shape=jax.ShapeDtypeStruct((tokens, grad_width), jnp.bfloat16),
        scratch_shapes=[
            pltpu.VMEM((seq_count, heads, sub, LANES), jnp.bfloat16),
            pltpu.VMEM((seq_count, heads, sub, LANES), jnp.bfloat16),
            pltpu.VMEM((seq_count, 2, segment, LANES), jnp.bfloat16),
            pltpu.VMEM((seq_count, 2, segment, LANES), jnp.bfloat16),
            pltpu.VMEM((seq_count, 2, segment, LANES), jnp.float32),
            pltpu.VMEM((seq_count, heads, 3, sub, LANES), jnp.bfloat16),
            pltpu.VMEM((seq_count, heads, 3, sub, LANES), jnp.bfloat16),
            paired,
            paired,
            pltpu.SemaphoreType.DMA((2, seq_count)),
            pltpu.SemaphoreType.DMA((2, seq_count, heads - 1)),
            paired,
            paired,
        ],
        compiler_params=pltpu.CompilerParams(
            collective_id=name, has_side_effects=True, vmem_limit_bytes=48 << 20
        ),
    )(lengths, grad_mixed, attended, entered, chosen, turn_cos, turn_sin, query, keys, values)


def gelu_tanh(values):
    return jax.nn.gelu(values, approximate=True)


def local(
    inputs,
    cotangent,
    routes,
    lengths,
    matrix,
    matrix_first,
    matrix_second,
    small,
    small_first,
    small_second,
):
    head_count = lax.axis_size("head")
    seq_count, sub_rows, width = inputs.shape
    segment = sub_rows * head_count
    tokens = seq_count * sub_rows
    router_cols = 2 * HEADS * EXPERTS
    group = HEADS * EXPERTS
    query_end, value_end, output_end, up_end = column_bounds()
    seq_start = lax.axis_index("seq") * segment
    positions = (
        seq_start + lax.axis_index("head") * sub_rows + jnp.arange(sub_rows, dtype=jnp.int32)
    )
    valid = (positions[None, :] < lengths[:, None]).astype(jnp.float32)
    cosines, sines = rotary_tables(positions)
    turn_cos = jnp.concatenate([cosines, cosines], axis=1)
    turn_sin = jnp.concatenate([-sines, sines], axis=1)
    chosen = jnp.sum(
        (routes[..., None] == jnp.arange(EXPERTS, dtype=jnp.int32)).astype(jnp.float32), axis=-2
    )
    load_part = jnp.sum(chosen * valid[None, :, :, None, None, None], axis=(1, 2))
    in_width = lane_whole(value_end + router_cols + 4)
    out_width = lane_whole(output_end - value_end)
    matrix_low = matrix.astype(jnp.bfloat16)
    small_low = small.astype(jnp.bfloat16)
    in_low = [
        padded([matrix_low[layer, :, :value_end], small_low[layer]], in_width)
        for layer in range(LAYERS)
    ]
    out_low = [
        padded([matrix_low[layer, :, value_end:output_end]], out_width) for layer in range(LAYERS)
    ]
    ffn_low = [matrix_low[layer, :, output_end:] for layer in range(LAYERS)]
    size = load_part.size
    counts = jnp.pad(load_part.reshape(-1), (0, (-size) % 1024)).reshape(8, -1)
    early = []
    for layer in range(LAYERS):
        early += [in_low[layer], out_low[layer]] + ([ffn_low[layer]] if layer + 1 < LAYERS else [])
    gathered, counts = gather_rows(jnp.concatenate(early, axis=1), counts, 128, 2)
    counts, late = lax.optimization_barrier((counts, ffn_low[-1]))
    loads = jnp.sum(counts.reshape(-1, size + (-size) % 1024), axis=0)[:size].reshape(
        load_part.shape
    )
    late = lax.all_gather(late, ("dp", "seq", "head"), axis=0, tiled=True)
    pieces, start = ([], 0)
    for value in early:
        pieces.append(gathered[:, start : start + value.shape[1]])
        start += value.shape[1]
    pieces.append(late)
    in_ws, out_ws, ffn_ws = (pieces[0::3], pieces[1::3], pieces[2::3])
    hidden = inputs.astype(jnp.float32).reshape(tokens, width)
    kept = []
    for layer in range(LAYERS):
        in_w, out_w, ffn_w = (in_ws[layer], out_ws[layer], ffn_ws[layer])
        gains = in_w[:, value_end + router_cols : value_end + router_cols + 4].astype(jnp.float32)
        normed_one, inverse_one = layer_stats(hidden)
        first_in = (normed_one * gains[:, 0] + gains[:, 1]).astype(jnp.bfloat16)
        entered = jnp.dot(first_in, in_w, preferred_element_type=jnp.float32)
        chosen_here = chosen[layer].reshape(tokens, router_cols)
        mixed, attended, *saved = attention_forward(
            entered,
            chosen_here,
            turn_cos,
            turn_sin,
            lengths,
            chunk_whole(out_width),
            3 + layer,
        )
        residual = hidden + contract_last(mixed[:, :out_width], out_w)
        normed_two, inverse_two = layer_stats(residual)
        second_in = (normed_two * gains[:, 2] + gains[:, 3]).astype(jnp.bfloat16)
        up = jnp.dot(second_in, ffn_w[:, :FF], preferred_element_type=jnp.float32)
        act = gelu_tanh(up).astype(jnp.bfloat16)
        hidden = residual + contract_last(act, ffn_w[:, FF:])
        kept.append(
            (
                normed_one,
                inverse_one,
                first_in,
                entered,
                chosen_here,
                mixed,
                attended,
                saved,
                normed_two,
                inverse_two,
                second_in,
                up,
                act,
            )
        )
    output = hidden.reshape(seq_count, sub_rows, width).astype(jnp.bfloat16)
    grad_hidden = (cotangent.astype(jnp.float32) * valid[:, :, None]).reshape(tokens, width)
    pairs, extras, native = ([], [], {})
    for layer in reversed(range(LAYERS)):
        (
            normed_one,
            inverse_one,
            first_in,
            entered,
            chosen_here,
            mixed,
            attended,
            saved,
            normed_two,
            inverse_two,
            second_in,
            up,
            act,
        ) = kept[layer]
        in_w, out_w, ffn_w = (in_ws[layer], out_ws[layer], ffn_ws[layer])
        gains = in_w[:, value_end + router_cols : value_end + router_cols + 4].astype(jnp.float32)
        grad_low = grad_hidden.astype(jnp.bfloat16)
        grad_act = jnp.dot(grad_low, ffn_w[:, FF:], preferred_element_type=jnp.float32)
        gelu_value, gelu_pull = jax.vjp(gelu_tanh, up)
        grad_up = gelu_pull(grad_act)[0].astype(jnp.bfloat16)
        grad_second = contract_last(grad_up, ffn_w[:, :FF])
        gain_two_grad = jnp.sum(grad_second * normed_two, axis=0)
        bias_two_grad = jnp.sum(grad_second, axis=0)
        grad_residual = grad_hidden + norm_back(grad_second, normed_two, inverse_two, gains[:, 2])
        residual_low = grad_residual.astype(jnp.bfloat16)
        grad_in = attention_backward(
            jnp.dot(residual_low, out_w, preferred_element_type=jnp.float32),
            attended,
            entered,
            chosen_here,
            turn_cos,
            turn_sin,
            lengths,
            saved,
            chunk_whole(in_width),
            3 + LAYERS + layer,
        )
        grad_first = contract_last(grad_in[:, :in_width], in_w)
        gain_one_grad = jnp.sum(grad_first * normed_one, axis=0)
        bias_one_grad = jnp.sum(grad_first, axis=0)
        grad_hidden = grad_residual + norm_back(grad_first, normed_one, inverse_one, gains[:, 0])
        norm_grads = jnp.stack(
            [gain_one_grad, bias_one_grad, gain_two_grad, bias_two_grad], axis=1
        ).astype(jnp.bfloat16)
        at = value_end + router_cols
        near = at // 128 * 128
        norm_grads = jnp.pad(norm_grads, ((0, 0), (at - near, 128 - 4 - (at - near))))
        extras.append((norm_grads, len(pairs), near))
        pairs += [(first_in, grad_in), (residual_low, mixed)]
        for kind, pair in (("up", (second_in, grad_up)), ("down", (grad_low, act))):
            if (layer, kind) in NATIVE:
                native[layer, kind] = reduced_natively(*pair)
            else:
                pairs.append(pair)
    names = list(native)
    halves, begun = lax.optimization_barrier(([native[name] for name in names], pairs[0][1]))
    pairs[0] = (pairs[0][0], begun)
    for name, half in zip(names, halves):
        native[name] = lax.psum_scatter(half, "head", scatter_dimension=0, tiled=True).astype(
            jnp.float32
        )
    reduced = reduce_weight_grads(pairs, extras, CHUNK)
    matrix_rows = [None] * LAYERS
    small_rows = [None] * LAYERS
    start = 0
    for layer in reversed(range(LAYERS)):
        shares = {}
        for kind, used in (("in", in_width), ("out", output_end - value_end), ("up", FF), ("down", FF)):
            if (layer, kind) in NATIVE:
                shares[kind] = native[layer, kind]
            else:
                shares[kind] = reduced[:, start : start + used]
                start += chunk_whole(used)
        small_rows[layer] = shares["in"][:, value_end : value_end + router_cols + 4]
        shares["in"] = shares["in"][:, :value_end]
        matrix_rows[layer] = jnp.concatenate(list(shares.values()), axis=1)
    input_grad = grad_hidden.reshape(seq_count, sub_rows, width).astype(jnp.bfloat16)
    matrix_grad = jnp.stack(matrix_rows, axis=0)
    small_grad = jnp.stack(small_rows, axis=0)
    matrix_new, matrix_first_new, matrix_second_new = adam_update(
        matrix, matrix_grad, matrix_first, matrix_second, column_rates(segment), WEIGHT_DECAY
    )
    small_new, small_first_new, small_second_new = adam_update(
        small, small_grad, small_first, small_second, small_rates(), 0.0
    )
    return (
        output,
        input_grad,
        matrix_grad,
        matrix_new,
        matrix_new.astype(jnp.bfloat16),
        matrix_first_new,
        matrix_second_new,
        small_grad,
        small_new,
        small_new.astype(jnp.bfloat16),
        small_first_new,
        small_second_new,
        loads,
    )


def solution(mesh):
    in_specs = (
        P("dp", ("seq", "head"), None),
        P("dp", ("seq", "head"), None),
        P(None, "dp", ("seq", "head"), None, None, None),
        P("dp"),
        P(None, ("dp", "seq", "head"), None),
        P(None, ("dp", "seq", "head"), None),
        P(None, ("dp", "seq", "head"), None),
        P(None, ("dp", "seq", "head"), None),
        P(None, ("dp", "seq", "head"), None),
        P(None, ("dp", "seq", "head"), None),
    )
    out_specs = (
        P("dp", ("seq", "head"), None),
        P("dp", ("seq", "head"), None),
        P(None, ("dp", "seq", "head"), None),
        P(None, ("dp", "seq", "head"), None),
        P(None, ("dp", "seq", "head"), None),
        P(None, ("dp", "seq", "head"), None),
        P(None, ("dp", "seq", "head"), None),
        P(None, ("dp", "seq", "head"), None),
        P(None, ("dp", "seq", "head"), None),
        P(None, ("dp", "seq", "head"), None),
        P(None, ("dp", "seq", "head"), None),
        P(None, ("dp", "seq", "head"), None),
        P(),
    )
    return jax.shard_map(local, mesh=mesh, in_specs=in_specs, out_specs=out_specs, check_vma=False)
```

```python
import math

import jax
import jax.numpy as jnp
from jax import lax
from jax.experimental import pallas as pl
from jax.experimental.pallas import tpu as pltpu
from jax.sharding import PartitionSpec as P

D = 1024
HEADS = 4
HEAD_DIM = 112
EXPERTS = 5
FF = 4096
LAYERS = 2
STEP = 10


NORM_EPS = 1e-05
BETA_ONE = 0.9
BETA_TWO = 0.95
ADAM_EPS = 1e-08
WEIGHT_DECAY = 0.1
NORM_RATE = 0.5
MASKED = -1e30
CHUNK = 512
NATIVE = ((LAYERS - 1, "down"),)


def column_bounds():
    query_end = 2 * HEADS * HEAD_DIM
    value_end = query_end + HEADS * EXPERTS * HEAD_DIM
    output_end = value_end + HEADS * EXPERTS * HEAD_DIM
    return (query_end, value_end, output_end, output_end + FF)


def column_rates(segment):
    query_end, value_end, output_end, up_end = column_bounds()
    column = jnp.arange(up_end + FF)
    inner = D ** (-0.5)
    outer = 0.7 * math.sqrt(segment) / HEAD_DIM
    rates = jnp.where(
        column < value_end,
        inner,
        jnp.where(column < output_end, outer, jnp.where(column < up_end, inner, FF ** (-0.5))),
    )
    return rates.astype(jnp.float32)


def small_rates():
    column = jnp.arange(2 * HEADS * EXPERTS + 4)
    return jnp.where(column < 2 * HEADS * EXPERTS, 0.7 * D ** (-0.5), NORM_RATE).astype(jnp.float32)


def adam_update(weight, grad, first, second, rates, decay):
    first_new = BETA_ONE * first + (1.0 - BETA_ONE) * grad
    second_new = BETA_TWO * second + (1.0 - BETA_TWO) * grad * grad
    first_hat = first_new / (1.0 - BETA_ONE**STEP)
    second_hat = second_new / (1.0 - BETA_TWO**STEP)
    new = weight - rates * (first_hat / (jnp.sqrt(second_hat) + ADAM_EPS) + decay * weight)
    return (new, first_new, second_new)


def rotary_tables(positions):
    half = HEAD_DIM // 2
    inverse = jnp.exp(-math.log(10000.0) * jnp.arange(half, dtype=jnp.float32) / half)
    angle = positions.astype(jnp.float32)[:, None] * inverse[None, :]
    return (jnp.cos(angle), jnp.sin(angle))


def layer_stats(values):
    mean = jnp.mean(values, axis=-1, keepdims=True)
    centered = values - mean
    variance = jnp.mean(centered * centered, axis=-1, keepdims=True)
    inverse = lax.rsqrt(variance + NORM_EPS)
    return (centered * inverse, inverse)


def norm_back(grad_normed, normed, inverse, gain):
    scaled = grad_normed * gain
    return inverse * (
        scaled
        - jnp.mean(scaled, axis=-1, keepdims=True)
        - normed * jnp.mean(scaled * normed, axis=-1, keepdims=True)
    )


def contract_last(left, right):
    return lax.dot_general(
        left, right, (((1,), (1,)), ((), ())), preferred_element_type=jnp.float32
    )


def contract_first(left, right):
    return lax.dot_general(
        left, right, (((0,), (0,)), ((), ())), preferred_element_type=jnp.float32
    )


AXES = ("dp", "seq", "head")


def mesh_bits():
    dims = [
        (axis, bit)
        for axis in AXES
        for bit in reversed(range(lax.axis_size(axis).bit_length() - 1))
    ]
    groups = [[index for index, (axis, _) in enumerate(dims) if axis == name] for name in AXES]
    return (dims, *groups)


def my_bits(dims):
    place = {axis: lax.axis_index(axis) for axis in AXES}
    bits = [lax.rem(place[axis] // (1 << bit), 2) for axis, bit in dims]
    partners = [
        {axis: place[axis] + (1 << bit) * (1 - 2 * bits[index])}
        for index, (axis, bit) in enumerate(dims)
    ]
    return (bits, partners)


def greet(partners):
    barrier = pltpu.get_barrier_semaphore()
    for partner in partners:
        pl.semaphore_signal(
            barrier, inc=1, device_id=partner, device_id_type=pl.DeviceIdType.MESH
        )
    pl.semaphore_wait(barrier, len(partners))


def gather_rows(share, counts, unit, name):
    dims, dp_dims, seq_dims, head_dims = mesh_bits()
    orders = (
        head_dims + dp_dims[::-1] + seq_dims,
        head_dims + dp_dims + seq_dims,
        dp_dims + head_dims + seq_dims,
    )
    depth = len(dims)
    rows, width = share.shape
    units = width // unit
    near = (11 * units + 16) // 32
    pieces, start = ([], 0)
    for which, count in ((0, near), (1, near), (2, units - 2 * near)):
        pieces.append((start, count, which))
        start += count * unit
    lag, slots = (3, 6)
    local_slots = 2
    ring = (depth + 1) * lag + local_slots + 2
    steps = max(count for _, count, _ in pieces) + lag * depth

    def kernel(*refs):
        share_ref, counts_ref, out_ref, counts_out = refs[:4]
        send_sem, recv_sem, load_sem, store_sem, small_send, small_recv, small_load = refs[4:11]
        buffers = refs[11:]
        bits, partners = my_bits(dims)

        def at_stage(which, stage):
            done = orders[which][:stage]
            return tuple(slice(None) if dim in done else bits[dim] for dim in range(depth))

        def columns(number, chunk):
            return pl.ds(pl.multiple_of(pieces[number][0] + chunk * unit, 128), unit)

        def exchange(number, stage, chunk):
            which = pieces[number][2]
            view = buffers[number].at[(lax.rem(chunk, ring),) + at_stage(which, stage)]
            slot = lax.rem(chunk, slots)
            return sent_to(
                view,
                view,
                send_sem.at[number, stage, slot],
                recv_sem.at[number, stage, slot],
                partners[orders[which][stage]],
            )

        def load(number, chunk):
            return pltpu.make_async_copy(
                share_ref.at[:, columns(number, chunk)],
                buffers[number].at[(lax.rem(chunk, ring),) + tuple(bits)],
                load_sem.at[number, lax.rem(chunk, local_slots)],
            )

        def store(number, chunk):
            return pltpu.make_async_copy(
                buffers[number].at[lax.rem(chunk, ring)],
                out_ref.at[(slice(None),) * (depth + 1) + (columns(number, chunk),)],
                store_sem.at[number, lax.rem(chunk, local_slots)],
            )

        def small(stage):
            view = counts_out.at[at_stage(0, stage)]
            return sent_to(
                view, view, small_send.at[stage], small_recv.at[stage], partners[orders[0][stage]]
            )

        own_counts = pltpu.make_async_copy(counts_ref, counts_out.at[tuple(bits)], small_load)
        own_counts.start()
        for number in range(len(pieces)):
            for chunk in range(local_slots):
                load(number, jnp.int32(chunk)).start()
        greet(partners)
        own_counts.wait()

        def body(step, carry):
            for stage in range(depth, -1, -1):
                chunk = step - lag * stage
                for number, piece in enumerate(pieces):

                    @pl.when((chunk >= 0) & (chunk < piece[1]))
                    def _(stage=stage, chunk=chunk, number=number, piece=piece):
                        if stage > 0:
                            exchange(number, stage - 1, chunk).wait()
                        else:
                            load(number, chunk).wait()

                            @pl.when(chunk + local_slots < piece[1])
                            def _():
                                load(number, chunk + local_slots).start()

                        if stage < depth:
                            exchange(number, stage, chunk).start()
                        else:

                            @pl.when(chunk >= local_slots)
                            def _():
                                store(number, chunk - local_slots).wait()

                            store(number, chunk).start()

                @pl.when(chunk == 0)
                def _(stage=stage):
                    if stage > 0:
                        small(stage - 1).wait()
                    if stage < depth:
                        small(stage).start()

            return carry

        lax.fori_loop(0, steps, body, 0)
        for number, piece in enumerate(pieces):
            for back in range(min(local_slots, piece[1])):
                store(number, jnp.int32(piece[1] - 1 - back)).wait()

    in_place = pl.BlockSpec(memory_space=pl.ANY)
    semaphores = pltpu.SemaphoreType.DMA((len(pieces), depth, slots))
    local = pltpu.SemaphoreType.DMA((len(pieces), local_slots))
    gathered, all_counts = pl.pallas_call(
        kernel,
        in_specs=[in_place] * 2,
        out_specs=[in_place] * 2,
        out_shape=[
            jax.ShapeDtypeStruct((2,) * depth + value.shape, value.dtype)
            for value in (share, counts)
        ],
        scratch_shapes=[
            semaphores,
            semaphores,
            local,
            local,
            pltpu.SemaphoreType.DMA((depth,)),
            pltpu.SemaphoreType.DMA((depth,)),
            pltpu.SemaphoreType.DMA,
        ]
        + [pltpu.VMEM((ring,) + (2,) * depth + (rows, unit), share.dtype) for _ in pieces],
        compiler_params=pltpu.CompilerParams(
            collective_id=name, has_side_effects=True, vmem_limit_bytes=48 << 20
        ),
    )(share, counts)
    return (gathered.reshape(-1, width), all_counts.reshape(-1, counts.shape[1]))


def halving_plan(width):
    dims, dp_dims, seq_dims, head_dims = mesh_bits()
    first = seq_dims[::-1]
    orders = (
        (0, width // 2, first + dp_dims[::-1] + head_dims[::-1]),
        (width // 2, width // 4, first + dp_dims + head_dims[::-1]),
        (3 * width // 4, width // 4, first + head_dims[::-1] + dp_dims[::-1]),
    )
    stages = []
    for stage in range(len(dims)):
        parts = []
        for start, count, order in orders:
            left = [dim for dim in range(len(dims)) if dim not in order[:stage]]
            if parts and parts[-1][2:] == (order[stage], left):
                parts[-1] = (parts[-1][0], parts[-1][1] + count, order[stage], left)
            else:
                parts.append((start, count, order[stage], left))
        stages.append(parts)
    lags = [1 if stage < len(seq_dims) else 2 for stage in range(len(dims))]
    return dims, stages, lags


def reduce_weight_grads(lefts, segments, doubles, extras, width):
    dims, stages, lags = halving_plan(width)
    depth = len(dims)
    half = width // 2
    tokens, model = lefts[0].shape
    rows = model >> depth
    firsts = [0]
    for _, _, _, count in segments:
        firsts.append(firsts[-1] + count)
    chunks = firsts[-1] // 2
    spots = [(where // 2, where % 2 * half) for _, where in extras]
    starts = [sum(lags[:stage]) for stage in range(depth + 1)]
    rights = [right for _, right, _, _ in segments] + [right for _, _, _, right in doubles]
    count_lefts, count_rights, count_extras = (len(lefts), len(rights), len(extras))
    first_use = [
        min(firsts[index] // 2 for index, segment in enumerate(segments) if segment[0] == left)
        for left in range(count_lefts)
    ]
    for where, _, left, _ in doubles:
        first_use[left] = min(first_use[left], where // 2)

    def kernel(*refs):
        left_refs = refs[:count_lefts]
        right_refs = refs[count_lefts : count_lefts + count_rights]
        rest = refs[count_lefts + count_rights :]
        added, rest = (rest[:count_extras], rest[count_extras:])
        out_ref, left_buf, turned, right_buf, double_buf, left_sem, right_sem, double_sem = rest[:8]
        pool = iter(rest[8:])
        buffers = [[tuple(next(pool) for _ in range(4)) for _ in parts] for parts in stages]
        step = pl.program_id(0)
        bits, partners = my_bits(dims)

        def exchange(stage, part, slot):
            start, count, dim, left = stages[stage][part]
            own, got, send_sem, recv_sem = buffers[stage][part]
            lead = (slot,) + (slice(None),) * left.index(dim)
            return pltpu.make_async_remote_copy(
                src_ref=own.at[lead + (1 - bits[dim],)],
                dst_ref=got.at[slot],
                send_sem=send_sem.at[slot],
                recv_sem=recv_sem.at[slot],
                device_id=partners[dim],
                device_id_type=pl.DeviceIdType.MESH,
            )

        def load_left(index):
            return pltpu.make_async_copy(left_refs[index], left_buf.at[index], left_sem.at[index])

        def load_right(index, at, chunk, side):
            columns = pl.ds(pl.multiple_of(at * half, half), half)
            slot = lax.rem(chunk, 2)
            return pltpu.make_async_copy(
                right_refs[index].at[:, columns],
                right_buf.at[slot, side],
                right_sem.at[slot, side],
            )

        def load_double(index):
            return pltpu.make_async_copy(
                right_refs[len(segments) + index].at[:, 0:half], double_buf, double_sem
            )

        def prefetch(chunk):
            for side in range(2):
                place = 2 * chunk + side
                for index, (_, _, begin, _) in enumerate(segments):

                    @pl.when((place >= firsts[index]) & (place < firsts[index + 1]))
                    def _(index=index, begin=begin, place=place, side=side):
                        load_right(index, place - firsts[index] + begin, chunk, side).start()

            for index, (where, _, _, _) in enumerate(doubles):

                @pl.when(chunk == where // 2)
                def _(index=index):
                    load_double(index).start()

        @pl.when(step == 0)
        def _():
            for index in range(count_lefts):
                load_left(index).start()
            prefetch(step)
            greet(partners)

        @pl.when(step + 1 < chunks)
        def _():
            prefetch(step + 1)

        for stage in range(depth, -1, -1):
            chunk = step - starts[stage]

            @pl.when((chunk >= 0) & (chunk < chunks))
            def _(stage=stage, chunk=chunk):
                if stage == 0:
                    slot = lax.rem(chunk, 2 * lags[0])
                    near = lax.rem(chunk, 2)
                    own = buffers[0][0][0]
                    for index in range(count_lefts):

                        @pl.when(chunk == first_use[index])
                        def _(index=index):
                            load_left(index).wait()
                            turned[index] = left_buf[index].T

                    for side in range(2):
                        place = 2 * chunk + side
                        which = jnp.int32(segments[0][0])
                        for index, segment in enumerate(segments):
                            which = jnp.where(place >= firsts[index], segment[0], which)
                        load_right(0, 0, chunk, side).wait()
                        for where, kept, _, _ in doubles:
                            if where % 2 == side:

                                @pl.when(chunk == where // 2)
                                def _(kept=kept, side=side):
                                    right_buf[near, side, :, kept:] = jnp.zeros(
                                        (tokens, half - kept), jnp.bfloat16
                                    )

                        product = jnp.dot(
                            turned[which],
                            right_buf[near, side],
                            preferred_element_type=jnp.float32,
                        )
                        own[(slot, Ellipsis, slice(side * half, side * half + half))] = (
                            product.astype(jnp.bfloat16).reshape((2,) * depth + (rows, half))
                        )
                    for index, (where, _, left, _) in enumerate(doubles):

                        @pl.when(chunk == where // 2)
                        def _(index=index, where=where, left=left):
                            load_double(index).wait()
                            product = jnp.dot(
                                turned[left], double_buf[...], preferred_element_type=jnp.float32
                            ).reshape((2,) * depth + (rows, half))
                            begin = where % 2 * half
                            at = (slot, Ellipsis, slice(begin, begin + half))
                            own[at] = (own[at].astype(jnp.float32) + product).astype(jnp.bfloat16)

                    for index in range(count_extras):

                        @pl.when(chunk == spots[index][0])
                        def _(index=index):
                            at = (slot, Ellipsis, slice(spots[index][1], spots[index][1] + 128))
                            total = own[at].astype(jnp.float32) + added[index][...].astype(
                                jnp.float32
                            )
                            own[at] = total.astype(jnp.bfloat16)

                else:
                    back = lax.rem(chunk, 2 * lags[stage - 1])
                    for part, (start, count, dim, left) in enumerate(stages[stage - 1]):
                        exchange(stage - 1, part, back).wait()
                        own, got = buffers[stage - 1][part][:2]
                        lead = (back,) + (slice(None),) * left.index(dim)
                        total = own[lead + (bits[dim],)].astype(jnp.float32) + got[back].astype(
                            jnp.float32
                        )
                        if stage == depth:
                            out_ref[:, start : start + count] = total
                            continue
                        slot = lax.rem(chunk, 2 * lags[stage])
                        low = total.astype(jnp.bfloat16)
                        for other, (begin, length, _, kept) in enumerate(stages[stage]):
                            lo, hi = max(start, begin), min(start + count, begin + length)
                            if lo < hi:
                                at = (slot,) + (slice(None),) * (len(kept) + 1)
                                buffers[stage][other][0][at + (slice(lo - begin, hi - begin),)] = (
                                    low[..., lo - start : hi - start]
                                )
                if stage < depth:
                    for part in range(len(stages[stage])):
                        exchange(stage, part, lax.rem(chunk, 2 * lags[stage])).start()

    scratch = [
        pltpu.VMEM((count_lefts, tokens, model), jnp.bfloat16),
        pltpu.VMEM((count_lefts, model, tokens), jnp.bfloat16),
        pltpu.VMEM((2, 2, tokens, half), jnp.bfloat16),
        pltpu.VMEM((tokens, half), jnp.bfloat16),
        pltpu.SemaphoreType.DMA((count_lefts,)),
        pltpu.SemaphoreType.DMA((2, 2)),
        pltpu.SemaphoreType.DMA,
    ]
    for stage, parts in enumerate(stages):
        slots = 2 * lags[stage]
        for start, count, dim, left in parts:
            scratch += [
                pltpu.VMEM((slots,) + (2,) * len(left) + (rows, count), jnp.bfloat16),
                pltpu.VMEM((slots,) + (2,) * (len(left) - 1) + (rows, count), jnp.bfloat16),
                pltpu.SemaphoreType.DMA((slots,)),
                pltpu.SemaphoreType.DMA((slots,)),
            ]
    in_place = pl.BlockSpec(memory_space=pl.ANY)
    whole = [value.reshape((2,) * depth + (rows, 128)) for value, _ in extras]
    return pl.pallas_call(
        kernel,
        grid=(chunks + starts[depth],),
        in_specs=[in_place] * (count_lefts + count_rights)
        + [pl.BlockSpec(value.shape, lambda step: (0,) * (depth + 2)) for value in whole],
        out_specs=pl.BlockSpec(
            (rows, width), lambda step: (0, jnp.clip(step - starts[depth], 0, chunks - 1))
        ),
        out_shape=jax.ShapeDtypeStruct((rows, chunks * width), jnp.float32),
        scratch_shapes=scratch,
        compiler_params=pltpu.CompilerParams(
            collective_id=1,
            has_side_effects=True,
            vmem_limit_bytes=48 << 20,
            dimension_semantics=("arbitrary",),
        ),
    )(*lefts, *rights, *whole)


def reduction_order(tensor):
    dp, seq = (lax.axis_size("dp"), lax.axis_size("seq"))
    count, width = tensor.shape
    split = tensor.reshape(count, dp, seq, width // (dp * seq))
    return split.transpose(0, 2, 1, 3).reshape(count, width)


def reduced_natively(left, right):
    share = contract_first(reduction_order(left), right).astype(jnp.bfloat16)
    for axis in ("seq", "dp", "head"):
        share = lax.psum_scatter(share, axis, scatter_dimension=0, tiled=True)
    return share


def lane_whole(count):
    return count + (-count) % 128


def padded(pieces, width):
    have = sum(piece.shape[1] for piece in pieces)
    fill = jnp.zeros((pieces[0].shape[0], width - have), pieces[0].dtype)
    return jnp.concatenate(list(pieces) + [fill], axis=1)


LANES = 128
QUERY_TILE = 256


def swap_halves(tensor):
    half = HEAD_DIM // 2
    return jnp.concatenate([tensor[:, half:], tensor[:, :half]], axis=1)


def lane_filled(tensor):
    fill = jnp.zeros((tensor.shape[0], LANES - tensor.shape[1]), tensor.dtype)
    return jnp.concatenate([tensor, fill], axis=1)


def weights_block(keys_mem, keys_own, query, start, first, segment, length):
    contract = (((1,), (1,)), ((), ()))
    raw = jnp.concatenate(
        [
            lax.dot_general(keys, query, contract, preferred_element_type=jnp.float32)
            for keys in (keys_mem, keys_own)
        ],
        axis=0,
    )
    key_pos = start - segment + lax.broadcasted_iota(jnp.int32, raw.shape, 0)
    query_pos = start + first + lax.broadcasted_iota(jnp.int32, raw.shape, 1)
    used = (key_pos < length) & (key_pos < query_pos) & (key_pos >= 0)
    allowed = used | (key_pos == query_pos)
    scores = jnp.where(allowed, raw * HEAD_DIM ** (-0.5), MASKED)
    weights = jnp.exp(scores - jnp.max(scores, axis=0, keepdims=True))
    return weights * (1.0 / jnp.sum(weights, axis=0, keepdims=True))


def contract_rows(left, right):
    return lax.dot_general(
        left, right, (((0,), (0,)), ((), ())), preferred_element_type=jnp.float32
    )


def across(axis, offset):
    size = lax.axis_size(axis)
    return {axis: lax.rem(lax.axis_index(axis) + offset + size, size)}


def sent_to(source, target, send_sem, recv_sem, device):
    return pltpu.make_async_remote_copy(
        src_ref=source,
        dst_ref=target,
        send_sem=send_sem,
        recv_sem=recv_sem,
        device_id=device,
        device_id_type=pl.DeviceIdType.MESH,
    )


def meet(memory_step):
    barrier = pltpu.get_barrier_semaphore()
    heads = lax.axis_size("head")
    writers = [across("head", step) for step in range(1, heads)]
    writers.append(across("seq", -memory_step))
    for device in writers:
        pl.semaphore_signal(barrier, inc=1, device_id=device, device_id_type=pl.DeviceIdType.MESH)
    pl.semaphore_wait(barrier, len(writers))


def gate_values(entered_ref, chosen_ref, rows):
    at = column_bounds()[1]
    logits = entered_ref[rows, at : at + 2 * HEADS * EXPERTS]
    prob = 1.0 / (1.0 + jnp.exp(-logits))
    return (prob, prob * chosen_ref[rows, :])


def column(tensor, index):
    return tensor[:, index : index + 1]


def attention_forward(entered, chosen, turn_cos, turn_sin, lengths, shift, name):
    seq_count = lengths.shape[0]
    tokens = entered.shape[0]
    sub = tokens // seq_count
    heads = lax.axis_size("head")
    segment = heads * sub
    query_end = column_bounds()[0]
    sides = range(1, heads)

    def kernel(*refs):
        length_ref, entered_ref, chosen_ref, cos_ref, sin_ref = refs[:5]
        mixed_ref, attended_ref, query_ref, key_ref, value_ref = refs[5:10]
        out_buf, heads_buf, mem_buf, done_buf, back_buf = refs[10:15]
        out_sem, in_sem, mem_sem, done_sem, back_sem = refs[15:]
        me = lax.axis_index("head")
        start = lax.axis_index("seq") * segment
        turn, wind = (cos_ref[...], sin_ref[...])

        def outward(b, side):
            there = across("head", side)
            return sent_to(
                out_buf.at[b, there["head"]],
                heads_buf.at[b, :, me],
                out_sem.at[b, side - 1],
                in_sem.at[b, side - 1],
                there,
            )

        def onward(b):
            return sent_to(
                heads_buf.at[b, 1:3],
                mem_buf.at[b],
                mem_sem.at[0, b],
                mem_sem.at[1, b],
                across("seq", 1),
            )

        def homeward(b, side):
            there = across("head", side)
            return sent_to(
                done_buf.at[b, there["head"]],
                back_buf.at[b, me],
                done_sem.at[b, side - 1],
                back_sem.at[b, side - 1],
                there,
            )

        meet(1)
        gates_of = []
        for b in range(seq_count):
            rows = slice(b * sub, (b + 1) * sub)
            gates = gate_values(entered_ref, chosen_ref, rows)[1]
            gates_of.append(gates)
            for head in range(HEADS):
                for kind in range(2):
                    at = (kind * HEADS + head) * HEAD_DIM
                    vector = entered_ref[rows, at : at + HEAD_DIM]
                    turned = vector * turn + swap_halves(vector) * wind
                    out_buf[b, head, kind] = lane_filled(turned).astype(jnp.bfloat16)
                value = jnp.zeros((sub, HEAD_DIM), jnp.float32)
                for expert in range(EXPERTS):
                    index = head * EXPERTS + expert
                    at = query_end + index * HEAD_DIM
                    value += column(gates, index) * entered_ref[rows, at : at + HEAD_DIM]
                out_buf[b, head, 2] = lane_filled(value).astype(jnp.bfloat16)
            for side in sides:
                outward(b, side).start()
            for kind in range(3):
                heads_buf[b, kind, me] = out_buf[b, me, kind]
        for b in range(seq_count):
            for side in sides:
                outward(b, side).wait_recv()
            onward(b).start()
        for b in range(seq_count):
            onward(b).wait_recv()
            keys_own = heads_buf[b, 1].reshape(segment, LANES)
            values = jnp.concatenate(
                [mem_buf[b, 1].reshape(segment, LANES), heads_buf[b, 2].reshape(segment, LANES)],
                axis=0,
            )
            for first in range(0, segment, QUERY_TILE):
                tile = slice(first // sub, (first + QUERY_TILE) // sub)
                query = heads_buf[b, 0, tile].reshape(QUERY_TILE, LANES)
                probs = weights_block(
                    mem_buf[b, 0].reshape(segment, LANES),
                    keys_own,
                    query,
                    start,
                    first,
                    segment,
                    length_ref[b],
                ).astype(jnp.bfloat16)
                attended = contract_rows(values, probs).T.astype(jnp.bfloat16)
                done_buf[b, tile] = attended.reshape(QUERY_TILE // sub, sub, LANES)
            for side in sides:
                homeward(b, side).start()
            back_buf[b, me] = done_buf[b, me]
        for b in range(seq_count):
            query_ref[b] = heads_buf[b, 0]
            key_ref[b, 0] = mem_buf[b, 0]
            key_ref[b, 1] = heads_buf[b, 1]
            value_ref[b, 0] = mem_buf[b, 1]
            value_ref[b, 1] = heads_buf[b, 2]
        mixed_ref[:, :shift] = jnp.zeros((tokens, shift), jnp.bfloat16)
        for b in range(seq_count):
            rows = slice(b * sub, (b + 1) * sub)
            for side in sides:
                homeward(b, side).wait_recv()
            for head in range(HEADS):
                attended = back_buf[b, head]
                attended_ref[rows, head * LANES : (head + 1) * LANES] = attended
                wide = attended.astype(jnp.float32)[:, :HEAD_DIM]
                for expert in range(EXPERTS):
                    index = head * EXPERTS + expert
                    gate = column(gates_of[b], HEADS * EXPERTS + index)
                    at = shift + index * HEAD_DIM
                    mixed_ref[rows, at : at + HEAD_DIM] = (
                        gate * wide
                    ).astype(jnp.bfloat16)
        for b in range(seq_count):
            onward(b).wait_send()
            for side in sides:
                outward(b, side).wait_send()
                homeward(b, side).wait_send()

    def shape(*dims):
        return jax.ShapeDtypeStruct(dims, jnp.bfloat16)

    vmem = pl.BlockSpec(memory_space=pltpu.VMEM)
    paired = pltpu.SemaphoreType.DMA((seq_count, heads - 1))
    return pl.pallas_call(
        kernel,
        in_specs=[pl.BlockSpec(memory_space=pltpu.SMEM)] + [vmem] * 4,
        out_specs=[vmem] * 5,
        out_shape=[
            shape(tokens, shift + HEADS * EXPERTS * HEAD_DIM),
            shape(tokens, HEADS * LANES),
            shape(seq_count, heads, sub, LANES),
            shape(seq_count, 2, heads, sub, LANES),
            shape(seq_count, 2, heads, sub, LANES),
        ],
        scratch_shapes=[
            pltpu.VMEM((seq_count, heads, 3, sub, LANES), jnp.bfloat16),
            pltpu.VMEM((seq_count, 3, heads, sub, LANES), jnp.bfloat16),
            pltpu.VMEM((seq_count, 2, heads, sub, LANES), jnp.bfloat16),
            pltpu.VMEM((seq_count, heads, sub, LANES), jnp.bfloat16),
            pltpu.VMEM((seq_count, heads, sub, LANES), jnp.bfloat16),
            paired,
            paired,
            pltpu.SemaphoreType.DMA((2, seq_count)),
            paired,
            paired,
        ],
        compiler_params=pltpu.CompilerParams(
            collective_id=name, has_side_effects=True, vmem_limit_bytes=40 << 20
        ),
    )(lengths, entered, chosen, turn_cos, turn_sin)


def attention_backward(
    grad_mixed, attended, entered, chosen, turn_cos, turn_sin, lengths, saved, shift, grad_width, name
):
    query, keys, values = saved
    seq_count = lengths.shape[0]
    tokens = entered.shape[0]
    sub = tokens // seq_count
    heads = lax.axis_size("head")
    segment = heads * sub
    query_end, value_end = column_bounds()[:2]
    router_cols = 2 * HEADS * EXPERTS
    sides = range(1, heads)

    def kernel(*refs):
        length_ref, grad_ref, attended_ref, entered_ref, chosen_ref, cos_ref, sin_ref = refs[:7]
        query_ref, key_ref, value_ref, result_ref, logit_ref = refs[7:12]
        out_buf, heads_buf, mem_out, mem_in, own_buf, done_buf, back_buf = refs[12:19]
        out_sem, in_sem, mem_sem, query_sem, done_sem, back_sem = refs[19:]
        me = lax.axis_index("head")
        start = lax.axis_index("seq") * segment
        turn, wind = (cos_ref[...], sin_ref[...])

        def outward(b, side):
            there = across("head", side)
            return sent_to(
                out_buf.at[b, there["head"]],
                heads_buf.at[b, me],
                out_sem.at[b, side - 1],
                in_sem.at[b, side - 1],
                there,
            )

        def onward(b):
            return sent_to(
                mem_out.at[b], mem_in.at[b], mem_sem.at[0, b], mem_sem.at[1, b], across("seq", -1)
            )

        def queries_home(b, side):
            there = across("head", side)
            return sent_to(
                done_buf.at[b, there["head"], 0],
                back_buf.at[b, me, 0],
                query_sem.at[0, b, side - 1],
                query_sem.at[1, b, side - 1],
                there,
            )

        def homeward(b, side):
            there = across("head", side)
            return sent_to(
                done_buf.at[b, there["head"], 1:3],
                back_buf.at[b, me, 1:3],
                done_sem.at[b, side - 1],
                back_sem.at[b, side - 1],
                there,
            )

        def join_memory(b):
            onward(b).wait_recv()
            for kind in range(2):
                total = own_buf[b, kind] + mem_in[b, kind].astype(jnp.float32)
                done_buf[b, :, kind + 1] = total.astype(jnp.bfloat16).reshape(heads, sub, LANES)
            for side in sides:
                homeward(b, side).start()
            back_buf[b, me] = done_buf[b, me]

        meet(-1)
        lane = lax.broadcasted_iota(jnp.int32, (sub, router_cols), 1)
        gate_grads, probs_of, gates_of = ([], [], [])
        for b in range(seq_count):
            rows = slice(b * sub, (b + 1) * sub)
            prob, gates = gate_values(entered_ref, chosen_ref, rows)
            probs_of.append(prob)
            gates_of.append(gates)
            gate_grad = jnp.zeros((sub, router_cols), jnp.float32)
            for head in range(HEADS):
                seen = attended_ref[rows, head * LANES : head * LANES + HEAD_DIM].astype(
                    jnp.float32
                )
                total = jnp.zeros((sub, HEAD_DIM), jnp.float32)
                for expert in range(EXPERTS):
                    index = head * EXPERTS + expert
                    at = shift + index * HEAD_DIM
                    part = grad_ref[rows, at : at + HEAD_DIM]
                    total += column(gates, HEADS * EXPERTS + index) * part
                    gate_grad = jnp.where(
                        lane == HEADS * EXPERTS + index,
                        jnp.sum(part * seen, axis=1, keepdims=True),
                        gate_grad,
                    )
                out_buf[b, head] = lane_filled(total).astype(jnp.bfloat16)
            gate_grads.append(gate_grad)
            for side in sides:
                outward(b, side).start()
            heads_buf[b, me] = out_buf[b, me]
        for b in range(seq_count):
            for side in sides:
                outward(b, side).wait_recv()
            keys_mem = key_ref[b, 0].reshape(segment, LANES)
            keys_own = key_ref[b, 1].reshape(segment, LANES)
            keys_all = jnp.concatenate([keys_mem, keys_own], axis=0)
            values_all = jnp.concatenate(
                [value_ref[b, 0].reshape(segment, LANES), value_ref[b, 1].reshape(segment, LANES)],
                axis=0,
            )
            grad_keys = jnp.zeros((2 * segment, LANES), jnp.float32)
            grad_values = jnp.zeros((2 * segment, LANES), jnp.float32)
            for first in range(0, segment, QUERY_TILE):
                tile = slice(first // sub, (first + QUERY_TILE) // sub)
                here = query_ref[b, tile].reshape(QUERY_TILE, LANES)
                arrived = heads_buf[b, tile].reshape(QUERY_TILE, LANES)
                probs = weights_block(
                    keys_mem, keys_own, here, start, first, segment, length_ref[b]
                )
                grad_probs = contract_last(values_all, arrived)
                delta = jnp.sum(probs * grad_probs, axis=0, keepdims=True)
                grad_raw = (probs * (grad_probs - delta) * HEAD_DIM ** (-0.5)).astype(
                    jnp.bfloat16
                )
                grad_values += jnp.dot(
                    probs.astype(jnp.bfloat16), arrived, preferred_element_type=jnp.float32
                )
                grad_keys += jnp.dot(grad_raw, here, preferred_element_type=jnp.float32)
                grad_query = contract_rows(keys_all, grad_raw).T.astype(jnp.bfloat16)
                done_buf[b, tile, 0] = grad_query.reshape(QUERY_TILE // sub, sub, LANES)
                if b > 0 and first == 0:
                    join_memory(b - 1)
            for kind, grads in enumerate((grad_keys, grad_values)):
                mem_out[b, kind] = grads[:segment].astype(jnp.bfloat16)
                own_buf[b, kind] = grads[segment:]
            onward(b).start()
            for side in sides:
                queries_home(b, side).start()
        join_memory(seq_count - 1)
        used = value_end + router_cols
        result_ref[:, used:] = jnp.zeros((tokens, grad_width - used), jnp.bfloat16)
        logit_ref[:, router_cols:] = jnp.zeros((tokens, CHUNK // 2 - router_cols), jnp.bfloat16)
        for b in range(seq_count):
            rows = slice(b * sub, (b + 1) * sub)
            for side in sides:
                queries_home(b, side).wait_recv()
                homeward(b, side).wait_recv()
            gate_grad = gate_grads[b]
            for head in range(HEADS):
                for kind in range(2):
                    vector = back_buf[b, head, kind].astype(jnp.float32)[:, :HEAD_DIM]
                    turned = vector * turn - swap_halves(vector) * wind
                    at = (kind * HEADS + head) * HEAD_DIM
                    result_ref[rows, at : at + HEAD_DIM] = turned.astype(jnp.bfloat16)
                grad_value = back_buf[b, head, 2].astype(jnp.float32)[:, :HEAD_DIM]
                for expert in range(EXPERTS):
                    index = head * EXPERTS + expert
                    at = query_end + index * HEAD_DIM
                    gate_grad = jnp.where(
                        lane == index,
                        jnp.sum(
                            entered_ref[rows, at : at + HEAD_DIM] * grad_value,
                            axis=1,
                            keepdims=True,
                        ),
                        gate_grad,
                    )
                    result_ref[rows, at : at + HEAD_DIM] = (
                        column(gates_of[b], index) * grad_value
                    ).astype(jnp.bfloat16)
            prob = probs_of[b]
            grad_logit = (gate_grad * chosen_ref[rows, :] * prob * (1.0 - prob)).astype(
                jnp.bfloat16
            )
            result_ref[rows, value_end:used] = grad_logit
            logit_ref[rows, :router_cols] = grad_logit
        for b in range(seq_count):
            onward(b).wait_send()
            for side in sides:
                outward(b, side).wait_send()
                queries_home(b, side).wait_send()
                homeward(b, side).wait_send()

    vmem = pl.BlockSpec(memory_space=pltpu.VMEM)
    paired = pltpu.SemaphoreType.DMA((seq_count, heads - 1))
    return pl.pallas_call(
        kernel,
        in_specs=[pl.BlockSpec(memory_space=pltpu.SMEM)] + [vmem] * 9,
        out_specs=[vmem] * 2,
        out_shape=[
            jax.ShapeDtypeStruct((tokens, count), jnp.bfloat16)
            for count in (grad_width, CHUNK // 2)
        ],
        scratch_shapes=[
            pltpu.VMEM((seq_count, heads, sub, LANES), jnp.bfloat16),
            pltpu.VMEM((seq_count, heads, sub, LANES), jnp.bfloat16),
            pltpu.VMEM((seq_count, 2, segment, LANES), jnp.bfloat16),
            pltpu.VMEM((seq_count, 2, segment, LANES), jnp.bfloat16),
            pltpu.VMEM((seq_count, 2, segment, LANES), jnp.float32),
            pltpu.VMEM((seq_count, heads, 3, sub, LANES), jnp.bfloat16),
            pltpu.VMEM((seq_count, heads, 3, sub, LANES), jnp.bfloat16),
            paired,
            paired,
            pltpu.SemaphoreType.DMA((2, seq_count)),
            pltpu.SemaphoreType.DMA((2, seq_count, heads - 1)),
            paired,
            paired,
        ],
        compiler_params=pltpu.CompilerParams(
            collective_id=name, has_side_effects=True, vmem_limit_bytes=48 << 20
        ),
    )(lengths, grad_mixed, attended, entered, chosen, turn_cos, turn_sin, query, keys, values)


def gelu_tanh(values):
    return jax.nn.gelu(values, approximate=True)


def local(
    inputs,
    cotangent,
    routes,
    lengths,
    matrix,
    matrix_first,
    matrix_second,
    small,
    small_first,
    small_second,
):
    head_count = lax.axis_size("head")
    seq_count, sub_rows, width = inputs.shape
    segment = sub_rows * head_count
    tokens = seq_count * sub_rows
    router_cols = 2 * HEADS * EXPERTS
    group = HEADS * EXPERTS
    query_end, value_end, output_end, up_end = column_bounds()
    seq_start = lax.axis_index("seq") * segment
    positions = (
        seq_start + lax.axis_index("head") * sub_rows + jnp.arange(sub_rows, dtype=jnp.int32)
    )
    valid = (positions[None, :] < lengths[:, None]).astype(jnp.float32)
    cosines, sines = rotary_tables(positions)
    turn_cos = jnp.concatenate([cosines, cosines], axis=1)
    turn_sin = jnp.concatenate([-sines, sines], axis=1)
    chosen = jnp.sum(
        (routes[..., None] == jnp.arange(EXPERTS, dtype=jnp.int32)).astype(jnp.float32), axis=-2
    )
    load_part = jnp.sum(chosen * valid[None, :, :, None, None, None], axis=(1, 2))
    in_width = lane_whole(value_end + router_cols + 4)
    half = CHUNK // 2
    shift = value_end % half
    in_grad_width = value_end + (-value_end) % half
    out_width = shift + output_end - value_end
    matrix_low = matrix.astype(jnp.bfloat16)
    small_low = small.astype(jnp.bfloat16)
    in_low = [
        padded([matrix_low[layer, :, :value_end], small_low[layer]], in_width)
        for layer in range(LAYERS)
    ]
    out_low = [
        jnp.pad(matrix_low[layer, :, value_end:output_end], ((0, 0), (shift, 0)))
        for layer in range(LAYERS)
    ]
    ffn_low = [matrix_low[layer, :, output_end:] for layer in range(LAYERS)]
    size = load_part.size
    counts = jnp.pad(load_part.reshape(-1), (0, (-size) % 1024)).reshape(8, -1)
    early = []
    for layer in range(LAYERS):
        early += [in_low[layer], out_low[layer]] + ([ffn_low[layer]] if layer + 1 < LAYERS else [])
    gathered, counts = gather_rows(jnp.concatenate(early, axis=1), counts, 128, 2)
    counts, late = lax.optimization_barrier((counts, ffn_low[-1]))
    loads = jnp.sum(counts.reshape(-1, size + (-size) % 1024), axis=0)[:size].reshape(
        load_part.shape
    )
    late = lax.all_gather(late, ("dp", "seq", "head"), axis=0, tiled=True)
    pieces, start = ([], 0)
    for value in early:
        pieces.append(gathered[:, start : start + value.shape[1]])
        start += value.shape[1]
    pieces.append(late)
    in_ws, out_ws, ffn_ws = (pieces[0::3], pieces[1::3], pieces[2::3])
    hidden = inputs.astype(jnp.float32).reshape(tokens, width)
    kept = []
    for layer in range(LAYERS):
        in_w, out_w, ffn_w = (in_ws[layer], out_ws[layer], ffn_ws[layer])
        gains = in_w[:, value_end + router_cols : value_end + router_cols + 4].astype(jnp.float32)
        normed_one, inverse_one = layer_stats(hidden)
        first_in = (normed_one * gains[:, 0] + gains[:, 1]).astype(jnp.bfloat16)
        entered = jnp.dot(first_in, in_w, preferred_element_type=jnp.float32)
        chosen_here = chosen[layer].reshape(tokens, router_cols)
        mixed, attended, *saved = attention_forward(
            entered,
            chosen_here,
            turn_cos,
            turn_sin,
            lengths,
            shift,
            3 + layer,
        )
        residual = hidden + contract_last(mixed, out_w)
        normed_two, inverse_two = layer_stats(residual)
        second_in = (normed_two * gains[:, 2] + gains[:, 3]).astype(jnp.bfloat16)
        up = jnp.dot(second_in, ffn_w[:, :FF], preferred_element_type=jnp.float32)
        act = gelu_tanh(up).astype(jnp.bfloat16)
        hidden = residual + contract_last(act, ffn_w[:, FF:])
        kept.append(
            (
                normed_one,
                inverse_one,
                first_in,
                entered,
                chosen_here,
                mixed,
                attended,
                saved,
                normed_two,
                inverse_two,
                second_in,
                up,
                act,
            )
        )
    output = hidden.reshape(seq_count, sub_rows, width).astype(jnp.bfloat16)
    grad_hidden = (cotangent.astype(jnp.float32) * valid[:, :, None]).reshape(tokens, width)
    lefts, segments, doubles, extras, native, bases = ([], [], [], [], {}, {})
    for layer in reversed(range(LAYERS)):
        (
            normed_one,
            inverse_one,
            first_in,
            entered,
            chosen_here,
            mixed,
            attended,
            saved,
            normed_two,
            inverse_two,
            second_in,
            up,
            act,
        ) = kept[layer]
        in_w, out_w, ffn_w = (in_ws[layer], out_ws[layer], ffn_ws[layer])
        gains = in_w[:, value_end + router_cols : value_end + router_cols + 4].astype(jnp.float32)
        grad_low = grad_hidden.astype(jnp.bfloat16)
        grad_act = jnp.dot(grad_low, ffn_w[:, FF:], preferred_element_type=jnp.float32)
        gelu_value, gelu_pull = jax.vjp(gelu_tanh, up)
        grad_up = gelu_pull(grad_act)[0].astype(jnp.bfloat16)
        grad_second = contract_last(grad_up, ffn_w[:, :FF])
        gain_two_grad = jnp.sum(grad_second * normed_two, axis=0)
        bias_two_grad = jnp.sum(grad_second, axis=0)
        grad_residual = grad_hidden + norm_back(grad_second, normed_two, inverse_two, gains[:, 2])
        residual_low = grad_residual.astype(jnp.bfloat16)
        grad_in, grad_logit = attention_backward(
            jnp.dot(residual_low, out_w, preferred_element_type=jnp.float32),
            attended,
            entered,
            chosen_here,
            turn_cos,
            turn_sin,
            lengths,
            saved,
            shift,
            in_grad_width,
            3 + LAYERS + layer,
        )
        grad_first = contract_last(grad_in[:, :in_width], in_w)
        gain_one_grad = jnp.sum(grad_first * normed_one, axis=0)
        bias_one_grad = jnp.sum(grad_first, axis=0)
        grad_hidden = grad_residual + norm_back(grad_first, normed_one, inverse_one, gains[:, 0])
        norm_grads = jnp.stack(
            [gain_one_grad, bias_one_grad, gain_two_grad, bias_two_grad], axis=1
        ).astype(jnp.bfloat16)
        norm_grads = jnp.pad(norm_grads, ((0, 0), (router_cols, 128 - 4 - router_cols)))
        base = sum(segment[3] for segment in segments)
        bases[layer] = base * half
        one = len(lefts)
        lefts += [first_in, residual_low]
        in_halves = grad_in.shape[1] // half
        segments += [
            (one, grad_in, 0, in_halves),
            (one + 1, mixed, 1, mixed.shape[1] // half - 1),
        ]
        doubles.append((base + in_halves - 1, shift, one + 1, mixed))
        for kind, pair in (("up", (second_in, grad_up)), ("down", (grad_low, act))):
            if (layer, kind) in NATIVE:
                native[layer, kind] = reduced_natively(*pair)
            else:
                segments.append((len(lefts), pair[1], 0, FF // half))
                lefts.append(pair[0])
        extras.append((norm_grads, sum(segment[3] for segment in segments)))
        segments.append((one, grad_logit, 0, 1))
    names = list(native)
    begun = segments[-1][1]
    partial, begun = lax.optimization_barrier(([native[name] for name in names], begun))
    segments[-1] = (segments[-1][0], begun) + segments[-1][2:]
    for name, value in zip(names, partial):
        native[name] = value.astype(jnp.float32)
    reduced = reduce_weight_grads(lefts, segments, doubles, extras, CHUNK)
    matrix_rows = [None] * LAYERS
    small_rows = [None] * LAYERS
    for layer in range(LAYERS):
        base = bases[layer]
        rest = [native[layer, kind] for kind in ("up", "down") if (layer, kind) in NATIVE]
        used = output_end + FF * (2 - len(rest))
        matrix_rows[layer] = jnp.concatenate([reduced[:, base : base + used]] + rest, axis=1)
        small_rows[layer] = reduced[:, base + used : base + used + router_cols + 4]
    input_grad = grad_hidden.reshape(seq_count, sub_rows, width).astype(jnp.bfloat16)
    matrix_grad = jnp.stack(matrix_rows, axis=0)
    small_grad = jnp.stack(small_rows, axis=0)
    matrix_new, matrix_first_new, matrix_second_new = adam_update(
        matrix, matrix_grad, matrix_first, matrix_second, column_rates(segment), WEIGHT_DECAY
    )
    small_new, small_first_new, small_second_new = adam_update(
        small, small_grad, small_first, small_second, small_rates(), 0.0
    )
    return (
        output,
        input_grad,
        matrix_grad,
        matrix_new,
        matrix_new.astype(jnp.bfloat16),
        matrix_first_new,
        matrix_second_new,
        small_grad,
        small_new,
        small_new.astype(jnp.bfloat16),
        small_first_new,
        small_second_new,
        loads,
    )


def solution(mesh):
    in_specs = (
        P("dp", ("seq", "head"), None),
        P("dp", ("seq", "head"), None),
        P(None, "dp", ("seq", "head"), None, None, None),
        P("dp"),
        P(None, ("dp", "seq", "head"), None),
        P(None, ("dp", "seq", "head"), None),
        P(None, ("dp", "seq", "head"), None),
        P(None, ("dp", "seq", "head"), None),
        P(None, ("dp", "seq", "head"), None),
        P(None, ("dp", "seq", "head"), None),
    )
    out_specs = (
        P("dp", ("seq", "head"), None),
        P("dp", ("seq", "head"), None),
        P(None, ("dp", "seq", "head"), None),
        P(None, ("dp", "seq", "head"), None),
        P(None, ("dp", "seq", "head"), None),
        P(None, ("dp", "seq", "head"), None),
        P(None, ("dp", "seq", "head"), None),
        P(None, ("dp", "seq", "head"), None),
        P(None, ("dp", "seq", "head"), None),
        P(None, ("dp", "seq", "head"), None),
        P(None, ("dp", "seq", "head"), None),
        P(None, ("dp", "seq", "head"), None),
        P(),
    )
    return jax.shard_map(local, mesh=mesh, in_specs=in_specs, out_specs=out_specs, check_vma=False)
```

```python
import math

import jax
import jax.numpy as jnp
from jax import lax
from jax.experimental import pallas as pl
from jax.experimental.pallas import tpu as pltpu
from jax.sharding import PartitionSpec as P

D = 1024
HEADS = 4
HEAD_DIM = 112
EXPERTS = 5
FF = 4096
LAYERS = 2
STEP = 10


NORM_EPS = 1e-05
BETA_ONE = 0.9
BETA_TWO = 0.95
ADAM_EPS = 1e-08
WEIGHT_DECAY = 0.1
NORM_RATE = 0.5
MASKED = -1e30
CHUNK = 512
NATIVE = ((LAYERS - 1, "down"),)


def column_bounds():
    query_end = 2 * HEADS * HEAD_DIM
    value_end = query_end + HEADS * EXPERTS * HEAD_DIM
    output_end = value_end + HEADS * EXPERTS * HEAD_DIM
    return (query_end, value_end, output_end, output_end + FF)


def column_rates(segment):
    query_end, value_end, output_end, up_end = column_bounds()
    column = jnp.arange(up_end + FF)
    inner = D ** (-0.5)
    outer = 0.7 * math.sqrt(segment) / HEAD_DIM
    rates = jnp.where(
        column < value_end,
        inner,
        jnp.where(column < output_end, outer, jnp.where(column < up_end, inner, FF ** (-0.5))),
    )
    return rates.astype(jnp.float32)


def small_rates():
    column = jnp.arange(2 * HEADS * EXPERTS + 4)
    return jnp.where(column < 2 * HEADS * EXPERTS, 0.7 * D ** (-0.5), NORM_RATE).astype(jnp.float32)


def adam_update(weight, grad, first, second, rates, decay):
    first_new = BETA_ONE * first + (1.0 - BETA_ONE) * grad
    second_new = BETA_TWO * second + (1.0 - BETA_TWO) * grad * grad
    first_hat = first_new / (1.0 - BETA_ONE**STEP)
    second_hat = second_new / (1.0 - BETA_TWO**STEP)
    new = weight - rates * (first_hat / (jnp.sqrt(second_hat) + ADAM_EPS) + decay * weight)
    return (new, first_new, second_new)


def rotary_tables(positions):
    half = HEAD_DIM // 2
    inverse = jnp.exp(-math.log(10000.0) * jnp.arange(half, dtype=jnp.float32) / half)
    angle = positions.astype(jnp.float32)[:, None] * inverse[None, :]
    return (jnp.cos(angle), jnp.sin(angle))


def layer_stats(values):
    mean = jnp.mean(values, axis=-1, keepdims=True)
    centered = values - mean
    variance = jnp.mean(centered * centered, axis=-1, keepdims=True)
    inverse = lax.rsqrt(variance + NORM_EPS)
    return (centered * inverse, inverse)


def norm_back(grad_normed, normed, inverse, gain):
    scaled = grad_normed * gain
    return inverse * (
        scaled
        - jnp.mean(scaled, axis=-1, keepdims=True)
        - normed * jnp.mean(scaled * normed, axis=-1, keepdims=True)
    )


def contract_last(left, right):
    return lax.dot_general(
        left, right, (((1,), (1,)), ((), ())), preferred_element_type=jnp.float32
    )


def contract_first(left, right):
    return lax.dot_general(
        left, right, (((0,), (0,)), ((), ())), preferred_element_type=jnp.float32
    )


AXES = ("dp", "seq", "head")


def mesh_bits():
    dims = [
        (axis, bit)
        for axis in AXES
        for bit in reversed(range(lax.axis_size(axis).bit_length() - 1))
    ]
    groups = [[index for index, (axis, _) in enumerate(dims) if axis == name] for name in AXES]
    return (dims, *groups)


def my_bits(dims):
    place = {axis: lax.axis_index(axis) for axis in AXES}
    bits = [lax.rem(place[axis] // (1 << bit), 2) for axis, bit in dims]
    partners = [
        {axis: place[axis] + (1 << bit) * (1 - 2 * bits[index])}
        for index, (axis, bit) in enumerate(dims)
    ]
    return (bits, partners)


def greet(partners):
    barrier = pltpu.get_barrier_semaphore()
    for partner in partners:
        pl.semaphore_signal(
            barrier, inc=1, device_id=partner, device_id_type=pl.DeviceIdType.MESH
        )
    pl.semaphore_wait(barrier, len(partners))


def gather_rows(share, counts, unit, name):
    dims, dp_dims, seq_dims, head_dims = mesh_bits()
    orders = (
        head_dims + dp_dims[::-1] + seq_dims,
        head_dims + dp_dims + seq_dims,
        dp_dims + head_dims + seq_dims,
    )
    depth = len(dims)
    rows, width = share.shape
    units = width // unit
    near = (11 * units + 16) // 32
    pieces, start = ([], 0)
    for which, count in ((0, near), (1, near), (2, units - 2 * near)):
        pieces.append((start, count, which))
        start += count * unit
    lag, slots = (3, 6)
    local_slots = 2
    ring = (depth + 1) * lag + local_slots + 2
    steps = max(count for _, count, _ in pieces) + lag * depth

    def kernel(*refs):
        share_ref, counts_ref, out_ref, counts_out = refs[:4]
        send_sem, recv_sem, load_sem, store_sem, small_send, small_recv, small_load = refs[4:11]
        buffers = refs[11:]
        bits, partners = my_bits(dims)

        def at_stage(which, stage):
            done = orders[which][:stage]
            return tuple(slice(None) if dim in done else bits[dim] for dim in range(depth))

        def columns(number, chunk):
            return pl.ds(pl.multiple_of(pieces[number][0] + chunk * unit, 128), unit)

        def exchange(number, stage, chunk):
            which = pieces[number][2]
            view = buffers[number].at[(lax.rem(chunk, ring),) + at_stage(which, stage)]
            slot = lax.rem(chunk, slots)
            return sent_to(
                view,
                view,
                send_sem.at[number, stage, slot],
                recv_sem.at[number, stage, slot],
                partners[orders[which][stage]],
            )

        def load(number, chunk):
            return pltpu.make_async_copy(
                share_ref.at[:, columns(number, chunk)],
                buffers[number].at[(lax.rem(chunk, ring),) + tuple(bits)],
                load_sem.at[number, lax.rem(chunk, local_slots)],
            )

        def store(number, chunk):
            return pltpu.make_async_copy(
                buffers[number].at[lax.rem(chunk, ring)],
                out_ref.at[(slice(None),) * (depth + 1) + (columns(number, chunk),)],
                store_sem.at[number, lax.rem(chunk, local_slots)],
            )

        def small(stage):
            view = counts_out.at[at_stage(0, stage)]
            return sent_to(
                view, view, small_send.at[stage], small_recv.at[stage], partners[orders[0][stage]]
            )

        own_counts = pltpu.make_async_copy(counts_ref, counts_out.at[tuple(bits)], small_load)
        own_counts.start()
        for number in range(len(pieces)):
            for chunk in range(local_slots):
                load(number, jnp.int32(chunk)).start()
        greet(partners)
        own_counts.wait()

        def body(step, carry):
            for stage in range(depth, -1, -1):
                chunk = step - lag * stage
                for number, piece in enumerate(pieces):

                    @pl.when((chunk >= 0) & (chunk < piece[1]))
                    def _(stage=stage, chunk=chunk, number=number, piece=piece):
                        if stage > 0:
                            exchange(number, stage - 1, chunk).wait()
                        else:
                            load(number, chunk).wait()

                            @pl.when(chunk + local_slots < piece[1])
                            def _():
                                load(number, chunk + local_slots).start()

                        if stage < depth:
                            exchange(number, stage, chunk).start()
                        else:

                            @pl.when(chunk >= local_slots)
                            def _():
                                store(number, chunk - local_slots).wait()

                            store(number, chunk).start()

                @pl.when(chunk == 0)
                def _(stage=stage):
                    if stage > 0:
                        small(stage - 1).wait()
                    if stage < depth:
                        small(stage).start()

            return carry

        lax.fori_loop(0, steps, body, 0)
        for number, piece in enumerate(pieces):
            for back in range(min(local_slots, piece[1])):
                store(number, jnp.int32(piece[1] - 1 - back)).wait()

    in_place = pl.BlockSpec(memory_space=pl.ANY)
    semaphores = pltpu.SemaphoreType.DMA((len(pieces), depth, slots))
    local = pltpu.SemaphoreType.DMA((len(pieces), local_slots))
    gathered, all_counts = pl.pallas_call(
        kernel,
        in_specs=[in_place] * 2,
        out_specs=[in_place] * 2,
        out_shape=[
            jax.ShapeDtypeStruct((2,) * depth + value.shape, value.dtype)
            for value in (share, counts)
        ],
        scratch_shapes=[
            semaphores,
            semaphores,
            local,
            local,
            pltpu.SemaphoreType.DMA((depth,)),
            pltpu.SemaphoreType.DMA((depth,)),
            pltpu.SemaphoreType.DMA,
        ]
        + [pltpu.VMEM((ring,) + (2,) * depth + (rows, unit), share.dtype) for _ in pieces],
        compiler_params=pltpu.CompilerParams(
            collective_id=name, has_side_effects=True, vmem_limit_bytes=48 << 20
        ),
    )(share, counts)
    return (gathered.reshape(-1, width), all_counts.reshape(-1, counts.shape[1]))


def halving_plan(width):
    dims, dp_dims, seq_dims, head_dims = mesh_bits()
    first = seq_dims[::-1]
    orders = (
        (0, width // 2, first + dp_dims[::-1] + head_dims[::-1]),
        (width // 2, width // 4, first + dp_dims + head_dims[::-1]),
        (3 * width // 4, width // 4, first + head_dims[::-1] + dp_dims),
    )
    stages = []
    for stage in range(len(dims)):
        parts = []
        for start, count, order in orders:
            left = [dim for dim in range(len(dims)) if dim not in order[:stage]]
            if parts and parts[-1][2:] == (order[stage], left):
                parts[-1] = (parts[-1][0], parts[-1][1] + count, order[stage], left)
            else:
                parts.append((start, count, order[stage], left))
        stages.append(parts)
    lags = [1 if stage < len(seq_dims) else 2 for stage in range(len(dims))]
    return dims, stages, lags


def reduce_weight_grads(lefts, segments, doubles, extras, width):
    dims, stages, lags = halving_plan(width)
    depth = len(dims)
    half = width // 2
    tokens, model = lefts[0].shape
    rows = model >> depth
    firsts = [0]
    for _, _, _, count in segments:
        firsts.append(firsts[-1] + count)
    chunks = firsts[-1] // 2
    spots = [(where // 2, where % 2 * half) for _, where in extras]
    starts = [sum(lags[:stage]) for stage in range(depth + 1)]
    rights = [right for _, right, _, _ in segments] + [right for _, _, _, right in doubles]
    count_lefts, count_rights, count_extras = (len(lefts), len(rights), len(extras))
    first_use = [
        min(firsts[index] // 2 for index, segment in enumerate(segments) if segment[0] == left)
        for left in range(count_lefts)
    ]
    for where, _, left, _ in doubles:
        first_use[left] = min(first_use[left], where // 2)

    def kernel(*refs):
        left_refs = refs[:count_lefts]
        right_refs = refs[count_lefts : count_lefts + count_rights]
        rest = refs[count_lefts + count_rights :]
        added, rest = (rest[:count_extras], rest[count_extras:])
        out_ref, left_buf, turned, right_buf, double_buf, left_sem, right_sem, double_sem = rest[:8]
        pool = iter(rest[8:])
        buffers = [[tuple(next(pool) for _ in range(4)) for _ in parts] for parts in stages]
        step = pl.program_id(0)
        bits, partners = my_bits(dims)

        def exchange(stage, part, slot):
            start, count, dim, left = stages[stage][part]
            own, got, send_sem, recv_sem = buffers[stage][part]
            lead = (slot,) + (slice(None),) * left.index(dim)
            return pltpu.make_async_remote_copy(
                src_ref=own.at[lead + (1 - bits[dim],)],
                dst_ref=got.at[slot],
                send_sem=send_sem.at[slot],
                recv_sem=recv_sem.at[slot],
                device_id=partners[dim],
                device_id_type=pl.DeviceIdType.MESH,
            )

        def load_left(index):
            return pltpu.make_async_copy(left_refs[index], left_buf.at[index], left_sem.at[index])

        def load_right(index, at, chunk, side):
            columns = pl.ds(pl.multiple_of(at * half, half), half)
            slot = lax.rem(chunk, 2)
            return pltpu.make_async_copy(
                right_refs[index].at[:, columns],
                right_buf.at[slot, side],
                right_sem.at[slot, side],
            )

        def load_double(index):
            return pltpu.make_async_copy(
                right_refs[len(segments) + index].at[:, 0:half], double_buf, double_sem
            )

        def prefetch(chunk):
            for side in range(2):
                place = 2 * chunk + side
                for index, (_, _, begin, _) in enumerate(segments):

                    @pl.when((place >= firsts[index]) & (place < firsts[index + 1]))
                    def _(index=index, begin=begin, place=place, side=side):
                        load_right(index, place - firsts[index] + begin, chunk, side).start()

            for index, (where, _, _, _) in enumerate(doubles):

                @pl.when(chunk == where // 2)
                def _(index=index):
                    load_double(index).start()

        @pl.when(step == 0)
        def _():
            for index in range(count_lefts):
                load_left(index).start()
            prefetch(step)
            greet(partners)

        @pl.when(step + 1 < chunks)
        def _():
            prefetch(step + 1)

        for stage in range(depth, -1, -1):
            chunk = step - starts[stage]

            @pl.when((chunk >= 0) & (chunk < chunks))
            def _(stage=stage, chunk=chunk):
                if stage == 0:
                    slot = lax.rem(chunk, 2 * lags[0])
                    near = lax.rem(chunk, 2)
                    own = buffers[0][0][0]
                    for index in range(count_lefts):

                        @pl.when(chunk == first_use[index])
                        def _(index=index):
                            load_left(index).wait()
                            turned[index] = left_buf[index].T

                    for side in range(2):
                        place = 2 * chunk + side
                        which = jnp.int32(segments[0][0])
                        for index, segment in enumerate(segments):
                            which = jnp.where(place >= firsts[index], segment[0], which)
                        load_right(0, 0, chunk, side).wait()
                        for where, kept, _, _ in doubles:
                            if where % 2 == side:

                                @pl.when(chunk == where // 2)
                                def _(kept=kept, side=side):
                                    right_buf[near, side, :, kept:] = jnp.zeros(
                                        (tokens, half - kept), jnp.bfloat16
                                    )

                        product = jnp.dot(
                            turned[which],
                            right_buf[near, side],
                            preferred_element_type=jnp.float32,
                        )
                        own[(slot, Ellipsis, slice(side * half, side * half + half))] = (
                            product.astype(jnp.bfloat16).reshape((2,) * depth + (rows, half))
                        )
                    for index, (where, _, left, _) in enumerate(doubles):

                        @pl.when(chunk == where // 2)
                        def _(index=index, where=where, left=left):
                            load_double(index).wait()
                            product = jnp.dot(
                                turned[left], double_buf[...], preferred_element_type=jnp.float32
                            ).reshape((2,) * depth + (rows, half))
                            begin = where % 2 * half
                            at = (slot, Ellipsis, slice(begin, begin + half))
                            own[at] = (own[at].astype(jnp.float32) + product).astype(jnp.bfloat16)

                    for index in range(count_extras):

                        @pl.when(chunk == spots[index][0])
                        def _(index=index):
                            at = (slot, Ellipsis, slice(spots[index][1], spots[index][1] + 128))
                            total = own[at].astype(jnp.float32) + added[index][...].astype(
                                jnp.float32
                            )
                            own[at] = total.astype(jnp.bfloat16)

                else:
                    back = lax.rem(chunk, 2 * lags[stage - 1])
                    for part, (start, count, dim, left) in enumerate(stages[stage - 1]):
                        exchange(stage - 1, part, back).wait()
                        own, got = buffers[stage - 1][part][:2]
                        lead = (back,) + (slice(None),) * left.index(dim)
                        total = own[lead + (bits[dim],)].astype(jnp.float32) + got[back].astype(
                            jnp.float32
                        )
                        if stage == depth:
                            out_ref[:, start : start + count] = total
                            continue
                        slot = lax.rem(chunk, 2 * lags[stage])
                        low = total.astype(jnp.bfloat16)
                        for other, (begin, length, _, kept) in enumerate(stages[stage]):
                            lo, hi = max(start, begin), min(start + count, begin + length)
                            if lo < hi:
                                at = (slot,) + (slice(None),) * (len(kept) + 1)
                                buffers[stage][other][0][at + (slice(lo - begin, hi - begin),)] = (
                                    low[..., lo - start : hi - start]
                                )
                if stage < depth:
                    for part in range(len(stages[stage])):
                        exchange(stage, part, lax.rem(chunk, 2 * lags[stage])).start()

    scratch = [
        pltpu.VMEM((count_lefts, tokens, model), jnp.bfloat16),
        pltpu.VMEM((count_lefts, model, tokens), jnp.bfloat16),
        pltpu.VMEM((2, 2, tokens, half), jnp.bfloat16),
        pltpu.VMEM((tokens, half), jnp.bfloat16),
        pltpu.SemaphoreType.DMA((count_lefts,)),
        pltpu.SemaphoreType.DMA((2, 2)),
        pltpu.SemaphoreType.DMA,
    ]
    for stage, parts in enumerate(stages):
        slots = 2 * lags[stage]
        for start, count, dim, left in parts:
            scratch += [
                pltpu.VMEM((slots,) + (2,) * len(left) + (rows, count), jnp.bfloat16),
                pltpu.VMEM((slots,) + (2,) * (len(left) - 1) + (rows, count), jnp.bfloat16),
                pltpu.SemaphoreType.DMA((slots,)),
                pltpu.SemaphoreType.DMA((slots,)),
            ]
    in_place = pl.BlockSpec(memory_space=pl.ANY)
    whole = [value.reshape((2,) * depth + (rows, 128)) for value, _ in extras]
    return pl.pallas_call(
        kernel,
        grid=(chunks + starts[depth],),
        in_specs=[in_place] * (count_lefts + count_rights)
        + [pl.BlockSpec(value.shape, lambda step: (0,) * (depth + 2)) for value in whole],
        out_specs=pl.BlockSpec(
            (rows, width), lambda step: (0, jnp.clip(step - starts[depth], 0, chunks - 1))
        ),
        out_shape=jax.ShapeDtypeStruct((rows, chunks * width), jnp.float32),
        scratch_shapes=scratch,
        compiler_params=pltpu.CompilerParams(
            collective_id=1,
            has_side_effects=True,
            vmem_limit_bytes=48 << 20,
            dimension_semantics=("arbitrary",),
        ),
    )(*lefts, *rights, *whole)


def reduction_order(tensor):
    dp, seq = (lax.axis_size("dp"), lax.axis_size("seq"))
    count, width = tensor.shape
    split = tensor.reshape(count, dp, seq, width // (dp * seq))
    return split.transpose(0, 2, 1, 3).reshape(count, width)


def reduced_natively(left, right):
    share = contract_first(reduction_order(left), right).astype(jnp.bfloat16)
    for axis in ("seq", "dp", "head"):
        share = lax.psum_scatter(share, axis, scatter_dimension=0, tiled=True)
    return share


def lane_whole(count):
    return count + (-count) % 128


def padded(pieces, width):
    have = sum(piece.shape[1] for piece in pieces)
    fill = jnp.zeros((pieces[0].shape[0], width - have), pieces[0].dtype)
    return jnp.concatenate(list(pieces) + [fill], axis=1)


LANES = 128
QUERY_TILE = 256


def swap_halves(tensor):
    half = HEAD_DIM // 2
    return jnp.concatenate([tensor[:, half:], tensor[:, :half]], axis=1)


def lane_filled(tensor):
    fill = jnp.zeros((tensor.shape[0], LANES - tensor.shape[1]), tensor.dtype)
    return jnp.concatenate([tensor, fill], axis=1)


def weights_block(keys_mem, keys_own, query, start, first, segment, length):
    contract = (((1,), (1,)), ((), ()))
    raw = jnp.concatenate(
        [
            lax.dot_general(keys, query, contract, preferred_element_type=jnp.float32)
            for keys in (keys_mem, keys_own)
        ],
        axis=0,
    )
    key_pos = start - segment + lax.broadcasted_iota(jnp.int32, raw.shape, 0)
    query_pos = start + first + lax.broadcasted_iota(jnp.int32, raw.shape, 1)
    used = (key_pos < length) & (key_pos < query_pos) & (key_pos >= 0)
    allowed = used | (key_pos == query_pos)
    scores = jnp.where(allowed, raw * HEAD_DIM ** (-0.5), MASKED)
    weights = jnp.exp(scores - jnp.max(scores, axis=0, keepdims=True))
    return weights * (1.0 / jnp.sum(weights, axis=0, keepdims=True))


def contract_rows(left, right):
    return lax.dot_general(
        left, right, (((0,), (0,)), ((), ())), preferred_element_type=jnp.float32
    )


def across(axis, offset):
    size = lax.axis_size(axis)
    return {axis: lax.rem(lax.axis_index(axis) + offset + size, size)}


def sent_to(source, target, send_sem, recv_sem, device):
    return pltpu.make_async_remote_copy(
        src_ref=source,
        dst_ref=target,
        send_sem=send_sem,
        recv_sem=recv_sem,
        device_id=device,
        device_id_type=pl.DeviceIdType.MESH,
    )


def meet(memory_step):
    barrier = pltpu.get_barrier_semaphore()
    heads = lax.axis_size("head")
    writers = [across("head", step) for step in range(1, heads)]
    writers.append(across("seq", -memory_step))
    for device in writers:
        pl.semaphore_signal(barrier, inc=1, device_id=device, device_id_type=pl.DeviceIdType.MESH)
    pl.semaphore_wait(barrier, len(writers))


def gate_values(entered_ref, chosen_ref, rows):
    at = column_bounds()[1]
    logits = entered_ref[rows, at : at + 2 * HEADS * EXPERTS]
    prob = 1.0 / (1.0 + jnp.exp(-logits))
    return (prob, prob * chosen_ref[rows, :])


def column(tensor, index):
    return tensor[:, index : index + 1]


def attention_forward(entered, chosen, turn_cos, turn_sin, lengths, shift, name):
    seq_count = lengths.shape[0]
    tokens = entered.shape[0]
    sub = tokens // seq_count
    heads = lax.axis_size("head")
    segment = heads * sub
    query_end = column_bounds()[0]
    sides = range(1, heads)

    def kernel(*refs):
        length_ref, entered_ref, chosen_ref, cos_ref, sin_ref = refs[:5]
        mixed_ref, attended_ref, query_ref, key_ref, value_ref = refs[5:10]
        out_buf, heads_buf, mem_buf, done_buf, back_buf = refs[10:15]
        out_sem, in_sem, mem_sem, done_sem, back_sem = refs[15:]
        me = lax.axis_index("head")
        start = lax.axis_index("seq") * segment
        turn, wind = (cos_ref[...], sin_ref[...])

        def outward(b, side):
            there = across("head", side)
            return sent_to(
                out_buf.at[b, there["head"]],
                heads_buf.at[b, :, me],
                out_sem.at[b, side - 1],
                in_sem.at[b, side - 1],
                there,
            )

        def onward(b):
            return sent_to(
                heads_buf.at[b, 1:3],
                mem_buf.at[b],
                mem_sem.at[0, b],
                mem_sem.at[1, b],
                across("seq", 1),
            )

        def homeward(b, side):
            there = across("head", side)
            return sent_to(
                done_buf.at[b, there["head"]],
                back_buf.at[b, me],
                done_sem.at[b, side - 1],
                back_sem.at[b, side - 1],
                there,
            )

        meet(1)
        gates_of = []
        for b in range(seq_count):
            rows = slice(b * sub, (b + 1) * sub)
            gates = gate_values(entered_ref, chosen_ref, rows)[1]
            gates_of.append(gates)
            for head in range(HEADS):
                for kind in range(2):
                    at = (kind * HEADS + head) * HEAD_DIM
                    vector = entered_ref[rows, at : at + HEAD_DIM]
                    turned = vector * turn + swap_halves(vector) * wind
                    out_buf[b, head, kind] = lane_filled(turned).astype(jnp.bfloat16)
                value = jnp.zeros((sub, HEAD_DIM), jnp.float32)
                for expert in range(EXPERTS):
                    index = head * EXPERTS + expert
                    at = query_end + index * HEAD_DIM
                    value += column(gates, index) * entered_ref[rows, at : at + HEAD_DIM]
                out_buf[b, head, 2] = lane_filled(value).astype(jnp.bfloat16)
            for side in sides:
                outward(b, side).start()
            for kind in range(3):
                heads_buf[b, kind, me] = out_buf[b, me, kind]
        for b in range(seq_count):
            for side in sides:
                outward(b, side).wait_recv()
            onward(b).start()
        for b in range(seq_count):
            onward(b).wait_recv()
            keys_own = heads_buf[b, 1].reshape(segment, LANES)
            values = jnp.concatenate(
                [mem_buf[b, 1].reshape(segment, LANES), heads_buf[b, 2].reshape(segment, LANES)],
                axis=0,
            )
            for first in range(0, segment, QUERY_TILE):
                tile = slice(first // sub, (first + QUERY_TILE) // sub)
                query = heads_buf[b, 0, tile].reshape(QUERY_TILE, LANES)
                probs = weights_block(
                    mem_buf[b, 0].reshape(segment, LANES),
                    keys_own,
                    query,
                    start,
                    first,
                    segment,
                    length_ref[b],
                ).astype(jnp.bfloat16)
                attended = contract_rows(values, probs).T.astype(jnp.bfloat16)
                done_buf[b, tile] = attended.reshape(QUERY_TILE // sub, sub, LANES)
            for side in sides:
                homeward(b, side).start()
            back_buf[b, me] = done_buf[b, me]
        for b in range(seq_count):
            query_ref[b] = heads_buf[b, 0]
            key_ref[b, 0] = mem_buf[b, 0]
            key_ref[b, 1] = heads_buf[b, 1]
            value_ref[b, 0] = mem_buf[b, 1]
            value_ref[b, 1] = heads_buf[b, 2]
        mixed_ref[:, :shift] = jnp.zeros((tokens, shift), jnp.bfloat16)
        for b in range(seq_count):
            rows = slice(b * sub, (b + 1) * sub)
            for side in sides:
                homeward(b, side).wait_recv()
            for head in range(HEADS):
                attended = back_buf[b, head]
                attended_ref[rows, head * LANES : (head + 1) * LANES] = attended
                wide = attended.astype(jnp.float32)[:, :HEAD_DIM]
                for expert in range(EXPERTS):
                    index = head * EXPERTS + expert
                    gate = column(gates_of[b], HEADS * EXPERTS + index)
                    at = shift + index * HEAD_DIM
                    mixed_ref[rows, at : at + HEAD_DIM] = (
                        gate * wide
                    ).astype(jnp.bfloat16)
        for b in range(seq_count):
            onward(b).wait_send()
            for side in sides:
                outward(b, side).wait_send()
                homeward(b, side).wait_send()

    def shape(*dims):
        return jax.ShapeDtypeStruct(dims, jnp.bfloat16)

    vmem = pl.BlockSpec(memory_space=pltpu.VMEM)
    paired = pltpu.SemaphoreType.DMA((seq_count, heads - 1))
    return pl.pallas_call(
        kernel,
        in_specs=[pl.BlockSpec(memory_space=pltpu.SMEM)] + [vmem] * 4,
        out_specs=[vmem] * 5,
        out_shape=[
            shape(tokens, shift + HEADS * EXPERTS * HEAD_DIM),
            shape(tokens, HEADS * LANES),
            shape(seq_count, heads, sub, LANES),
            shape(seq_count, 2, heads, sub, LANES),
            shape(seq_count, 2, heads, sub, LANES),
        ],
        scratch_shapes=[
            pltpu.VMEM((seq_count, heads, 3, sub, LANES), jnp.bfloat16),
            pltpu.VMEM((seq_count, 3, heads, sub, LANES), jnp.bfloat16),
            pltpu.VMEM((seq_count, 2, heads, sub, LANES), jnp.bfloat16),
            pltpu.VMEM((seq_count, heads, sub, LANES), jnp.bfloat16),
            pltpu.VMEM((seq_count, heads, sub, LANES), jnp.bfloat16),
            paired,
            paired,
            pltpu.SemaphoreType.DMA((2, seq_count)),
            paired,
            paired,
        ],
        compiler_params=pltpu.CompilerParams(
            collective_id=name, has_side_effects=True, vmem_limit_bytes=40 << 20
        ),
    )(lengths, entered, chosen, turn_cos, turn_sin)


def attention_backward(
    grad_mixed, attended, entered, chosen, turn_cos, turn_sin, lengths, saved, shift, grad_width, name
):
    query, keys, values = saved
    seq_count = lengths.shape[0]
    tokens = entered.shape[0]
    sub = tokens // seq_count
    heads = lax.axis_size("head")
    segment = heads * sub
    query_end, value_end = column_bounds()[:2]
    router_cols = 2 * HEADS * EXPERTS
    sides = range(1, heads)

    def kernel(*refs):
        length_ref, grad_ref, attended_ref, entered_ref, chosen_ref, cos_ref, sin_ref = refs[:7]
        query_ref, key_ref, value_ref, result_ref, logit_ref = refs[7:12]
        out_buf, heads_buf, mem_out, mem_in, own_buf, done_buf, back_buf = refs[12:19]
        out_sem, in_sem, mem_sem, query_sem, done_sem, back_sem = refs[19:]
        me = lax.axis_index("head")
        start = lax.axis_index("seq") * segment
        turn, wind = (cos_ref[...], sin_ref[...])

        def outward(b, side):
            there = across("head", side)
            return sent_to(
                out_buf.at[b, there["head"]],
                heads_buf.at[b, me],
                out_sem.at[b, side - 1],
                in_sem.at[b, side - 1],
                there,
            )

        def onward(b):
            return sent_to(
                mem_out.at[b], mem_in.at[b], mem_sem.at[0, b], mem_sem.at[1, b], across("seq", -1)
            )

        def queries_home(b, side):
            there = across("head", side)
            return sent_to(
                done_buf.at[b, there["head"], 0],
                back_buf.at[b, me, 0],
                query_sem.at[0, b, side - 1],
                query_sem.at[1, b, side - 1],
                there,
            )

        def homeward(b, side):
            there = across("head", side)
            return sent_to(
                done_buf.at[b, there["head"], 1:3],
                back_buf.at[b, me, 1:3],
                done_sem.at[b, side - 1],
                back_sem.at[b, side - 1],
                there,
            )

        def join_memory(b):
            onward(b).wait_recv()
            for kind in range(2):
                total = own_buf[b, kind] + mem_in[b, kind].astype(jnp.float32)
                done_buf[b, :, kind + 1] = total.astype(jnp.bfloat16).reshape(heads, sub, LANES)
            for side in sides:
                homeward(b, side).start()
            back_buf[b, me] = done_buf[b, me]

        meet(-1)
        lane = lax.broadcasted_iota(jnp.int32, (sub, router_cols), 1)
        gate_grads, probs_of, gates_of = ([], [], [])
        for b in range(seq_count):
            rows = slice(b * sub, (b + 1) * sub)
            prob, gates = gate_values(entered_ref, chosen_ref, rows)
            probs_of.append(prob)
            gates_of.append(gates)
            gate_grad = jnp.zeros((sub, router_cols), jnp.float32)
            for head in range(HEADS):
                seen = attended_ref[rows, head * LANES : head * LANES + HEAD_DIM].astype(
                    jnp.float32
                )
                total = jnp.zeros((sub, HEAD_DIM), jnp.float32)
                for expert in range(EXPERTS):
                    index = head * EXPERTS + expert
                    at = shift + index * HEAD_DIM
                    part = grad_ref[rows, at : at + HEAD_DIM]
                    total += column(gates, HEADS * EXPERTS + index) * part
                    gate_grad = jnp.where(
                        lane == HEADS * EXPERTS + index,
                        jnp.sum(part * seen, axis=1, keepdims=True),
                        gate_grad,
                    )
                out_buf[b, head] = lane_filled(total).astype(jnp.bfloat16)
            gate_grads.append(gate_grad)
            for side in sides:
                outward(b, side).start()
            heads_buf[b, me] = out_buf[b, me]
        for b in range(seq_count):
            for side in sides:
                outward(b, side).wait_recv()
            keys_mem = key_ref[b, 0].reshape(segment, LANES)
            keys_own = key_ref[b, 1].reshape(segment, LANES)
            keys_all = jnp.concatenate([keys_mem, keys_own], axis=0)
            values_all = jnp.concatenate(
                [value_ref[b, 0].reshape(segment, LANES), value_ref[b, 1].reshape(segment, LANES)],
                axis=0,
            )
            grad_keys = jnp.zeros((2 * segment, LANES), jnp.float32)
            grad_values = jnp.zeros((2 * segment, LANES), jnp.float32)
            for first in range(0, segment, QUERY_TILE):
                tile = slice(first // sub, (first + QUERY_TILE) // sub)
                here = query_ref[b, tile].reshape(QUERY_TILE, LANES)
                arrived = heads_buf[b, tile].reshape(QUERY_TILE, LANES)
                probs = weights_block(
                    keys_mem, keys_own, here, start, first, segment, length_ref[b]
                )
                grad_probs = contract_last(values_all, arrived)
                delta = jnp.sum(probs * grad_probs, axis=0, keepdims=True)
                grad_raw = (probs * (grad_probs - delta) * HEAD_DIM ** (-0.5)).astype(
                    jnp.bfloat16
                )
                grad_values += jnp.dot(
                    probs.astype(jnp.bfloat16), arrived, preferred_element_type=jnp.float32
                )
                grad_keys += jnp.dot(grad_raw, here, preferred_element_type=jnp.float32)
                grad_query = contract_rows(keys_all, grad_raw).T.astype(jnp.bfloat16)
                done_buf[b, tile, 0] = grad_query.reshape(QUERY_TILE // sub, sub, LANES)
                if b > 0 and first == 0:
                    join_memory(b - 1)
            for kind, grads in enumerate((grad_keys, grad_values)):
                mem_out[b, kind] = grads[:segment].astype(jnp.bfloat16)
                own_buf[b, kind] = grads[segment:]
            onward(b).start()
            for side in sides:
                queries_home(b, side).start()
        join_memory(seq_count - 1)
        used = value_end + router_cols
        result_ref[:, used:] = jnp.zeros((tokens, grad_width - used), jnp.bfloat16)
        logit_ref[:, router_cols:] = jnp.zeros((tokens, CHUNK // 2 - router_cols), jnp.bfloat16)
        for b in range(seq_count):
            rows = slice(b * sub, (b + 1) * sub)
            for side in sides:
                queries_home(b, side).wait_recv()
                homeward(b, side).wait_recv()
            gate_grad = gate_grads[b]
            for head in range(HEADS):
                for kind in range(2):
                    vector = back_buf[b, head, kind].astype(jnp.float32)[:, :HEAD_DIM]
                    turned = vector * turn - swap_halves(vector) * wind
                    at = (kind * HEADS + head) * HEAD_DIM
                    result_ref[rows, at : at + HEAD_DIM] = turned.astype(jnp.bfloat16)
                grad_value = back_buf[b, head, 2].astype(jnp.float32)[:, :HEAD_DIM]
                for expert in range(EXPERTS):
                    index = head * EXPERTS + expert
                    at = query_end + index * HEAD_DIM
                    gate_grad = jnp.where(
                        lane == index,
                        jnp.sum(
                            entered_ref[rows, at : at + HEAD_DIM] * grad_value,
                            axis=1,
                            keepdims=True,
                        ),
                        gate_grad,
                    )
                    result_ref[rows, at : at + HEAD_DIM] = (
                        column(gates_of[b], index) * grad_value
                    ).astype(jnp.bfloat16)
            prob = probs_of[b]
            grad_logit = (gate_grad * chosen_ref[rows, :] * prob * (1.0 - prob)).astype(
                jnp.bfloat16
            )
            result_ref[rows, value_end:used] = grad_logit
            logit_ref[rows, :router_cols] = grad_logit
        for b in range(seq_count):
            onward(b).wait_send()
            for side in sides:
                outward(b, side).wait_send()
                queries_home(b, side).wait_send()
                homeward(b, side).wait_send()

    vmem = pl.BlockSpec(memory_space=pltpu.VMEM)
    paired = pltpu.SemaphoreType.DMA((seq_count, heads - 1))
    return pl.pallas_call(
        kernel,
        in_specs=[pl.BlockSpec(memory_space=pltpu.SMEM)] + [vmem] * 9,
        out_specs=[vmem] * 2,
        out_shape=[
            jax.ShapeDtypeStruct((tokens, count), jnp.bfloat16)
            for count in (grad_width, CHUNK // 2)
        ],
        scratch_shapes=[
            pltpu.VMEM((seq_count, heads, sub, LANES), jnp.bfloat16),
            pltpu.VMEM((seq_count, heads, sub, LANES), jnp.bfloat16),
            pltpu.VMEM((seq_count, 2, segment, LANES), jnp.bfloat16),
            pltpu.VMEM((seq_count, 2, segment, LANES), jnp.bfloat16),
            pltpu.VMEM((seq_count, 2, segment, LANES), jnp.float32),
            pltpu.VMEM((seq_count, heads, 3, sub, LANES), jnp.bfloat16),
            pltpu.VMEM((seq_count, heads, 3, sub, LANES), jnp.bfloat16),
            paired,
            paired,
            pltpu.SemaphoreType.DMA((2, seq_count)),
            pltpu.SemaphoreType.DMA((2, seq_count, heads - 1)),
            paired,
            paired,
        ],
        compiler_params=pltpu.CompilerParams(
            collective_id=name, has_side_effects=True, vmem_limit_bytes=48 << 20
        ),
    )(lengths, grad_mixed, attended, entered, chosen, turn_cos, turn_sin, query, keys, values)


def gelu_tanh(values):
    return jax.nn.gelu(values, approximate=True)


def local(
    inputs,
    cotangent,
    routes,
    lengths,
    matrix,
    matrix_first,
    matrix_second,
    small,
    small_first,
    small_second,
):
    head_count = lax.axis_size("head")
    seq_count, sub_rows, width = inputs.shape
    segment = sub_rows * head_count
    tokens = seq_count * sub_rows
    router_cols = 2 * HEADS * EXPERTS
    group = HEADS * EXPERTS
    query_end, value_end, output_end, up_end = column_bounds()
    seq_start = lax.axis_index("seq") * segment
    positions = (
        seq_start + lax.axis_index("head") * sub_rows + jnp.arange(sub_rows, dtype=jnp.int32)
    )
    valid = (positions[None, :] < lengths[:, None]).astype(jnp.float32)
    cosines, sines = rotary_tables(positions)
    turn_cos = jnp.concatenate([cosines, cosines], axis=1)
    turn_sin = jnp.concatenate([-sines, sines], axis=1)
    chosen = jnp.sum(
        (routes[..., None] == jnp.arange(EXPERTS, dtype=jnp.int32)).astype(jnp.float32), axis=-2
    )
    load_part = jnp.sum(chosen * valid[None, :, :, None, None, None], axis=(1, 2))
    in_width = lane_whole(value_end + router_cols + 4)
    half = CHUNK // 2
    shift = value_end % half
    in_grad_width = value_end + (-value_end) % half
    out_width = shift + output_end - value_end
    matrix_low = matrix.astype(jnp.bfloat16)
    small_low = small.astype(jnp.bfloat16)
    in_low = [
        padded([matrix_low[layer, :, :value_end], small_low[layer]], in_width)
        for layer in range(LAYERS)
    ]
    out_low = [
        jnp.pad(matrix_low[layer, :, value_end:output_end], ((0, 0), (shift, 0)))
        for layer in range(LAYERS)
    ]
    ffn_low = [matrix_low[layer, :, output_end:] for layer in range(LAYERS)]
    size = load_part.size
    counts = jnp.pad(load_part.reshape(-1), (0, (-size) % 1024)).reshape(8, -1)
    early = []
    for layer in range(LAYERS):
        early += [in_low[layer], out_low[layer]] + ([ffn_low[layer]] if layer + 1 < LAYERS else [])
    gathered, counts = gather_rows(jnp.concatenate(early, axis=1), counts, 128, 2)
    counts, late = lax.optimization_barrier((counts, ffn_low[-1]))
    loads = jnp.sum(counts.reshape(-1, size + (-size) % 1024), axis=0)[:size].reshape(
        load_part.shape
    )
    late = lax.all_gather(late, ("dp", "seq", "head"), axis=0, tiled=True)
    pieces, start = ([], 0)
    for value in early:
        pieces.append(gathered[:, start : start + value.shape[1]])
        start += value.shape[1]
    pieces.append(late)
    in_ws, out_ws, ffn_ws = (pieces[0::3], pieces[1::3], pieces[2::3])
    hidden = inputs.astype(jnp.float32).reshape(tokens, width)
    kept = []
    for layer in range(LAYERS):
        in_w, out_w, ffn_w = (in_ws[layer], out_ws[layer], ffn_ws[layer])
        gains = in_w[:, value_end + router_cols : value_end + router_cols + 4].astype(jnp.float32)
        normed_one, inverse_one = layer_stats(hidden)
        first_in = (normed_one * gains[:, 0] + gains[:, 1]).astype(jnp.bfloat16)
        entered = jnp.dot(first_in, in_w, preferred_element_type=jnp.float32)
        chosen_here = chosen[layer].reshape(tokens, router_cols)
        mixed, attended, *saved = attention_forward(
            entered,
            chosen_here,
            turn_cos,
            turn_sin,
            lengths,
            shift,
            3 + layer,
        )
        residual = hidden + contract_last(mixed, out_w)
        normed_two, inverse_two = layer_stats(residual)
        second_in = (normed_two * gains[:, 2] + gains[:, 3]).astype(jnp.bfloat16)
        up = jnp.dot(second_in, ffn_w[:, :FF], preferred_element_type=jnp.float32)
        act = gelu_tanh(up).astype(jnp.bfloat16)
        hidden = residual + contract_last(act, ffn_w[:, FF:])
        kept.append(
            (
                normed_one,
                inverse_one,
                first_in,
                entered,
                chosen_here,
                mixed,
                attended,
                saved,
                normed_two,
                inverse_two,
                second_in,
                up,
                act,
            )
        )
    output = hidden.reshape(seq_count, sub_rows, width).astype(jnp.bfloat16)
    grad_hidden = (cotangent.astype(jnp.float32) * valid[:, :, None]).reshape(tokens, width)
    lefts, segments, doubles, extras, native, bases = ([], [], [], [], {}, {})
    for layer in reversed(range(LAYERS)):
        (
            normed_one,
            inverse_one,
            first_in,
            entered,
            chosen_here,
            mixed,
            attended,
            saved,
            normed_two,
            inverse_two,
            second_in,
            up,
            act,
        ) = kept[layer]
        in_w, out_w, ffn_w = (in_ws[layer], out_ws[layer], ffn_ws[layer])
        gains = in_w[:, value_end + router_cols : value_end + router_cols + 4].astype(jnp.float32)
        grad_low = grad_hidden.astype(jnp.bfloat16)
        grad_act = jnp.dot(grad_low, ffn_w[:, FF:], preferred_element_type=jnp.float32)
        gelu_value, gelu_pull = jax.vjp(gelu_tanh, up)
        grad_up = gelu_pull(grad_act)[0].astype(jnp.bfloat16)
        grad_second = contract_last(grad_up, ffn_w[:, :FF])
        gain_two_grad = jnp.sum(grad_second * normed_two, axis=0)
        bias_two_grad = jnp.sum(grad_second, axis=0)
        grad_residual = grad_hidden + norm_back(grad_second, normed_two, inverse_two, gains[:, 2])
        residual_low = grad_residual.astype(jnp.bfloat16)
        grad_in, grad_logit = attention_backward(
            jnp.dot(residual_low, out_w, preferred_element_type=jnp.float32),
            attended,
            entered,
            chosen_here,
            turn_cos,
            turn_sin,
            lengths,
            saved,
            shift,
            in_grad_width,
            3 + LAYERS + layer,
        )
        grad_first = contract_last(grad_in[:, :in_width], in_w)
        gain_one_grad = jnp.sum(grad_first * normed_one, axis=0)
        bias_one_grad = jnp.sum(grad_first, axis=0)
        grad_hidden = grad_residual + norm_back(grad_first, normed_one, inverse_one, gains[:, 0])
        norm_grads = jnp.stack(
            [gain_one_grad, bias_one_grad, gain_two_grad, bias_two_grad], axis=1
        ).astype(jnp.bfloat16)
        norm_grads = jnp.pad(norm_grads, ((0, 0), (router_cols, 128 - 4 - router_cols)))
        base = sum(segment[3] for segment in segments)
        bases[layer] = base * half
        one = len(lefts)
        lefts += [first_in, residual_low]
        in_halves = grad_in.shape[1] // half
        segments += [
            (one, grad_in, 0, in_halves),
            (one + 1, mixed, 1, mixed.shape[1] // half - 1),
        ]
        doubles.append((base + in_halves - 1, shift, one + 1, mixed))
        for kind, pair in (("up", (second_in, grad_up)), ("down", (grad_low, act))):
            if (layer, kind) in NATIVE:
                native[layer, kind] = reduced_natively(*pair)
            else:
                segments.append((len(lefts), pair[1], 0, FF // half))
                lefts.append(pair[0])
        extras.append((norm_grads, sum(segment[3] for segment in segments)))
        segments.append((one, grad_logit, 0, 1))
    names = list(native)
    begun = segments[-1][1]
    partial, begun = lax.optimization_barrier(([native[name] for name in names], begun))
    segments[-1] = (segments[-1][0], begun) + segments[-1][2:]
    for name, value in zip(names, partial):
        native[name] = value.astype(jnp.float32)
    reduced = reduce_weight_grads(lefts, segments, doubles, extras, CHUNK)
    matrix_rows = [None] * LAYERS
    small_rows = [None] * LAYERS
    for layer in range(LAYERS):
        base = bases[layer]
        rest = [native[layer, kind] for kind in ("up", "down") if (layer, kind) in NATIVE]
        used = output_end + FF * (2 - len(rest))
        matrix_rows[layer] = jnp.concatenate([reduced[:, base : base + used]] + rest, axis=1)
        small_rows[layer] = reduced[:, base + used : base + used + router_cols + 4]
    input_grad = grad_hidden.reshape(seq_count, sub_rows, width).astype(jnp.bfloat16)
    matrix_grad = jnp.stack(matrix_rows, axis=0)
    small_grad = jnp.stack(small_rows, axis=0)
    matrix_new, matrix_first_new, matrix_second_new = adam_update(
        matrix, matrix_grad, matrix_first, matrix_second, column_rates(segment), WEIGHT_DECAY
    )
    small_new, small_first_new, small_second_new = adam_update(
        small, small_grad, small_first, small_second, small_rates(), 0.0
    )
    return (
        output,
        input_grad,
        matrix_grad,
        matrix_new,
        matrix_new.astype(jnp.bfloat16),
        matrix_first_new,
        matrix_second_new,
        small_grad,
        small_new,
        small_new.astype(jnp.bfloat16),
        small_first_new,
        small_second_new,
        loads,
    )


def solution(mesh):
    in_specs = (
        P("dp", ("seq", "head"), None),
        P("dp", ("seq", "head"), None),
        P(None, "dp", ("seq", "head"), None, None, None),
        P("dp"),
        P(None, ("dp", "seq", "head"), None),
        P(None, ("dp", "seq", "head"), None),
        P(None, ("dp", "seq", "head"), None),
        P(None, ("dp", "seq", "head"), None),
        P(None, ("dp", "seq", "head"), None),
        P(None, ("dp", "seq", "head"), None),
    )
    out_specs = (
        P("dp", ("seq", "head"), None),
        P("dp", ("seq", "head"), None),
        P(None, ("dp", "seq", "head"), None),
        P(None, ("dp", "seq", "head"), None),
        P(None, ("dp", "seq", "head"), None),
        P(None, ("dp", "seq", "head"), None),
        P(None, ("dp", "seq", "head"), None),
        P(None, ("dp", "seq", "head"), None),
        P(None, ("dp", "seq", "head"), None),
        P(None, ("dp", "seq", "head"), None),
        P(None, ("dp", "seq", "head"), None),
        P(None, ("dp", "seq", "head"), None),
        P(),
    )
    return jax.shard_map(local, mesh=mesh, in_specs=in_specs, out_specs=out_specs, check_vma=False)
```

```python
import math

import jax
import jax.numpy as jnp
from jax import lax
from jax.experimental import pallas as pl
from jax.experimental.pallas import tpu as pltpu
from jax.sharding import PartitionSpec as P

D = 1024
HEADS = 4
HEAD_DIM = 112
EXPERTS = 5
FF = 4096
LAYERS = 2
STEP = 10


NORM_EPS = 1e-05
BETA_ONE = 0.9
BETA_TWO = 0.95
ADAM_EPS = 1e-08
WEIGHT_DECAY = 0.1
NORM_RATE = 0.5
MASKED = -1e30
CHUNK = 512
NATIVE = ((LAYERS - 1, "down"),)


def column_bounds():
    query_end = 2 * HEADS * HEAD_DIM
    value_end = query_end + HEADS * EXPERTS * HEAD_DIM
    output_end = value_end + HEADS * EXPERTS * HEAD_DIM
    return (query_end, value_end, output_end, output_end + FF)


def column_rates(segment):
    query_end, value_end, output_end, up_end = column_bounds()
    column = jnp.arange(up_end + FF)
    inner = D ** (-0.5)
    outer = 0.7 * math.sqrt(segment) / HEAD_DIM
    rates = jnp.where(
        column < value_end,
        inner,
        jnp.where(column < output_end, outer, jnp.where(column < up_end, inner, FF ** (-0.5))),
    )
    return rates.astype(jnp.float32)


def small_rates():
    column = jnp.arange(2 * HEADS * EXPERTS + 4)
    return jnp.where(column < 2 * HEADS * EXPERTS, 0.7 * D ** (-0.5), NORM_RATE).astype(jnp.float32)


def adam_update(weight, grad, first, second, rates, decay):
    first_new = BETA_ONE * first + (1.0 - BETA_ONE) * grad
    second_new = BETA_TWO * second + (1.0 - BETA_TWO) * grad * grad
    first_hat = first_new / (1.0 - BETA_ONE**STEP)
    second_hat = second_new / (1.0 - BETA_TWO**STEP)
    new = weight - rates * (first_hat / (jnp.sqrt(second_hat) + ADAM_EPS) + decay * weight)
    return (new, first_new, second_new)


def rotary_tables(positions):
    half = HEAD_DIM // 2
    inverse = jnp.exp(-math.log(10000.0) * jnp.arange(half, dtype=jnp.float32) / half)
    angle = positions.astype(jnp.float32)[:, None] * inverse[None, :]
    return (jnp.cos(angle), jnp.sin(angle))


def layer_stats(values):
    mean = jnp.mean(values, axis=-1, keepdims=True)
    centered = values - mean
    variance = jnp.mean(centered * centered, axis=-1, keepdims=True)
    inverse = lax.rsqrt(variance + NORM_EPS)
    return (centered * inverse, inverse)


def norm_back(grad_normed, normed, inverse, gain):
    scaled = grad_normed * gain
    return inverse * (
        scaled
        - jnp.mean(scaled, axis=-1, keepdims=True)
        - normed * jnp.mean(scaled * normed, axis=-1, keepdims=True)
    )


def contract_last(left, right):
    return lax.dot_general(
        left, right, (((1,), (1,)), ((), ())), preferred_element_type=jnp.float32
    )


def contract_first(left, right):
    return lax.dot_general(
        left, right, (((0,), (0,)), ((), ())), preferred_element_type=jnp.float32
    )


AXES = ("dp", "seq", "head")


def mesh_bits():
    dims = [
        (axis, bit)
        for axis in AXES
        for bit in reversed(range(lax.axis_size(axis).bit_length() - 1))
    ]
    groups = [[index for index, (axis, _) in enumerate(dims) if axis == name] for name in AXES]
    return (dims, *groups)


def my_bits(dims):
    place = {axis: lax.axis_index(axis) for axis in AXES}
    bits = [lax.rem(place[axis] // (1 << bit), 2) for axis, bit in dims]
    partners = [
        {axis: place[axis] + (1 << bit) * (1 - 2 * bits[index])}
        for index, (axis, bit) in enumerate(dims)
    ]
    return (bits, partners)


def greet(partners):
    barrier = pltpu.get_barrier_semaphore()
    for partner in partners:
        pl.semaphore_signal(
            barrier, inc=1, device_id=partner, device_id_type=pl.DeviceIdType.MESH
        )
    pl.semaphore_wait(barrier, len(partners))


def gather_rows(share, counts, unit, name):
    dims, dp_dims, seq_dims, head_dims = mesh_bits()
    orders = (
        head_dims + dp_dims[::-1] + seq_dims,
        head_dims + dp_dims + seq_dims,
        dp_dims + head_dims + seq_dims,
    )
    depth = len(dims)
    rows, width = share.shape
    units = width // unit
    near = (11 * units + 16) // 32
    pieces, start = ([], 0)
    for which, count in ((0, near), (1, near), (2, units - 2 * near)):
        pieces.append((start, count, which))
        start += count * unit
    lag, slots = (3, 6)
    local_slots = 2
    ring = (depth + 1) * lag + local_slots + 2
    steps = max(count for _, count, _ in pieces) + lag * depth

    def kernel(*refs):
        share_ref, counts_ref, out_ref, counts_out = refs[:4]
        send_sem, recv_sem, load_sem, store_sem, small_send, small_recv, small_load = refs[4:11]
        buffers = refs[11:]
        bits, partners = my_bits(dims)

        def at_stage(which, stage):
            done = orders[which][:stage]
            return tuple(slice(None) if dim in done else bits[dim] for dim in range(depth))

        def columns(number, chunk):
            return pl.ds(pl.multiple_of(pieces[number][0] + chunk * unit, 128), unit)

        def exchange(number, stage, chunk):
            which = pieces[number][2]
            view = buffers[number].at[(lax.rem(chunk, ring),) + at_stage(which, stage)]
            slot = lax.rem(chunk, slots)
            return sent_to(
                view,
                view,
                send_sem.at[number, stage, slot],
                recv_sem.at[number, stage, slot],
                partners[orders[which][stage]],
            )

        def load(number, chunk):
            return pltpu.make_async_copy(
                share_ref.at[:, columns(number, chunk)],
                buffers[number].at[(lax.rem(chunk, ring),) + tuple(bits)],
                load_sem.at[number, lax.rem(chunk, local_slots)],
            )

        def store(number, chunk):
            return pltpu.make_async_copy(
                buffers[number].at[lax.rem(chunk, ring)],
                out_ref.at[(slice(None),) * (depth + 1) + (columns(number, chunk),)],
                store_sem.at[number, lax.rem(chunk, local_slots)],
            )

        def small(stage):
            view = counts_out.at[at_stage(0, stage)]
            return sent_to(
                view, view, small_send.at[stage], small_recv.at[stage], partners[orders[0][stage]]
            )

        own_counts = pltpu.make_async_copy(counts_ref, counts_out.at[tuple(bits)], small_load)
        own_counts.start()
        for number in range(len(pieces)):
            for chunk in range(local_slots):
                load(number, jnp.int32(chunk)).start()
        greet(partners)
        own_counts.wait()

        def body(step, carry):
            for stage in range(depth, -1, -1):
                chunk = step - lag * stage
                for number, piece in enumerate(pieces):

                    @pl.when((chunk >= 0) & (chunk < piece[1]))
                    def _(stage=stage, chunk=chunk, number=number, piece=piece):
                        if stage > 0:
                            exchange(number, stage - 1, chunk).wait()
                        else:
                            load(number, chunk).wait()

                            @pl.when(chunk + local_slots < piece[1])
                            def _():
                                load(number, chunk + local_slots).start()

                        if stage < depth:
                            exchange(number, stage, chunk).start()
                        else:

                            @pl.when(chunk >= local_slots)
                            def _():
                                store(number, chunk - local_slots).wait()

                            store(number, chunk).start()

                @pl.when(chunk == 0)
                def _(stage=stage):
                    if stage > 0:
                        small(stage - 1).wait()
                    if stage < depth:
                        small(stage).start()

            return carry

        lax.fori_loop(0, steps, body, 0)
        for number, piece in enumerate(pieces):
            for back in range(min(local_slots, piece[1])):
                store(number, jnp.int32(piece[1] - 1 - back)).wait()

    in_place = pl.BlockSpec(memory_space=pl.ANY)
    semaphores = pltpu.SemaphoreType.DMA((len(pieces), depth, slots))
    local = pltpu.SemaphoreType.DMA((len(pieces), local_slots))
    gathered, all_counts = pl.pallas_call(
        kernel,
        in_specs=[in_place] * 2,
        out_specs=[in_place] * 2,
        out_shape=[
            jax.ShapeDtypeStruct((2,) * depth + value.shape, value.dtype)
            for value in (share, counts)
        ],
        scratch_shapes=[
            semaphores,
            semaphores,
            local,
            local,
            pltpu.SemaphoreType.DMA((depth,)),
            pltpu.SemaphoreType.DMA((depth,)),
            pltpu.SemaphoreType.DMA,
        ]
        + [pltpu.VMEM((ring,) + (2,) * depth + (rows, unit), share.dtype) for _ in pieces],
        compiler_params=pltpu.CompilerParams(
            collective_id=name, has_side_effects=True, vmem_limit_bytes=48 << 20
        ),
    )(share, counts)
    return (gathered.reshape(-1, width), all_counts.reshape(-1, counts.shape[1]))


def halving_plan(width):
    dims, dp_dims, seq_dims, head_dims = mesh_bits()
    first = seq_dims[::-1]
    orders = (
        (0, width // 2, first + dp_dims[::-1] + head_dims[::-1]),
        (width // 2, width // 4, first + dp_dims + head_dims[::-1]),
        (3 * width // 4, width // 4, first + head_dims[::-1] + dp_dims),
    )
    stages = []
    for stage in range(len(dims)):
        parts = []
        for start, count, order in orders:
            left = [dim for dim in range(len(dims)) if dim not in order[:stage]]
            if parts and parts[-1][2:] == (order[stage], left):
                parts[-1] = (parts[-1][0], parts[-1][1] + count, order[stage], left)
            else:
                parts.append((start, count, order[stage], left))
        stages.append(parts)
    lags = [1 if stage < len(seq_dims) else 2 for stage in range(len(dims))]
    return dims, stages, lags


def reduce_weight_grads(lefts, segments, doubles, extras, width):
    dims, stages, lags = halving_plan(width)
    depth = len(dims)
    half = width // 2
    tokens, model = lefts[0].shape
    rows = model >> depth
    firsts = [0]
    for _, _, _, count in segments:
        firsts.append(firsts[-1] + count)
    chunks = firsts[-1] // 2
    spots = [(where // 2, where % 2 * half) for _, where in extras]
    starts = [sum(lags[:stage]) for stage in range(depth + 1)]
    rights = [right for _, right, _, _ in segments] + [right for _, _, _, right in doubles]
    count_lefts, count_rights, count_extras = (len(lefts), len(rights), len(extras))
    first_use = [
        min(firsts[index] // 2 for index, segment in enumerate(segments) if segment[0] == left)
        for left in range(count_lefts)
    ]
    for where, _, left, _ in doubles:
        first_use[left] = min(first_use[left], where // 2)

    def kernel(*refs):
        left_refs = refs[:count_lefts]
        right_refs = refs[count_lefts : count_lefts + count_rights]
        rest = refs[count_lefts + count_rights :]
        added, rest = (rest[:count_extras], rest[count_extras:])
        out_ref, left_buf, turned, right_buf, double_buf, left_sem, right_sem, double_sem = rest[:8]
        pool = iter(rest[8:])
        buffers = [[tuple(next(pool) for _ in range(4)) for _ in parts] for parts in stages]
        step = pl.program_id(0)
        bits, partners = my_bits(dims)

        def exchange(stage, part, slot):
            start, count, dim, left = stages[stage][part]
            own, got, send_sem, recv_sem = buffers[stage][part]
            lead = (slot,) + (slice(None),) * left.index(dim)
            return pltpu.make_async_remote_copy(
                src_ref=own.at[lead + (1 - bits[dim],)],
                dst_ref=got.at[slot],
                send_sem=send_sem.at[slot],
                recv_sem=recv_sem.at[slot],
                device_id=partners[dim],
                device_id_type=pl.DeviceIdType.MESH,
            )

        def load_left(index):
            return pltpu.make_async_copy(left_refs[index], left_buf.at[index], left_sem.at[index])

        def load_right(index, at, chunk, side):
            columns = pl.ds(pl.multiple_of(at * half, half), half)
            slot = lax.rem(chunk, 2)
            return pltpu.make_async_copy(
                right_refs[index].at[:, columns],
                right_buf.at[slot, side],
                right_sem.at[slot, side],
            )

        def load_double(index):
            return pltpu.make_async_copy(
                right_refs[len(segments) + index].at[:, 0:half], double_buf, double_sem
            )

        def prefetch(chunk):
            for side in range(2):
                place = 2 * chunk + side
                for index, (_, _, begin, _) in enumerate(segments):

                    @pl.when((place >= firsts[index]) & (place < firsts[index + 1]))
                    def _(index=index, begin=begin, place=place, side=side):
                        load_right(index, place - firsts[index] + begin, chunk, side).start()

            for index, (where, _, _, _) in enumerate(doubles):

                @pl.when(chunk == where // 2)
                def _(index=index):
                    load_double(index).start()

        @pl.when(step == 0)
        def _():
            for index in range(count_lefts):
                load_left(index).start()
            prefetch(step)
            greet(partners)

        @pl.when(step + 1 < chunks)
        def _():
            prefetch(step + 1)

        for stage in range(depth, -1, -1):
            chunk = step - starts[stage]

            @pl.when((chunk >= 0) & (chunk < chunks))
            def _(stage=stage, chunk=chunk):
                if stage == 0:
                    slot = lax.rem(chunk, 2 * lags[0])
                    near = lax.rem(chunk, 2)
                    own = buffers[0][0][0]
                    for index in range(count_lefts):

                        @pl.when(chunk == first_use[index])
                        def _(index=index):
                            load_left(index).wait()
                            turned[index] = left_buf[index].T

                    for side in range(2):
                        place = 2 * chunk + side
                        which = jnp.int32(segments[0][0])
                        for index, segment in enumerate(segments):
                            which = jnp.where(place >= firsts[index], segment[0], which)
                        load_right(0, 0, chunk, side).wait()
                        for where, kept, _, _ in doubles:
                            if where % 2 == side:

                                @pl.when(chunk == where // 2)
                                def _(kept=kept, side=side):
                                    right_buf[near, side, :, kept:] = jnp.zeros(
                                        (tokens, half - kept), jnp.bfloat16
                                    )

                        product = jnp.dot(
                            turned[which],
                            right_buf[near, side],
                            preferred_element_type=jnp.float32,
                        )
                        own[(slot, Ellipsis, slice(side * half, side * half + half))] = (
                            product.astype(jnp.bfloat16).reshape((2,) * depth + (rows, half))
                        )
                    for index, (where, _, left, _) in enumerate(doubles):

                        @pl.when(chunk == where // 2)
                        def _(index=index, where=where, left=left):
                            load_double(index).wait()
                            product = jnp.dot(
                                turned[left], double_buf[...], preferred_element_type=jnp.float32
                            ).reshape((2,) * depth + (rows, half))
                            begin = where % 2 * half
                            at = (slot, Ellipsis, slice(begin, begin + half))
                            own[at] = (own[at].astype(jnp.float32) + product).astype(jnp.bfloat16)

                    for index in range(count_extras):

                        @pl.when(chunk == spots[index][0])
                        def _(index=index):
                            at = (slot, Ellipsis, slice(spots[index][1], spots[index][1] + 128))
                            total = own[at].astype(jnp.float32) + added[index][...].astype(
                                jnp.float32
                            )
                            own[at] = total.astype(jnp.bfloat16)

                else:
                    back = lax.rem(chunk, 2 * lags[stage - 1])
                    for part, (start, count, dim, left) in enumerate(stages[stage - 1]):
                        exchange(stage - 1, part, back).wait()
                        own, got = buffers[stage - 1][part][:2]
                        lead = (back,) + (slice(None),) * left.index(dim)
                        total = own[lead + (bits[dim],)].astype(jnp.float32) + got[back].astype(
                            jnp.float32
                        )
                        if stage == depth:
                            out_ref[:, start : start + count] = total
                            continue
                        slot = lax.rem(chunk, 2 * lags[stage])
                        low = total.astype(jnp.bfloat16)
                        for other, (begin, length, _, kept) in enumerate(stages[stage]):
                            lo, hi = max(start, begin), min(start + count, begin + length)
                            if lo < hi:
                                at = (slot,) + (slice(None),) * (len(kept) + 1)
                                buffers[stage][other][0][at + (slice(lo - begin, hi - begin),)] = (
                                    low[..., lo - start : hi - start]
                                )
                if stage < depth:
                    for part in range(len(stages[stage])):
                        exchange(stage, part, lax.rem(chunk, 2 * lags[stage])).start()

    scratch = [
        pltpu.VMEM((count_lefts, tokens, model), jnp.bfloat16),
        pltpu.VMEM((count_lefts, model, tokens), jnp.bfloat16),
        pltpu.VMEM((2, 2, tokens, half), jnp.bfloat16),
        pltpu.VMEM((tokens, half), jnp.bfloat16),
        pltpu.SemaphoreType.DMA((count_lefts,)),
        pltpu.SemaphoreType.DMA((2, 2)),
        pltpu.SemaphoreType.DMA,
    ]
    for stage, parts in enumerate(stages):
        slots = 2 * lags[stage]
        for start, count, dim, left in parts:
            scratch += [
                pltpu.VMEM((slots,) + (2,) * len(left) + (rows, count), jnp.bfloat16),
                pltpu.VMEM((slots,) + (2,) * (len(left) - 1) + (rows, count), jnp.bfloat16),
                pltpu.SemaphoreType.DMA((slots,)),
                pltpu.SemaphoreType.DMA((slots,)),
            ]
    in_place = pl.BlockSpec(memory_space=pl.ANY)
    whole = [value.reshape((2,) * depth + (rows, 128)) for value, _ in extras]
    return pl.pallas_call(
        kernel,
        grid=(chunks + starts[depth],),
        in_specs=[in_place] * (count_lefts + count_rights)
        + [pl.BlockSpec(value.shape, lambda step: (0,) * (depth + 2)) for value in whole],
        out_specs=pl.BlockSpec(
            (rows, width), lambda step: (0, jnp.clip(step - starts[depth], 0, chunks - 1))
        ),
        out_shape=jax.ShapeDtypeStruct((rows, chunks * width), jnp.float32),
        scratch_shapes=scratch,
        compiler_params=pltpu.CompilerParams(
            collective_id=1,
            has_side_effects=True,
            vmem_limit_bytes=48 << 20,
            dimension_semantics=("arbitrary",),
        ),
    )(*lefts, *rights, *whole)


def reduction_order(tensor):
    dp, seq = (lax.axis_size("dp"), lax.axis_size("seq"))
    count, width = tensor.shape
    split = tensor.reshape(count, dp, seq, width // (dp * seq))
    return split.transpose(0, 2, 1, 3).reshape(count, width)


def reduced_natively(left, right):
    share = contract_first(reduction_order(left), right).astype(jnp.bfloat16)
    for axis in ("seq", "dp", "head"):
        share = lax.psum_scatter(share, axis, scatter_dimension=0, tiled=True)
    return share


def lane_whole(count):
    return count + (-count) % 128


def padded(pieces, width):
    have = sum(piece.shape[1] for piece in pieces)
    fill = jnp.zeros((pieces[0].shape[0], width - have), pieces[0].dtype)
    return jnp.concatenate(list(pieces) + [fill], axis=1)


LANES = 128
QUERY_TILE = 256


def swap_halves(tensor):
    half = HEAD_DIM // 2
    return jnp.concatenate([tensor[:, half:], tensor[:, :half]], axis=1)


def lane_filled(tensor):
    fill = jnp.zeros((tensor.shape[0], LANES - tensor.shape[1]), tensor.dtype)
    return jnp.concatenate([tensor, fill], axis=1)


def weights_block(keys_mem, keys_own, query, start, first, segment, length):
    contract = (((1,), (1,)), ((), ()))
    raw = jnp.concatenate(
        [
            lax.dot_general(keys, query, contract, preferred_element_type=jnp.float32)
            for keys in (keys_mem, keys_own)
        ],
        axis=0,
    )
    key_pos = start - segment + lax.broadcasted_iota(jnp.int32, raw.shape, 0)
    query_pos = start + first + lax.broadcasted_iota(jnp.int32, raw.shape, 1)
    used = (key_pos < length) & (key_pos < query_pos) & (key_pos >= 0)
    allowed = used | (key_pos == query_pos)
    scores = jnp.where(allowed, raw * HEAD_DIM ** (-0.5), MASKED)
    weights = jnp.exp(scores - jnp.max(scores, axis=0, keepdims=True))
    return weights * (1.0 / jnp.sum(weights, axis=0, keepdims=True))


def contract_rows(left, right):
    return lax.dot_general(
        left, right, (((0,), (0,)), ((), ())), preferred_element_type=jnp.float32
    )


def across(axis, offset):
    size = lax.axis_size(axis)
    return {axis: lax.rem(lax.axis_index(axis) + offset + size, size)}


def sent_to(source, target, send_sem, recv_sem, device):
    return pltpu.make_async_remote_copy(
        src_ref=source,
        dst_ref=target,
        send_sem=send_sem,
        recv_sem=recv_sem,
        device_id=device,
        device_id_type=pl.DeviceIdType.MESH,
    )


def meet(memory_step):
    barrier = pltpu.get_barrier_semaphore()
    heads = lax.axis_size("head")
    writers = [across("head", step) for step in range(1, heads)]
    writers.append(across("seq", -memory_step))
    for device in writers:
        pl.semaphore_signal(barrier, inc=1, device_id=device, device_id_type=pl.DeviceIdType.MESH)
    pl.semaphore_wait(barrier, len(writers))


def gate_values(entered_ref, chosen_ref, rows):
    at = column_bounds()[1]
    logits = entered_ref[rows, at : at + 2 * HEADS * EXPERTS]
    prob = 1.0 / (1.0 + jnp.exp(-logits))
    return (prob, prob * chosen_ref[rows, :])


def column(tensor, index):
    return tensor[:, index : index + 1]


def attention_forward(entered, chosen, turn_cos, turn_sin, lengths, shift, name):
    seq_count = lengths.shape[0]
    tokens = entered.shape[0]
    sub = tokens // seq_count
    heads = lax.axis_size("head")
    segment = heads * sub
    query_end = column_bounds()[0]
    sides = range(1, heads)

    def kernel(*refs):
        length_ref, entered_ref, chosen_ref, cos_ref, sin_ref = refs[:5]
        mixed_ref, attended_ref, query_ref, key_ref, value_ref = refs[5:10]
        out_buf, heads_buf, mem_buf, done_buf, back_buf = refs[10:15]
        out_sem, in_sem, mem_sem, done_sem, back_sem = refs[15:]
        me = lax.axis_index("head")
        start = lax.axis_index("seq") * segment
        turn, wind = (cos_ref[...], sin_ref[...])

        def outward(b, side):
            there = across("head", side)
            return sent_to(
                out_buf.at[b, there["head"]],
                heads_buf.at[b, :, me],
                out_sem.at[b, side - 1],
                in_sem.at[b, side - 1],
                there,
            )

        def onward(b):
            return sent_to(
                heads_buf.at[b, 1:3],
                mem_buf.at[b],
                mem_sem.at[0, b],
                mem_sem.at[1, b],
                across("seq", 1),
            )

        def homeward(b, side):
            there = across("head", side)
            return sent_to(
                done_buf.at[b, there["head"]],
                back_buf.at[b, me],
                done_sem.at[b, side - 1],
                back_sem.at[b, side - 1],
                there,
            )

        meet(1)
        gates_of = []
        for b in range(seq_count):
            rows = slice(b * sub, (b + 1) * sub)
            gates = gate_values(entered_ref, chosen_ref, rows)[1]
            gates_of.append(gates)
            for head in range(HEADS):
                for kind in range(2):
                    at = (kind * HEADS + head) * HEAD_DIM
                    vector = entered_ref[rows, at : at + HEAD_DIM]
                    turned = vector * turn + swap_halves(vector) * wind
                    out_buf[b, head, kind] = lane_filled(turned).astype(jnp.bfloat16)
                value = jnp.zeros((sub, HEAD_DIM), jnp.float32)
                for expert in range(EXPERTS):
                    index = head * EXPERTS + expert
                    at = query_end + index * HEAD_DIM
                    value += column(gates, index) * entered_ref[rows, at : at + HEAD_DIM]
                out_buf[b, head, 2] = lane_filled(value).astype(jnp.bfloat16)
            for side in sides:
                outward(b, side).start()
            for kind in range(3):
                heads_buf[b, kind, me] = out_buf[b, me, kind]
        for b in range(seq_count):
            for side in sides:
                outward(b, side).wait_recv()
            onward(b).start()
        for b in range(seq_count):
            onward(b).wait_recv()
            keys_own = heads_buf[b, 1].reshape(segment, LANES)
            values = jnp.concatenate(
                [mem_buf[b, 1].reshape(segment, LANES), heads_buf[b, 2].reshape(segment, LANES)],
                axis=0,
            )
            for first in range(0, segment, QUERY_TILE):
                tile = slice(first // sub, (first + QUERY_TILE) // sub)
                query = heads_buf[b, 0, tile].reshape(QUERY_TILE, LANES)
                probs = weights_block(
                    mem_buf[b, 0].reshape(segment, LANES),
                    keys_own,
                    query,
                    start,
                    first,
                    segment,
                    length_ref[b],
                ).astype(jnp.bfloat16)
                attended = contract_rows(values, probs).T.astype(jnp.bfloat16)
                done_buf[b, tile] = attended.reshape(QUERY_TILE // sub, sub, LANES)
            for side in sides:
                homeward(b, side).start()
            back_buf[b, me] = done_buf[b, me]
        for b in range(seq_count):
            query_ref[b] = heads_buf[b, 0]
            key_ref[b, 0] = mem_buf[b, 0]
            key_ref[b, 1] = heads_buf[b, 1]
            value_ref[b, 0] = mem_buf[b, 1]
            value_ref[b, 1] = heads_buf[b, 2]
        mixed_ref[:, :shift] = jnp.zeros((tokens, shift), jnp.bfloat16)
        for b in range(seq_count):
            rows = slice(b * sub, (b + 1) * sub)
            for side in sides:
                homeward(b, side).wait_recv()
            for head in range(HEADS):
                attended = back_buf[b, head]
                attended_ref[rows, head * LANES : (head + 1) * LANES] = attended
                wide = attended.astype(jnp.float32)[:, :HEAD_DIM]
                for expert in range(EXPERTS):
                    index = head * EXPERTS + expert
                    gate = column(gates_of[b], HEADS * EXPERTS + index)
                    at = shift + index * HEAD_DIM
                    mixed_ref[rows, at : at + HEAD_DIM] = (
                        gate * wide
                    ).astype(jnp.bfloat16)
        for b in range(seq_count):
            onward(b).wait_send()
            for side in sides:
                outward(b, side).wait_send()
                homeward(b, side).wait_send()

    def shape(*dims):
        return jax.ShapeDtypeStruct(dims, jnp.bfloat16)

    vmem = pl.BlockSpec(memory_space=pltpu.VMEM)
    paired = pltpu.SemaphoreType.DMA((seq_count, heads - 1))
    return pl.pallas_call(
        kernel,
        in_specs=[pl.BlockSpec(memory_space=pltpu.SMEM)] + [vmem] * 4,
        out_specs=[vmem] * 5,
        out_shape=[
            shape(tokens, shift + HEADS * EXPERTS * HEAD_DIM),
            shape(tokens, HEADS * LANES),
            shape(seq_count, heads, sub, LANES),
            shape(seq_count, 2, heads, sub, LANES),
            shape(seq_count, 2, heads, sub, LANES),
        ],
        scratch_shapes=[
            pltpu.VMEM((seq_count, heads, 3, sub, LANES), jnp.bfloat16),
            pltpu.VMEM((seq_count, 3, heads, sub, LANES), jnp.bfloat16),
            pltpu.VMEM((seq_count, 2, heads, sub, LANES), jnp.bfloat16),
            pltpu.VMEM((seq_count, heads, sub, LANES), jnp.bfloat16),
            pltpu.VMEM((seq_count, heads, sub, LANES), jnp.bfloat16),
            paired,
            paired,
            pltpu.SemaphoreType.DMA((2, seq_count)),
            paired,
            paired,
        ],
        compiler_params=pltpu.CompilerParams(
            collective_id=name, has_side_effects=True, vmem_limit_bytes=40 << 20
        ),
    )(lengths, entered, chosen, turn_cos, turn_sin)


def attention_backward(
    grad_mixed, attended, entered, chosen, turn_cos, turn_sin, lengths, saved, shift, grad_width, name
):
    query, keys, values = saved
    seq_count = lengths.shape[0]
    tokens = entered.shape[0]
    sub = tokens // seq_count
    heads = lax.axis_size("head")
    segment = heads * sub
    query_end, value_end = column_bounds()[:2]
    router_cols = 2 * HEADS * EXPERTS
    sides = range(1, heads)

    def kernel(*refs):
        length_ref, grad_ref, attended_ref, entered_ref, chosen_ref, cos_ref, sin_ref = refs[:7]
        query_ref, key_ref, value_ref, result_ref, logit_ref = refs[7:12]
        out_buf, heads_buf, mem_out, mem_in, own_buf, done_buf, back_buf = refs[12:19]
        out_sem, in_sem, mem_sem, query_sem, done_sem, back_sem = refs[19:]
        me = lax.axis_index("head")
        start = lax.axis_index("seq") * segment
        turn, wind = (cos_ref[...], sin_ref[...])

        def outward(b, side):
            there = across("head", side)
            return sent_to(
                out_buf.at[b, there["head"]],
                heads_buf.at[b, me],
                out_sem.at[b, side - 1],
                in_sem.at[b, side - 1],
                there,
            )

        def onward(b):
            return sent_to(
                mem_out.at[b], mem_in.at[b], mem_sem.at[0, b], mem_sem.at[1, b], across("seq", -1)
            )

        def queries_home(b, side):
            there = across("head", side)
            return sent_to(
                done_buf.at[b, there["head"], 0],
                back_buf.at[b, me, 0],
                query_sem.at[0, b, side - 1],
                query_sem.at[1, b, side - 1],
                there,
            )

        def homeward(b, side):
            there = across("head", side)
            return sent_to(
                done_buf.at[b, there["head"], 1:3],
                back_buf.at[b, me, 1:3],
                done_sem.at[b, side - 1],
                back_sem.at[b, side - 1],
                there,
            )

        def join_memory(b):
            onward(b).wait_recv()
            for kind in range(2):
                total = own_buf[b, kind] + mem_in[b, kind].astype(jnp.float32)
                done_buf[b, :, kind + 1] = total.astype(jnp.bfloat16).reshape(heads, sub, LANES)
            for side in sides:
                homeward(b, side).start()
            back_buf[b, me] = done_buf[b, me]

        meet(-1)
        lane = lax.broadcasted_iota(jnp.int32, (sub, router_cols), 1)
        gate_grads, probs_of, gates_of = ([], [], [])
        for b in range(seq_count):
            rows = slice(b * sub, (b + 1) * sub)
            prob, gates = gate_values(entered_ref, chosen_ref, rows)
            probs_of.append(prob)
            gates_of.append(gates)
            gate_grad = jnp.zeros((sub, router_cols), jnp.float32)
            for head in range(HEADS):
                seen = attended_ref[rows, head * LANES : head * LANES + HEAD_DIM].astype(
                    jnp.float32
                )
                total = jnp.zeros((sub, HEAD_DIM), jnp.float32)
                for expert in range(EXPERTS):
                    index = head * EXPERTS + expert
                    at = shift + index * HEAD_DIM
                    part = grad_ref[rows, at : at + HEAD_DIM]
                    total += column(gates, HEADS * EXPERTS + index) * part
                    gate_grad = jnp.where(
                        lane == HEADS * EXPERTS + index,
                        jnp.sum(part * seen, axis=1, keepdims=True),
                        gate_grad,
                    )
                out_buf[b, head] = lane_filled(total).astype(jnp.bfloat16)
            gate_grads.append(gate_grad)
            for side in sides:
                outward(b, side).start()
            heads_buf[b, me] = out_buf[b, me]
        for b in range(seq_count):
            for side in sides:
                outward(b, side).wait_recv()
            keys_mem = key_ref[b, 0].reshape(segment, LANES)
            keys_own = key_ref[b, 1].reshape(segment, LANES)
            keys_all = jnp.concatenate([keys_mem, keys_own], axis=0)
            values_all = jnp.concatenate(
                [value_ref[b, 0].reshape(segment, LANES), value_ref[b, 1].reshape(segment, LANES)],
                axis=0,
            )
            grad_keys = jnp.zeros((2 * segment, LANES), jnp.float32)
            grad_values = jnp.zeros((2 * segment, LANES), jnp.float32)
            for first in range(0, segment, QUERY_TILE):
                tile = slice(first // sub, (first + QUERY_TILE) // sub)
                here = query_ref[b, tile].reshape(QUERY_TILE, LANES)
                arrived = heads_buf[b, tile].reshape(QUERY_TILE, LANES)
                probs = weights_block(
                    keys_mem, keys_own, here, start, first, segment, length_ref[b]
                )
                grad_probs = contract_last(values_all, arrived)
                delta = jnp.sum(probs * grad_probs, axis=0, keepdims=True)
                grad_raw = (probs * (grad_probs - delta) * HEAD_DIM ** (-0.5)).astype(
                    jnp.bfloat16
                )
                grad_values += jnp.dot(
                    probs.astype(jnp.bfloat16), arrived, preferred_element_type=jnp.float32
                )
                grad_keys += jnp.dot(grad_raw, here, preferred_element_type=jnp.float32)
                grad_query = contract_rows(keys_all, grad_raw).T.astype(jnp.bfloat16)
                done_buf[b, tile, 0] = grad_query.reshape(QUERY_TILE // sub, sub, LANES)
                if b > 0 and first == 0:
                    join_memory(b - 1)
            for kind, grads in enumerate((grad_keys, grad_values)):
                mem_out[b, kind] = grads[:segment].astype(jnp.bfloat16)
                own_buf[b, kind] = grads[segment:]
            onward(b).start()
            for side in sides:
                queries_home(b, side).start()
        join_memory(seq_count - 1)
        used = value_end + router_cols
        result_ref[:, used:] = jnp.zeros((tokens, grad_width - used), jnp.bfloat16)
        logit_ref[:, router_cols:] = jnp.zeros((tokens, CHUNK // 2 - router_cols), jnp.bfloat16)
        for b in range(seq_count):
            rows = slice(b * sub, (b + 1) * sub)
            for side in sides:
                queries_home(b, side).wait_recv()
                homeward(b, side).wait_recv()
            gate_grad = gate_grads[b]
            for head in range(HEADS):
                for kind in range(2):
                    vector = back_buf[b, head, kind].astype(jnp.float32)[:, :HEAD_DIM]
                    turned = vector * turn - swap_halves(vector) * wind
                    at = (kind * HEADS + head) * HEAD_DIM
                    result_ref[rows, at : at + HEAD_DIM] = turned.astype(jnp.bfloat16)
                grad_value = back_buf[b, head, 2].astype(jnp.float32)[:, :HEAD_DIM]
                for expert in range(EXPERTS):
                    index = head * EXPERTS + expert
                    at = query_end + index * HEAD_DIM
                    gate_grad = jnp.where(
                        lane == index,
                        jnp.sum(
                            entered_ref[rows, at : at + HEAD_DIM] * grad_value,
                            axis=1,
                            keepdims=True,
                        ),
                        gate_grad,
                    )
                    result_ref[rows, at : at + HEAD_DIM] = (
                        column(gates_of[b], index) * grad_value
                    ).astype(jnp.bfloat16)
            prob = probs_of[b]
            grad_logit = (gate_grad * chosen_ref[rows, :] * prob * (1.0 - prob)).astype(
                jnp.bfloat16
            )
            result_ref[rows, value_end:used] = grad_logit
            logit_ref[rows, :router_cols] = grad_logit
        for b in range(seq_count):
            onward(b).wait_send()
            for side in sides:
                outward(b, side).wait_send()
                queries_home(b, side).wait_send()
                homeward(b, side).wait_send()

    vmem = pl.BlockSpec(memory_space=pltpu.VMEM)
    paired = pltpu.SemaphoreType.DMA((seq_count, heads - 1))
    return pl.pallas_call(
        kernel,
        in_specs=[pl.BlockSpec(memory_space=pltpu.SMEM)] + [vmem] * 9,
        out_specs=[vmem] * 2,
        out_shape=[
            jax.ShapeDtypeStruct((tokens, count), jnp.bfloat16)
            for count in (grad_width, CHUNK // 2)
        ],
        scratch_shapes=[
            pltpu.VMEM((seq_count, heads, sub, LANES), jnp.bfloat16),
            pltpu.VMEM((seq_count, heads, sub, LANES), jnp.bfloat16),
            pltpu.VMEM((seq_count, 2, segment, LANES), jnp.bfloat16),
            pltpu.VMEM((seq_count, 2, segment, LANES), jnp.bfloat16),
            pltpu.VMEM((seq_count, 2, segment, LANES), jnp.float32),
            pltpu.VMEM((seq_count, heads, 3, sub, LANES), jnp.bfloat16),
            pltpu.VMEM((seq_count, heads, 3, sub, LANES), jnp.bfloat16),
            paired,
            paired,
            pltpu.SemaphoreType.DMA((2, seq_count)),
            pltpu.SemaphoreType.DMA((2, seq_count, heads - 1)),
            paired,
            paired,
        ],
        compiler_params=pltpu.CompilerParams(
            collective_id=name, has_side_effects=True, vmem_limit_bytes=48 << 20
        ),
    )(lengths, grad_mixed, attended, entered, chosen, turn_cos, turn_sin, query, keys, values)


def gelu_tanh(values):
    return jax.nn.gelu(values, approximate=True)


def local(
    inputs,
    cotangent,
    routes,
    lengths,
    matrix,
    matrix_first,
    matrix_second,
    small,
    small_first,
    small_second,
):
    head_count = lax.axis_size("head")
    seq_count, sub_rows, width = inputs.shape
    segment = sub_rows * head_count
    tokens = seq_count * sub_rows
    router_cols = 2 * HEADS * EXPERTS
    group = HEADS * EXPERTS
    query_end, value_end, output_end, up_end = column_bounds()
    seq_start = lax.axis_index("seq") * segment
    positions = (
        seq_start + lax.axis_index("head") * sub_rows + jnp.arange(sub_rows, dtype=jnp.int32)
    )
    valid = (positions[None, :] < lengths[:, None]).astype(jnp.float32)
    cosines, sines = rotary_tables(positions)
    turn_cos = jnp.concatenate([cosines, cosines], axis=1)
    turn_sin = jnp.concatenate([-sines, sines], axis=1)
    chosen = jnp.sum(
        (routes[..., None] == jnp.arange(EXPERTS, dtype=jnp.int32)).astype(jnp.float32), axis=-2
    )
    load_part = jnp.sum(chosen * valid[None, :, :, None, None, None], axis=(1, 2))
    in_width = lane_whole(value_end + router_cols + 4)
    half = CHUNK // 2
    shift = value_end % half
    in_grad_width = value_end + (-value_end) % half
    out_width = shift + output_end - value_end
    matrix_low = matrix.astype(jnp.bfloat16)
    small_low = small.astype(jnp.bfloat16)
    in_low = [
        padded([matrix_low[layer, :, :value_end], small_low[layer]], in_width)
        for layer in range(LAYERS)
    ]
    out_low = [
        jnp.pad(matrix_low[layer, :, value_end:output_end], ((0, 0), (shift, 0)))
        for layer in range(LAYERS)
    ]
    ffn_low = [matrix_low[layer, :, output_end:] for layer in range(LAYERS)]
    size = load_part.size
    counts = jnp.pad(load_part.reshape(-1), (0, (-size) % 1024)).reshape(8, -1)
    early = []
    for layer in range(LAYERS):
        early += [in_low[layer], out_low[layer]] + ([ffn_low[layer]] if layer + 1 < LAYERS else [])
    gathered, counts = gather_rows(jnp.concatenate(early, axis=1), counts, 256, 2)
    counts, late = lax.optimization_barrier((counts, ffn_low[-1]))
    loads = jnp.sum(counts.reshape(-1, size + (-size) % 1024), axis=0)[:size].reshape(
        load_part.shape
    )
    late = lax.all_gather(late, ("dp", "seq", "head"), axis=0, tiled=True)
    pieces, start = ([], 0)
    for value in early:
        pieces.append(gathered[:, start : start + value.shape[1]])
        start += value.shape[1]
    pieces.append(late)
    in_ws, out_ws, ffn_ws = (pieces[0::3], pieces[1::3], pieces[2::3])
    hidden = inputs.astype(jnp.float32).reshape(tokens, width)
    kept = []
    for layer in range(LAYERS):
        in_w, out_w, ffn_w = (in_ws[layer], out_ws[layer], ffn_ws[layer])
        gains = in_w[:, value_end + router_cols : value_end + router_cols + 4].astype(jnp.float32)
        normed_one, inverse_one = layer_stats(hidden)
        first_in = (normed_one * gains[:, 0] + gains[:, 1]).astype(jnp.bfloat16)
        entered = jnp.dot(first_in, in_w, preferred_element_type=jnp.float32)
        chosen_here = chosen[layer].reshape(tokens, router_cols)
        mixed, attended, *saved = attention_forward(
            entered,
            chosen_here,
            turn_cos,
            turn_sin,
            lengths,
            shift,
            3 + layer,
        )
        residual = hidden + contract_last(mixed, out_w)
        normed_two, inverse_two = layer_stats(residual)
        second_in = (normed_two * gains[:, 2] + gains[:, 3]).astype(jnp.bfloat16)
        up = jnp.dot(second_in, ffn_w[:, :FF], preferred_element_type=jnp.float32)
        act = gelu_tanh(up).astype(jnp.bfloat16)
        hidden = residual + contract_last(act, ffn_w[:, FF:])
        kept.append(
            (
                normed_one,
                inverse_one,
                first_in,
                entered,
                chosen_here,
                mixed,
                attended,
                saved,
                normed_two,
                inverse_two,
                second_in,
                up,
                act,
            )
        )
    output = hidden.reshape(seq_count, sub_rows, width).astype(jnp.bfloat16)
    grad_hidden = (cotangent.astype(jnp.float32) * valid[:, :, None]).reshape(tokens, width)
    lefts, segments, doubles, extras, native, bases = ([], [], [], [], {}, {})
    for layer in reversed(range(LAYERS)):
        (
            normed_one,
            inverse_one,
            first_in,
            entered,
            chosen_here,
            mixed,
            attended,
            saved,
            normed_two,
            inverse_two,
            second_in,
            up,
            act,
        ) = kept[layer]
        in_w, out_w, ffn_w = (in_ws[layer], out_ws[layer], ffn_ws[layer])
        gains = in_w[:, value_end + router_cols : value_end + router_cols + 4].astype(jnp.float32)
        grad_low = grad_hidden.astype(jnp.bfloat16)
        grad_act = jnp.dot(grad_low, ffn_w[:, FF:], preferred_element_type=jnp.float32)
        gelu_value, gelu_pull = jax.vjp(gelu_tanh, up)
        grad_up = gelu_pull(grad_act)[0].astype(jnp.bfloat16)
        grad_second = contract_last(grad_up, ffn_w[:, :FF])
        gain_two_grad = jnp.sum(grad_second * normed_two, axis=0)
        bias_two_grad = jnp.sum(grad_second, axis=0)
        grad_residual = grad_hidden + norm_back(grad_second, normed_two, inverse_two, gains[:, 2])
        residual_low = grad_residual.astype(jnp.bfloat16)
        grad_in, grad_logit = attention_backward(
            jnp.dot(residual_low, out_w, preferred_element_type=jnp.float32),
            attended,
            entered,
            chosen_here,
            turn_cos,
            turn_sin,
            lengths,
            saved,
            shift,
            in_grad_width,
            3 + LAYERS + layer,
        )
        grad_first = contract_last(grad_in[:, :in_width], in_w)
        gain_one_grad = jnp.sum(grad_first * normed_one, axis=0)
        bias_one_grad = jnp.sum(grad_first, axis=0)
        grad_hidden = grad_residual + norm_back(grad_first, normed_one, inverse_one, gains[:, 0])
        norm_grads = jnp.stack(
            [gain_one_grad, bias_one_grad, gain_two_grad, bias_two_grad], axis=1
        ).astype(jnp.bfloat16)
        norm_grads = jnp.pad(norm_grads, ((0, 0), (router_cols, 128 - 4 - router_cols)))
        base = sum(segment[3] for segment in segments)
        bases[layer] = base * half
        one = len(lefts)
        lefts += [first_in, residual_low]
        in_halves = grad_in.shape[1] // half
        segments += [
            (one, grad_in, 0, in_halves),
            (one + 1, mixed, 1, mixed.shape[1] // half - 1),
        ]
        doubles.append((base + in_halves - 1, shift, one + 1, mixed))
        for kind, pair in (("up", (second_in, grad_up)), ("down", (grad_low, act))):
            if (layer, kind) in NATIVE:
                native[layer, kind] = reduced_natively(*pair)
            else:
                segments.append((len(lefts), pair[1], 0, FF // half))
                lefts.append(pair[0])
        extras.append((norm_grads, sum(segment[3] for segment in segments)))
        segments.append((one, grad_logit, 0, 1))
    names = list(native)
    begun = segments[-1][1]
    partial, begun = lax.optimization_barrier(([native[name] for name in names], begun))
    segments[-1] = (segments[-1][0], begun) + segments[-1][2:]
    for name, value in zip(names, partial):
        native[name] = value.astype(jnp.float32)
    reduced = reduce_weight_grads(lefts, segments, doubles, extras, CHUNK)
    matrix_rows = [None] * LAYERS
    small_rows = [None] * LAYERS
    for layer in range(LAYERS):
        base = bases[layer]
        rest = [native[layer, kind] for kind in ("up", "down") if (layer, kind) in NATIVE]
        used = output_end + FF * (2 - len(rest))
        matrix_rows[layer] = jnp.concatenate([reduced[:, base : base + used]] + rest, axis=1)
        small_rows[layer] = reduced[:, base + used : base + used + router_cols + 4]
    input_grad = grad_hidden.reshape(seq_count, sub_rows, width).astype(jnp.bfloat16)
    matrix_grad = jnp.stack(matrix_rows, axis=0)
    small_grad = jnp.stack(small_rows, axis=0)
    matrix_new, matrix_first_new, matrix_second_new = adam_update(
        matrix, matrix_grad, matrix_first, matrix_second, column_rates(segment), WEIGHT_DECAY
    )
    small_new, small_first_new, small_second_new = adam_update(
        small, small_grad, small_first, small_second, small_rates(), 0.0
    )
    return (
        output,
        input_grad,
        matrix_grad,
        matrix_new,
        matrix_new.astype(jnp.bfloat16),
        matrix_first_new,
        matrix_second_new,
        small_grad,
        small_new,
        small_new.astype(jnp.bfloat16),
        small_first_new,
        small_second_new,
        loads,
    )


def solution(mesh):
    in_specs = (
        P("dp", ("seq", "head"), None),
        P("dp", ("seq", "head"), None),
        P(None, "dp", ("seq", "head"), None, None, None),
        P("dp"),
        P(None, ("dp", "seq", "head"), None),
        P(None, ("dp", "seq", "head"), None),
        P(None, ("dp", "seq", "head"), None),
        P(None, ("dp", "seq", "head"), None),
        P(None, ("dp", "seq", "head"), None),
        P(None, ("dp", "seq", "head"), None),
    )
    out_specs = (
        P("dp", ("seq", "head"), None),
        P("dp", ("seq", "head"), None),
        P(None, ("dp", "seq", "head"), None),
        P(None, ("dp", "seq", "head"), None),
        P(None, ("dp", "seq", "head"), None),
        P(None, ("dp", "seq", "head"), None),
        P(None, ("dp", "seq", "head"), None),
        P(None, ("dp", "seq", "head"), None),
        P(None, ("dp", "seq", "head"), None),
        P(None, ("dp", "seq", "head"), None),
        P(None, ("dp", "seq", "head"), None),
        P(None, ("dp", "seq", "head"), None),
        P(),
    )
    return jax.shard_map(local, mesh=mesh, in_specs=in_specs, out_specs=out_specs, check_vma=False)
```

```python
import math

import jax
import jax.numpy as jnp
from jax import lax
from jax.experimental import pallas as pl
from jax.experimental.pallas import tpu as pltpu
from jax.sharding import PartitionSpec as P

D = 1024
HEADS = 4
HEAD_DIM = 112
EXPERTS = 5
FF = 4096
LAYERS = 2
STEP = 10


NORM_EPS = 1e-05
BETA_ONE = 0.9
BETA_TWO = 0.95
ADAM_EPS = 1e-08
WEIGHT_DECAY = 0.1
NORM_RATE = 0.5
MASKED = -1e30
CHUNK = 512
NATIVE = ((LAYERS - 1, "down"),)


def column_bounds():
    query_end = 2 * HEADS * HEAD_DIM
    value_end = query_end + HEADS * EXPERTS * HEAD_DIM
    output_end = value_end + HEADS * EXPERTS * HEAD_DIM
    return (query_end, value_end, output_end, output_end + FF)


def column_rates(segment):
    query_end, value_end, output_end, up_end = column_bounds()
    column = jnp.arange(up_end + FF)
    inner = D ** (-0.5)
    outer = 0.7 * math.sqrt(segment) / HEAD_DIM
    rates = jnp.where(
        column < value_end,
        inner,
        jnp.where(column < output_end, outer, jnp.where(column < up_end, inner, FF ** (-0.5))),
    )
    return rates.astype(jnp.float32)


def small_rates():
    column = jnp.arange(2 * HEADS * EXPERTS + 4)
    return jnp.where(column < 2 * HEADS * EXPERTS, 0.7 * D ** (-0.5), NORM_RATE).astype(jnp.float32)


def adam_update(weight, grad, first, second, rates, decay):
    first_new = BETA_ONE * first + (1.0 - BETA_ONE) * grad
    second_new = BETA_TWO * second + (1.0 - BETA_TWO) * grad * grad
    first_hat = first_new / (1.0 - BETA_ONE**STEP)
    second_hat = second_new / (1.0 - BETA_TWO**STEP)
    new = weight - rates * (first_hat / (jnp.sqrt(second_hat) + ADAM_EPS) + decay * weight)
    return (new, first_new, second_new)


def rotary_tables(positions):
    half = HEAD_DIM // 2
    inverse = jnp.exp(-math.log(10000.0) * jnp.arange(half, dtype=jnp.float32) / half)
    angle = positions.astype(jnp.float32)[:, None] * inverse[None, :]
    return (jnp.cos(angle), jnp.sin(angle))


def layer_stats(values):
    mean = jnp.mean(values, axis=-1, keepdims=True)
    centered = values - mean
    variance = jnp.mean(centered * centered, axis=-1, keepdims=True)
    inverse = lax.rsqrt(variance + NORM_EPS)
    return (centered * inverse, inverse)


def norm_back(grad_normed, normed, inverse, gain):
    scaled = grad_normed * gain
    return inverse * (
        scaled
        - jnp.mean(scaled, axis=-1, keepdims=True)
        - normed * jnp.mean(scaled * normed, axis=-1, keepdims=True)
    )


def contract_last(left, right):
    return lax.dot_general(
        left, right, (((1,), (1,)), ((), ())), preferred_element_type=jnp.float32
    )


def contract_first(left, right):
    return lax.dot_general(
        left, right, (((0,), (0,)), ((), ())), preferred_element_type=jnp.float32
    )


AXES = ("dp", "seq", "head")


def mesh_bits():
    dims = [
        (axis, bit)
        for axis in AXES
        for bit in reversed(range(lax.axis_size(axis).bit_length() - 1))
    ]
    groups = [[index for index, (axis, _) in enumerate(dims) if axis == name] for name in AXES]
    return (dims, *groups)


def my_bits(dims):
    place = {axis: lax.axis_index(axis) for axis in AXES}
    bits = [lax.rem(place[axis] // (1 << bit), 2) for axis, bit in dims]
    partners = [
        {axis: place[axis] + (1 << bit) * (1 - 2 * bits[index])}
        for index, (axis, bit) in enumerate(dims)
    ]
    return (bits, partners)


def greet(partners):
    barrier = pltpu.get_barrier_semaphore()
    for partner in partners:
        pl.semaphore_signal(
            barrier, inc=1, device_id=partner, device_id_type=pl.DeviceIdType.MESH
        )
    pl.semaphore_wait(barrier, len(partners))


def gather_rows(share, counts, unit, name):
    dims, dp_dims, seq_dims, head_dims = mesh_bits()
    orders = (
        head_dims + dp_dims[::-1] + seq_dims,
        head_dims + dp_dims + seq_dims,
        dp_dims + head_dims + seq_dims,
    )
    depth = len(dims)
    rows, width = share.shape
    units = width // unit
    near = (11 * units + 16) // 32
    pieces, start = ([], 0)
    for which, count in ((0, near), (1, near), (2, units - 2 * near)):
        pieces.append((start, count, which))
        start += count * unit
    lag, slots = (3, 6)
    local_slots = 2
    ring = (depth + 1) * lag + local_slots + 2
    steps = max(count for _, count, _ in pieces) + lag * depth - 1

    def kernel(*refs):
        share_ref, counts_ref, out_ref, counts_out = refs[:4]
        send_sem, recv_sem, load_sem, store_sem, small_send, small_recv, small_load = refs[4:11]
        buffers = refs[11:]
        bits, partners = my_bits(dims)

        def at_stage(which, stage):
            done = orders[which][:stage]
            return tuple(slice(None) if dim in done else bits[dim] for dim in range(depth))

        def columns(number, chunk):
            return pl.ds(pl.multiple_of(pieces[number][0] + chunk * unit, 128), unit)

        def exchange(number, stage, chunk):
            which = pieces[number][2]
            view = buffers[number].at[(lax.rem(chunk, ring),) + at_stage(which, stage)]
            slot = lax.rem(chunk, slots)
            return sent_to(
                view,
                view,
                send_sem.at[number, stage, slot],
                recv_sem.at[number, stage, slot],
                partners[orders[which][stage]],
            )

        def load(number, chunk):
            return pltpu.make_async_copy(
                share_ref.at[:, columns(number, chunk)],
                buffers[number].at[(lax.rem(chunk, ring),) + tuple(bits)],
                load_sem.at[number, lax.rem(chunk, local_slots)],
            )

        def store(number, chunk):
            return pltpu.make_async_copy(
                buffers[number].at[lax.rem(chunk, ring)],
                out_ref.at[(slice(None),) * (depth + 1) + (columns(number, chunk),)],
                store_sem.at[number, lax.rem(chunk, local_slots)],
            )

        def small(stage):
            view = counts_out.at[at_stage(0, stage)]
            return sent_to(
                view, view, small_send.at[stage], small_recv.at[stage], partners[orders[0][stage]]
            )

        own_counts = pltpu.make_async_copy(counts_ref, counts_out.at[tuple(bits)], small_load)
        own_counts.start()
        for number in range(len(pieces)):
            for chunk in range(local_slots):
                load(number, jnp.int32(chunk)).start()
        greet(partners)
        own_counts.wait()

        def body(step, carry):
            for stage in range(depth, -1, -1):
                chunk = step - lag * stage + (1 if stage == depth else 0)
                for number, piece in enumerate(pieces):

                    @pl.when((chunk >= 0) & (chunk < piece[1]))
                    def _(stage=stage, chunk=chunk, number=number, piece=piece):
                        if stage > 0:
                            exchange(number, stage - 1, chunk).wait()
                        else:
                            load(number, chunk).wait()

                            @pl.when(chunk + local_slots < piece[1])
                            def _():
                                load(number, chunk + local_slots).start()

                        if stage < depth:
                            exchange(number, stage, chunk).start()
                        else:

                            @pl.when(chunk >= local_slots)
                            def _():
                                store(number, chunk - local_slots).wait()

                            store(number, chunk).start()

                @pl.when(chunk == 0)
                def _(stage=stage):
                    if stage > 0:
                        small(stage - 1).wait()
                    if stage < depth:
                        small(stage).start()

            return carry

        lax.fori_loop(0, steps, body, 0)
        for number, piece in enumerate(pieces):
            for back in range(min(local_slots, piece[1])):
                store(number, jnp.int32(piece[1] - 1 - back)).wait()

    in_place = pl.BlockSpec(memory_space=pl.ANY)
    semaphores = pltpu.SemaphoreType.DMA((len(pieces), depth, slots))
    local = pltpu.SemaphoreType.DMA((len(pieces), local_slots))
    gathered, all_counts = pl.pallas_call(
        kernel,
        in_specs=[in_place] * 2,
        out_specs=[in_place] * 2,
        out_shape=[
            jax.ShapeDtypeStruct((2,) * depth + value.shape, value.dtype)
            for value in (share, counts)
        ],
        scratch_shapes=[
            semaphores,
            semaphores,
            local,
            local,
            pltpu.SemaphoreType.DMA((depth,)),
            pltpu.SemaphoreType.DMA((depth,)),
            pltpu.SemaphoreType.DMA,
        ]
        + [pltpu.VMEM((ring,) + (2,) * depth + (rows, unit), share.dtype) for _ in pieces],
        compiler_params=pltpu.CompilerParams(
            collective_id=name, has_side_effects=True, vmem_limit_bytes=48 << 20
        ),
    )(share, counts)
    return (gathered.reshape(-1, width), all_counts.reshape(-1, counts.shape[1]))


def halving_plan(width):
    dims, dp_dims, seq_dims, head_dims = mesh_bits()
    first = seq_dims[::-1]
    orders = (
        (0, width // 2, first + dp_dims[::-1] + head_dims[::-1]),
        (width // 2, width // 4, first + dp_dims + head_dims[::-1]),
        (3 * width // 4, width // 4, first + head_dims[::-1] + dp_dims),
    )
    stages = []
    for stage in range(len(dims)):
        parts = []
        for start, count, order in orders:
            left = [dim for dim in range(len(dims)) if dim not in order[:stage]]
            if parts and parts[-1][2:] == (order[stage], left):
                parts[-1] = (parts[-1][0], parts[-1][1] + count, order[stage], left)
            else:
                parts.append((start, count, order[stage], left))
        stages.append(parts)
    lags = [1 if stage < len(seq_dims) else 2 for stage in range(len(dims))]
    return dims, stages, lags


def reduce_weight_grads(lefts, segments, doubles, extras, width):
    dims, stages, lags = halving_plan(width)
    depth = len(dims)
    half = width // 2
    tokens, model = lefts[0].shape
    rows = model >> depth
    firsts = [0]
    for _, _, _, count in segments:
        firsts.append(firsts[-1] + count)
    chunks = firsts[-1] // 2
    spots = [(where // 2, where % 2 * half) for _, where in extras]
    starts = [sum(lags[:stage]) for stage in range(depth + 1)]
    rights = [right for _, right, _, _ in segments] + [right for _, _, _, right in doubles]
    count_lefts, count_rights, count_extras = (len(lefts), len(rights), len(extras))
    first_use = [
        min(firsts[index] // 2 for index, segment in enumerate(segments) if segment[0] == left)
        for left in range(count_lefts)
    ]
    for where, _, left, _ in doubles:
        first_use[left] = min(first_use[left], where // 2)

    def kernel(*refs):
        left_refs = refs[:count_lefts]
        right_refs = refs[count_lefts : count_lefts + count_rights]
        rest = refs[count_lefts + count_rights :]
        added, rest = (rest[:count_extras], rest[count_extras:])
        out_ref, left_buf, turned, right_buf, double_buf, left_sem, right_sem, double_sem = rest[:8]
        pool = iter(rest[8:])
        buffers = [[tuple(next(pool) for _ in range(4)) for _ in parts] for parts in stages]
        step = pl.program_id(0)
        bits, partners = my_bits(dims)

        def exchange(stage, part, slot):
            start, count, dim, left = stages[stage][part]
            own, got, send_sem, recv_sem = buffers[stage][part]
            lead = (slot,) + (slice(None),) * left.index(dim)
            return pltpu.make_async_remote_copy(
                src_ref=own.at[lead + (1 - bits[dim],)],
                dst_ref=got.at[slot],
                send_sem=send_sem.at[slot],
                recv_sem=recv_sem.at[slot],
                device_id=partners[dim],
                device_id_type=pl.DeviceIdType.MESH,
            )

        def load_left(index):
            return pltpu.make_async_copy(left_refs[index], left_buf.at[index], left_sem.at[index])

        def load_right(index, at, chunk, side):
            columns = pl.ds(pl.multiple_of(at * half, half), half)
            slot = lax.rem(chunk, 2)
            return pltpu.make_async_copy(
                right_refs[index].at[:, columns],
                right_buf.at[slot, side],
                right_sem.at[slot, side],
            )

        def load_double(index):
            return pltpu.make_async_copy(
                right_refs[len(segments) + index].at[:, 0:half], double_buf, double_sem
            )

        def prefetch(chunk):
            for side in range(2):
                place = 2 * chunk + side
                for index, (_, _, begin, _) in enumerate(segments):

                    @pl.when((place >= firsts[index]) & (place < firsts[index + 1]))
                    def _(index=index, begin=begin, place=place, side=side):
                        load_right(index, place - firsts[index] + begin, chunk, side).start()

            for index, (where, _, _, _) in enumerate(doubles):

                @pl.when(chunk == where // 2)
                def _(index=index):
                    load_double(index).start()

        @pl.when(step == 0)
        def _():
            for index in range(count_lefts):
                load_left(index).start()
            prefetch(step)
            greet(partners)

        @pl.when(step + 1 < chunks)
        def _():
            prefetch(step + 1)

        for stage in range(depth, -1, -1):
            chunk = step - starts[stage]

            @pl.when((chunk >= 0) & (chunk < chunks))
            def _(stage=stage, chunk=chunk):
                if stage == 0:
                    slot = lax.rem(chunk, 2 * lags[0])
                    near = lax.rem(chunk, 2)
                    own = buffers[0][0][0]
                    for index in range(count_lefts):

                        @pl.when(chunk == first_use[index])
                        def _(index=index):
                            load_left(index).wait()
                            turned[index] = left_buf[index].T

                    for side in range(2):
                        place = 2 * chunk + side
                        which = jnp.int32(segments[0][0])
                        for index, segment in enumerate(segments):
                            which = jnp.where(place >= firsts[index], segment[0], which)
                        load_right(0, 0, chunk, side).wait()
                        for where, kept, _, _ in doubles:
                            if where % 2 == side:

                                @pl.when(chunk == where // 2)
                                def _(kept=kept, side=side):
                                    right_buf[near, side, :, kept:] = jnp.zeros(
                                        (tokens, half - kept), jnp.bfloat16
                                    )

                        product = jnp.dot(
                            turned[which],
                            right_buf[near, side],
                            preferred_element_type=jnp.float32,
                        )
                        own[(slot, Ellipsis, slice(side * half, side * half + half))] = (
                            product.astype(jnp.bfloat16).reshape((2,) * depth + (rows, half))
                        )
                    for index, (where, _, left, _) in enumerate(doubles):

                        @pl.when(chunk == where // 2)
                        def _(index=index, where=where, left=left):
                            load_double(index).wait()
                            product = jnp.dot(
                                turned[left], double_buf[...], preferred_element_type=jnp.float32
                            ).reshape((2,) * depth + (rows, half))
                            begin = where % 2 * half
                            at = (slot, Ellipsis, slice(begin, begin + half))
                            own[at] = (own[at].astype(jnp.float32) + product).astype(jnp.bfloat16)

                    for index in range(count_extras):

                        @pl.when(chunk == spots[index][0])
                        def _(index=index):
                            at = (slot, Ellipsis, slice(spots[index][1], spots[index][1] + 128))
                            total = own[at].astype(jnp.float32) + added[index][...].astype(
                                jnp.float32
                            )
                            own[at] = total.astype(jnp.bfloat16)

                else:
                    back = lax.rem(chunk, 2 * lags[stage - 1])
                    for part, (start, count, dim, left) in enumerate(stages[stage - 1]):
                        exchange(stage - 1, part, back).wait()
                        own, got = buffers[stage - 1][part][:2]
                        lead = (back,) + (slice(None),) * left.index(dim)
                        total = own[lead + (bits[dim],)].astype(jnp.float32) + got[back].astype(
                            jnp.float32
                        )
                        if stage == depth:
                            out_ref[:, start : start + count] = total
                            continue
                        slot = lax.rem(chunk, 2 * lags[stage])
                        low = total.astype(jnp.bfloat16)
                        for other, (begin, length, _, kept) in enumerate(stages[stage]):
                            lo, hi = max(start, begin), min(start + count, begin + length)
                            if lo < hi:
                                at = (slot,) + (slice(None),) * (len(kept) + 1)
                                buffers[stage][other][0][at + (slice(lo - begin, hi - begin),)] = (
                                    low[..., lo - start : hi - start]
                                )
                if stage < depth:
                    for part in range(len(stages[stage])):
                        exchange(stage, part, lax.rem(chunk, 2 * lags[stage])).start()

    scratch = [
        pltpu.VMEM((count_lefts, tokens, model), jnp.bfloat16),
        pltpu.VMEM((count_lefts, model, tokens), jnp.bfloat16),
        pltpu.VMEM((2, 2, tokens, half), jnp.bfloat16),
        pltpu.VMEM((tokens, half), jnp.bfloat16),
        pltpu.SemaphoreType.DMA((count_lefts,)),
        pltpu.SemaphoreType.DMA((2, 2)),
        pltpu.SemaphoreType.DMA,
    ]
    for stage, parts in enumerate(stages):
        slots = 2 * lags[stage]
        for start, count, dim, left in parts:
            scratch += [
                pltpu.VMEM((slots,) + (2,) * len(left) + (rows, count), jnp.bfloat16),
                pltpu.VMEM((slots,) + (2,) * (len(left) - 1) + (rows, count), jnp.bfloat16),
                pltpu.SemaphoreType.DMA((slots,)),
                pltpu.SemaphoreType.DMA((slots,)),
            ]
    in_place = pl.BlockSpec(memory_space=pl.ANY)
    whole = [value.reshape((2,) * depth + (rows, 128)) for value, _ in extras]
    return pl.pallas_call(
        kernel,
        grid=(chunks + starts[depth],),
        in_specs=[in_place] * (count_lefts + count_rights)
        + [pl.BlockSpec(value.shape, lambda step: (0,) * (depth + 2)) for value in whole],
        out_specs=pl.BlockSpec(
            (rows, width), lambda step: (0, jnp.clip(step - starts[depth], 0, chunks - 1))
        ),
        out_shape=jax.ShapeDtypeStruct((rows, chunks * width), jnp.float32),
        scratch_shapes=scratch,
        compiler_params=pltpu.CompilerParams(
            collective_id=1,
            has_side_effects=True,
            vmem_limit_bytes=48 << 20,
            dimension_semantics=("arbitrary",),
        ),
    )(*lefts, *rights, *whole)


def reduction_order(tensor):
    dp, seq = (lax.axis_size("dp"), lax.axis_size("seq"))
    count, width = tensor.shape
    split = tensor.reshape(count, dp, seq, width // (dp * seq))
    return split.transpose(0, 2, 1, 3).reshape(count, width)


def reduced_natively(left, right):
    share = contract_first(reduction_order(left), right).astype(jnp.bfloat16)
    for axis in ("seq", "dp", "head"):
        share = lax.psum_scatter(share, axis, scatter_dimension=0, tiled=True)
    return share


def lane_whole(count):
    return count + (-count) % 128


def padded(pieces, width):
    have = sum(piece.shape[1] for piece in pieces)
    fill = jnp.zeros((pieces[0].shape[0], width - have), pieces[0].dtype)
    return jnp.concatenate(list(pieces) + [fill], axis=1)


LANES = 128
QUERY_TILE = 256


def swap_halves(tensor):
    half = HEAD_DIM // 2
    return jnp.concatenate([tensor[:, half:], tensor[:, :half]], axis=1)


def lane_filled(tensor):
    fill = jnp.zeros((tensor.shape[0], LANES - tensor.shape[1]), tensor.dtype)
    return jnp.concatenate([tensor, fill], axis=1)


def weights_block(keys_mem, keys_own, query, start, first, segment, length):
    contract = (((1,), (1,)), ((), ()))
    raw = jnp.concatenate(
        [
            lax.dot_general(keys, query, contract, preferred_element_type=jnp.float32)
            for keys in (keys_mem, keys_own)
        ],
        axis=0,
    )
    key_pos = start - segment + lax.broadcasted_iota(jnp.int32, raw.shape, 0)
    query_pos = start + first + lax.broadcasted_iota(jnp.int32, raw.shape, 1)
    used = (key_pos < length) & (key_pos < query_pos) & (key_pos >= 0)
    allowed = used | (key_pos == query_pos)
    scores = jnp.where(allowed, raw * HEAD_DIM ** (-0.5), MASKED)
    weights = jnp.exp(scores - jnp.max(scores, axis=0, keepdims=True))
    return weights * (1.0 / jnp.sum(weights, axis=0, keepdims=True))


def contract_rows(left, right):
    return lax.dot_general(
        left, right, (((0,), (0,)), ((), ())), preferred_element_type=jnp.float32
    )


def across(axis, offset):
    size = lax.axis_size(axis)
    return {axis: lax.rem(lax.axis_index(axis) + offset + size, size)}


def sent_to(source, target, send_sem, recv_sem, device):
    return pltpu.make_async_remote_copy(
        src_ref=source,
        dst_ref=target,
        send_sem=send_sem,
        recv_sem=recv_sem,
        device_id=device,
        device_id_type=pl.DeviceIdType.MESH,
    )


def meet(memory_step):
    barrier = pltpu.get_barrier_semaphore()
    heads = lax.axis_size("head")
    writers = [across("head", step) for step in range(1, heads)]
    writers.append(across("seq", -memory_step))
    for device in writers:
        pl.semaphore_signal(barrier, inc=1, device_id=device, device_id_type=pl.DeviceIdType.MESH)
    pl.semaphore_wait(barrier, len(writers))


def gate_values(entered_ref, chosen_ref, rows):
    at = column_bounds()[1]
    logits = entered_ref[rows, at : at + 2 * HEADS * EXPERTS]
    prob = 1.0 / (1.0 + jnp.exp(-logits))
    return (prob, prob * chosen_ref[rows, :])


def column(tensor, index):
    return tensor[:, index : index + 1]


def attention_forward(entered, chosen, turn_cos, turn_sin, lengths, shift, name):
    seq_count = lengths.shape[0]
    tokens = entered.shape[0]
    sub = tokens // seq_count
    heads = lax.axis_size("head")
    segment = heads * sub
    query_end = column_bounds()[0]
    sides = range(1, heads)

    def kernel(*refs):
        length_ref, entered_ref, chosen_ref, cos_ref, sin_ref = refs[:5]
        mixed_ref, attended_ref, query_ref, key_ref, value_ref = refs[5:10]
        out_buf, heads_buf, mem_buf, done_buf, back_buf = refs[10:15]
        out_sem, in_sem, mem_sem, done_sem, back_sem = refs[15:]
        me = lax.axis_index("head")
        start = lax.axis_index("seq") * segment
        turn, wind = (cos_ref[...], sin_ref[...])

        def outward(b, side):
            there = across("head", side)
            return sent_to(
                out_buf.at[b, there["head"]],
                heads_buf.at[b, :, me],
                out_sem.at[b, side - 1],
                in_sem.at[b, side - 1],
                there,
            )

        def onward(b):
            return sent_to(
                heads_buf.at[b, 1:3],
                mem_buf.at[b],
                mem_sem.at[0, b],
                mem_sem.at[1, b],
                across("seq", 1),
            )

        def homeward(b, side):
            there = across("head", side)
            return sent_to(
                done_buf.at[b, there["head"]],
                back_buf.at[b, me],
                done_sem.at[b, side - 1],
                back_sem.at[b, side - 1],
                there,
            )

        meet(1)
        gates_of = []
        for b in range(seq_count):
            rows = slice(b * sub, (b + 1) * sub)
            gates = gate_values(entered_ref, chosen_ref, rows)[1]
            gates_of.append(gates)
            for head in range(HEADS):
                for kind in range(2):
                    at = (kind * HEADS + head) * HEAD_DIM
                    vector = entered_ref[rows, at : at + HEAD_DIM]
                    turned = vector * turn + swap_halves(vector) * wind
                    out_buf[b, head, kind] = lane_filled(turned).astype(jnp.bfloat16)
                value = jnp.zeros((sub, HEAD_DIM), jnp.float32)
                for expert in range(EXPERTS):
                    index = head * EXPERTS + expert
                    at = query_end + index * HEAD_DIM
                    value += column(gates, index) * entered_ref[rows, at : at + HEAD_DIM]
                out_buf[b, head, 2] = lane_filled(value).astype(jnp.bfloat16)
            for side in sides:
                outward(b, side).start()
            for kind in range(3):
                heads_buf[b, kind, me] = out_buf[b, me, kind]
        for b in range(seq_count):
            for side in sides:
                outward(b, side).wait_recv()
            onward(b).start()
        for b in range(seq_count):
            onward(b).wait_recv()
            keys_own = heads_buf[b, 1].reshape(segment, LANES)
            values = jnp.concatenate(
                [mem_buf[b, 1].reshape(segment, LANES), heads_buf[b, 2].reshape(segment, LANES)],
                axis=0,
            )
            for first in range(0, segment, QUERY_TILE):
                tile = slice(first // sub, (first + QUERY_TILE) // sub)
                query = heads_buf[b, 0, tile].reshape(QUERY_TILE, LANES)
                probs = weights_block(
                    mem_buf[b, 0].reshape(segment, LANES),
                    keys_own,
                    query,
                    start,
                    first,
                    segment,
                    length_ref[b],
                ).astype(jnp.bfloat16)
                attended = contract_rows(values, probs).T.astype(jnp.bfloat16)
                done_buf[b, tile] = attended.reshape(QUERY_TILE // sub, sub, LANES)
            for side in sides:
                homeward(b, side).start()
            back_buf[b, me] = done_buf[b, me]
        for b in range(seq_count):
            query_ref[b] = heads_buf[b, 0]
            key_ref[b, 0] = mem_buf[b, 0]
            key_ref[b, 1] = heads_buf[b, 1]
            value_ref[b, 0] = mem_buf[b, 1]
            value_ref[b, 1] = heads_buf[b, 2]
        mixed_ref[:, :shift] = jnp.zeros((tokens, shift), jnp.bfloat16)
        for b in range(seq_count):
            rows = slice(b * sub, (b + 1) * sub)
            for side in sides:
                homeward(b, side).wait_recv()
            for head in range(HEADS):
                attended = back_buf[b, head]
                attended_ref[rows, head * LANES : (head + 1) * LANES] = attended
                wide = attended.astype(jnp.float32)[:, :HEAD_DIM]
                for expert in range(EXPERTS):
                    index = head * EXPERTS + expert
                    gate = column(gates_of[b], HEADS * EXPERTS + index)
                    at = shift + index * HEAD_DIM
                    mixed_ref[rows, at : at + HEAD_DIM] = (
                        gate * wide
                    ).astype(jnp.bfloat16)
        for b in range(seq_count):
            onward(b).wait_send()
            for side in sides:
                outward(b, side).wait_send()
                homeward(b, side).wait_send()

    def shape(*dims):
        return jax.ShapeDtypeStruct(dims, jnp.bfloat16)

    vmem = pl.BlockSpec(memory_space=pltpu.VMEM)
    paired = pltpu.SemaphoreType.DMA((seq_count, heads - 1))
    return pl.pallas_call(
        kernel,
        in_specs=[pl.BlockSpec(memory_space=pltpu.SMEM)] + [vmem] * 4,
        out_specs=[vmem] * 5,
        out_shape=[
            shape(tokens, shift + HEADS * EXPERTS * HEAD_DIM),
            shape(tokens, HEADS * LANES),
            shape(seq_count, heads, sub, LANES),
            shape(seq_count, 2, heads, sub, LANES),
            shape(seq_count, 2, heads, sub, LANES),
        ],
        scratch_shapes=[
            pltpu.VMEM((seq_count, heads, 3, sub, LANES), jnp.bfloat16),
            pltpu.VMEM((seq_count, 3, heads, sub, LANES), jnp.bfloat16),
            pltpu.VMEM((seq_count, 2, heads, sub, LANES), jnp.bfloat16),
            pltpu.VMEM((seq_count, heads, sub, LANES), jnp.bfloat16),
            pltpu.VMEM((seq_count, heads, sub, LANES), jnp.bfloat16),
            paired,
            paired,
            pltpu.SemaphoreType.DMA((2, seq_count)),
            paired,
            paired,
        ],
        compiler_params=pltpu.CompilerParams(
            collective_id=name, has_side_effects=True, vmem_limit_bytes=40 << 20
        ),
    )(lengths, entered, chosen, turn_cos, turn_sin)


def attention_backward(
    grad_mixed, attended, entered, chosen, turn_cos, turn_sin, lengths, saved, shift, grad_width, name
):
    query, keys, values = saved
    seq_count = lengths.shape[0]
    tokens = entered.shape[0]
    sub = tokens // seq_count
    heads = lax.axis_size("head")
    segment = heads * sub
    query_end, value_end = column_bounds()[:2]
    router_cols = 2 * HEADS * EXPERTS
    sides = range(1, heads)

    def kernel(*refs):
        length_ref, grad_ref, attended_ref, entered_ref, chosen_ref, cos_ref, sin_ref = refs[:7]
        query_ref, key_ref, value_ref, result_ref, logit_ref = refs[7:12]
        out_buf, heads_buf, mem_out, mem_in, own_buf, done_buf, back_buf = refs[12:19]
        out_sem, in_sem, mem_sem, query_sem, done_sem, back_sem = refs[19:]
        me = lax.axis_index("head")
        start = lax.axis_index("seq") * segment
        turn, wind = (cos_ref[...], sin_ref[...])

        def outward(b, side):
            there = across("head", side)
            return sent_to(
                out_buf.at[b, there["head"]],
                heads_buf.at[b, me],
                out_sem.at[b, side - 1],
                in_sem.at[b, side - 1],
                there,
            )

        def onward(b):
            return sent_to(
                mem_out.at[b], mem_in.at[b], mem_sem.at[0, b], mem_sem.at[1, b], across("seq", -1)
            )

        def queries_home(b, side):
            there = across("head", side)
            return sent_to(
                done_buf.at[b, there["head"], 0],
                back_buf.at[b, me, 0],
                query_sem.at[0, b, side - 1],
                query_sem.at[1, b, side - 1],
                there,
            )

        def homeward(b, side):
            there = across("head", side)
            return sent_to(
                done_buf.at[b, there["head"], 1:3],
                back_buf.at[b, me, 1:3],
                done_sem.at[b, side - 1],
                back_sem.at[b, side - 1],
                there,
            )

        def join_memory(b):
            onward(b).wait_recv()
            for kind in range(2):
                total = own_buf[b, kind] + mem_in[b, kind].astype(jnp.float32)
                done_buf[b, :, kind + 1] = total.astype(jnp.bfloat16).reshape(heads, sub, LANES)
            for side in sides:
                homeward(b, side).start()
            back_buf[b, me] = done_buf[b, me]

        meet(-1)
        lane = lax.broadcasted_iota(jnp.int32, (sub, router_cols), 1)
        gate_grads, probs_of, gates_of = ([], [], [])
        for b in range(seq_count):
            rows = slice(b * sub, (b + 1) * sub)
            prob, gates = gate_values(entered_ref, chosen_ref, rows)
            probs_of.append(prob)
            gates_of.append(gates)
            gate_grad = jnp.zeros((sub, router_cols), jnp.float32)
            for head in range(HEADS):
                seen = attended_ref[rows, head * LANES : head * LANES + HEAD_DIM].astype(
                    jnp.float32
                )
                total = jnp.zeros((sub, HEAD_DIM), jnp.float32)
                for expert in range(EXPERTS):
                    index = head * EXPERTS + expert
                    at = shift + index * HEAD_DIM
                    part = grad_ref[rows, at : at + HEAD_DIM]
                    total += column(gates, HEADS * EXPERTS + index) * part
                    gate_grad = jnp.where(
                        lane == HEADS * EXPERTS + index,
                        jnp.sum(part * seen, axis=1, keepdims=True),
                        gate_grad,
                    )
                out_buf[b, head] = lane_filled(total).astype(jnp.bfloat16)
            gate_grads.append(gate_grad)
            for side in sides:
                outward(b, side).start()
            heads_buf[b, me] = out_buf[b, me]
        for b in range(seq_count):
            for side in sides:
                outward(b, side).wait_recv()
            keys_mem = key_ref[b, 0].reshape(segment, LANES)
            keys_own = key_ref[b, 1].reshape(segment, LANES)
            keys_all = jnp.concatenate([keys_mem, keys_own], axis=0)
            values_all = jnp.concatenate(
                [value_ref[b, 0].reshape(segment, LANES), value_ref[b, 1].reshape(segment, LANES)],
                axis=0,
            )
            grad_keys = jnp.zeros((2 * segment, LANES), jnp.float32)
            grad_values = jnp.zeros((2 * segment, LANES), jnp.float32)
            for first in range(0, segment, QUERY_TILE):
                tile = slice(first // sub, (first + QUERY_TILE) // sub)
                here = query_ref[b, tile].reshape(QUERY_TILE, LANES)
                arrived = heads_buf[b, tile].reshape(QUERY_TILE, LANES)
                probs = weights_block(
                    keys_mem, keys_own, here, start, first, segment, length_ref[b]
                )
                grad_probs = contract_last(values_all, arrived)
                delta = jnp.sum(probs * grad_probs, axis=0, keepdims=True)
                grad_raw = (probs * (grad_probs - delta) * HEAD_DIM ** (-0.5)).astype(
                    jnp.bfloat16
                )
                grad_values += jnp.dot(
                    probs.astype(jnp.bfloat16), arrived, preferred_element_type=jnp.float32
                )
                grad_keys += jnp.dot(grad_raw, here, preferred_element_type=jnp.float32)
                grad_query = contract_rows(keys_all, grad_raw).T.astype(jnp.bfloat16)
                done_buf[b, tile, 0] = grad_query.reshape(QUERY_TILE // sub, sub, LANES)
                if b > 0 and first == 0:
                    join_memory(b - 1)
            for kind, grads in enumerate((grad_keys, grad_values)):
                mem_out[b, kind] = grads[:segment].astype(jnp.bfloat16)
                own_buf[b, kind] = grads[segment:]
            onward(b).start()
            for side in sides:
                queries_home(b, side).start()
        join_memory(seq_count - 1)
        used = value_end + router_cols
        result_ref[:, used:] = jnp.zeros((tokens, grad_width - used), jnp.bfloat16)
        logit_ref[:, router_cols:] = jnp.zeros((tokens, CHUNK // 2 - router_cols), jnp.bfloat16)
        for b in range(seq_count):
            rows = slice(b * sub, (b + 1) * sub)
            for side in sides:
                queries_home(b, side).wait_recv()
                homeward(b, side).wait_recv()
            gate_grad = gate_grads[b]
            for head in range(HEADS):
                for kind in range(2):
                    vector = back_buf[b, head, kind].astype(jnp.float32)[:, :HEAD_DIM]
                    turned = vector * turn - swap_halves(vector) * wind
                    at = (kind * HEADS + head) * HEAD_DIM
                    result_ref[rows, at : at + HEAD_DIM] = turned.astype(jnp.bfloat16)
                grad_value = back_buf[b, head, 2].astype(jnp.float32)[:, :HEAD_DIM]
                for expert in range(EXPERTS):
                    index = head * EXPERTS + expert
                    at = query_end + index * HEAD_DIM
                    gate_grad = jnp.where(
                        lane == index,
                        jnp.sum(
                            entered_ref[rows, at : at + HEAD_DIM] * grad_value,
                            axis=1,
                            keepdims=True,
                        ),
                        gate_grad,
                    )
                    result_ref[rows, at : at + HEAD_DIM] = (
                        column(gates_of[b], index) * grad_value
                    ).astype(jnp.bfloat16)
            prob = probs_of[b]
            grad_logit = (gate_grad * chosen_ref[rows, :] * prob * (1.0 - prob)).astype(
                jnp.bfloat16
            )
            result_ref[rows, value_end:used] = grad_logit
            logit_ref[rows, :router_cols] = grad_logit
        for b in range(seq_count):
            onward(b).wait_send()
            for side in sides:
                outward(b, side).wait_send()
                queries_home(b, side).wait_send()
                homeward(b, side).wait_send()

    vmem = pl.BlockSpec(memory_space=pltpu.VMEM)
    paired = pltpu.SemaphoreType.DMA((seq_count, heads - 1))
    return pl.pallas_call(
        kernel,
        in_specs=[pl.BlockSpec(memory_space=pltpu.SMEM)] + [vmem] * 9,
        out_specs=[vmem] * 2,
        out_shape=[
            jax.ShapeDtypeStruct((tokens, count), jnp.bfloat16)
            for count in (grad_width, CHUNK // 2)
        ],
        scratch_shapes=[
            pltpu.VMEM((seq_count, heads, sub, LANES), jnp.bfloat16),
            pltpu.VMEM((seq_count, heads, sub, LANES), jnp.bfloat16),
            pltpu.VMEM((seq_count, 2, segment, LANES), jnp.bfloat16),
            pltpu.VMEM((seq_count, 2, segment, LANES), jnp.bfloat16),
            pltpu.VMEM((seq_count, 2, segment, LANES), jnp.float32),
            pltpu.VMEM((seq_count, heads, 3, sub, LANES), jnp.bfloat16),
            pltpu.VMEM((seq_count, heads, 3, sub, LANES), jnp.bfloat16),
            paired,
            paired,
            pltpu.SemaphoreType.DMA((2, seq_count)),
            pltpu.SemaphoreType.DMA((2, seq_count, heads - 1)),
            paired,
            paired,
        ],
        compiler_params=pltpu.CompilerParams(
            collective_id=name, has_side_effects=True, vmem_limit_bytes=48 << 20
        ),
    )(lengths, grad_mixed, attended, entered, chosen, turn_cos, turn_sin, query, keys, values)


def gelu_tanh(values):
    return jax.nn.gelu(values, approximate=True)


def local(
    inputs,
    cotangent,
    routes,
    lengths,
    matrix,
    matrix_first,
    matrix_second,
    small,
    small_first,
    small_second,
):
    head_count = lax.axis_size("head")
    seq_count, sub_rows, width = inputs.shape
    segment = sub_rows * head_count
    tokens = seq_count * sub_rows
    router_cols = 2 * HEADS * EXPERTS
    group = HEADS * EXPERTS
    query_end, value_end, output_end, up_end = column_bounds()
    seq_start = lax.axis_index("seq") * segment
    positions = (
        seq_start + lax.axis_index("head") * sub_rows + jnp.arange(sub_rows, dtype=jnp.int32)
    )
    valid = (positions[None, :] < lengths[:, None]).astype(jnp.float32)
    cosines, sines = rotary_tables(positions)
    turn_cos = jnp.concatenate([cosines, cosines], axis=1)
    turn_sin = jnp.concatenate([-sines, sines], axis=1)
    chosen = jnp.sum(
        (routes[..., None] == jnp.arange(EXPERTS, dtype=jnp.int32)).astype(jnp.float32), axis=-2
    )
    load_part = jnp.sum(chosen * valid[None, :, :, None, None, None], axis=(1, 2))
    in_width = lane_whole(value_end + router_cols + 4)
    half = CHUNK // 2
    shift = value_end % half
    in_grad_width = value_end + (-value_end) % half
    out_width = shift + output_end - value_end
    matrix_low = matrix.astype(jnp.bfloat16)
    small_low = small.astype(jnp.bfloat16)
    in_low = [
        padded([matrix_low[layer, :, :value_end], small_low[layer]], in_width)
        for layer in range(LAYERS)
    ]
    out_low = [
        jnp.pad(matrix_low[layer, :, value_end:output_end], ((0, 0), (shift, 0)))
        for layer in range(LAYERS)
    ]
    ffn_low = [matrix_low[layer, :, output_end:] for layer in range(LAYERS)]
    size = load_part.size
    counts = jnp.pad(load_part.reshape(-1), (0, (-size) % 1024)).reshape(8, -1)
    early = []
    for layer in range(LAYERS):
        early += [in_low[layer], out_low[layer]] + ([ffn_low[layer]] if layer + 1 < LAYERS else [])
    gathered, counts = gather_rows(jnp.concatenate(early, axis=1), counts, 256, 2)
    counts, late = lax.optimization_barrier((counts, ffn_low[-1]))
    loads = jnp.sum(counts.reshape(-1, size + (-size) % 1024), axis=0)[:size].reshape(
        load_part.shape
    )
    late = lax.all_gather(late, ("dp", "seq", "head"), axis=0, tiled=True)
    pieces, start = ([], 0)
    for value in early:
        pieces.append(gathered[:, start : start + value.shape[1]])
        start += value.shape[1]
    pieces.append(late)
    in_ws, out_ws, ffn_ws = (pieces[0::3], pieces[1::3], pieces[2::3])
    hidden = inputs.astype(jnp.float32).reshape(tokens, width)
    kept = []
    for layer in range(LAYERS):
        in_w, out_w, ffn_w = (in_ws[layer], out_ws[layer], ffn_ws[layer])
        gains = in_w[:, value_end + router_cols : value_end + router_cols + 4].astype(jnp.float32)
        normed_one, inverse_one = layer_stats(hidden)
        first_in = (normed_one * gains[:, 0] + gains[:, 1]).astype(jnp.bfloat16)
        entered = jnp.dot(first_in, in_w, preferred_element_type=jnp.float32)
        chosen_here = chosen[layer].reshape(tokens, router_cols)
        mixed, attended, *saved = attention_forward(
            entered,
            chosen_here,
            turn_cos,
            turn_sin,
            lengths,
            shift,
            3 + layer,
        )
        residual = hidden + contract_last(mixed, out_w)
        normed_two, inverse_two = layer_stats(residual)
        second_in = (normed_two * gains[:, 2] + gains[:, 3]).astype(jnp.bfloat16)
        up = jnp.dot(second_in, ffn_w[:, :FF], preferred_element_type=jnp.float32)
        act = gelu_tanh(up).astype(jnp.bfloat16)
        hidden = residual + contract_last(act, ffn_w[:, FF:])
        kept.append(
            (
                normed_one,
                inverse_one,
                first_in,
                entered,
                chosen_here,
                mixed,
                attended,
                saved,
                normed_two,
                inverse_two,
                second_in,
                up,
                act,
            )
        )
    output = hidden.reshape(seq_count, sub_rows, width).astype(jnp.bfloat16)
    grad_hidden = (cotangent.astype(jnp.float32) * valid[:, :, None]).reshape(tokens, width)
    lefts, segments, doubles, extras, native, bases = ([], [], [], [], {}, {})
    for layer in reversed(range(LAYERS)):
        (
            normed_one,
            inverse_one,
            first_in,
            entered,
            chosen_here,
            mixed,
            attended,
            saved,
            normed_two,
            inverse_two,
            second_in,
            up,
            act,
        ) = kept[layer]
        in_w, out_w, ffn_w = (in_ws[layer], out_ws[layer], ffn_ws[layer])
        gains = in_w[:, value_end + router_cols : value_end + router_cols + 4].astype(jnp.float32)
        grad_low = grad_hidden.astype(jnp.bfloat16)
        grad_act = jnp.dot(grad_low, ffn_w[:, FF:], preferred_element_type=jnp.float32)
        gelu_value, gelu_pull = jax.vjp(gelu_tanh, up)
        grad_up = gelu_pull(grad_act)[0].astype(jnp.bfloat16)
        grad_second = contract_last(grad_up, ffn_w[:, :FF])
        gain_two_grad = jnp.sum(grad_second * normed_two, axis=0)
        bias_two_grad = jnp.sum(grad_second, axis=0)
        grad_residual = grad_hidden + norm_back(grad_second, normed_two, inverse_two, gains[:, 2])
        residual_low = grad_residual.astype(jnp.bfloat16)
        grad_in, grad_logit = attention_backward(
            jnp.dot(residual_low, out_w, preferred_element_type=jnp.float32),
            attended,
            entered,
            chosen_here,
            turn_cos,
            turn_sin,
            lengths,
            saved,
            shift,
            in_grad_width,
            3 + LAYERS + layer,
        )
        grad_first = contract_last(grad_in[:, :in_width], in_w)
        gain_one_grad = jnp.sum(grad_first * normed_one, axis=0)
        bias_one_grad = jnp.sum(grad_first, axis=0)
        grad_hidden = grad_residual + norm_back(grad_first, normed_one, inverse_one, gains[:, 0])
        norm_grads = jnp.stack(
            [gain_one_grad, bias_one_grad, gain_two_grad, bias_two_grad], axis=1
        ).astype(jnp.bfloat16)
        norm_grads = jnp.pad(norm_grads, ((0, 0), (router_cols, 128 - 4 - router_cols)))
        base = sum(segment[3] for segment in segments)
        bases[layer] = base * half
        one = len(lefts)
        lefts += [first_in, residual_low]
        in_halves = grad_in.shape[1] // half
        segments += [
            (one, grad_in, 0, in_halves),
            (one + 1, mixed, 1, mixed.shape[1] // half - 1),
        ]
        doubles.append((base + in_halves - 1, shift, one + 1, mixed))
        for kind, pair in (("up", (second_in, grad_up)), ("down", (grad_low, act))):
            if (layer, kind) in NATIVE:
                native[layer, kind] = reduced_natively(*pair)
            else:
                segments.append((len(lefts), pair[1], 0, FF // half))
                lefts.append(pair[0])
        extras.append((norm_grads, sum(segment[3] for segment in segments)))
        segments.append((one, grad_logit, 0, 1))
    names = list(native)
    begun = segments[-1][1]
    partial, begun = lax.optimization_barrier(([native[name] for name in names], begun))
    segments[-1] = (segments[-1][0], begun) + segments[-1][2:]
    for name, value in zip(names, partial):
        native[name] = value.astype(jnp.float32)
    reduced = reduce_weight_grads(lefts, segments, doubles, extras, CHUNK)
    matrix_rows = [None] * LAYERS
    small_rows = [None] * LAYERS
    for layer in range(LAYERS):
        base = bases[layer]
        rest = [native[layer, kind] for kind in ("up", "down") if (layer, kind) in NATIVE]
        used = output_end + FF * (2 - len(rest))
        matrix_rows[layer] = jnp.concatenate([reduced[:, base : base + used]] + rest, axis=1)
        small_rows[layer] = reduced[:, base + used : base + used + router_cols + 4]
    input_grad = grad_hidden.reshape(seq_count, sub_rows, width).astype(jnp.bfloat16)
    matrix_grad = jnp.stack(matrix_rows, axis=0)
    small_grad = jnp.stack(small_rows, axis=0)
    matrix_new, matrix_first_new, matrix_second_new = adam_update(
        matrix, matrix_grad, matrix_first, matrix_second, column_rates(segment), WEIGHT_DECAY
    )
    small_new, small_first_new, small_second_new = adam_update(
        small, small_grad, small_first, small_second, small_rates(), 0.0
    )
    return (
        output,
        input_grad,
        matrix_grad,
        matrix_new,
        matrix_new.astype(jnp.bfloat16),
        matrix_first_new,
        matrix_second_new,
        small_grad,
        small_new,
        small_new.astype(jnp.bfloat16),
        small_first_new,
        small_second_new,
        loads,
    )


def solution(mesh):
    in_specs = (
        P("dp", ("seq", "head"), None),
        P("dp", ("seq", "head"), None),
        P(None, "dp", ("seq", "head"), None, None, None),
        P("dp"),
        P(None, ("dp", "seq", "head"), None),
        P(None, ("dp", "seq", "head"), None),
        P(None, ("dp", "seq", "head"), None),
        P(None, ("dp", "seq", "head"), None),
        P(None, ("dp", "seq", "head"), None),
        P(None, ("dp", "seq", "head"), None),
    )
    out_specs = (
        P("dp", ("seq", "head"), None),
        P("dp", ("seq", "head"), None),
        P(None, ("dp", "seq", "head"), None),
        P(None, ("dp", "seq", "head"), None),
        P(None, ("dp", "seq", "head"), None),
        P(None, ("dp", "seq", "head"), None),
        P(None, ("dp", "seq", "head"), None),
        P(None, ("dp", "seq", "head"), None),
        P(None, ("dp", "seq", "head"), None),
        P(None, ("dp", "seq", "head"), None),
        P(None, ("dp", "seq", "head"), None),
        P(None, ("dp", "seq", "head"), None),
        P(),
    )
    return jax.shard_map(local, mesh=mesh, in_specs=in_specs, out_specs=out_specs, check_vma=False)
```
